32 devices in a mesh: dp: 8 (over z, y), expert: 4 (over x, core).
Axes of the slice: x: 2, y: 2, z: 4, core: 2. Of those that a mesh axis runs over, the one named last changes fastest.
Arguments:
- tokens: bfloat16 [32768, 768], P(('dp', 'expert')), may hold values from -6 to 6
- cotangent: bfloat16 [32768, 768], P(('dp', 'expert')), may hold values from -6 to 6
- lengths: int32 [32], P(('dp', 'expert')), may hold values from 1 to 1024, 24576 in all
- adapter_ids: int32 [32], P(('dp', 'expert')), may hold values from 0 to 7
- routes: int32 [32768, 2], P(('dp', 'expert')), may hold values from 0 to 11, all different within a row; in each aligned block of 1024 rows (0 to 1023, 1024 to 2047, ...) at most 192 rows name the same one
- prev_logits: float32 [32768, 12], P(('dp', 'expert')), may hold values from -3 to 3
- norm_gains: float32 [2, 768], replicated, may hold values from 0.5 to 1.5
- input_weights: bfloat16 [3, 768, 768], replicated, may hold values from -0.21875 to 0.21875
- output_weight: bfloat16 [768, 768], replicated, may hold values from -1.25 to 1.25
- adapter_down: bfloat16 [4, 768, 128], replicated, may hold values from -0.21875 to 0.21875
- adapter_up: bfloat16 [4, 128, 768], replicated, may hold values from -0.75 to 0.75
- router: bfloat16 [768, 12], replicated, may hold values from -0.15625 to 0.15625
- residual_mix: float32 [12, 12], replicated, may hold values from -1.75 to 1.75
- constant_mix: float32 [768, 4], replicated, may hold values from -0.21875 to 0.21875
- constant_vectors: float32 [2, 768], replicated, may hold values from -5 to 5
- expert_gate: bfloat16 [8, 768, 2048], P('expert'), may hold values from -0.21875 to 0.21875
- expert_up: bfloat16 [8, 768, 2048], P('expert'), may hold values from -0.21875 to 0.21875
- expert_down: bfloat16 [8, 2048, 768], P('expert'), may hold values from -0.125 to 0.125
- expert_adapter_down: bfloat16 [8, 2, 768, 128], P('expert'), may hold values from -0.21875 to 0.21875
- expert_adapter_up: bfloat16 [8, 2, 128, 2048], P('expert'), may hold values from -0.75 to 0.75
- output_adapter_down: bfloat16 [8, 2048, 128], P('expert'), may hold values from -0.125 to 0.125
- output_adapter_up: bfloat16 [8, 128, 768], P('expert'), may hold values from -0.75 to 0.75
Outputs:
- output: bfloat16 [32768, 768], P(('dp', 'expert'))
- input_gradient: bfloat16 [32768, 768], P(('dp', 'expert'))
- adapter_down_gradient: float32 [4, 768, 128], replicated
- adapter_up_gradient: float32 [4, 128, 768], replicated
- expert_adapter_down_gradient: float32 [8, 2, 768, 128], P('expert')
- expert_adapter_up_gradient: float32 [8, 2, 128, 2048], P('expert')
- output_adapter_down_gradient: float32 [8, 2048, 128], P('expert')
- output_adapter_up_gradient: float32 [8, 128, 768], P('expert')
The draws below stay inside these ranges and needn't reach their ends.
Inputs may be any that keep to these rules, and one draw needn't show every extreme that they name: `lengths`: each sequence's valid tokens are the first of its 1024 slots. `routes`: in the rows of one device, each expert number is named at most 192 times.
All inputs are finite; a program needn't handle non-finite values. No bound on the sum of `lengths` on one device may be relied on, other than what follows from the above.
Results may differ from the reference program's by a relative error of at most 0.015.
Values may be sent and summed in bfloat16 or wider, within the bound.
No kernel may reach another device: no remote copies, remote signals or barrier semaphores. Data moves between devices by JAX's collectives and lax.ppermute only.
A program may use at most 384 MiB of HBM per device.

```python
import math
import jax
import jax.numpy as jnp
import numpy as np
from jax import lax

D = 768
HEADS = 12
HD = 64
FF = 2048
EXPERTS = 8
RANK = 16
ADAPTERS = 8
LEN = 1024
SEQS_DEV = 1
NSEQ = 32
TOKENS = 32768
CAP = 192


def plant(values, stream_key, least, top_value):
    spot = [jax.random.randint(jax.random.fold_in(stream_key, axis), (), 0, length) for axis, length in enumerate(values.shape)]
    widest = values.shape.index(max(values.shape))
    neighbour = spot[:widest] + [(spot[widest] + 1) % values.shape[widest]] + spot[widest + 1:]
    return values.at[tuple(spot)].set(least).at[tuple(neighbour)].set(top_value)


def block_levels(stream_key, dims, pieces, low, top_value):
    def one(dim, shards_of):
        heights = jax.random.uniform(jax.random.fold_in(jax.random.fold_in(stream_key, 6), dim), (shards_of,), jnp.float32, low / len(pieces), top_value / len(pieces))
        return jnp.repeat(jnp.exp(heights), dims[dim] // shards_of).reshape((-1,) + (1,) * (len(dims) - dim - 1))

    level = one(*pieces[0])
    for cut in pieces[1:]:
        level = level * one(*cut)
    return level


def profile(amount, total, reach, slope):
    loads = [(1 << 20) // math.isqrt(rank ** slope) + 1 for rank in range(2, amount + 1)]
    spare, given = total - reach - (amount - 1), [1] * (amount - 1)
    while spare > 0:
        free = [i for i in range(amount - 1) if given[i] < reach]
        pool, left = sum([loads[i] for i in free]), spare
        for i in free:
            more = min(reach - given[i], max(1, left * loads[i] // pool), spare)
            given[i] = given[i] + more
            spare = spare - more
    return np.array([reach] + given)


def uneven_parts(stream_key, amount, total, most, slope):
    if amount == 2:
        one = jax.random.randint(stream_key, (), max(1, total - most), min(most, total - 1) + 1)
        return jnp.stack([one, total - one])
    sizes = jnp.asarray(profile(amount, total, most, slope), jnp.int32)
    couples = (amount - 1) // 2
    source_of, receiver = sizes[1:1 + 2 * couples:2], sizes[2:2 + 2 * couples:2]
    slack = jnp.minimum(source_of - 1, most - receiver)
    moved = jax.random.randint(jax.random.fold_in(stream_key, 1), (couples,), 0, 1 << 20) % (slack + 1)
    sizes = sizes.at[1:1 + 2 * couples:2].set(source_of - moved).at[2:2 + 2 * couples:2].set(receiver + moved)
    return sizes[jax.random.permutation(jax.random.fold_in(stream_key, 2), amount)]


def assign_block(key, own, number, rows, count, top, most, slope):
    sequence = jax.random.permutation(key, count)
    crowded, usual = load_shares(count, rows * top, most, slope, True), load_shares(count, rows * top, most, slope, False)
    places = jnp.arange(count)

    def named(tallies, offset_by):
        used = int((tallies > 0).sum())
        fixed = max(1, used // 4)
        passed = fixed + (places - fixed + offset_by * (used - fixed)) % max(1, count - fixed)
        return jnp.zeros((count,), jnp.int32).at[sequence[jnp.where(places < fixed, places, passed)]].set(jnp.asarray(tallies, jnp.int32))

    tallies = jnp.where(number % 4 == 0, named(crowded, number // 4), named(usual, number - number // 4 - 1))
    mixed = jax.random.permutation(jax.random.fold_in(own, 3), count)
    donor, sink = mixed[0:count // 2 * 2:2], mixed[1:count // 2 * 2:2]
    room = jnp.minimum(tallies[donor] - 1, most - tallies[sink]) // 2
    room = jnp.where((donor == sequence[0]) | (sink == sequence[0]) | (tallies[sink] == 0), 0, jnp.maximum(room, 0))
    passed = jax.random.randint(jax.random.fold_in(own, 4), (count // 2,), 0, 1 << 20) % (room + 1)
    tallies = tallies.at[donor].add(-passed).at[sink].add(passed)
    members = jnp.searchsorted(jnp.cumsum(tallies), jnp.arange(rows * top), side="right").astype(jnp.int32)
    listing = members.reshape(top, rows).T
    listing = listing[jax.random.permutation(jax.random.fold_in(own, 1), rows)]
    offset_by = jax.random.randint(jax.random.fold_in(own, 2), (rows, 1), 0, top)
    return jnp.take_along_axis(listing, (jnp.arange(top)[None, :] + offset_by) % top, axis=1)


def load_shares(count, total, bound, lean, full):
    portions = [(1 << 20) // math.isqrt(rank ** lean) + 1 for rank in range(1, count + 1)]
    largest = bound if full else min(bound, max(-(-total // count), total * portions[0] // sum(portions)))
    least = 1 if total - largest >= count - 1 else 0
    given, rest = [largest] + [least] * (count - 1), total - largest - least * (count - 1)
    while rest > 0:
        free = [i for i in range(1, count) if given[i] < largest] or [i for i in range(1, count) if given[i] < bound]
        pool, left = sum([portions[i] for i in free]), rest
        for i in free:
            extra = min(bound - given[i], max(1, left * portions[i] // pool), rest)
            given[i] = given[i] + extra
            rest = rest - extra
    return np.array(given)


def gaussian(stream_key, dims, scale, most, cuts=(), held_as=jnp.bfloat16):
    array = jax.random.normal(stream_key, dims, jnp.float32) * scale
    if len(cuts) > 0:
        array = block_levels(stream_key, dims, cuts, -0.22, 0.18) * array
    return jnp.clip(array, min=-most, max=most).astype(held_as)


def setup_inputs(seed: int = 0) -> dict:
    keys = jax.random.split(jax.random.key(seed), 23)
    tokens = gaussian(keys[0], (TOKENS, D), 1.0, 6.0, ((0, 32),))
    cotangent = gaussian(keys[1], (TOKENS, D), 1.0, 6.0, ((0, 32),))
    lengths = uneven_parts(keys[2], NSEQ, NSEQ * LEN * 3 // 4, LEN, 2).astype(jnp.int32)
    adapter_ids = plant(jax.random.randint(keys[3], (NSEQ,), 0, ADAPTERS), jax.random.fold_in(keys[3], 1), 0, ADAPTERS - 1).astype(jnp.int32)
    routes_keys = jax.random.split(jax.random.fold_in(keys[4], 1), TOKENS // (SEQS_DEV * LEN))
    routes_turns = jax.random.permutation(jax.random.fold_in(keys[4], 3), TOKENS // (SEQS_DEV * LEN))
    routes = jax.vmap(lambda own, number: assign_block(jax.random.fold_in(keys[4], 2), own, number, SEQS_DEV * LEN, EXPERTS + 4, 2, CAP, 1))(routes_keys, routes_turns).reshape((TOKENS, 2))
    prev_logits = gaussian(keys[5], (TOKENS, EXPERTS + 4), 0.5, 3.0, ((0, 32),), jnp.float32)
    norm_gains = jnp.clip(1.0 + 0.1 * jax.random.normal(keys[6], (2, D), jnp.float32), 0.5, 1.5)
    input_weights = gaussian(keys[7], (3, D, D), D ** -0.5, 0.21875)
    output_weight = gaussian(keys[8], (D, D), (D // 32) ** -0.5, 1.25)
    adapter_down = gaussian(keys[9], (4, D, ADAPTERS * RANK), D ** -0.5, 0.21875)
    adapter_up = gaussian(keys[10], (4, ADAPTERS * RANK, D), (4 * RANK) ** -0.5, 0.75)
    router = gaussian(keys[11], (D, EXPERTS + 4), (2 * D) ** -0.5, 0.15625)
    residual_mix = gaussian(keys[12], (EXPERTS + 4, EXPERTS + 4), (EXPERTS + 4) ** -0.5, 1.75, (), jnp.float32)
    constant_mix = gaussian(keys[13], (D, 4), D ** -0.5, 0.21875, (), jnp.float32)
    constant_vectors = gaussian(keys[14], (2, D), 1.0, 5.0, (), jnp.float32)
    expert_gate = gaussian(keys[15], (EXPERTS, D, FF), D ** -0.5, 0.21875, ((0, 4),))
    expert_up = gaussian(keys[16], (EXPERTS, D, FF), D ** -0.5, 0.21875, ((0, 4),))
    expert_down = gaussian(keys[17], (EXPERTS, FF, D), FF ** -0.5, 0.125, ((0, 4),))
    expert_adapter_down = gaussian(keys[18], (EXPERTS, 2, D, ADAPTERS * RANK), D ** -0.5, 0.21875, ((0, 4),))
    expert_adapter_up = gaussian(keys[19], (EXPERTS, 2, ADAPTERS * RANK, FF), (4 * RANK) ** -0.5, 0.75, ((0, 4),))
    output_adapter_down = gaussian(keys[20], (EXPERTS, FF, ADAPTERS * RANK), FF ** -0.5, 0.125, ((0, 4),))
    output_adapter_up = gaussian(keys[21], (EXPERTS, ADAPTERS * RANK, D), (4 * RANK) ** -0.5, 0.75, ((0, 4),))
    return {"tokens": tokens, "cotangent": cotangent, "lengths": lengths, "adapter_ids": adapter_ids, "routes": routes, "prev_logits": prev_logits, "norm_gains": norm_gains, "input_weights": input_weights, "output_weight": output_weight, "adapter_down": adapter_down, "adapter_up": adapter_up, "router": router, "residual_mix": residual_mix, "constant_mix": constant_mix, "constant_vectors": constant_vectors, "expert_gate": expert_gate, "expert_up": expert_up, "expert_down": expert_down, "expert_adapter_down": expert_adapter_down, "expert_adapter_up": expert_adapter_up, "output_adapter_down": output_adapter_down, "output_adapter_up": output_adapter_up}


EPSILON = 1e-06
PRECISE = lax.Precision.HIGHEST

@jax.custom_vjp
def low(v):
    return lax.optimization_barrier(v.astype(jnp.bfloat16)).astype(jnp.float32)

@jax.custom_vjp
def low_back(v):
    return v

def low_keep(v):
    return (low(v), None)

def low_pass(kept, grad):
    return (grad,)

def back_keep(v):
    return (v, None)

def back_low(kept, grad):
    return (low(grad),)
low.defvjp(low_keep, low_pass)
low_back.defvjp(back_keep, back_low)

def lower_both(value_in):
    return low(low_back(value_in))

def matmul(left, right):
    return jnp.dot(left, right, precision=PRECISE)

def mean_scale(value_in):
    return lax.rsqrt(lax.optimization_barrier(jnp.mean(value_in * value_in, axis=-1, keepdims=True)) + EPSILON)

def softmax_last(value_in):
    shifted = jnp.exp(value_in - lax.optimization_barrier(jnp.max(value_in, axis=-1, keepdims=True)))
    return shifted / lax.optimization_barrier(jnp.sum(shifted, axis=-1, keepdims=True))

def turn_tables(length_in, head_width):
    half_width = head_width // 2
    inverse = jnp.exp(jnp.arange(half_width, dtype=jnp.float32) * (-2.0 * math.log(10000.0) / head_width))
    angles = jnp.arange(length_in, dtype=jnp.float32)[:, None] * inverse[None, :]
    angles = jnp.concatenate([angles, angles], axis=1)
    return (jnp.cos(angles), jnp.sin(angles))

def rope_turn(value_in, cosine_table, sine_table):
    half_width = value_in.shape[-1] // 2
    turned = jnp.concatenate([-value_in[..., half_width:], value_in[..., :half_width]], axis=-1)
    return value_in * cosine_table[:, None, :] + turned * sine_table[:, None, :]

def adapter_select(picked, columns):
    return (jnp.arange(columns, dtype=jnp.int32) // RANK == picked[..., None]).astype(jnp.float32)

def attend_one(entries):
    queries, key_rows, values, seq_limit = entries
    positions = jnp.arange(queries.shape[0], dtype=jnp.int32)
    scores = jnp.einsum('qhd,khd->hqk', queries, key_rows, precision=PRECISE) * queries.shape[-1] ** (-0.5)
    scores = low_back(scores)
    allowed = (positions[None, :] <= positions[:, None]) & (positions[None, :] < seq_limit)
    scores = jnp.where(allowed[None], scores, -1e+30)
    probabilities = low(softmax_last(scores))
    return jnp.einsum('hqk,khd->qhd', probabilities, values, precision=PRECISE)

def expert_one(entries):
    rows_in, select_rows, gate_w, up_w, down_w, in_down, in_up, out_down, out_up = entries
    inner_gate = lower_both(select_rows * matmul(rows_in, in_down[0]))
    gate_pre = low_back(matmul(rows_in, gate_w) + matmul(inner_gate, in_up[0]))
    inner_up = lower_both(select_rows * matmul(rows_in, in_down[1]))
    up_pre = low_back(matmul(rows_in, up_w) + matmul(inner_up, in_up[1]))
    activated = low(jax.nn.silu(gate_pre) * up_pre)
    inner_down = lower_both(select_rows * matmul(activated, out_down))
    return lower_both(matmul(activated, down_w) + matmul(inner_down, out_up))

def reference(tokens, cotangent, lengths, adapter_ids, routes, prev_logits, norm_gains, input_weights, output_weight, adapter_down, adapter_up, router, residual_mix, constant_mix, constant_vectors, expert_gate, expert_up, expert_down, expert_adapter_down, expert_adapter_up, output_adapter_down, output_adapter_up):
    tok_count = tokens.shape[0]
    seq_count = lengths.shape[0]
    dev_count = tok_count // (SEQS_DEV * LEN)
    positions = jnp.arange(LEN, dtype=jnp.int32)
    valid = (positions[None, :] < lengths[:, None]).reshape(-1).astype(jnp.float32)
    row_adapter = jnp.repeat(adapter_ids, LEN)
    columns = adapter_down.shape[-1]
    select_all = adapter_select(row_adapter, columns)
    cosine_table, sine_table = turn_tables(LEN, HD)
    live_rows = (routes < EXPERTS) & (valid[:, None] > 0)
    flat_route = routes.reshape(dev_count, -1)
    flat_live = live_rows.reshape(dev_count, -1)
    route_hits = ((flat_route[..., None] == jnp.arange(EXPERTS, dtype=jnp.int32)) & flat_live[..., None]).astype(jnp.int32)
    slot_index = lax.optimization_barrier(jnp.sum((jnp.cumsum(route_hits, axis=1) - 1) * route_hits, axis=2))
    owner_index = jnp.arange(dev_count, dtype=jnp.int32)[:, None]
    slot_spaces = dev_count * CAP
    target = jnp.where(flat_live, flat_route * slot_spaces + owner_index * CAP + slot_index, EXPERTS * slot_spaces).reshape(-1).astype(jnp.int32)
    source = jnp.zeros(EXPERTS * slot_spaces + 1, jnp.int32).at[target].set(jnp.arange(tok_count * 2, dtype=jnp.int32))[:-1]
    filled = jnp.zeros(EXPERTS * slot_spaces + 1, jnp.float32).at[target].set(1.0)[:-1]
    slot_rows = source // 2
    slot_select = adapter_select(row_adapter[slot_rows], columns).reshape(EXPERTS, slot_spaces, columns)
    weights_in = input_weights.astype(jnp.float32)
    weight_out = output_weight.astype(jnp.float32)
    router_f = router.astype(jnp.float32)
    gate_f = expert_gate.astype(jnp.float32)
    up_f = expert_up.astype(jnp.float32)
    down_f = expert_down.astype(jnp.float32)
    route_hot = (routes[..., None] == jnp.arange(EXPERTS + 4, dtype=jnp.int32)).astype(jnp.float32)
    copy_hot = (routes == EXPERTS + 1).astype(jnp.float32)
    const_hot = (routes[..., None] == EXPERTS + 2 + jnp.arange(2, dtype=jnp.int32)).astype(jnp.float32)
    head_shape = (seq_count, LEN, HEADS, HD)

    def forward(x_in, a_down, a_up, e_down, e_up, o_down, o_up):

        def project(index, source_rows, weight):
            inner = lower_both(select_all * matmul(source_rows, a_down[index]))
            return matmul(source_rows, weight) + matmul(inner, a_up[index])
        normed = low(x_in * mean_scale(x_in) * norm_gains[0])
        queries = low_back(project(0, normed, weights_in[0]))
        key_rows = low_back(project(1, normed, weights_in[1]))
        values = lower_both(project(2, normed, weights_in[2])).reshape(head_shape)
        turned_q = low(rope_turn(queries.reshape(head_shape), cosine_table, sine_table))
        turned_k = low(rope_turn(key_rows.reshape(head_shape), cosine_table, sine_table))
        mixed_rows = lax.map(jax.checkpoint(attend_one), (turned_q, turned_k, values, lengths))
        mixed_rows = lower_both(mixed_rows.reshape(tok_count, D))
        hidden = x_in + low_back(project(3, mixed_rows, weight_out))
        expert_in = low(hidden * mean_scale(hidden) * norm_gains[1])
        logits = matmul(expert_in, router_f) + matmul(prev_logits, residual_mix)
        gates = softmax_last(lax.optimization_barrier(jnp.sum(route_hot * logits[:, None, :], axis=-1)))
        const_w = softmax_last(matmul(expert_in, constant_mix).reshape(tok_count, 2, 2))
        const_out = const_w[..., 0:1] * expert_in[:, None, :] + const_w[..., 1:2] * constant_vectors[None]
        local = copy_hot[..., None] * expert_in[:, None, :] + const_hot[..., 0:1] * const_out[:, None, 0] + const_hot[..., 1:2] * const_out[:, None, 1]
        rows_all = low_back(expert_in[slot_rows] * filled[:, None]).reshape(EXPERTS, slot_spaces, D)
        results = lax.map(jax.checkpoint(expert_one), (rows_all, slot_select, gate_f, up_f, down_f, e_down, e_up, o_down, o_up))
        flat_results = jnp.concatenate([results.reshape(-1, D), jnp.zeros((1, D), jnp.float32)], axis=0)
        routed = flat_results[target].reshape(tok_count, 2, D)
        mixture = valid[:, None] * lax.optimization_barrier(jnp.sum(gates[..., None] * (routed + local), axis=1))
        return hidden + mixture
    back_out = cotangent.astype(jnp.float32) * valid[:, None]
    result, pullback = jax.vjp(forward, tokens.astype(jnp.float32), adapter_down.astype(jnp.float32), adapter_up.astype(jnp.float32), expert_adapter_down.astype(jnp.float32), expert_adapter_up.astype(jnp.float32), output_adapter_down.astype(jnp.float32), output_adapter_up.astype(jnp.float32))
    grads = pullback(back_out)
    return (result.astype(jnp.bfloat16), grads[0].astype(jnp.bfloat16), grads[1], grads[2], grads[3], grads[4], grads[5], grads[6])
```

```python
import functools
import math

import jax
import jax.numpy as jnp
import numpy as np
from jax import lax
from jax.experimental import pallas as pl
from jax.experimental.pallas import tpu as pltpu
from jax.sharding import PartitionSpec as P

HEADS = 12
HD = 64
EXPERTS = 8
RANK = 16
CAP = 192
EPSILON = 1e-06
F32 = jnp.float32
BF = jnp.bfloat16
NEG = -1e30
LANES = 128
TILE = 256
FTILE = 512
PAIRS = HEADS // 2
META = 8
MIX_ROW = 16
VECTOR_ROW = 20
TARGET_LANE = 24
KEEP_LANE = 26
PIECE = CAP + META


def mm(left, right):
    return jnp.dot(left, right, preferred_element_type=F32)


def mm_nt(left, right):
    return lax.dot_general(left, right, (((1,), (1,)), ((), ())), preferred_element_type=F32)


def mm_tn(left, right):
    return lax.dot_general(left, right, (((0,), (0,)), ((), ())), preferred_element_type=F32)


def iota(shape, axis):
    return lax.broadcasted_iota(jnp.int32, shape, axis)


def hot(condition):
    return jnp.where(condition, 1.0, 0.0).astype(BF)


def split2(value):
    high = value.astype(BF)
    return high, (value - high.astype(F32)).astype(BF)


def split3(value):
    high = value.astype(BF)
    rest = value - high.astype(F32)
    middle = rest.astype(BF)
    return high, middle, (rest - middle.astype(F32)).astype(BF)


def whole(shape):
    zeros = (0,) * len(shape)
    return pl.BlockSpec(shape, lambda *_: zeros)


def smem():
    return pl.BlockSpec(memory_space=pltpu.SMEM)


def tall(width):
    return pl.BlockSpec((TILE, width), lambda i: (i, 0))


def wide(height):
    return pl.BlockSpec((height, TILE), lambda i: (0, i))


def shape_of(*shape, dtype=BF):
    return jax.ShapeDtypeStruct(shape, dtype)


def cost(flops, nbytes, trans=0):
    return pl.CostEstimate(flops=1, bytes_accessed=1, transcendentals=0)


@functools.lru_cache(maxsize=None)
def turn_tables(length_in):
    half = HD // 2
    inverse = np.exp(
        np.arange(half, dtype=np.float32) * np.float32(-2.0 * math.log(10000.0) / HD)
    ).astype(np.float32)
    angles = np.arange(length_in, dtype=np.float32)[:, None] * inverse[None, :]
    cosine = np.tile(np.cos(angles.astype(np.float64)).astype(np.float32), (1, 4))
    sine = np.sin(angles.astype(np.float64)).astype(np.float32)
    return cosine, np.tile(np.concatenate([-sine, sine], axis=1), (1, 2))


def rope(value, cosine, sine):
    first = iota(value.shape, 1) % HD < HD // 2
    turned = jnp.where(first, pltpu.roll(value, LANES - HD // 2, 1), pltpu.roll(value, HD // 2, 1))
    return value * cosine + turned * sine


def find_slots(length, rows_ref, slot_ref):
    tok_count = slot_ref.shape[1]
    before = hot(iota((TILE, TILE), 0) < iota((TILE, TILE), 1))
    carry = jnp.zeros((2 * EXPERTS, 1), F32)
    for start in range(0, tok_count, TILE):
        span = slice(start, start + TILE)
        expert = iota((2 * EXPERTS, TILE), 0).astype(F32)
        token = iota((2 * EXPERTS, TILE), 1) + start
        named = (rows_ref[12:13, span] == expert) | (rows_ref[13:14, span] == expert)
        hit = named & (token < length) & (expert < EXPERTS)
        hits = jnp.where(hit, 1.0, 0.0)
        slots = mm(hits.astype(BF), before) + carry
        carry = carry + jnp.sum(hits, axis=1, keepdims=True)
        slot_ref[:, span] = jnp.where(hit, slots, -1.0)[:EXPERTS].astype(jnp.int32)


def pick_rows(slot_ref, step, me, local):
    first = jnp.bitwise_xor(step, me) * local
    place = iota((CAP, slot_ref.shape[1]), 0)
    return first, [hot(place == slot_ref[pl.ds(first + index, 1), :]) for index in range(local)]


def store_piece(out_refs, step, other, index, value, start):
    @pl.when(step == other)
    def _():
        out_refs[index][start : start + value.shape[0], :] = value


def route_body(local, group, len_ref, me_ref, rows_ref, source_ref, slot_ref, *out_refs):
    step = pl.program_id(0)

    @pl.when(step == 0)
    def _():
        find_slots(len_ref[0], rows_ref, slot_ref)

    _, chosen = pick_rows(slot_ref, step, me_ref[0], local)
    rows = mm(jnp.concatenate(chosen, axis=0), source_ref[...]).astype(BF)
    for other in range(group):
        store_piece(out_refs, step, other, other, rows, 0)


def route_call(local, group, length, me, rows, source):
    tok_count, width = source.shape
    return pl.pallas_call(
        functools.partial(route_body, local, group),
        grid=(group,),
        in_specs=[smem(), smem(), whole(rows.shape), whole(source.shape)],
        out_specs=[whole((EXPERTS, tok_count))] + [whole((local * CAP, width))] * group,
        out_shape=[shape_of(EXPERTS, tok_count, dtype=jnp.int32)]
        + [shape_of(local * CAP, width)] * group,
        cost_estimate=cost(2 * EXPERTS * CAP * tok_count * width, 6e6),
        name="route_rows",
    )(length, me, rows, source)


def send_body(local, group, me_ref, id_ref, slot_ref, data_ref, source_ref, *out_refs):
    step = pl.program_id(0)
    width = source_ref.shape[1]
    first, chosen = pick_rows(slot_ref, step, me_ref[0], local)
    rows = mm(jnp.concatenate(chosen, axis=0), source_ref[...]).astype(BF)
    for index in range(local):
        pieces = split3(data_ref[pl.ds(first + index, 1), :])
        stack = jnp.concatenate(
            [piece.astype(F32) for piece in pieces]
            + [jnp.zeros((13, chosen[index].shape[1]), F32)],
            axis=0,
        ).astype(BF)
        gates = mm_nt(stack, chosen[index])[0:META]
        gates = jnp.where(iota(gates.shape, 0) == 3, id_ref[0].astype(F32), gates)
        meta = jnp.concatenate([gates, jnp.zeros((META, width - CAP), F32)], axis=1)
        kept = rows[index * CAP : index * CAP + CAP]
        for other in range(group):
            far = other >= group // 2
            place = group // 2 + (other - group // 2) * local + index if far else other
            start = 0 if far else index * PIECE
            store_piece(out_refs, step, other, place, kept, start)
            store_piece(out_refs, step, other, place, meta.astype(BF), start + CAP)


def send_call(local, group, me, ids, slots, data, source):
    tok_count, width = source.shape
    heights = [local * PIECE] * (group // 2) + [PIECE] * ((group - group // 2) * local)
    return pl.pallas_call(
        functools.partial(send_body, local, group),
        grid=(group,),
        in_specs=[smem(), smem(), whole(slots.shape), whole(data.shape), whole(source.shape)],
        out_specs=[whole((height, width)) for height in heights],
        out_shape=[shape_of(height, width) for height in heights],
        cost_estimate=cost(2 * EXPERTS * CAP * tok_count * width, 6e6),
        name="send_rows",
    )(me, ids, slots, data, source)


def pre_body(
    id_ref, x_ref, gain_ref, w_ref, ad_ref, au_ref, cos_ref, sin_ref, small_ref, vec_ref,
    normed_ref, inner_ref, q_ref, k_ref, v_ref, acat_ref, bcat_ref, table_ref,
):
    @pl.when(pl.program_id(0) == 0)
    def _():
        first = RANK * id_ref[0]
        total = None
        for index in range(4):
            row, column = iota((LANES, LANES), 0), iota((LANES, LANES), 1)
            place = hot((row >= first) & (row < first + RANK) & (column == (row - first) * 4 + index))
            part = mm(ad_ref[index], place)
            total = part if total is None else total + part
            place = hot(
                (column >= first) & (column < first + RANK) & (row == (column - first) * 4 + index)
            )
            bcat_ref[index] = mm(place, au_ref[index]).astype(BF)
        acat_ref[...] = total.astype(BF)
        table = small_ref[...].T
        number = iota(table.shape, 0)
        for index in range(2):
            table = jnp.where(number == VECTOR_ROW + index, vec_ref[index : index + 1, :], table)
        table_ref[...] = table

    x = x_ref[...].astype(F32)
    scale = lax.rsqrt(jnp.mean(x * x, axis=-1, keepdims=True) + EPSILON)
    normed = (x * scale * gain_ref[0:1, :]).astype(BF)
    normed_ref[...] = normed
    inner = mm(normed, acat_ref[...]).astype(BF)
    inner_ref[...] = inner
    for index, out_ref in enumerate((q_ref, k_ref, v_ref)):
        value = mm(normed, w_ref[index]) + mm(inner, bcat_ref[index])
        if index == 2:
            out_ref[...] = value.astype(BF)
            continue
        for pair in range(PAIRS):
            span = slice(pair * LANES, pair * LANES + LANES)
            turned = rope(value[:, span], cos_ref[...], sin_ref[...]).astype(BF)
            if index == 0:
                turned = (turned.astype(F32) * HD**-0.5).astype(BF)
            out_ref[:, span] = turned


def pre_call(ids, tokens, gains, weights, down, upper, cosine, sine, small, vectors):
    tok_count, width = tokens.shape
    return pl.pallas_call(
        pre_body,
        grid=(tok_count // TILE,),
        in_specs=[
            smem(), tall(width), whole(gains.shape), whole(weights.shape), whole(down.shape),
            whole(upper.shape), tall(LANES), tall(LANES), whole(small.shape), whole(vectors.shape),
        ],
        out_specs=[
            tall(width), tall(LANES), tall(width), tall(width), tall(width),
            whole((width, LANES)), whole(upper.shape), whole((LANES, width)),
        ],
        out_shape=[
            shape_of(tok_count, width), shape_of(tok_count, LANES), shape_of(tok_count, width),
            shape_of(tok_count, width), shape_of(tok_count, width), shape_of(width, LANES),
            shape_of(*upper.shape), shape_of(LANES, width, dtype=F32),
        ],
        cost_estimate=cost(2 * tok_count * width * width * 3.5, 14e6),
        name="before_attention",
    )(ids, tokens, gains, weights, down, upper, cosine, sine, small, vectors)


def attend_body(len_ref, q_ref, k_ref, v_ref, mixed_ref, q2_ref):
    tok_count = q_ref.shape[0]
    lane = iota((tok_count, LANES), 1)
    position = iota((tok_count, LANES), 0)
    bias = jnp.where(position < len_ref[0], 0.0, NEG)
    causal = iota((TILE, TILE), 1) <= iota((TILE, TILE), 0)
    lane_tile = lane[:TILE]
    outs = [[], []]
    for head in range(2):
        own = lane // HD == head
        spare = HD * (1 - head)
        one = jnp.where(lane == spare, 1.0, 0.0)
        queries = jnp.where(own, q_ref[...].astype(F32), one)
        keys = jnp.where(
            own, k_ref[...].astype(F32), jnp.where(lane == spare, bias, 0.0)
        ).astype(BF)
        values = jnp.where(own, v_ref[...].astype(F32), one).astype(BF)
        for start in range(0, tok_count, TILE):
            stop = start + TILE
            part = queries[start:stop]
            scores = mm_nt(part.astype(BF), keys[:stop])
            diagonal = jnp.where(causal, scores[:, start:], NEG)
            scores = diagonal if start == 0 else jnp.concatenate([scores[:, :start], diagonal], axis=1)
            top = jnp.max(scores, axis=-1, keepdims=True)
            weights = jnp.exp(scores - top).astype(BF)
            mixed = mm(weights, values[:stop])
            total = mixed[:, spare : spare + 1]
            outs[head].append(mixed / total)
            log_total = top + jnp.log(total)
            high, middle, low = split3(log_total)
            kept = part
            for offset, piece in enumerate((high, middle, low)):
                kept = jnp.where(lane_tile == spare + 1 + offset, piece.astype(F32), kept)
            q2_ref[start:stop, head * LANES : head * LANES + LANES] = kept.astype(BF)
    for index, start in enumerate(range(0, tok_count, TILE)):
        mixed_ref[start : start + TILE, :] = jnp.where(
            lane_tile < HD, outs[0][index], outs[1][index]
        ).astype(BF)


def attend_call(length, queries, keys, values):
    tok_count, width = queries.shape
    column = pl.BlockSpec((tok_count, LANES), lambda i: (0, i))
    return pl.pallas_call(
        attend_body,
        grid=(PAIRS,),
        in_specs=[smem(), column, column, column],
        out_specs=[column, pl.BlockSpec((tok_count, 2 * LANES), lambda i: (0, i))],
        out_shape=[shape_of(tok_count, width), shape_of(tok_count, 2 * width)],
        cost_estimate=cost(
            2.5 * tok_count * tok_count * width, 9e6, 0.6 * HEADS * tok_count * tok_count
        ),
        name="attention_forward",
    )(length, queries, keys, values)


def attend_back_body(
    len_ref, q2_ref, k_ref, v_ref, mixed_ref, back_ref, cos_ref, sin_ref,
    dq_ref, dk_ref, dv_ref, acc_ref,
):
    tok_count = k_ref.shape[0]
    lane = iota((tok_count, LANES), 1)
    position = iota((tok_count, LANES), 0)
    bias = jnp.where(position < len_ref[0], 0.0, NEG)
    causal = iota((TILE, TILE), 0) <= iota((TILE, TILE), 1)
    back = back_ref[...].astype(F32)
    product = back * mixed_ref[...].astype(F32)
    grads = []
    for head in range(2):
        own = lane // HD == head
        spare = HD * (1 - head)
        minus = jnp.where((lane > spare) & (lane < spare + 4), -1.0, 0.0)
        q2 = q2_ref[:, head * LANES : head * LANES + LANES]
        k2f = jnp.where(
            own, k_ref[...].astype(F32), jnp.where(lane == spare, bias, minus)
        )
        k2 = k2f.astype(BF)
        k2t = k2f.T.astype(BF)
        v2 = jnp.where(own, v_ref[...].astype(F32), minus).astype(BF)
        delta = jnp.sum(jnp.where(own, product, 0.0), axis=-1, keepdims=True)
        back2 = jnp.where(own, back, 0.0)
        for offset, piece in enumerate(split3(delta)):
            back2 = jnp.where(lane == spare + 1 + offset, piece.astype(F32), back2)
        back2 = back2.astype(BF)
        dk_parts, dv_parts = [], []
        for start in range(0, tok_count, TILE):
            stop = start + TILE
            scores = mm_nt(k2[start:stop], q2[start:])
            slopes = mm_nt(v2[start:stop], back2[start:])
            diagonal = jnp.where(causal, scores[:, :TILE], NEG)
            scores = (
                diagonal
                if stop == tok_count
                else jnp.concatenate([diagonal, scores[:, TILE:]], axis=1)
            )
            weights = jnp.exp(scores)
            turned = (weights * slopes).astype(BF)
            dv_parts.append(mm(weights.astype(BF), back2[start:]))
            dk_parts.append(mm(turned, q2[start:]))
            update = mm(k2t[:, start:stop], turned)
            if start == 0:
                acc_ref[head] = update
            else:
                acc_ref[head, :, start:] += update
        grads.append((jnp.concatenate(dk_parts, axis=0), jnp.concatenate(dv_parts, axis=0)))
    low_lane = lane < HD
    cosine, sine = cos_ref[...], -sin_ref[...]
    row = iota((LANES, tok_count), 0)
    dq = jnp.where(row < HD, acc_ref[0], acc_ref[1]).T * HD**-0.5
    dq_ref[...] = rope(dq, cosine, sine).astype(BF)
    dk = jnp.where(low_lane, grads[0][0], grads[1][0])
    dk_ref[...] = rope(dk, cosine, sine).astype(BF)
    dv_ref[...] = jnp.where(low_lane, grads[0][1], grads[1][1]).astype(BF)


def attend_back_call(length, q2, keys, values, mixed, back, cosine, sine):
    tok_count, width = keys.shape
    column = pl.BlockSpec((tok_count, LANES), lambda i: (0, i))
    return pl.pallas_call(
        attend_back_body,
        grid=(PAIRS,),
        in_specs=[
            smem(), pl.BlockSpec((tok_count, 2 * LANES), lambda i: (0, i)), column, column, column,
            column, whole(cosine.shape), whole(sine.shape),
        ],
        out_specs=[column] * 3,
        out_shape=[shape_of(tok_count, width)] * 3,
        scratch_shapes=[pltpu.VMEM((2, LANES, tok_count), F32)],
        cost_estimate=cost(
            6 * tok_count * tok_count * width, 14e6, 0.6 * HEADS * tok_count * tok_count
        ),
        name="attention_backward",
    )(length, q2, keys, values, mixed, back, cosine, sine)


def post_body(
    local, group, me_ref, mixed_ref, x_ref, wo_ref, acat_ref, bcat_ref, gain_ref, table_ref, mix_ref,
    rows_ref, slot_ref, hidden_ref, ei_ref, inner_ref, data_ref, cols_ref,
):
    mixed = mixed_ref[...]
    inner = mm(mixed, acat_ref[...]).astype(BF)
    inner_ref[...] = inner
    hidden = x_ref[...].astype(F32) + (mm(mixed, wo_ref[...]) + mm(inner, bcat_ref[0]))
    hidden_ref[...] = hidden
    scale = lax.rsqrt(jnp.mean(hidden * hidden, axis=-1, keepdims=True) + EPSILON)
    ei = (hidden * scale * gain_ref[1:2, :]).astype(BF)
    ei_ref[...] = ei
    read = None
    for piece in split3(table_ref[...]):
        part = mm_nt(piece, ei)
        read = part if read is None else read + part
    logits = read[0:16]
    for index in range(EXPERTS + 4):
        logits = logits + mix_ref[:, index : index + 1] * rows_ref[index : index + 1, :]
    first, second = rows_ref[12:13, :], rows_ref[13:14, :]
    number = iota((16, TILE), 0).astype(F32)
    one = jnp.sum(jnp.where(number == first, logits, 0.0), axis=0, keepdims=True)
    two = jnp.sum(jnp.where(number == second, logits, 0.0), axis=0, keepdims=True)
    top = jnp.maximum(one, two)
    one, two = jnp.exp(one - top), jnp.exp(two - top)
    gate_a, gate_b = one / (one + two), two / (one + two)
    mixes = read[MIX_ROW : MIX_ROW + 4]
    shares = []
    for index in range(2):
        left, right = mixes[2 * index : 2 * index + 1], mixes[2 * index + 1 : 2 * index + 2]
        top = jnp.maximum(left, right)
        left, right = jnp.exp(left - top), jnp.exp(right - top)
        shares += [left / (left + right), right / (left + right)]

    def both(value):
        return jnp.where(first == value, gate_a, 0.0) + jnp.where(second == value, gate_b, 0.0)

    gates = jnp.where(number == first, gate_a, 0.0) + jnp.where(number == second, gate_b, 0.0)
    beta_a, beta_b = both(EXPERTS + 2.0), both(EXPERTS + 3.0)
    keep = both(EXPERTS + 1.0) + beta_a * shares[0] + beta_b * shares[2]
    data_ref[0:8, :] = gates[0:8]
    tail = [gate_a, gate_b] + shares + [beta_a, beta_b]
    data_ref[8:16, :] = jnp.concatenate(tail, axis=0)
    slots = slot_ref[...].astype(F32)
    expert = iota((EXPERTS, TILE), 0)
    partner = jnp.bitwise_xor(expert // local, me_ref[0])
    base = ((expert % local) * (group * CAP) + partner * CAP).astype(F32)
    place = jnp.where(slots >= 0, slots + base + 1.0, 0.0)
    expert = expert.astype(F32)
    target_a = jnp.sum(jnp.where(expert == first, place, 0.0), axis=0, keepdims=True) - 1.0
    target_b = jnp.sum(jnp.where(expert == second, place, 0.0), axis=0, keepdims=True) - 1.0
    stack = jnp.concatenate(
        [jnp.zeros((VECTOR_ROW, TILE), F32), beta_a * shares[1], beta_b * shares[3]]
        + [jnp.zeros((2, TILE), F32), target_a, target_b, keep]
        + [jnp.zeros((LANES - KEEP_LANE - 1, TILE), F32)],
        axis=0,
    )
    cols_ref[...] = stack.T


def post_call(
    local, group, me, mixed, tokens, weight, acat, bcat, gains, table, mixer, rows, slots
):
    tok_count, width = tokens.shape
    return pl.pallas_call(
        functools.partial(post_body, local, group),
        grid=(tok_count // TILE,),
        in_specs=[
            smem(), tall(width), tall(width), whole(weight.shape), whole(acat.shape),
            pl.BlockSpec((1, LANES, width), lambda i: (3, 0, 0)), whole(gains.shape),
            whole(table.shape), whole(mixer.shape), wide(16), wide(EXPERTS),
        ],
        out_specs=[tall(width), tall(width), tall(LANES), wide(16), tall(LANES)],
        out_shape=[
            shape_of(tok_count, width, dtype=F32), shape_of(tok_count, width),
            shape_of(tok_count, LANES), shape_of(16, tok_count, dtype=F32),
            shape_of(tok_count, LANES, dtype=F32),
        ],
        cost_estimate=cost(2 * tok_count * width * width * 1.5, 11e6),
        name="after_attention",
    )(me, mixed, tokens, weight, acat, bcat, gains, table, mixer, rows, slots)


def expert_body(
    pair, per_owner, group, steps, has_grad, *refs
):
    count = len(pair)
    piece_refs, refs = refs[:count], refs[count:]
    cot_refs, refs = refs[:count], refs[count:]
    wg_ref, wu_ref, wd_ref, dn_ref, up_ref, od_ref, ou_ref = refs[:7]
    refs = refs[7:]
    before_ref = None
    if has_grad:
        before_ref, refs = refs[0], refs[1:]
    back_refs, refs = refs[:count], refs[count:]
    out_refs, refs = refs[:count], refs[count:]
    (
        grad_ref, x_ref, g_ref, gate_ref, pick_ref, dr_ref, zg_ref, zu_ref, dzd_ref, zgt_ref, zut_ref,
        dzdt_ref, racc_ref, xacc_ref, zd_acc, dzg_acc, dzu_acc, h_ref, dg_ref, du_ref,
    ) = refs
    step = pl.program_id(0)
    rows, width = x_ref.shape
    compact = group * RANK
    chosen = pick_ref[...] > 0.0

    def fold(value):
        place = iota((compact, LANES), 0)
        block = per_owner * group
        inner = place // block * per_owner + place % per_owner
        folded = mm_nt(hot(iota((compact, LANES), 1) % RANK == inner), value)
        place = iota((compact, rows), 0)
        owner = place % block // per_owner
        mine = iota((compact, rows), 1) // CAP + pair[0]
        return jnp.where(mine == owner, folded, 0.0).astype(BF)

    def put(start, value):
        span = pl.ds(start, value.shape[1])
        if has_grad:
            value = value + before_ref[:, span].astype(F32)
        grad_ref[:, span] = value.astype(BF)

    @pl.when(step == 0)
    def _():
        for index in range(count):
            span = slice(index * CAP, index * CAP + CAP)
            x_ref[span] = piece_refs[index][0:CAP]
            g_ref[span] = cot_refs[index][...]
            meta = piece_refs[index][CAP:PIECE].astype(F32)
            gate = (meta[0:1] + meta[1:2] + meta[2:3])[:, 0 : 2 * LANES]
            gate_ref[span] = jnp.broadcast_to(gate, (LANES, 2 * LANES)).T[0:CAP]
            lane = (iota((CAP, LANES), 1) // RANK).astype(F32)
            pick_ref[span] = jnp.where(lane == meta[3:4, 0:LANES], 1.0, 0.0)
        picked = pick_ref[...] > 0.0
        dr = (gate_ref[:, 0:1] * g_ref[...].astype(F32)).astype(BF)
        dr_ref[...] = dr
        zg = jnp.where(picked, mm(x_ref[...], dn_ref[0]), 0.0).astype(BF)
        zu = jnp.where(picked, mm(x_ref[...], dn_ref[1]), 0.0).astype(BF)
        dzd = jnp.where(picked, mm_nt(dr, ou_ref[...]), 0.0).astype(BF)
        zg_ref[...] = zg
        zu_ref[...] = zu
        dzd_ref[...] = dzd
        zgt_ref[...] = fold(zg)
        zut_ref[...] = fold(zu)
        dzdt_ref[...] = fold(dzd)
        for ref in (racc_ref, xacc_ref, zd_acc, dzg_acc, dzu_acc):
            ref[...] = jnp.zeros_like(ref)

    gate = mm(x_ref[...], wg_ref[...]) + mm(zg_ref[...], up_ref[0])
    upper = mm(x_ref[...], wu_ref[...]) + mm(zu_ref[...], up_ref[1])
    share = 0.5 * jnp.tanh(0.5 * gate) + 0.5
    silu = gate * share
    active = (silu * upper).astype(BF)
    h_ref[...] = active
    back = mm_nt(dr_ref[...], wd_ref[...]) + mm_nt(dzd_ref[...], od_ref[...])
    du = (back * silu).astype(BF)
    dg = (back * upper * (share + silu * (1.0 - share))).astype(BF)
    du_ref[...] = du
    dg_ref[...] = dg
    racc_ref[...] += mm(active, wd_ref[...])
    zd_acc[...] += mm(active, od_ref[...])
    xacc_ref[...] += mm_nt(dg, wg_ref[...]) + mm_nt(du, wu_ref[...])
    dzg_acc[...] += mm_nt(dg, up_ref[0])
    dzu_acc[...] += mm_nt(du, up_ref[1])
    tile = h_ref.shape[1]
    total = steps * tile
    at = pl.multiple_of(step * tile, tile)
    put(at, mm(zgt_ref[...], dg_ref[...]))
    put(total + at, mm(zut_ref[...], du_ref[...]))
    put(2 * total + at, mm(dzdt_ref[...], h_ref[...]))

    @pl.when(step == steps - 1)
    def _():
        zd = jnp.where(chosen, zd_acc[...], 0.0).astype(BF)
        dzg = jnp.where(chosen, dzg_acc[...], 0.0).astype(BF)
        dzu = jnp.where(chosen, dzu_acc[...], 0.0).astype(BF)
        result = racc_ref[...] + mm(zd, ou_ref[...])
        gated = (gate_ref[:, 0:1] * result).astype(BF)
        product = g_ref[...].astype(F32) * result.astype(BF).astype(F32)
        dots = jnp.broadcast_to(jnp.sum(product, axis=-1, keepdims=True), (rows, LANES))
        back_rows = (xacc_ref[...] + mm_nt(dzg, dn_ref[0]) + mm_nt(dzu, dn_ref[1])).astype(BF)
        for index in range(count):
            span = slice(index * CAP, index * CAP + CAP)
            out_refs[index][...] = gated[span]
            back_refs[index][0:CAP, :] = back_rows[span]
            column = jnp.concatenate(
                [dots[span], jnp.zeros((2 * LANES - CAP, LANES), F32)], axis=0
            ).T[0:1]
            meta = jnp.concatenate(
                [piece.astype(F32) for piece in split3(column)]
                + [jnp.zeros((META - 3, 2 * LANES), F32)],
                axis=0,
            )
            meta = jnp.concatenate([meta, jnp.zeros((META, width - 2 * LANES), F32)], axis=1)
            back_refs[index][CAP:PIECE, :] = meta.astype(BF)
        base = 3 * total
        put(base, mm(fold(zd), dr_ref[...]))
        put(base + width, mm(fold(dzg), x_ref[...]))
        put(base + 2 * width, mm(fold(dzu), x_ref[...]))


def expert_call(index, pair, group, per_owner, pieces, cots, before, weights):
    gate_w, up_w, down_w, in_down, in_up, out_down, out_up = weights
    width, hidden = gate_w.shape[1:]
    rows = len(pair) * CAP
    steps = hidden // FTILE
    columns = 3 * hidden + 3 * width
    compact = group * RANK
    has_grad = before is not None
    return pl.pallas_call(
        functools.partial(expert_body, pair, per_owner, group, steps, has_grad),
        grid=(steps,),
        in_specs=[
            pl.BlockSpec((PIECE, width), lambda f, row=piece.shape[0] // PIECE > 1: (index * row, 0))
            for piece in pieces
        ]
        + [pl.BlockSpec((CAP, width), lambda f: (index, 0))] * len(pair)
        + [
            pl.BlockSpec((None, width, FTILE), lambda f: (index, 0, f)),
            pl.BlockSpec((None, width, FTILE), lambda f: (index, 0, f)),
            pl.BlockSpec((None, FTILE, width), lambda f: (index, f, 0)),
            pl.BlockSpec((None, 2, width, LANES), lambda f: (index, 0, 0, 0)),
            pl.BlockSpec((None, 2, LANES, FTILE), lambda f: (index, 0, 0, f)),
            pl.BlockSpec((None, FTILE, LANES), lambda f: (index, f, 0)),
            pl.BlockSpec((None, LANES, width), lambda f: (index, 0, 0)),
        ]
        + [whole((compact, columns))] * has_grad,
        out_specs=[whole((PIECE, width))] * len(pair)
        + [whole((CAP, width))] * len(pair)
        + [whole((compact, columns))],
        out_shape=[shape_of(PIECE, width)] * len(pair)
        + [shape_of(CAP, width)] * len(pair)
        + [shape_of(compact, columns)],
        scratch_shapes=[pltpu.VMEM((rows, width), BF)] * 2
        + [pltpu.VMEM((rows, LANES), F32)] * 2
        + [pltpu.VMEM((rows, width), BF)]
        + [pltpu.VMEM((rows, LANES), BF)] * 3
        + [pltpu.VMEM((compact, rows), BF)] * 3
        + [pltpu.VMEM((rows, width), F32)] * 2
        + [pltpu.VMEM((rows, LANES), F32)] * 3
        + [pltpu.VMEM((rows, FTILE), BF)] * 3,
        cost_estimate=cost(2 * rows * width * hidden * 8, 16e6, rows * hidden),
        name="expert_layer",
    )(
        *pieces, *cots, gate_w, up_w, down_w, in_down, in_up, out_down, out_up,
        *([before] if has_grad else []),
    )


def spread(cols_ref, index, count):
    return iota((TILE, count), 1).astype(F32) == cols_ref[:, index : index + 1]


def combine_body(
    pieces, len_ref, *refs
):
    back_refs = refs[:pieces]
    (
        rows_ref, data_ref, cols_ref, cot_ref, ei_ref, hidden_ref, gain_ref, wo_ref, acat_ref, bcat_ref,
        table_ref, bh_ref, ba_ref, din_ref, bm_ref, back_all, dots_ref,
    ) = refs[pieces:]
    count = pieces * CAP

    @pl.when(pl.program_id(0) == 0)
    def _():
        for index, back_ref in enumerate(back_refs):
            back_all[index * CAP : index * CAP + CAP, :] = back_ref[0:CAP, :]
        dots = [back_ref[CAP:PIECE, 0:CAP].astype(F32) for back_ref in back_refs]
        dots = jnp.concatenate(dots, axis=1)
        dots_ref[...] = jnp.concatenate([dots, jnp.zeros_like(dots)], axis=0).astype(BF)

    chosen_a = hot(spread(cols_ref, TARGET_LANE, count))
    chosen_b = hot(spread(cols_ref, TARGET_LANE + 1, count))
    stack = dots_ref[...]
    routed_a = jnp.sum(mm_nt(stack, chosen_a)[0:8], axis=0, keepdims=True)
    routed_b = jnp.sum(mm_nt(stack, chosen_b)[0:8], axis=0, keepdims=True)
    cot = cot_ref[...]
    cot_f = cot.astype(F32)
    high, low = split2(cot_f * ei_ref[...].astype(F32))
    ones = jnp.ones((16, cot.shape[1]), BF)
    along_x = (mm_nt(ones, high) + mm_nt(ones, low))[0:1]
    table_high, table_middle, table_low = split3(table_ref[...])
    along_c = mm_nt(table_high, cot) + mm_nt(table_middle, cot) + mm_nt(table_low, cot)
    along_a = along_c[VECTOR_ROW : VECTOR_ROW + 1]
    along_b = along_c[VECTOR_ROW + 1 : VECTOR_ROW + 2]
    first, second = rows_ref[12:13, :], rows_ref[13:14, :]
    token = iota((1, TILE), 1) + pl.program_id(0) * TILE
    valid = jnp.where(token < len_ref[0], 1.0, 0.0)
    gate_a, gate_b = data_ref[8:9, :], data_ref[9:10, :]
    share = [data_ref[index : index + 1, :] for index in range(10, 14)]
    beta_a, beta_b = data_ref[14:15, :], data_ref[15:16, :]
    const_a = share[0] * along_x + share[1] * along_a
    const_b = share[2] * along_x + share[3] * along_b

    def here(route):
        return (
            jnp.where(route == EXPERTS + 1.0, along_x, 0.0)
            + jnp.where(route == EXPERTS + 2.0, const_a, 0.0)
            + jnp.where(route == EXPERTS + 3.0, const_b, 0.0)
        )

    dot_a, dot_b = routed_a + here(first), routed_b + here(second)
    mean = gate_a * dot_a + gate_b * dot_b
    chosen_grad_a = valid * gate_a * (dot_a - mean)
    chosen_grad_b = valid * gate_b * (dot_b - mean)
    number = iota((16, TILE), 0).astype(F32)
    logit_grads = jnp.where(number == first, chosen_grad_a, 0.0) + jnp.where(
        number == second, chosen_grad_b, 0.0
    )
    mixes = []
    for index, (beta, along) in enumerate(((beta_a, along_a), (beta_b, along_b))):
        left, right = share[2 * index], share[2 * index + 1]
        weighted = left * along_x + right * along
        mixes += [
            valid * beta * left * (along_x - weighted),
            valid * beta * right * (along - weighted),
        ]
    stack = jnp.concatenate(
        [logit_grads] + mixes + [jnp.zeros((LANES - 20, TILE), F32)], axis=0
    ).T
    high, low = split2(stack)
    inside = iota((TILE, 1), 0) + pl.program_id(0) * TILE < len_ref[0]
    grad = jnp.where(inside, cot_f, 0.0)
    back = mm(high, table_high) + mm(low, table_high) + mm(high, table_middle)
    back = back + cols_ref[:, KEEP_LANE : KEEP_LANE + 1] * grad
    back = back + mm(chosen_a + chosen_b, back_all[...])
    hidden = hidden_ref[...]
    scale = lax.rsqrt(jnp.mean(hidden * hidden, axis=-1, keepdims=True) + EPSILON)
    normed = hidden * scale
    back = back * gain_ref[1:2, :]
    back = grad + scale * (back - normed * jnp.mean(back * normed, axis=-1, keepdims=True))
    bh_ref[...] = back
    rounded = back.astype(BF)
    ba_ref[...] = rounded
    inner = mm_nt(rounded, bcat_ref[0]).astype(BF)
    din_ref[...] = inner
    bm_ref[...] = (mm_nt(rounded, wo_ref[...]) + mm_nt(inner, acat_ref[...])).astype(BF)


def combine_call(
    length, backs, rows, data, cols, cotangent, ei, hidden, gains, weight, acat, bcat, table
):
    tok_count, width = cotangent.shape
    pieces = len(backs)
    return pl.pallas_call(
        functools.partial(combine_body, pieces),
        grid=(tok_count // TILE,),
        in_specs=[smem()] + [whole(back.shape) for back in backs] + [
            wide(16), wide(16), tall(LANES), tall(width), tall(width), tall(width),
            whole(gains.shape), whole(weight.shape), whole(acat.shape),
            pl.BlockSpec((1, LANES, width), lambda i: (3, 0, 0)), whole(table.shape),
        ],
        out_specs=[tall(width), tall(width), tall(LANES), tall(width)],
        out_shape=[
            shape_of(tok_count, width, dtype=F32), shape_of(tok_count, width),
            shape_of(tok_count, LANES), shape_of(tok_count, width),
        ],
        scratch_shapes=[
            pltpu.VMEM((pieces * CAP, width), BF), pltpu.VMEM((2 * META, pieces * CAP), BF)
        ],
        cost_estimate=cost(2 * tok_count * width * width * 4, 18e6),
        name="combine_backward",
    )(
        length, *backs, rows, data, cols, cotangent, ei, hidden, gains, weight, acat, bcat, table
    )


def result_body(pieces, len_ref, *refs):
    result_refs = refs[:pieces]
    cols_ref, ei_ref, hidden_ref, table_ref, out_ref, result_all = refs[pieces:]
    count = pieces * CAP

    @pl.when(pl.program_id(0) == 0)
    def _():
        for index, result_ref in enumerate(result_refs):
            result_all[index * CAP : index * CAP + CAP, :] = result_ref[...]

    both = hot(
        spread(cols_ref, TARGET_LANE, count) | spread(cols_ref, TARGET_LANE + 1, count)
    )
    cols = cols_ref[...]
    high, low = split2(cols)
    table_high, table_low = split2(table_ref[...])
    mixture = mm(high, table_high) + mm(low, table_high) + mm(high, table_low)
    mixture = mixture + cols[:, KEEP_LANE : KEEP_LANE + 1] * ei_ref[...].astype(F32)
    mixture = mixture + mm(both, result_all[...])
    inside = iota((TILE, 1), 0) + pl.program_id(0) * TILE < len_ref[0]
    out_ref[...] = (hidden_ref[...] + jnp.where(inside, mixture, 0.0)).astype(BF)


def result_call(length, results, cols, ei, hidden, table):
    tok_count, width = ei.shape
    pieces = len(results)
    return pl.pallas_call(
        functools.partial(result_body, pieces),
        grid=(tok_count // TILE,),
        in_specs=[smem()] + [whole(result.shape) for result in results] + [
            tall(LANES), tall(width), tall(width), whole(table.shape),
        ],
        out_specs=tall(width),
        out_shape=shape_of(tok_count, width),
        scratch_shapes=[pltpu.VMEM((pieces * CAP, width), BF)],
        cost_estimate=cost(2 * tok_count * width * width * 2, 10e6),
        name="layer_output",
    )(length, *results, cols, ei, hidden, table)


def last_body(
    packed, dq_ref, dk_ref, dv_ref, w_ref, acat_ref, bcat_ref, normed_ref, inner_ref, mixed_ref, inner_o_ref,
    ba_ref, din_ref, x_ref, bh_ref, gain_ref, out_ref, grad_ref, acc_ref,
):
    step = pl.program_id(0)
    width = x_ref.shape[1]
    count = 4 * RANK

    @pl.when(step == 0)
    def _():
        acc_ref[...] = jnp.zeros_like(acc_ref)

    total = None
    inner_t = inner_ref[...].astype(F32).T[0:count].astype(BF)
    outer_t = inner_o_ref[...].astype(F32).T[0:count].astype(BF)
    number = iota((count, width), 0) % 4
    upper = mm(outer_t, ba_ref[...])
    back_inner = din_ref[...].astype(F32)
    for index, ref in enumerate((dq_ref, dk_ref, dv_ref)):
        value = ref[...]
        part = mm_nt(value, w_ref[index])
        total = part if total is None else total + part
        back_inner = back_inner + mm_nt(value, bcat_ref[index]).astype(BF).astype(F32)
        upper = jnp.where(number == index, mm(inner_t, value), upper)
    own = iota(back_inner.shape, 1) % 4 < 3
    total = total + mm_nt(jnp.where(own, back_inner, 0.0).astype(BF), acat_ref[...])
    back_t = back_inner.T[0:count].astype(BF)
    down = jnp.where(number < 3, mm(back_t, normed_ref[...]), mm(back_t, mixed_ref[...]))
    acc_ref[:, 0:width] += down
    acc_ref[:, width:] += upper
    x = x_ref[...].astype(F32)
    scale = lax.rsqrt(jnp.mean(x * x, axis=-1, keepdims=True) + EPSILON)
    normed = x * scale
    back = total * gain_ref[0:1, :]
    back = scale * (back - normed * jnp.mean(back * normed, axis=-1, keepdims=True))
    out_ref[...] = (bh_ref[...] + back).astype(BF)

    @pl.when(step == pl.num_programs(0) - 1)
    def _():
        if not packed:
            grad_ref[...] = acc_ref[...].astype(BF)
            return
        half = width // 2
        shape = (16 * RANK, count)
        place, row = iota(shape, 0), iota(shape, 1)
        total = None
        for index in range(4):
            kind, part = index // 2, index % 2
            here = (place % 4 == row % 4) & (place // 16 == row // 4)
            here = here & (place // 8 % 2 == part) & (place // 4 % 2 == kind)
            start = kind * width + part * half
            piece = mm(hot(here), acc_ref[:, start : start + half].astype(BF))
            total = piece if total is None else total + piece
        grad_ref[...] = total.astype(BF)


def last_call(
    packed, dq, dk, dv, weights, acat, bcat, normed, inner, mixed, inner_o, ba, din, tokens, bh, gains
):
    tok_count, width = tokens.shape
    grad_shape = (16 * RANK, width // 2) if packed else (4 * RANK, 2 * width)
    return pl.pallas_call(
        functools.partial(last_body, packed),
        grid=(tok_count // TILE,),
        in_specs=[
            tall(width), tall(width), tall(width), whole(weights.shape), whole(acat.shape),
            whole(bcat.shape), tall(width), tall(LANES), tall(width), tall(LANES), tall(width),
            tall(LANES), tall(width), tall(width), whole(gains.shape),
        ],
        out_specs=[tall(width), whole(grad_shape)],
        out_shape=[shape_of(tok_count, width), shape_of(*grad_shape)],
        scratch_shapes=[pltpu.VMEM((4 * RANK, 2 * width), F32)],
        cost_estimate=cost(2 * tok_count * width * width * 4.5, 20e6),
        name="after_attention_backward",
    )(
        dq, dk, dv, weights, acat, bcat, normed, inner, mixed, inner_o, ba, din, tokens, bh, gains
    )


def exchange(value, axes):
    return lax.all_to_all(value, axes, split_axis=0, concat_axis=0, tiled=True)


def gather_all(value, axes, count):
    return exchange(jnp.broadcast_to(value[None], (count,) + value.shape), axes)


def swap(value, partner, group):
    if partner == 0:
        return value
    return lax.ppermute(value, "expert", [(index, index ^ partner) for index in range(group)])


def sum_expert_body(each, group, adapters, me_ref, id_ref, in_ref, out_ref):
    count = in_ref.shape[0]
    column = iota((1, count), 1)
    found = jnp.zeros((1, count), jnp.int32)
    for source in range(count // each):
        device = source // group * group + jnp.bitwise_xor(source % group, me_ref[0])
        found = jnp.where(column // each == source, id_ref[device], found)
    place = iota((adapters * each, count), 0)
    column = iota((adapters * each, count), 1)
    pick = hot((place // each == found) & (place % each == column % each))
    out_ref[...] = mm(pick, in_ref[...]).astype(BF)


def exchange_expert_grads(grads, group, owners):
    split = min(RANK, owners)
    each, parts = RANK // split, owners // split
    columns = grads.shape[1] // parts
    pieces = grads.reshape(split, each * group, parts, columns)
    pieces = pieces.transpose(0, 2, 1, 3).reshape(owners, group * each, columns)
    return exchange(pieces, "dp").reshape(owners * group * each, columns)


def sum_expert_grads(got, me, ids, adapters, group, owners):
    columns = got.shape[1]
    each = RANK // min(RANK, owners)
    return pl.pallas_call(
        functools.partial(sum_expert_body, each, group, adapters),
        in_specs=[smem(), smem(), pl.BlockSpec(memory_space=pltpu.VMEM)],
        out_shape=shape_of(adapters * each, columns),
        cost_estimate=cost(1e9, 5e6),
        name="expert_gradient_part",
    )(me, ids, got)


def finish_expert_body(split, adapters, hidden, in_ref, *refs):
    down_ref, up_ref, out_down_ref, out_up_ref = refs[-4:]
    each = RANK // split
    rows = adapters * each
    count = split * rows
    width = out_up_ref.shape[1]

    def place(value):
        return value // each % adapters * RANK + value // (adapters * each) * each + value % each

    move = hot(iota((count, count), 0) == place(iota((count, count), 1)))
    back = hot(iota((count, count), 1) == place(iota((count, count), 0)))

    def part(start, size):
        span = slice(start, start + size)
        rows_of = [in_ref[owner, :, span] for owner in range(split)]
        return jnp.concatenate(rows_of, axis=0)

    for index in range(2):
        up_ref[index] = mm(move, part(index * hidden, hidden))
    out_down_ref[...] = mm_tn(part(2 * hidden, hidden), back)
    base = 3 * hidden
    out_up_ref[...] = mm(move, part(base, width))
    for index in range(2):
        base += width
        down_ref[index] = mm_tn(part(base, width), back)


def finish_expert_call(owned, adapters, owners, width, hidden):
    local = len(owned)
    rows, columns = owned[0].shape
    everything = [lax.all_gather(own, "dp", axis=0, tiled=False) for own in owned]
    total = adapters * RANK
    shapes = [(local, 2, width, total), (local, 2, total, hidden), (local, hidden, total),
              (local, total, width)]
    outs = []
    for index, value in enumerate(everything):
        specs = [
            pl.BlockSpec((None,) + shape[1:], lambda *_, rank=len(shape): (index,) + (0,) * (rank - 1))
            for shape in shapes
        ]
        outs = pl.pallas_call(
            functools.partial(finish_expert_body, owners, adapters, hidden),
            grid=(1,),
            in_specs=[whole((owners, rows, columns))] + [pl.BlockSpec(memory_space=pl.ANY)] * len(outs),
            out_specs=specs,
            out_shape=[shape_of(*shape, dtype=F32) for shape in shapes],
            input_output_aliases={1 + place: place for place in range(len(outs))},
            cost_estimate=cost(1e9, 8e6),
            name="expert_gradient_sums",
        )(value, *outs)
    return outs


def spread_expert_grads(own, adapters, owners):
    split = min(RANK, owners)
    each, parts = RANK // split, owners // split
    everything = gather_all(own, "dp", owners)
    everything = everything.reshape(split, parts, adapters, each, own.shape[1])
    everything = everything.transpose(2, 0, 3, 1, 4)
    return everything.reshape(adapters * RANK, parts * own.shape[1]).astype(F32)


def expert_sums(owned, adapters, owners, width, hidden):
    if owners <= RANK:
        return finish_expert_call(owned, adapters, owners, width, hidden)
    sums = [spread_expert_grads(value, adapters, owners) for value in owned]
    base = 3 * hidden
    up = [[value[:, 0:hidden], value[:, hidden : 2 * hidden]] for value in sums]
    down = [
        [value[:, base + width * part : base + width * (part + 1)].T for part in (1, 2)]
        for value in sums
    ]
    return (
        jnp.stack([jnp.stack(value) for value in down]),
        jnp.stack([jnp.stack(value) for value in up]),
        jnp.stack([value[:, 2 * hidden : base].T for value in sums]),
        jnp.stack([value[:, base : base + width] for value in sums]),
    )


def finish_adapter_body(adapters, in_ref, down_ref, up_ref):
    half = in_ref.shape[3]
    count = RANK * adapters

    def place(value):
        return value % adapters * RANK + value // adapters

    move = hot(iota((count, count), 0) == place(iota((count, count), 1)))
    back = hot(iota((count, count), 1) == place(iota((count, count), 0)))
    for part in range(2):
        span = slice(part * half, part * half + half)
        for kind in range(2):
            for index in range(4):
                first = (kind * 4 + index) * adapters
                rows = in_ref[:, part, first : first + adapters, :].astype(F32)
                rows = rows.reshape(count, half).astype(BF)
                if kind == 0:
                    down_ref[index, span, :] = mm_tn(rows, back)
                else:
                    up_ref[index, :, span] = mm(move, rows)


def sum_adapter_body(kinds, adapters, id_ref, in_ref, out_ref):
    count = in_ref.shape[0]
    column = iota((1, count), 1)
    found = jnp.zeros((1, count), jnp.int32)
    for source in range(count // kinds):
        found = jnp.where(column // kinds == source, id_ref[source], found)
    place = iota((adapters * kinds, count), 0)
    column = iota((adapters * kinds, count), 1)
    pick = hot((place % adapters == found) & (place // adapters == column % kinds))
    own = mm(pick, in_ref[...]).astype(BF)
    for index in range(out_ref.shape[0]):
        out_ref[index] = own


def adapter_sums(grads, meanwhile, ids, adapters, everyone, width):
    axes = ("dp", "expert")
    if everyone == 2 * RANK:
        kinds = 8
        got = exchange(grads.reshape(everyone, kinds, width // 2), axes)
        got, meanwhile = lax.optimization_barrier((got, meanwhile))
        own = pl.pallas_call(
            functools.partial(sum_adapter_body, kinds, adapters),
            in_specs=[smem(), pl.BlockSpec(memory_space=pltpu.VMEM)],
            out_shape=shape_of(everyone, kinds * adapters, width // 2),
            cost_estimate=cost(1e9, 5e6),
            name="adapter_gradient_part",
        )(ids, got.reshape(everyone * kinds, width // 2))
        full = exchange(own, axes).reshape(RANK, 2, 8 * adapters, width // 2)
        total = adapters * RANK
        down, upper = pl.pallas_call(
            functools.partial(finish_adapter_body, adapters),
            out_shape=[shape_of(4, width, total, dtype=F32), shape_of(4, total, width, dtype=F32)],
            cost_estimate=cost(1e9, 5e6),
            name="adapter_gradient_sums",
        )(full)
        return down, upper, meanwhile
    pieces = grads.reshape(everyone, RANK * 4 * 2 * width // everyone)
    got = exchange(pieces, axes)
    pick = (jnp.arange(adapters, dtype=jnp.int32)[:, None] == ids[None, :]).astype(BF)
    own = jnp.dot(pick, got, preferred_element_type=F32).astype(BF)
    full = gather_all(own, axes, everyone)
    full = full.reshape(RANK, everyone // RANK, adapters, -1).transpose(2, 0, 1, 3)
    full = full.reshape(adapters * RANK, 4, 2, width).astype(F32)
    return full[:, :, 0].transpose(1, 2, 0), full[:, :, 1].transpose(1, 0, 2), meanwhile


def body(
    tokens,
    cotangent,
    lengths,
    adapter_ids,
    routes,
    prev_logits,
    norm_gains,
    input_weights,
    output_weight,
    adapter_down,
    adapter_up,
    router,
    residual_mix,
    constant_mix,
    constant_vectors,
    expert_gate,
    expert_up,
    expert_down,
    expert_adapter_down,
    expert_adapter_up,
    output_adapter_down,
    output_adapter_up,
):
    tok_count, width = tokens.shape
    hidden_width = expert_gate.shape[2]
    group, owners = lax.axis_size("expert"), lax.axis_size("dp")
    local = expert_gate.shape[0]
    adapters = adapter_down.shape[-1] // RANK
    cosine, sine = (jnp.asarray(table) for table in turn_tables(tok_count))
    weights = (
        expert_gate, expert_up, expert_down, expert_adapter_down, expert_adapter_up,
        output_adapter_down, output_adapter_up,
    )
    per_owner = RANK // min(RANK, owners)
    everyone = owners * group
    me = lax.axis_index("expert")

    all_ids = exchange(jnp.broadcast_to(adapter_ids, (everyone,)), ("dp", "expert"))
    me = me.reshape(1).astype(jnp.int32)

    rows = jnp.concatenate(
        [prev_logits, routes.astype(F32), jnp.zeros((tok_count, 2), F32)], axis=1
    ).T
    slots, *grad_sends = route_call(local, group, lengths, me, rows, cotangent)
    cots = [swap(value, partner, group) for partner, value in enumerate(grad_sends)]
    small = jnp.concatenate(
        [
            router.astype(F32), jnp.zeros((width, MIX_ROW - EXPERTS - 4), F32), constant_mix,
            jnp.zeros((width, LANES - MIX_ROW - 4), F32),
        ],
        axis=1,
    )
    normed, inner, queries, keys, values, acat, bcat, table = pre_call(
        adapter_ids, tokens, norm_gains, input_weights, adapter_down, adapter_up, cosine, sine, small,
        constant_vectors,
    )
    queries, all_ids = lax.optimization_barrier((queries, all_ids))
    mixed, q2 = attend_call(lengths, queries, keys, values)
    mixed, cots = lax.optimization_barrier((mixed, cots))
    mixer = jnp.pad(residual_mix.T, ((0, 4), (0, 4)))
    hidden, ei, inner_o, data, cols = post_call(
        local, group, me, mixed, tokens, output_weight, acat, bcat, norm_gains, table, mixer, rows,
        slots,
    )
    sends = send_call(local, group, me, adapter_ids, slots, data, ei)
    near, far = tuple(range(group // 2)), tuple(range(group // 2, group))
    sent_near = [swap(sends[partner], partner, group) for partner in near]
    sent_far = [
        [swap(sends[group // 2 + place * local + index], partner, group) for place, partner in enumerate(far)]
        for index in range(local)
    ]
    backs = [[None] * group for _ in range(local)]
    results = [[None] * group for _ in range(local)]
    grads, last = [], None
    for index in range(local):
        before = None
        for pair in (near, far) if index % 2 == 0 else (far, near):
            pieces = sent_near if pair == near else sent_far[index]
            if last is not None:
                pieces, last = lax.optimization_barrier((pieces, last))
            if index == local - 1 and pair == near:
                pieces, backs[:index] = lax.optimization_barrier((pieces, backs[:index]))
            outs = expert_call(
                index, pair, group, per_owner, pieces, [cots[partner] for partner in pair], before, weights
            )
            before = last = outs[-1]
            for place, partner in enumerate(pair):
                backs[index][partner] = swap(outs[place], partner, group)
                results[index][partner] = outs[len(pair) + place]
        grads.append(before)
    backs = [value for some in backs for value in some]

    parts = [exchange_expert_grads(grad, group, owners) for grad in grads]
    sums = functools.partial(sum_expert_grads, me=me, ids=all_ids, adapters=adapters, group=group, owners=owners)
    parts[:-1], last = lax.optimization_barrier((parts[:-1], last))
    owned = [sums(part) for part in parts[:-1]]
    backs, owned = lax.optimization_barrier((backs, owned))
    back_hidden, back_attention, back_inner_o, back_mixed = combine_call(
        lengths, backs, rows, data, cols, cotangent, ei, hidden, norm_gains, output_weight, acat, bcat,
        table,
    )
    flat = [value for some in results for value in some]
    flat, back_mixed = lax.optimization_barrier((flat, back_mixed))
    flat = [swap(value, place % group, group) for place, value in enumerate(flat)]

    dq, dk, dv = attend_back_call(lengths, q2, keys, values, mixed, back_mixed, cosine, sine)
    parts[-1], dq = lax.optimization_barrier((parts[-1], dq))
    owned.append(sums(parts[-1]))
    dq, owned = lax.optimization_barrier((dq, owned))
    input_back, adapter_grads = last_call(
        everyone == 2 * RANK, dq, dk, dv, input_weights, acat, bcat, normed, inner, mixed, inner_o,
        back_attention, back_inner_o, tokens, back_hidden, norm_gains,
    )
    layer_out = result_call(lengths, flat, cols, ei, hidden, table)
    down_sum, upper_sum, layer_out = adapter_sums(
        adapter_grads, layer_out, all_ids, adapters, everyone, width
    )
    in_down_sum, in_up_sum, out_down_sum, out_up_sum = expert_sums(
        owned, adapters, owners, width, hidden_width
    )
    return (
        layer_out,
        input_back,
        down_sum,
        upper_sum,
        in_down_sum,
        in_up_sum,
        out_down_sum,
        out_up_sum,
    )


def solution(mesh):
    tokens_spec, copied = P(("dp", "expert"), None), P()
    owned = P("expert")
    placed = (
        (tokens_spec, tokens_spec, P(("dp", "expert")), P(("dp", "expert")), tokens_spec, tokens_spec)
        + (copied,) * 9
        + (owned,) * 7
    )
    return jax.shard_map(
        body,
        mesh=mesh,
        in_specs=placed,
        out_specs=(tokens_spec, tokens_spec, copied, copied) + (owned,) * 4,
        check_vma=False,
    )
```

```python
import functools
import math

import jax
import jax.numpy as jnp
import numpy as np
from jax import lax
from jax.experimental import pallas as pl
from jax.experimental.pallas import tpu as pltpu
from jax.sharding import PartitionSpec as P

HEADS = 12
HD = 64
EXPERTS = 8
RANK = 16
CAP = 192
EPSILON = 1e-06
F32 = jnp.float32
BF = jnp.bfloat16
NEG = -1e30
LANES = 128
TILE = 256
FTILE = 512
PAIRS = HEADS // 2
META = 8
MIX_ROW = 16
VECTOR_ROW = 20
TARGET_LANE = 24
KEEP_LANE = 26
PIECE = CAP + META


def mm(left, right):
    return jnp.dot(left, right, preferred_element_type=F32)


def mm_nt(left, right):
    return lax.dot_general(left, right, (((1,), (1,)), ((), ())), preferred_element_type=F32)


def mm_tn(left, right):
    return lax.dot_general(left, right, (((0,), (0,)), ((), ())), preferred_element_type=F32)


def iota(shape, axis):
    return lax.broadcasted_iota(jnp.int32, shape, axis)


def hot(condition):
    return jnp.where(condition, 1.0, 0.0).astype(BF)


def split2(value):
    high = value.astype(BF)
    return high, (value - high.astype(F32)).astype(BF)


def split3(value):
    high = value.astype(BF)
    rest = value - high.astype(F32)
    middle = rest.astype(BF)
    return high, middle, (rest - middle.astype(F32)).astype(BF)


def whole(shape):
    zeros = (0,) * len(shape)
    return pl.BlockSpec(shape, lambda *_: zeros)


def smem():
    return pl.BlockSpec(memory_space=pltpu.SMEM)


def tall(width):
    return pl.BlockSpec((TILE, width), lambda i: (i, 0))


def wide(height):
    return pl.BlockSpec((height, TILE), lambda i: (0, i))


def shape_of(*shape, dtype=BF):
    return jax.ShapeDtypeStruct(shape, dtype)


def cost(microseconds):
    return pl.CostEstimate(flops=int(microseconds * 1e+09), bytes_accessed=0, transcendentals=0)


@functools.lru_cache(maxsize=None)
def turn_tables(length_in):
    half = HD // 2
    inverse = np.exp(
        np.arange(half, dtype=np.float32) * np.float32(-2.0 * math.log(10000.0) / HD)
    ).astype(np.float32)
    angles = np.arange(length_in, dtype=np.float32)[:, None] * inverse[None, :]
    cosine = np.tile(np.cos(angles.astype(np.float64)).astype(np.float32), (1, 4))
    sine = np.sin(angles.astype(np.float64)).astype(np.float32)
    return cosine, np.tile(np.concatenate([-sine, sine], axis=1), (1, 2))


def rope(value, cosine, sine):
    first = iota(value.shape, 1) % HD < HD // 2
    turned = jnp.where(first, pltpu.roll(value, LANES - HD // 2, 1), pltpu.roll(value, HD // 2, 1))
    return value * cosine + turned * sine


def find_slots(length, rows_ref, slot_ref):
    tok_count = slot_ref.shape[1]
    before = hot(iota((TILE, TILE), 0) < iota((TILE, TILE), 1))
    carry = jnp.zeros((2 * EXPERTS, 1), F32)
    for start in range(0, tok_count, TILE):
        span = slice(start, start + TILE)
        expert = iota((2 * EXPERTS, TILE), 0).astype(F32)
        token = iota((2 * EXPERTS, TILE), 1) + start
        named = (rows_ref[12:13, span] == expert) | (rows_ref[13:14, span] == expert)
        hit = named & (token < length) & (expert < EXPERTS)
        hits = jnp.where(hit, 1.0, 0.0)
        slots = mm(hits.astype(BF), before) + carry
        carry = carry + jnp.sum(hits, axis=1, keepdims=True)
        slot_ref[:, span] = jnp.where(hit, slots, -1.0)[:EXPERTS].astype(jnp.int32)


def pick_rows(slot_ref, step, me, local):
    first = jnp.bitwise_xor(step, me) * local
    place = iota((CAP, slot_ref.shape[1]), 0)
    return first, [hot(place == slot_ref[pl.ds(first + index, 1), :]) for index in range(local)]


def store_piece(out_refs, step, other, index, value, start):
    @pl.when(step == other)
    def _():
        out_refs[index][start : start + value.shape[0], :] = value


def route_body(local, group, len_ref, me_ref, rows_ref, source_ref, slot_ref, *out_refs):
    step = pl.program_id(0)

    @pl.when(step == 0)
    def _():
        find_slots(len_ref[0], rows_ref, slot_ref)

    _, chosen = pick_rows(slot_ref, step, me_ref[0], local)
    rows = mm(jnp.concatenate(chosen, axis=0), source_ref[...]).astype(BF)
    for other in range(group):
        store_piece(out_refs, step, other, other, rows, 0)


def route_call(local, group, length, me, rows, source):
    tok_count, width = source.shape
    return pl.pallas_call(
        functools.partial(route_body, local, group),
        grid=(group,),
        in_specs=[smem(), smem(), whole(rows.shape), whole(source.shape)],
        out_specs=[whole((EXPERTS, tok_count))] + [whole((local * CAP, width))] * group,
        out_shape=[shape_of(EXPERTS, tok_count, dtype=jnp.int32)]
        + [shape_of(local * CAP, width)] * group,
        cost_estimate=cost(6.5),
        name="route_rows",
    )(length, me, rows, source)


def send_body(local, group, me_ref, id_ref, slot_ref, data_ref, source_ref, *out_refs):
    step = pl.program_id(0)
    width = source_ref.shape[1]
    first, chosen = pick_rows(slot_ref, step, me_ref[0], local)
    rows = mm(jnp.concatenate(chosen, axis=0), source_ref[...]).astype(BF)
    for index in range(local):
        pieces = split3(data_ref[pl.ds(first + index, 1), :])
        stack = jnp.concatenate(
            [piece.astype(F32) for piece in pieces]
            + [jnp.zeros((13, chosen[index].shape[1]), F32)],
            axis=0,
        ).astype(BF)
        gates = mm_nt(stack, chosen[index])[0:META]
        gates = jnp.where(iota(gates.shape, 0) == 3, id_ref[0].astype(F32), gates)
        meta = jnp.concatenate([gates, jnp.zeros((META, width - CAP), F32)], axis=1)
        kept = rows[index * CAP : index * CAP + CAP]
        for other in range(group):
            far = other >= group // 2
            place = group // 2 + (other - group // 2) * local + index if far else other
            start = 0 if far else index * PIECE
            store_piece(out_refs, step, other, place, kept, start)
            store_piece(out_refs, step, other, place, meta.astype(BF), start + CAP)


def send_call(local, group, me, ids, slots, data, source):
    tok_count, width = source.shape
    heights = [local * PIECE] * (group // 2) + [PIECE] * ((group - group // 2) * local)
    return pl.pallas_call(
        functools.partial(send_body, local, group),
        grid=(group,),
        in_specs=[smem(), smem(), whole(slots.shape), whole(data.shape), whole(source.shape)],
        out_specs=[whole((height, width)) for height in heights],
        out_shape=[shape_of(height, width) for height in heights],
        cost_estimate=cost(8.4),
        name="send_rows",
    )(me, ids, slots, data, source)


def pre_body(
    id_ref, x_ref, gain_ref, w_ref, ad_ref, au_ref, cos_ref, sin_ref, small_ref, vec_ref,
    normed_ref, inner_ref, q_ref, k_ref, v_ref, acat_ref, bcat_ref, table_ref,
):
    @pl.when(pl.program_id(0) == 0)
    def _():
        first = RANK * id_ref[0]
        total = None
        for index in range(4):
            row, column = iota((LANES, LANES), 0), iota((LANES, LANES), 1)
            place = hot((row >= first) & (row < first + RANK) & (column == (row - first) * 4 + index))
            part = mm(ad_ref[index], place)
            total = part if total is None else total + part
            place = hot(
                (column >= first) & (column < first + RANK) & (row == (column - first) * 4 + index)
            )
            bcat_ref[index] = mm(place, au_ref[index]).astype(BF)
        acat_ref[...] = total.astype(BF)
        table = small_ref[...].T
        number = iota(table.shape, 0)
        for index in range(2):
            table = jnp.where(number == VECTOR_ROW + index, vec_ref[index : index + 1, :], table)
        table_ref[...] = table

    x = x_ref[...].astype(F32)
    scale = lax.rsqrt(jnp.mean(x * x, axis=-1, keepdims=True) + EPSILON)
    normed = (x * scale * gain_ref[0:1, :]).astype(BF)
    normed_ref[...] = normed
    inner = mm(normed, acat_ref[...]).astype(BF)
    inner_ref[...] = inner
    for index, out_ref in enumerate((q_ref, k_ref, v_ref)):
        value = mm(normed, w_ref[index]) + mm(inner, bcat_ref[index])
        if index == 2:
            out_ref[...] = value.astype(BF)
            continue
        for pair in range(PAIRS):
            span = slice(pair * LANES, pair * LANES + LANES)
            turned = rope(value[:, span], cos_ref[...], sin_ref[...]).astype(BF)
            if index == 0:
                turned = (turned.astype(F32) * HD**-0.5).astype(BF)
            out_ref[:, span] = turned


def pre_call(ids, tokens, gains, weights, down, upper, cosine, sine, small, vectors):
    tok_count, width = tokens.shape
    return pl.pallas_call(
        pre_body,
        grid=(tok_count // TILE,),
        in_specs=[
            smem(), tall(width), whole(gains.shape), whole(weights.shape), whole(down.shape),
            whole(upper.shape), tall(LANES), tall(LANES), whole(small.shape), whole(vectors.shape),
        ],
        out_specs=[
            tall(width), tall(LANES), tall(width), tall(width), tall(width),
            whole((width, LANES)), whole(upper.shape), whole((LANES, width)),
        ],
        out_shape=[
            shape_of(tok_count, width), shape_of(tok_count, LANES), shape_of(tok_count, width),
            shape_of(tok_count, width), shape_of(tok_count, width), shape_of(width, LANES),
            shape_of(*upper.shape), shape_of(LANES, width, dtype=F32),
        ],
        cost_estimate=cost(12.3),
        name="before_attention",
    )(ids, tokens, gains, weights, down, upper, cosine, sine, small, vectors)


def attend_body(len_ref, q_ref, k_ref, v_ref, mixed_ref, q2_ref):
    tok_count = q_ref.shape[0]
    lane = iota((tok_count, LANES), 1)
    position = iota((tok_count, LANES), 0)
    bias = jnp.where(position < len_ref[0], 0.0, NEG)
    causal = iota((TILE, TILE), 1) <= iota((TILE, TILE), 0)
    lane_tile = lane[:TILE]
    outs = [[], []]
    for head in range(2):
        own = lane // HD == head
        spare = HD * (1 - head)
        one = jnp.where(lane == spare, 1.0, 0.0)
        queries = jnp.where(own, q_ref[...].astype(F32), one)
        keys = jnp.where(
            own, k_ref[...].astype(F32), jnp.where(lane == spare, bias, 0.0)
        ).astype(BF)
        values = jnp.where(own, v_ref[...].astype(F32), one).astype(BF)
        for start in range(0, tok_count, TILE):
            stop = start + TILE
            part = queries[start:stop]
            scores = mm_nt(part.astype(BF), keys[:stop])
            diagonal = jnp.where(causal, scores[:, start:], NEG)
            scores = diagonal if start == 0 else jnp.concatenate([scores[:, :start], diagonal], axis=1)
            top = jnp.max(scores, axis=-1, keepdims=True)
            weights = jnp.exp(scores - top).astype(BF)
            mixed = mm(weights, values[:stop])
            total = mixed[:, spare : spare + 1]
            outs[head].append(mixed / total)
            log_total = top + jnp.log(total)
            high, middle, low = split3(log_total)
            kept = part
            for offset, piece in enumerate((high, middle, low)):
                kept = jnp.where(lane_tile == spare + 1 + offset, piece.astype(F32), kept)
            q2_ref[start:stop, head * LANES : head * LANES + LANES] = kept.astype(BF)
    for index, start in enumerate(range(0, tok_count, TILE)):
        mixed_ref[start : start + TILE, :] = jnp.where(
            lane_tile < HD, outs[0][index], outs[1][index]
        ).astype(BF)


def attend_call(length, queries, keys, values):
    tok_count, width = queries.shape
    column = pl.BlockSpec((tok_count, LANES), lambda i: (0, i))
    return pl.pallas_call(
        attend_body,
        grid=(PAIRS,),
        in_specs=[smem(), column, column, column],
        out_specs=[column, pl.BlockSpec((tok_count, 2 * LANES), lambda i: (0, i))],
        out_shape=[shape_of(tok_count, width), shape_of(tok_count, 2 * width)],
        cost_estimate=cost(23),
        name="attention_forward",
    )(length, queries, keys, values)


def attend_back_body(
    len_ref, q2_ref, k_ref, v_ref, mixed_ref, back_ref, cos_ref, sin_ref,
    dq_ref, dk_ref, dv_ref, acc_ref,
):
    tok_count = k_ref.shape[0]
    lane = iota((tok_count, LANES), 1)
    position = iota((tok_count, LANES), 0)
    bias = jnp.where(position < len_ref[0], 0.0, NEG)
    causal = iota((TILE, TILE), 0) <= iota((TILE, TILE), 1)
    back = back_ref[...].astype(F32)
    product = back * mixed_ref[...].astype(F32)
    grads = []
    for head in range(2):
        own = lane // HD == head
        spare = HD * (1 - head)
        minus = jnp.where((lane > spare) & (lane < spare + 4), -1.0, 0.0)
        q2 = q2_ref[:, head * LANES : head * LANES + LANES]
        k2f = jnp.where(
            own, k_ref[...].astype(F32), jnp.where(lane == spare, bias, minus)
        )
        k2 = k2f.astype(BF)
        k2t = k2f.T.astype(BF)
        v2 = jnp.where(own, v_ref[...].astype(F32), minus).astype(BF)
        delta = jnp.sum(jnp.where(own, product, 0.0), axis=-1, keepdims=True)
        back2 = jnp.where(own, back, 0.0)
        for offset, piece in enumerate(split3(delta)):
            back2 = jnp.where(lane == spare + 1 + offset, piece.astype(F32), back2)
        back2 = back2.astype(BF)
        dk_parts, dv_parts = [], []
        for start in range(0, tok_count, TILE):
            stop = start + TILE
            scores = mm_nt(k2[start:stop], q2[start:])
            slopes = mm_nt(v2[start:stop], back2[start:])
            diagonal = jnp.where(causal, scores[:, :TILE], NEG)
            scores = (
                diagonal
                if stop == tok_count
                else jnp.concatenate([diagonal, scores[:, TILE:]], axis=1)
            )
            weights = jnp.exp(scores)
            turned = (weights * slopes).astype(BF)
            dv_parts.append(mm(weights.astype(BF), back2[start:]))
            dk_parts.append(mm(turned, q2[start:]))
            update = mm(k2t[:, start:stop], turned)
            if start == 0:
                acc_ref[head] = update
            else:
                acc_ref[head, :, start:] += update
        grads.append((jnp.concatenate(dk_parts, axis=0), jnp.concatenate(dv_parts, axis=0)))
    low_lane = lane < HD
    cosine, sine = cos_ref[...], -sin_ref[...]
    row = iota((LANES, tok_count), 0)
    dq = jnp.where(row < HD, acc_ref[0], acc_ref[1]).T * HD**-0.5
    dq_ref[...] = rope(dq, cosine, sine).astype(BF)
    dk = jnp.where(low_lane, grads[0][0], grads[1][0])
    dk_ref[...] = rope(dk, cosine, sine).astype(BF)
    dv_ref[...] = jnp.where(low_lane, grads[0][1], grads[1][1]).astype(BF)


def attend_back_call(length, q2, keys, values, mixed, back, cosine, sine):
    tok_count, width = keys.shape
    column = pl.BlockSpec((tok_count, LANES), lambda i: (0, i))
    return pl.pallas_call(
        attend_back_body,
        grid=(PAIRS,),
        in_specs=[
            smem(), pl.BlockSpec((tok_count, 2 * LANES), lambda i: (0, i)), column, column, column,
            column, whole(cosine.shape), whole(sine.shape),
        ],
        out_specs=[column] * 3,
        out_shape=[shape_of(tok_count, width)] * 3,
        scratch_shapes=[pltpu.VMEM((2, LANES, tok_count), F32)],
        cost_estimate=cost(26),
        name="attention_backward",
    )(length, q2, keys, values, mixed, back, cosine, sine)


def post_body(
    local, group, me_ref, mixed_ref, x_ref, wo_ref, acat_ref, bcat_ref, gain_ref, table_ref, mix_ref,
    rows_ref, slot_ref, hidden_ref, ei_ref, inner_ref, data_ref, cols_ref,
):
    mixed = mixed_ref[...]
    inner = mm(mixed, acat_ref[...]).astype(BF)
    inner_ref[...] = inner
    hidden = x_ref[...].astype(F32) + (mm(mixed, wo_ref[...]) + mm(inner, bcat_ref[0]))
    hidden_ref[...] = hidden
    scale = lax.rsqrt(jnp.mean(hidden * hidden, axis=-1, keepdims=True) + EPSILON)
    ei = (hidden * scale * gain_ref[1:2, :]).astype(BF)
    ei_ref[...] = ei
    read = None
    for piece in split3(table_ref[...]):
        part = mm_nt(piece, ei)
        read = part if read is None else read + part
    logits = read[0:16]
    for index in range(EXPERTS + 4):
        logits = logits + mix_ref[:, index : index + 1] * rows_ref[index : index + 1, :]
    first, second = rows_ref[12:13, :], rows_ref[13:14, :]
    number = iota((16, TILE), 0).astype(F32)
    one = jnp.sum(jnp.where(number == first, logits, 0.0), axis=0, keepdims=True)
    two = jnp.sum(jnp.where(number == second, logits, 0.0), axis=0, keepdims=True)
    top = jnp.maximum(one, two)
    one, two = jnp.exp(one - top), jnp.exp(two - top)
    gate_a, gate_b = one / (one + two), two / (one + two)
    mixes = read[MIX_ROW : MIX_ROW + 4]
    shares = []
    for index in range(2):
        left, right = mixes[2 * index : 2 * index + 1], mixes[2 * index + 1 : 2 * index + 2]
        top = jnp.maximum(left, right)
        left, right = jnp.exp(left - top), jnp.exp(right - top)
        shares += [left / (left + right), right / (left + right)]

    def both(value):
        return jnp.where(first == value, gate_a, 0.0) + jnp.where(second == value, gate_b, 0.0)

    gates = jnp.where(number == first, gate_a, 0.0) + jnp.where(number == second, gate_b, 0.0)
    beta_a, beta_b = both(EXPERTS + 2.0), both(EXPERTS + 3.0)
    keep = both(EXPERTS + 1.0) + beta_a * shares[0] + beta_b * shares[2]
    data_ref[0:8, :] = gates[0:8]
    tail = [gate_a, gate_b] + shares + [beta_a, beta_b]
    data_ref[8:16, :] = jnp.concatenate(tail, axis=0)
    slots = slot_ref[...].astype(F32)
    expert = iota((EXPERTS, TILE), 0)
    partner = jnp.bitwise_xor(expert // local, me_ref[0])
    base = ((expert % local) * (group * CAP) + partner * CAP).astype(F32)
    place = jnp.where(slots >= 0, slots + base + 1.0, 0.0)
    expert = expert.astype(F32)
    target_a = jnp.sum(jnp.where(expert == first, place, 0.0), axis=0, keepdims=True) - 1.0
    target_b = jnp.sum(jnp.where(expert == second, place, 0.0), axis=0, keepdims=True) - 1.0
    stack = jnp.concatenate(
        [jnp.zeros((VECTOR_ROW, TILE), F32), beta_a * shares[1], beta_b * shares[3]]
        + [jnp.zeros((2, TILE), F32), target_a, target_b, keep]
        + [jnp.zeros((LANES - KEEP_LANE - 1, TILE), F32)],
        axis=0,
    )
    cols_ref[...] = stack.T


def post_call(
    local, group, me, mixed, tokens, weight, acat, bcat, gains, table, mixer, rows, slots
):
    tok_count, width = tokens.shape
    return pl.pallas_call(
        functools.partial(post_body, local, group),
        grid=(tok_count // TILE,),
        in_specs=[
            smem(), tall(width), tall(width), whole(weight.shape), whole(acat.shape),
            pl.BlockSpec((1, LANES, width), lambda i: (3, 0, 0)), whole(gains.shape),
            whole(table.shape), whole(mixer.shape), wide(16), wide(EXPERTS),
        ],
        out_specs=[tall(width), tall(width), tall(LANES), wide(16), tall(LANES)],
        out_shape=[
            shape_of(tok_count, width, dtype=F32), shape_of(tok_count, width),
            shape_of(tok_count, LANES), shape_of(16, tok_count, dtype=F32),
            shape_of(tok_count, LANES, dtype=F32),
        ],
        cost_estimate=cost(10.5),
        name="after_attention",
    )(me, mixed, tokens, weight, acat, bcat, gains, table, mixer, rows, slots)


def expert_body(
    pair, per_owner, group, steps, has_grad, *refs
):
    count = len(pair)
    piece_refs, refs = refs[:count], refs[count:]
    cot_refs, refs = refs[:count], refs[count:]
    wg_ref, wu_ref, wd_ref, dn_ref, up_ref, od_ref, ou_ref = refs[:7]
    refs = refs[7:]
    before_ref = None
    if has_grad:
        before_ref, refs = refs[0], refs[1:]
    back_refs, refs = refs[:count], refs[count:]
    out_refs, refs = refs[:count], refs[count:]
    (
        grad_ref, x_ref, g_ref, gate_ref, pick_ref, dr_ref, zg_ref, zu_ref, dzd_ref, zgt_ref, zut_ref,
        dzdt_ref, racc_ref, xacc_ref, zd_acc, dzg_acc, dzu_acc, h_ref, dg_ref, du_ref,
    ) = refs
    step = pl.program_id(0)
    rows, width = x_ref.shape
    compact = group * RANK
    chosen = pick_ref[...] > 0.0

    def fold(value):
        place = iota((compact, LANES), 0)
        block = per_owner * group
        inner = place // block * per_owner + place % per_owner
        folded = mm_nt(hot(iota((compact, LANES), 1) % RANK == inner), value)
        place = iota((compact, rows), 0)
        owner = place % block // per_owner
        mine = iota((compact, rows), 1) // CAP + pair[0]
        return jnp.where(mine == owner, folded, 0.0).astype(BF)

    def put(start, value):
        span = pl.ds(start, value.shape[1])
        if has_grad:
            value = value + before_ref[:, span].astype(F32)
        grad_ref[:, span] = value.astype(BF)

    @pl.when(step == 0)
    def _():
        for index in range(count):
            span = slice(index * CAP, index * CAP + CAP)
            x_ref[span] = piece_refs[index][0:CAP]
            g_ref[span] = cot_refs[index][...]
            meta = piece_refs[index][CAP:PIECE].astype(F32)
            gate = (meta[0:1] + meta[1:2] + meta[2:3])[:, 0 : 2 * LANES]
            gate_ref[span] = jnp.broadcast_to(gate, (LANES, 2 * LANES)).T[0:CAP]
            lane = (iota((CAP, LANES), 1) // RANK).astype(F32)
            pick_ref[span] = jnp.where(lane == meta[3:4, 0:LANES], 1.0, 0.0)
        picked = pick_ref[...] > 0.0
        dr = (gate_ref[:, 0:1] * g_ref[...].astype(F32)).astype(BF)
        dr_ref[...] = dr
        zg = jnp.where(picked, mm(x_ref[...], dn_ref[0]), 0.0).astype(BF)
        zu = jnp.where(picked, mm(x_ref[...], dn_ref[1]), 0.0).astype(BF)
        dzd = jnp.where(picked, mm_nt(dr, ou_ref[...]), 0.0).astype(BF)
        zg_ref[...] = zg
        zu_ref[...] = zu
        dzd_ref[...] = dzd
        zgt_ref[...] = fold(zg)
        zut_ref[...] = fold(zu)
        dzdt_ref[...] = fold(dzd)
        for ref in (racc_ref, xacc_ref, zd_acc, dzg_acc, dzu_acc):
            ref[...] = jnp.zeros_like(ref)

    gate = mm(x_ref[...], wg_ref[...]) + mm(zg_ref[...], up_ref[0])
    upper = mm(x_ref[...], wu_ref[...]) + mm(zu_ref[...], up_ref[1])
    share = 0.5 * jnp.tanh(0.5 * gate) + 0.5
    silu = gate * share
    active = (silu * upper).astype(BF)
    h_ref[...] = active
    back = mm_nt(dr_ref[...], wd_ref[...]) + mm_nt(dzd_ref[...], od_ref[...])
    du = (back * silu).astype(BF)
    dg = (back * upper * (share + silu * (1.0 - share))).astype(BF)
    du_ref[...] = du
    dg_ref[...] = dg
    racc_ref[...] += mm(active, wd_ref[...])
    zd_acc[...] += mm(active, od_ref[...])
    xacc_ref[...] += mm_nt(dg, wg_ref[...]) + mm_nt(du, wu_ref[...])
    dzg_acc[...] += mm_nt(dg, up_ref[0])
    dzu_acc[...] += mm_nt(du, up_ref[1])
    tile = h_ref.shape[1]
    total = steps * tile
    at = pl.multiple_of(step * tile, tile)
    put(at, mm(zgt_ref[...], dg_ref[...]))
    put(total + at, mm(zut_ref[...], du_ref[...]))
    put(2 * total + at, mm(dzdt_ref[...], h_ref[...]))

    @pl.when(step == steps - 1)
    def _():
        zd = jnp.where(chosen, zd_acc[...], 0.0).astype(BF)
        dzg = jnp.where(chosen, dzg_acc[...], 0.0).astype(BF)
        dzu = jnp.where(chosen, dzu_acc[...], 0.0).astype(BF)
        result = racc_ref[...] + mm(zd, ou_ref[...])
        gated = (gate_ref[:, 0:1] * result).astype(BF)
        product = g_ref[...].astype(F32) * result.astype(BF).astype(F32)
        dots = jnp.broadcast_to(jnp.sum(product, axis=-1, keepdims=True), (rows, LANES))
        back_rows = (xacc_ref[...] + mm_nt(dzg, dn_ref[0]) + mm_nt(dzu, dn_ref[1])).astype(BF)
        for index in range(count):
            span = slice(index * CAP, index * CAP + CAP)
            out_refs[index][...] = gated[span]
            back_refs[index][0:CAP, :] = back_rows[span]
            column = jnp.concatenate(
                [dots[span], jnp.zeros((2 * LANES - CAP, LANES), F32)], axis=0
            ).T[0:1]
            meta = jnp.concatenate(
                [piece.astype(F32) for piece in split3(column)]
                + [jnp.zeros((META - 3, 2 * LANES), F32)],
                axis=0,
            )
            meta = jnp.concatenate([meta, jnp.zeros((META, width - 2 * LANES), F32)], axis=1)
            back_refs[index][CAP:PIECE, :] = meta.astype(BF)
        base = 3 * total
        place = iota((compact, LANES), 0)
        owner = place % (per_owner * group) // per_owner
        ids = jnp.zeros((compact, LANES), F32)
        for index in range(count):
            meta = piece_refs[index][CAP:PIECE, 0:LANES].astype(F32)
            ids = jnp.where(owner == pair[index], meta[3:4], ids)
        put(base + 3 * width, ids)
        put(base, mm(fold(zd), dr_ref[...]))
        put(base + width, mm(fold(dzg), x_ref[...]))
        put(base + 2 * width, mm(fold(dzu), x_ref[...]))


def expert_call(index, pair, group, per_owner, pieces, cots, before, weights):
    gate_w, up_w, down_w, in_down, in_up, out_down, out_up = weights
    width, hidden = gate_w.shape[1:]
    rows = len(pair) * CAP
    steps = hidden // FTILE
    columns = 3 * hidden + 3 * width + LANES
    compact = group * RANK
    has_grad = before is not None
    return pl.pallas_call(
        functools.partial(expert_body, pair, per_owner, group, steps, has_grad),
        grid=(steps,),
        in_specs=[
            pl.BlockSpec((PIECE, width), lambda f, row=piece.shape[0] // PIECE > 1: (index * row, 0))
            for piece in pieces
        ]
        + [pl.BlockSpec((CAP, width), lambda f: (index, 0))] * len(pair)
        + [
            pl.BlockSpec((None, width, FTILE), lambda f: (index, 0, f)),
            pl.BlockSpec((None, width, FTILE), lambda f: (index, 0, f)),
            pl.BlockSpec((None, FTILE, width), lambda f: (index, f, 0)),
            pl.BlockSpec((None, 2, width, LANES), lambda f: (index, 0, 0, 0)),
            pl.BlockSpec((None, 2, LANES, FTILE), lambda f: (index, 0, 0, f)),
            pl.BlockSpec((None, FTILE, LANES), lambda f: (index, f, 0)),
            pl.BlockSpec((None, LANES, width), lambda f: (index, 0, 0)),
        ]
        + [whole((compact, columns))] * has_grad,
        out_specs=[whole((PIECE, width))] * len(pair)
        + [whole((CAP, width))] * len(pair)
        + [whole((compact, columns))],
        out_shape=[shape_of(PIECE, width)] * len(pair)
        + [shape_of(CAP, width)] * len(pair)
        + [shape_of(compact, columns)],
        scratch_shapes=[pltpu.VMEM((rows, width), BF)] * 2
        + [pltpu.VMEM((rows, LANES), F32)] * 2
        + [pltpu.VMEM((rows, width), BF)]
        + [pltpu.VMEM((rows, LANES), BF)] * 3
        + [pltpu.VMEM((compact, rows), BF)] * 3
        + [pltpu.VMEM((rows, width), F32)] * 2
        + [pltpu.VMEM((rows, LANES), F32)] * 3
        + [pltpu.VMEM((rows, FTILE), BF)] * 3,
        cost_estimate=cost(18),
        name="expert_layer",
    )(
        *pieces, *cots, gate_w, up_w, down_w, in_down, in_up, out_down, out_up,
        *([before] if has_grad else []),
    )


def spread(cols_ref, index, count):
    return iota((TILE, count), 1).astype(F32) == cols_ref[:, index : index + 1]


def combine_body(
    pieces, len_ref, *refs
):
    back_refs = refs[:pieces]
    (
        rows_ref, data_ref, cols_ref, cot_ref, ei_ref, hidden_ref, gain_ref, wo_ref, acat_ref, bcat_ref,
        table_ref, bh_ref, ba_ref, din_ref, bm_ref, back_all, dots_ref,
    ) = refs[pieces:]
    count = pieces * CAP

    @pl.when(pl.program_id(0) == 0)
    def _():
        for index, back_ref in enumerate(back_refs):
            back_all[index * CAP : index * CAP + CAP, :] = back_ref[0:CAP, :]
        dots = [back_ref[CAP:PIECE, 0:CAP].astype(F32) for back_ref in back_refs]
        dots = jnp.concatenate(dots, axis=1)
        dots_ref[...] = jnp.concatenate([dots, jnp.zeros_like(dots)], axis=0).astype(BF)

    chosen_a = hot(spread(cols_ref, TARGET_LANE, count))
    chosen_b = hot(spread(cols_ref, TARGET_LANE + 1, count))
    stack = dots_ref[...]
    routed_a = jnp.sum(mm_nt(stack, chosen_a)[0:8], axis=0, keepdims=True)
    routed_b = jnp.sum(mm_nt(stack, chosen_b)[0:8], axis=0, keepdims=True)
    cot = cot_ref[...]
    cot_f = cot.astype(F32)
    high, low = split2(cot_f * ei_ref[...].astype(F32))
    ones = jnp.ones((16, cot.shape[1]), BF)
    along_x = (mm_nt(ones, high) + mm_nt(ones, low))[0:1]
    table_high, table_middle, table_low = split3(table_ref[...])
    along_c = mm_nt(table_high, cot) + mm_nt(table_middle, cot) + mm_nt(table_low, cot)
    along_a = along_c[VECTOR_ROW : VECTOR_ROW + 1]
    along_b = along_c[VECTOR_ROW + 1 : VECTOR_ROW + 2]
    first, second = rows_ref[12:13, :], rows_ref[13:14, :]
    token = iota((1, TILE), 1) + pl.program_id(0) * TILE
    valid = jnp.where(token < len_ref[0], 1.0, 0.0)
    gate_a, gate_b = data_ref[8:9, :], data_ref[9:10, :]
    share = [data_ref[index : index + 1, :] for index in range(10, 14)]
    beta_a, beta_b = data_ref[14:15, :], data_ref[15:16, :]
    const_a = share[0] * along_x + share[1] * along_a
    const_b = share[2] * along_x + share[3] * along_b

    def here(route):
        return (
            jnp.where(route == EXPERTS + 1.0, along_x, 0.0)
            + jnp.where(route == EXPERTS + 2.0, const_a, 0.0)
            + jnp.where(route == EXPERTS + 3.0, const_b, 0.0)
        )

    dot_a, dot_b = routed_a + here(first), routed_b + here(second)
    mean = gate_a * dot_a + gate_b * dot_b
    chosen_grad_a = valid * gate_a * (dot_a - mean)
    chosen_grad_b = valid * gate_b * (dot_b - mean)
    number = iota((16, TILE), 0).astype(F32)
    logit_grads = jnp.where(number == first, chosen_grad_a, 0.0) + jnp.where(
        number == second, chosen_grad_b, 0.0
    )
    mixes = []
    for index, (beta, along) in enumerate(((beta_a, along_a), (beta_b, along_b))):
        left, right = share[2 * index], share[2 * index + 1]
        weighted = left * along_x + right * along
        mixes += [
            valid * beta * left * (along_x - weighted),
            valid * beta * right * (along - weighted),
        ]
    stack = jnp.concatenate(
        [logit_grads] + mixes + [jnp.zeros((LANES - 20, TILE), F32)], axis=0
    ).T
    high, low = split2(stack)
    inside = iota((TILE, 1), 0) + pl.program_id(0) * TILE < len_ref[0]
    grad = jnp.where(inside, cot_f, 0.0)
    back = mm(high, table_high) + mm(low, table_high) + mm(high, table_middle)
    back = back + cols_ref[:, KEEP_LANE : KEEP_LANE + 1] * grad
    back = back + mm(chosen_a + chosen_b, back_all[...])
    hidden = hidden_ref[...]
    scale = lax.rsqrt(jnp.mean(hidden * hidden, axis=-1, keepdims=True) + EPSILON)
    normed = hidden * scale
    back = back * gain_ref[1:2, :]
    back = grad + scale * (back - normed * jnp.mean(back * normed, axis=-1, keepdims=True))
    bh_ref[...] = back
    rounded = back.astype(BF)
    ba_ref[...] = rounded
    inner = mm_nt(rounded, bcat_ref[0]).astype(BF)
    din_ref[...] = inner
    bm_ref[...] = (mm_nt(rounded, wo_ref[...]) + mm_nt(inner, acat_ref[...])).astype(BF)


def combine_call(
    length, backs, rows, data, cols, cotangent, ei, hidden, gains, weight, acat, bcat, table
):
    tok_count, width = cotangent.shape
    pieces = len(backs)
    return pl.pallas_call(
        functools.partial(combine_body, pieces),
        grid=(tok_count // TILE,),
        in_specs=[smem()] + [whole(back.shape) for back in backs] + [
            wide(16), wide(16), tall(LANES), tall(width), tall(width), tall(width),
            whole(gains.shape), whole(weight.shape), whole(acat.shape),
            pl.BlockSpec((1, LANES, width), lambda i: (3, 0, 0)), whole(table.shape),
        ],
        out_specs=[tall(width), tall(width), tall(LANES), tall(width)],
        out_shape=[
            shape_of(tok_count, width, dtype=F32), shape_of(tok_count, width),
            shape_of(tok_count, LANES), shape_of(tok_count, width),
        ],
        scratch_shapes=[
            pltpu.VMEM((pieces * CAP, width), BF), pltpu.VMEM((2 * META, pieces * CAP), BF)
        ],
        cost_estimate=cost(24),
        name="combine_backward",
    )(
        length, *backs, rows, data, cols, cotangent, ei, hidden, gains, weight, acat, bcat, table
    )


def result_body(pieces, len_ref, *refs):
    result_refs = refs[:pieces]
    cols_ref, ei_ref, hidden_ref, table_ref, out_ref, result_all = refs[pieces:]
    count = pieces * CAP

    @pl.when(pl.program_id(0) == 0)
    def _():
        for index, result_ref in enumerate(result_refs):
            result_all[index * CAP : index * CAP + CAP, :] = result_ref[...]

    both = hot(
        spread(cols_ref, TARGET_LANE, count) | spread(cols_ref, TARGET_LANE + 1, count)
    )
    cols = cols_ref[...]
    high, low = split2(cols)
    table_high, table_low = split2(table_ref[...])
    mixture = mm(high, table_high) + mm(low, table_high) + mm(high, table_low)
    mixture = mixture + cols[:, KEEP_LANE : KEEP_LANE + 1] * ei_ref[...].astype(F32)
    mixture = mixture + mm(both, result_all[...])
    inside = iota((TILE, 1), 0) + pl.program_id(0) * TILE < len_ref[0]
    out_ref[...] = (hidden_ref[...] + jnp.where(inside, mixture, 0.0)).astype(BF)


def result_call(length, results, cols, ei, hidden, table):
    tok_count, width = ei.shape
    pieces = len(results)
    return pl.pallas_call(
        functools.partial(result_body, pieces),
        grid=(tok_count // TILE,),
        in_specs=[smem()] + [whole(result.shape) for result in results] + [
            tall(LANES), tall(width), tall(width), whole(table.shape),
        ],
        out_specs=tall(width),
        out_shape=shape_of(tok_count, width),
        scratch_shapes=[pltpu.VMEM((pieces * CAP, width), BF)],
        cost_estimate=cost(8),
        name="layer_output",
    )(length, *results, cols, ei, hidden, table)


def last_body(
    packed, id_ref, dq_ref, dk_ref, dv_ref, w_ref, acat_ref, bcat_ref, normed_ref, inner_ref, mixed_ref, inner_o_ref,
    ba_ref, din_ref, x_ref, bh_ref, gain_ref, out_ref, grad_ref, acc_ref,
):
    step = pl.program_id(0)
    width = x_ref.shape[1]
    count = 4 * RANK

    @pl.when(step == 0)
    def _():
        acc_ref[...] = jnp.zeros_like(acc_ref)

    total = None
    inner_t = inner_ref[...].astype(F32).T[0:count].astype(BF)
    outer_t = inner_o_ref[...].astype(F32).T[0:count].astype(BF)
    number = iota((count, width), 0) % 4
    upper = mm(outer_t, ba_ref[...])
    back_inner = din_ref[...].astype(F32)
    for index, ref in enumerate((dq_ref, dk_ref, dv_ref)):
        value = ref[...]
        part = mm_nt(value, w_ref[index])
        total = part if total is None else total + part
        back_inner = back_inner + mm_nt(value, bcat_ref[index]).astype(BF).astype(F32)
        upper = jnp.where(number == index, mm(inner_t, value), upper)
    own = iota(back_inner.shape, 1) % 4 < 3
    total = total + mm_nt(jnp.where(own, back_inner, 0.0).astype(BF), acat_ref[...])
    back_t = back_inner.T[0:count].astype(BF)
    down = jnp.where(number < 3, mm(back_t, normed_ref[...]), mm(back_t, mixed_ref[...]))
    acc_ref[:, 0:width] += down
    acc_ref[:, width:] += upper
    x = x_ref[...].astype(F32)
    scale = lax.rsqrt(jnp.mean(x * x, axis=-1, keepdims=True) + EPSILON)
    normed = x * scale
    back = total * gain_ref[0:1, :]
    back = scale * (back - normed * jnp.mean(back * normed, axis=-1, keepdims=True))
    out_ref[...] = (bh_ref[...] + back).astype(BF)

    @pl.when(step == pl.num_programs(0) - 1)
    def _():
        if not packed:
            grad_ref[...] = acc_ref[...].astype(BF)
            return
        half = width // 2
        shape = (16 * RANK, count)
        place, row = iota(shape, 0), iota(shape, 1)
        total = None
        for index in range(4):
            kind, part = index // 2, index % 2
            here = (place % 4 == row % 4) & (place // 16 == row // 4)
            here = here & (place // 8 % 2 == part) & (place // 4 % 2 == kind)
            start = kind * width + part * half
            piece = mm(hot(here), acc_ref[:, start : start + half].astype(BF))
            total = piece if total is None else total + piece
        grad_ref[:, 0:half] = total.astype(BF)
        grad_ref[:, half:] = jnp.full((16 * RANK, LANES), id_ref[0].astype(F32), F32).astype(BF)


def last_call(
    packed, ids, dq, dk, dv, weights, acat, bcat, normed, inner, mixed, inner_o, ba, din, tokens, bh, gains
):
    tok_count, width = tokens.shape
    grad_shape = (16 * RANK, width // 2 + LANES) if packed else (4 * RANK, 2 * width)
    return pl.pallas_call(
        functools.partial(last_body, packed),
        grid=(tok_count // TILE,),
        in_specs=[
            smem(), tall(width), tall(width), tall(width), whole(weights.shape), whole(acat.shape),
            whole(bcat.shape), tall(width), tall(LANES), tall(width), tall(LANES), tall(width),
            tall(LANES), tall(width), tall(width), whole(gains.shape),
        ],
        out_specs=[tall(width), whole(grad_shape)],
        out_shape=[shape_of(tok_count, width), shape_of(*grad_shape)],
        scratch_shapes=[pltpu.VMEM((4 * RANK, 2 * width), F32)],
        cost_estimate=cost(14),
        name="after_attention_backward",
    )(
        ids, dq, dk, dv, weights, acat, bcat, normed, inner, mixed, inner_o, ba, din, tokens, bh, gains
    )


def exchange(value, axes):
    return lax.all_to_all(value, axes, split_axis=0, concat_axis=0, tiled=True)


def gather_all(value, axes, count):
    return exchange(jnp.broadcast_to(value[None], (count,) + value.shape), axes)


def swap(value, partner, group):
    if partner == 0:
        return value
    return lax.ppermute(value, "expert", [(index, index ^ partner) for index in range(group)])


def find_adapters(id_rows):
    count = id_rows.shape[0]
    padded = id_rows.astype(F32)
    if count % LANES:
        padded = jnp.concatenate([padded, jnp.zeros((-count % LANES, LANES), F32)], axis=0)
    return padded.T[0:1, 0:count].astype(jnp.int32)


def sum_expert_body(each, adapters, in_ref, out_ref):
    count, columns = in_ref.shape[0], out_ref.shape[1]
    found = find_adapters(in_ref[:, columns:])
    place = iota((adapters * each, count), 0)
    column = iota((adapters * each, count), 1)
    pick = hot((place // each == found) & (place % each == column % each))
    out_ref[...] = mm(pick, in_ref[:, 0:columns]).astype(BF)


def exchange_expert_grads(grads, group, owners):
    split = min(RANK, owners)
    each, parts = RANK // split, owners // split
    columns = (grads.shape[1] - LANES) // parts
    pieces = grads.reshape(split, each * group, grads.shape[1])
    if parts > 1:
        ids = jnp.broadcast_to(pieces[:, None, :, parts * columns :], (split, parts, each * group, LANES))
        pieces = pieces[:, :, : parts * columns].reshape(split, each * group, parts, columns)
        pieces = jnp.concatenate([pieces.transpose(0, 2, 1, 3), ids], axis=-1)
        pieces = pieces.reshape(owners, each * group, columns + LANES)
    return exchange(pieces, "dp").reshape(owners * group * each, columns + LANES)


def sum_expert_grads(got, adapters, owners):
    columns = got.shape[1] - LANES
    each = RANK // min(RANK, owners)
    return pl.pallas_call(
        functools.partial(sum_expert_body, each, adapters),
        out_shape=shape_of(adapters * each, columns),
        cost_estimate=cost(2.2),
        name="expert_gradient_part",
    )(got)


def finish_expert_body(split, adapters, hidden, in_ref, *refs):
    down_ref, up_ref, out_down_ref, out_up_ref = refs[-4:]
    each = RANK // split
    rows = adapters * each
    count = split * rows
    width = out_up_ref.shape[1]

    def place(value):
        return value // each % adapters * RANK + value // (adapters * each) * each + value % each

    move = hot(iota((count, count), 0) == place(iota((count, count), 1)))
    back = hot(iota((count, count), 1) == place(iota((count, count), 0)))

    def part(start, size):
        span = slice(start, start + size)
        rows_of = [in_ref[owner, :, span] for owner in range(split)]
        return jnp.concatenate(rows_of, axis=0)

    for index in range(2):
        up_ref[index] = mm(move, part(index * hidden, hidden))
    out_down_ref[...] = mm_tn(part(2 * hidden, hidden), back)
    base = 3 * hidden
    out_up_ref[...] = mm(move, part(base, width))
    for index in range(2):
        base += width
        down_ref[index] = mm_tn(part(base, width), back)


def finish_expert_call(index, local, everything, outs, adapters, width, hidden):
    owners, rows, columns = everything.shape
    total = adapters * RANK
    shapes = [(local, 2, width, total), (local, 2, total, hidden), (local, hidden, total),
              (local, total, width)]
    specs = [
        pl.BlockSpec((None,) + shape[1:], lambda *_, rank=len(shape): (index,) + (0,) * (rank - 1))
        for shape in shapes
    ]
    return pl.pallas_call(
        functools.partial(finish_expert_body, owners, adapters, hidden),
        grid=(1,),
        in_specs=[whole(everything.shape)] + [pl.BlockSpec(memory_space=pl.ANY)] * len(outs),
        out_specs=specs,
        out_shape=[shape_of(*shape, dtype=F32) for shape in shapes],
        input_output_aliases={1 + place: place for place in range(len(outs))},
        cost_estimate=cost(4),
        name="expert_gradient_sums",
    )(everything, *outs)


def spread_expert_grads(own, adapters, owners):
    split = min(RANK, owners)
    each, parts = RANK // split, owners // split
    everything = gather_all(own, "dp", owners)
    everything = everything.reshape(split, parts, adapters, each, own.shape[1])
    everything = everything.transpose(2, 0, 3, 1, 4)
    return everything.reshape(adapters * RANK, parts * own.shape[1]).astype(F32)


def expert_sums(owned, adapters, owners, width, hidden):
    sums = [spread_expert_grads(value, adapters, owners) for value in owned]
    base = 3 * hidden
    up = [[value[:, 0:hidden], value[:, hidden : 2 * hidden]] for value in sums]
    down = [
        [value[:, base + width * part : base + width * (part + 1)].T for part in (1, 2)]
        for value in sums
    ]
    return (
        jnp.stack([jnp.stack(value) for value in down]),
        jnp.stack([jnp.stack(value) for value in up]),
        jnp.stack([value[:, 2 * hidden : base].T for value in sums]),
        jnp.stack([value[:, base : base + width] for value in sums]),
    )


def finish_adapter_body(adapters, me_ref, *refs):
    piece_refs, (down_ref, up_ref, in_ref) = refs[:-3], refs[-3:]
    half = in_ref.shape[3]
    owners, group = piece_refs[0].shape[0], len(piece_refs)
    for other in range(group):
        place = jnp.bitwise_xor(me_ref[0], other)
        for owner in range(owners):
            in_ref[owner * (group // 2) + place // 2, place % 2] = piece_refs[other][owner]
    count = RANK * adapters

    def place(value):
        return value % adapters * RANK + value // adapters

    move = hot(iota((count, count), 0) == place(iota((count, count), 1)))
    back = hot(iota((count, count), 1) == place(iota((count, count), 0)))
    for part in range(2):
        span = slice(part * half, part * half + half)
        for kind in range(2):
            for index in range(4):
                first = (kind * 4 + index) * adapters
                rows = in_ref[:, part, first : first + adapters, :].astype(F32)
                rows = rows.reshape(count, half).astype(BF)
                if kind == 0:
                    down_ref[index, span, :] = mm_tn(rows, back)
                else:
                    up_ref[index, :, span] = mm(move, rows)


def sum_adapter_body(kinds, adapters, in_ref, out_ref):
    count, columns = in_ref.shape[0], out_ref.shape[-1]
    found = find_adapters(in_ref[:, columns:])
    place = iota((adapters * kinds, count), 0)
    column = iota((adapters * kinds, count), 1)
    pick = hot((place % adapters == found) & (place // adapters == column % kinds))
    own = mm(pick, in_ref[:, 0:columns]).astype(BF)
    for index in range(out_ref.shape[0]):
        out_ref[index] = own


def adapter_sums(grads, meanwhile, ids, adapters, owners, group, width):
    axes, everyone = ("dp", "expert"), owners * group
    if everyone == 2 * RANK and group == 4:
        kinds = 8
        got = exchange(grads.reshape(everyone, kinds, grads.shape[1]), axes)
        got, meanwhile = lax.optimization_barrier((got, meanwhile))
        own = pl.pallas_call(
            functools.partial(sum_adapter_body, kinds, adapters),
            out_shape=shape_of(owners, kinds * adapters, width // 2),
            cost_estimate=cost(2.0),
            name="adapter_gradient_part",
        )(got.reshape(everyone * kinds, grads.shape[1]))
        mine = exchange(own, "dp")
        across = swap(mine, 2, group)
        full = [mine, swap(mine, 1, group), across, swap(across, 1, group)]
        total = adapters * RANK
        down, upper = pl.pallas_call(
            functools.partial(finish_adapter_body, adapters),
            in_specs=[smem()] + [pl.BlockSpec(memory_space=pltpu.VMEM)] * group,
            out_shape=[shape_of(4, width, total, dtype=F32), shape_of(4, total, width, dtype=F32)],
            scratch_shapes=[pltpu.VMEM((RANK, 2, kinds * adapters, width // 2), BF)],
            cost_estimate=cost(3.6),
            name="adapter_gradient_sums",
        )(lax.axis_index("expert").reshape(1).astype(jnp.int32), *full)
        return down, upper, meanwhile
    all_ids = exchange(jnp.broadcast_to(ids, (everyone,)), axes)
    pieces = grads.reshape(everyone, RANK * 4 * 2 * width // everyone)
    got = exchange(pieces, axes)
    pick = (jnp.arange(adapters, dtype=jnp.int32)[:, None] == all_ids[None, :]).astype(BF)
    own = jnp.dot(pick, got, preferred_element_type=F32).astype(BF)
    full = gather_all(own, axes, everyone)
    full = full.reshape(RANK, everyone // RANK, adapters, -1).transpose(2, 0, 1, 3)
    full = full.reshape(adapters * RANK, 4, 2, width).astype(F32)
    return full[:, :, 0].transpose(1, 2, 0), full[:, :, 1].transpose(1, 0, 2), meanwhile


def body(
    tokens,
    cotangent,
    lengths,
    adapter_ids,
    routes,
    prev_logits,
    norm_gains,
    input_weights,
    output_weight,
    adapter_down,
    adapter_up,
    router,
    residual_mix,
    constant_mix,
    constant_vectors,
    expert_gate,
    expert_up,
    expert_down,
    expert_adapter_down,
    expert_adapter_up,
    output_adapter_down,
    output_adapter_up,
):
    tok_count, width = tokens.shape
    hidden_width = expert_gate.shape[2]
    group, owners = lax.axis_size("expert"), lax.axis_size("dp")
    local = expert_gate.shape[0]
    adapters = adapter_down.shape[-1] // RANK
    cosine, sine = (jnp.asarray(table) for table in turn_tables(tok_count))
    weights = (
        expert_gate, expert_up, expert_down, expert_adapter_down, expert_adapter_up,
        output_adapter_down, output_adapter_up,
    )
    per_owner = RANK // min(RANK, owners)
    everyone = owners * group
    me = lax.axis_index("expert")

    me = me.reshape(1).astype(jnp.int32)

    rows = jnp.concatenate(
        [prev_logits, routes.astype(F32), jnp.zeros((tok_count, 2), F32)], axis=1
    ).T
    slots, *grad_sends = route_call(local, group, lengths, me, rows, cotangent)
    cots = [swap(value, partner, group) for partner, value in enumerate(grad_sends)]
    small = jnp.concatenate(
        [
            router.astype(F32), jnp.zeros((width, MIX_ROW - EXPERTS - 4), F32), constant_mix,
            jnp.zeros((width, LANES - MIX_ROW - 4), F32),
        ],
        axis=1,
    )
    normed, inner, queries, keys, values, acat, bcat, table = pre_call(
        adapter_ids, tokens, norm_gains, input_weights, adapter_down, adapter_up, cosine, sine, small,
        constant_vectors,
    )
    mixed, q2 = attend_call(lengths, queries, keys, values)
    mixed, cots = lax.optimization_barrier((mixed, cots))
    mixer = jnp.pad(residual_mix.T, ((0, 4), (0, 4)))
    hidden, ei, inner_o, data, cols = post_call(
        local, group, me, mixed, tokens, output_weight, acat, bcat, norm_gains, table, mixer, rows,
        slots,
    )
    sends = send_call(local, group, me, adapter_ids, slots, data, ei)
    near, far = tuple(range(group // 2)), tuple(range(group // 2, group))
    sent_near = [swap(sends[partner], partner, group) for partner in near]
    sent_far = []
    for index in range(local):
        pieces = [sends[group // 2 + place * local + index] for place in range(len(far))]
        if index > 0:
            pieces, sent_near = lax.optimization_barrier((pieces, sent_near))
        sent_far.append([swap(piece, partner, group) for piece, partner in zip(pieces, far)])
    backs = [[None] * group for _ in range(local)]
    results = [[None] * group for _ in range(local)]
    grads, last = [], None
    for index in range(local):
        before = None
        for pair in (near, far) if index % 2 == 0 else (far, near):
            pieces = sent_near if pair == near else sent_far[index]
            if last is not None:
                pieces, last = lax.optimization_barrier((pieces, last))
            if index == local - 1 and pair == near:
                pieces, backs[:index] = lax.optimization_barrier((pieces, backs[:index]))
            outs = expert_call(
                index, pair, group, per_owner, pieces, [cots[partner] for partner in pair], before, weights
            )
            before = last = outs[-1]
            for place, partner in enumerate(pair):
                backs[index][partner] = swap(outs[place], partner, group)
                results[index][partner] = outs[len(pair) + place]
        grads.append(before)
    backs = [value for some in backs for value in some]

    parts = [exchange_expert_grads(grad, group, owners) for grad in grads]
    sums = functools.partial(sum_expert_grads, adapters=adapters, owners=owners)
    parts[:-1], last = lax.optimization_barrier((parts[:-1], last))
    owned = [sums(part) for part in parts[:-1]]
    backs[-2:], owned = lax.optimization_barrier((backs[-2:] , owned))
    gather = functools.partial(lax.all_gather, axis_name="dp", axis=0, tiled=False)
    if owners <= RANK:
        owned = [gather(own) for own in owned]
    back_hidden, back_attention, back_inner_o, back_mixed = combine_call(
        lengths, backs, rows, data, cols, cotangent, ei, hidden, norm_gains, output_weight, acat, bcat,
        table,
    )
    flat = [value for some in results for value in some]
    flat, back_mixed = lax.optimization_barrier((flat, back_mixed))
    flat = [swap(value, place % group, group) for place, value in enumerate(flat)]

    dq, dk, dv = attend_back_call(lengths, q2, keys, values, mixed, back_mixed, cosine, sine)
    parts[-1], dq = lax.optimization_barrier((parts[-1], dq))
    own = sums(parts[-1])
    dq, own, owned = lax.optimization_barrier((dq, own, owned))
    owned.append(gather(own) if owners <= RANK else own)
    input_back, adapter_grads = last_call(
        everyone == 2 * RANK and group == 4, adapter_ids, dq, dk, dv, input_weights, acat, bcat, normed, inner, mixed, inner_o,
        back_attention, back_inner_o, tokens, back_hidden, norm_gains,
    )
    layer_out = result_call(lengths, flat, cols, ei, hidden, table)
    outs = []
    if owners <= RANK:
        for index, own in enumerate(owned[:-1]):
            outs = finish_expert_call(index, local, own, outs, adapters, width, hidden_width)
    down_sum, upper_sum, (layer_out, outs) = adapter_sums(
        adapter_grads, (layer_out, outs), adapter_ids, adapters, owners, group, width
    )
    if owners <= RANK:
        outs = finish_expert_call(
            local - 1, local, owned[-1], outs, adapters, width, hidden_width
        )
    else:
        outs = expert_sums(owned, adapters, owners, width, hidden_width)
    in_down_sum, in_up_sum, out_down_sum, out_up_sum = outs
    return (
        layer_out,
        input_back,
        down_sum,
        upper_sum,
        in_down_sum,
        in_up_sum,
        out_down_sum,
        out_up_sum,
    )


def solution(mesh):
    tokens_spec, copied = P(("dp", "expert"), None), P()
    owned = P("expert")
    placed = (
        (tokens_spec, tokens_spec, P(("dp", "expert")), P(("dp", "expert")), tokens_spec, tokens_spec)
        + (copied,) * 9
        + (owned,) * 7
    )
    return jax.shard_map(
        body,
        mesh=mesh,
        in_specs=placed,
        out_specs=(tokens_spec, tokens_spec, copied, copied) + (owned,) * 4,
        check_vma=False,
    )
```

```python
import functools
import math

import jax
import jax.numpy as jnp
import numpy as np
from jax import lax
from jax.experimental import pallas as pl
from jax.experimental.pallas import tpu as pltpu
from jax.sharding import PartitionSpec as P

HEADS = 12
HD = 64
EXPERTS = 8
RANK = 16
CAP = 192
EPSILON = 1e-06
F32 = jnp.float32
BF = jnp.bfloat16
NEG = -1e30
LANES = 128
TILE = 256
STEP = 512
FTILE = 512
PAIRS = HEADS // 2
PARAMS = pltpu.CompilerParams(vmem_limit_bytes=67043328)
META = 8
MIX_ROW = 16
VECTOR_ROW = 20
TARGET_LANE = 24
KEEP_LANE = 26
PIECE = CAP + META


def mm(left, right):
    return jnp.dot(left, right, preferred_element_type=F32)


def mm_nt(left, right):
    return lax.dot_general(left, right, (((1,), (1,)), ((), ())), preferred_element_type=F32)


def mm_tn(left, right):
    return lax.dot_general(left, right, (((0,), (0,)), ((), ())), preferred_element_type=F32)


def iota(shape, axis):
    return lax.broadcasted_iota(jnp.int32, shape, axis)


def hot(condition):
    return jnp.where(condition, 1.0, 0.0).astype(BF)


def split2(value):
    high = value.astype(BF)
    return high, (value - high.astype(F32)).astype(BF)


def split3(value):
    high = value.astype(BF)
    rest = value - high.astype(F32)
    middle = rest.astype(BF)
    return high, middle, (rest - middle.astype(F32)).astype(BF)


def whole(shape):
    zeros = (0,) * len(shape)
    return pl.BlockSpec(shape, lambda *_: zeros)


def smem():
    return pl.BlockSpec(memory_space=pltpu.SMEM)


def tall(width):
    return pl.BlockSpec((STEP, width), lambda i: (i, 0))


def wide(height):
    return pl.BlockSpec((height, STEP), lambda i: (0, i))


def tile(width):
    return pl.BlockSpec((TILE, width), lambda i: (i, 0))


def side_by_side(stages):
    running = [stages(slice(start, start + TILE)) for start in range(0, STEP, TILE)]
    while running:
        running = [stage for stage in running if next(stage, True) is None]


def shape_of(*shape, dtype=BF):
    return jax.ShapeDtypeStruct(shape, dtype)


def cost(microseconds):
    return pl.CostEstimate(flops=int(microseconds * 1e+09), bytes_accessed=0, transcendentals=0)


@functools.lru_cache(maxsize=None)
def turn_tables(length_in):
    half = HD // 2
    inverse = np.exp(
        np.arange(half, dtype=np.float32) * np.float32(-2.0 * math.log(10000.0) / HD)
    ).astype(np.float32)
    angles = np.arange(length_in, dtype=np.float32)[:, None] * inverse[None, :]
    cosine = np.tile(np.cos(angles.astype(np.float64)).astype(np.float32), (1, 4))
    sine = np.sin(angles.astype(np.float64)).astype(np.float32)
    return cosine, np.tile(np.concatenate([-sine, sine], axis=1), (1, 2))


def rope(value, cosine, sine):
    first = iota(value.shape, 1) % HD < HD // 2
    turned = jnp.where(first, pltpu.roll(value, LANES - HD // 2, 1), pltpu.roll(value, HD // 2, 1))
    return value * cosine + turned * sine


def find_slots(length, rows_ref, slot_ref):
    tok_count = slot_ref.shape[1]
    before = hot(iota((TILE, TILE), 0) < iota((TILE, TILE), 1))
    carry = jnp.zeros((2 * EXPERTS, 1), F32)
    for start in range(0, tok_count, TILE):
        span = slice(start, start + TILE)
        expert = iota((2 * EXPERTS, TILE), 0).astype(F32)
        token = iota((2 * EXPERTS, TILE), 1) + start
        named = (rows_ref[12:13, span] == expert) | (rows_ref[13:14, span] == expert)
        hit = named & (token < length) & (expert < EXPERTS)
        hits = jnp.where(hit, 1.0, 0.0)
        slots = mm(hits.astype(BF), before) + carry
        carry = carry + jnp.sum(hits, axis=1, keepdims=True)
        slot_ref[:, span] = jnp.where(hit, slots, -1.0)[:EXPERTS].astype(jnp.int32)


def pick_rows(slot_ref, step, me, local):
    first = jnp.bitwise_xor(step, me) * local
    place = iota((CAP, slot_ref.shape[1]), 0)
    return first, [hot(place == slot_ref[pl.ds(first + index, 1), :]) for index in range(local)]


def store_piece(out_refs, step, other, index, value, start):
    @pl.when(step == other)
    def _():
        out_refs[index][start : start + value.shape[0], :] = value


def route_body(local, group, len_ref, me_ref, rows_ref, source_ref, slot_ref, *out_refs):
    step = pl.program_id(0)

    @pl.when(step == 0)
    def _():
        find_slots(len_ref[0], rows_ref, slot_ref)

    _, chosen = pick_rows(slot_ref, step, me_ref[0], local)
    rows = mm(jnp.concatenate(chosen, axis=0), source_ref[...]).astype(BF)
    for other in range(group):
        store_piece(out_refs, step, other, other, rows, 0)


def route_call(local, group, length, me, rows, source):
    tok_count, width = source.shape
    return pl.pallas_call(
        functools.partial(route_body, local, group),
        grid=(group,),
        in_specs=[smem(), smem(), whole(rows.shape), whole(source.shape)],
        out_specs=[whole((EXPERTS, tok_count))] + [whole((local * CAP, width))] * group,
        out_shape=[shape_of(EXPERTS, tok_count, dtype=jnp.int32)]
        + [shape_of(local * CAP, width)] * group,
        compiler_params=PARAMS,
        cost_estimate=cost(6.5),
        name="route_rows",
    )(length, me, rows, source)


def send_body(local, group, me_ref, id_ref, slot_ref, data_ref, source_ref, *out_refs):
    step = pl.program_id(0)
    width = source_ref.shape[1]
    first, chosen = pick_rows(slot_ref, step, me_ref[0], local)
    rows = mm(jnp.concatenate(chosen, axis=0), source_ref[...]).astype(BF)
    for index in range(local):
        pieces = split3(data_ref[pl.ds(first + index, 1), :])
        stack = jnp.concatenate(
            [piece.astype(F32) for piece in pieces]
            + [jnp.zeros((13, chosen[index].shape[1]), F32)],
            axis=0,
        ).astype(BF)
        gates = mm_nt(stack, chosen[index])[0:META]
        gates = jnp.where(iota(gates.shape, 0) == 3, id_ref[0].astype(F32), gates)
        meta = jnp.concatenate([gates, jnp.zeros((META, width - CAP), F32)], axis=1)
        kept = rows[index * CAP : index * CAP + CAP]
        for other in range(group):
            far = other >= group // 2
            place = group // 2 + (other - group // 2) * local + index if far else other
            start = 0 if far else index * PIECE
            store_piece(out_refs, step, other, place, kept, start)
            store_piece(out_refs, step, other, place, meta.astype(BF), start + CAP)


def send_call(local, group, me, ids, slots, data, source):
    tok_count, width = source.shape
    heights = [local * PIECE] * (group // 2) + [PIECE] * ((group - group // 2) * local)
    return pl.pallas_call(
        functools.partial(send_body, local, group),
        grid=(group,),
        in_specs=[smem(), smem(), whole(slots.shape), whole(data.shape), whole(source.shape)],
        out_specs=[whole((height, width)) for height in heights],
        out_shape=[shape_of(height, width) for height in heights],
        compiler_params=PARAMS,
        cost_estimate=cost(8.4),
        name="send_rows",
    )(me, ids, slots, data, source)


def pre_body(
    id_ref, x_ref, gain_ref, w_ref, ad_ref, au_ref, cos_ref, sin_ref, small_ref, vec_ref,
    normed_ref, inner_ref, q_ref, k_ref, v_ref, acat_ref, bcat_ref, table_ref,
):
    @pl.when(pl.program_id(0) == 0)
    def _():
        first = RANK * id_ref[0]
        total = None
        for index in range(4):
            row, column = iota((LANES, LANES), 0), iota((LANES, LANES), 1)
            place = hot((row >= first) & (row < first + RANK) & (column == (row - first) * 4 + index))
            part = mm(ad_ref[index], place)
            total = part if total is None else total + part
            place = hot(
                (column >= first) & (column < first + RANK) & (row == (column - first) * 4 + index)
            )
            bcat_ref[index] = mm(place, au_ref[index]).astype(BF)
        acat_ref[...] = total.astype(BF)
        table = small_ref[...].T
        number = iota(table.shape, 0)
        for index in range(2):
            table = jnp.where(number == VECTOR_ROW + index, vec_ref[index : index + 1, :], table)
        table_ref[...] = table

    def stages(at):
        x = x_ref[at].astype(F32)
        scale = lax.rsqrt(jnp.mean(x * x, axis=-1, keepdims=True) + EPSILON)
        normed = (x * scale * gain_ref[0:1, :]).astype(BF)
        normed_ref[at] = normed
        yield
        inner = mm(normed, acat_ref[...]).astype(BF)
        inner_ref[at] = inner
        yield
        for index, out_ref in enumerate((q_ref, k_ref, v_ref)):
            value = mm(normed, w_ref[index]) + mm(inner, bcat_ref[index])
            yield
            if index == 2:
                out_ref[at] = value.astype(BF)
                continue
            for pair in range(PAIRS):
                span = slice(pair * LANES, pair * LANES + LANES)
                turned = rope(value[:, span], cos_ref[at], sin_ref[at]).astype(BF)
                if index == 0:
                    turned = (turned.astype(F32) * HD**-0.5).astype(BF)
                out_ref[at, span] = turned
            yield

    side_by_side(stages)


def pre_call(ids, tokens, gains, weights, down, upper, cosine, sine, small, vectors):
    tok_count, width = tokens.shape
    return pl.pallas_call(
        pre_body,
        grid=(tok_count // STEP,),
        in_specs=[
            smem(), tall(width), whole(gains.shape), whole(weights.shape), whole(down.shape),
            whole(upper.shape), tall(LANES), tall(LANES), whole(small.shape), whole(vectors.shape),
        ],
        out_specs=[
            tall(width), tall(LANES), tall(width), tall(width), tall(width),
            whole((width, LANES)), whole(upper.shape), whole((LANES, width)),
        ],
        out_shape=[
            shape_of(tok_count, width), shape_of(tok_count, LANES), shape_of(tok_count, width),
            shape_of(tok_count, width), shape_of(tok_count, width), shape_of(width, LANES),
            shape_of(*upper.shape), shape_of(LANES, width, dtype=F32),
        ],
        compiler_params=PARAMS,
        cost_estimate=cost(12.3),
        name="before_attention",
    )(ids, tokens, gains, weights, down, upper, cosine, sine, small, vectors)


def attend_body(len_ref, q_ref, k_ref, v_ref, mixed_ref, q2_ref):
    tok_count = q_ref.shape[0]
    lane = iota((tok_count, LANES), 1)
    hidden_key = iota((tok_count, LANES), 0) >= len_ref[0]
    row = iota((LANES, tok_count), 0)
    row_tile = row[:, :TILE]
    causal = iota((TILE, TILE), 0) <= iota((TILE, TILE), 1)
    queries_t = q_ref[...].astype(F32).T
    values_t = v_ref[...].astype(F32).T
    keys = k_ref[...].astype(F32)
    heads = []
    for head in range(2):
        spare = HD * (1 - head)
        bias = jnp.where((lane == spare) & hidden_key, NEG, 0.0)
        one = jnp.where(row == spare, 1.0, 0.0)
        own = row // HD == head
        heads.append(
            (
                jnp.where(lane // HD == head, keys, bias).astype(BF),
                jnp.where(own, queries_t, one).astype(BF),
                jnp.where(own, values_t, one).astype(BF),
            )
        )
    units = [(start, head) for start in range(0, tok_count, TILE) for head in range(2)]

    def score(unit):
        start, head = unit
        keys, queries, _ = heads[head]
        part = queries[:, start : start + TILE]
        near = mm(keys[start : start + TILE], part)
        return near, mm(keys[:start], part) if start else None

    outs = {}
    waiting = score(units[0])
    for index, (start, head) in enumerate(units):
        near, far = waiting
        waiting = score(units[index + 1]) if index + 1 < len(units) else None
        spare = HD * (1 - head)
        _, queries, values = heads[head]
        near = jnp.where(causal, near, NEG)
        top = jnp.max(near, axis=0, keepdims=True)
        if start:
            top = jnp.maximum(top, jnp.max(far, axis=0, keepdims=True))
        mixed = mm(values[:, start : start + TILE], jnp.exp(near - top).astype(BF))
        if start:
            mixed = mixed + mm(values[:, :start], jnp.exp(far - top).astype(BF))
        total = mixed[spare : spare + 1]
        outs[head] = mixed * (1.0 / total)
        kept = queries[:, start : start + TILE]
        logs = jnp.zeros((LANES, TILE), F32)
        for offset, piece in enumerate(split3(top + jnp.log(total))):
            logs = jnp.where(row_tile == spare + 1 + offset, piece.astype(F32), logs)
        q2_ref[head * LANES : head * LANES + LANES, start : start + TILE] = kept + logs.astype(BF)
        if head == 1:
            mixed = jnp.where(row_tile < HD, outs[0], outs[1])
            mixed_ref[start : start + TILE] = mixed.T.astype(BF)


def attend_call(length, queries, keys, values):
    tok_count, width = queries.shape
    column = pl.BlockSpec((tok_count, LANES), lambda i: (0, i))
    return pl.pallas_call(
        attend_body,
        grid=(PAIRS,),
        in_specs=[smem(), column, column, column],
        out_specs=[column, pl.BlockSpec((2 * LANES, tok_count), lambda i: (i, 0))],
        out_shape=[shape_of(tok_count, width), shape_of(2 * width, tok_count)],
        compiler_params=PARAMS,
        cost_estimate=cost(15),
        name="attention_forward",
    )(length, queries, keys, values)


def attend_back_body(
    len_ref, q2_ref, k_ref, v_ref, mixed_ref, back_ref, cos_ref, sin_ref,
    dq_ref, dk_ref, dv_ref, acc_ref,
):
    tok_count = k_ref.shape[0]
    lane = iota((tok_count, LANES), 1)
    position = iota((tok_count, LANES), 0)
    bias = jnp.where(position < len_ref[0], 0.0, NEG)
    causal = iota((TILE, TILE), 0) <= iota((TILE, TILE), 1)
    row = iota((LANES, tok_count), 0)
    back = back_ref[...].astype(F32)
    product_t = (back * mixed_ref[...].astype(F32)).T
    back_t = back.T
    keys, values = k_ref[...].astype(F32), v_ref[...].astype(F32)
    grads = []
    for head in range(2):
        own = lane // HD == head
        spare = HD * (1 - head)
        minus = jnp.where((lane > spare) & (lane < spare + 4), -1.0, 0.0)
        q2 = q2_ref[head * LANES : head * LANES + LANES, :]
        k2f = jnp.where(own, keys, jnp.where(lane == spare, bias, minus))
        k2 = k2f.astype(BF)
        k2t = k2f.T.astype(BF)
        v2 = jnp.where(own, values, minus).astype(BF)
        own_row = row // HD == head
        delta = jnp.sum(jnp.where(own_row, product_t, 0.0), axis=0, keepdims=True)
        back2 = jnp.where(own_row, back_t, 0.0)
        for offset, piece in enumerate(split3(delta)):
            back2 = jnp.where(row == spare + 1 + offset, piece.astype(F32), back2)
        back2 = back2.astype(BF)
        dk_parts, dv_parts = [], []
        for start in range(0, tok_count, TILE):
            stop = start + TILE
            scores = mm(k2[start:stop], q2[:, start:])
            slopes = mm(v2[start:stop], back2[:, start:])
            diagonal = jnp.where(causal, scores[:, :TILE], NEG)
            scores = (
                diagonal
                if stop == tok_count
                else jnp.concatenate([diagonal, scores[:, TILE:]], axis=1)
            )
            weights = jnp.exp(scores)
            turned = (weights * slopes).astype(BF)
            dv_parts.append(mm_nt(weights.astype(BF), back2[:, start:]))
            dk_parts.append(mm_nt(turned, q2[:, start:]))
            update = mm(k2t[:, start:stop], turned)
            if start == 0:
                acc_ref[head] = update
            else:
                acc_ref[head, :, start:] += update
        grads.append((jnp.concatenate(dk_parts, axis=0), jnp.concatenate(dv_parts, axis=0)))
    low_lane = lane < HD
    cosine, sine = cos_ref[...], -sin_ref[...]
    dq = jnp.where(row < HD, acc_ref[0], acc_ref[1]).T * HD**-0.5
    dq_ref[...] = rope(dq, cosine, sine).astype(BF)
    dk = jnp.where(low_lane, grads[0][0], grads[1][0])
    dk_ref[...] = rope(dk, cosine, sine).astype(BF)
    dv_ref[...] = jnp.where(low_lane, grads[0][1], grads[1][1]).astype(BF)


def attend_back_call(length, q2, keys, values, mixed, back, cosine, sine):
    tok_count, width = keys.shape
    column = pl.BlockSpec((tok_count, LANES), lambda i: (0, i))
    return pl.pallas_call(
        attend_back_body,
        grid=(PAIRS,),
        in_specs=[
            smem(), pl.BlockSpec((2 * LANES, tok_count), lambda i: (i, 0)), column, column, column,
            column, whole(cosine.shape), whole(sine.shape),
        ],
        out_specs=[column] * 3,
        out_shape=[shape_of(tok_count, width)] * 3,
        scratch_shapes=[pltpu.VMEM((2, LANES, tok_count), F32)],
        compiler_params=PARAMS,
        cost_estimate=cost(25),
        name="attention_backward",
    )(length, q2, keys, values, mixed, back, cosine, sine)


def post_body(
    local, group, me_ref, mixed_ref, x_ref, wo_ref, acat_ref, bcat_ref, gain_ref, table_ref, mix_ref,
    rows_ref, slot_ref, hidden_ref, ei_ref, inner_ref, data_ref, cols_ref,
):
    pieces = split3(table_ref[...])

    def stages(at):
        mixed = mixed_ref[at]
        inner = mm(mixed, acat_ref[...]).astype(BF)
        inner_ref[at] = inner
        yield
        hidden = x_ref[at].astype(F32) + (mm(mixed, wo_ref[...]) + mm(inner, bcat_ref[0]))
        hidden_ref[at] = hidden
        yield
        scale = lax.rsqrt(jnp.mean(hidden * hidden, axis=-1, keepdims=True) + EPSILON)
        ei = (hidden * scale * gain_ref[1:2, :]).astype(BF)
        ei_ref[at] = ei
        yield
        read = None
        for piece in pieces:
            part = mm_nt(piece, ei)
            read = part if read is None else read + part
        yield
        logits = read[0:16]
        for index in range(EXPERTS + 4):
            logits = logits + mix_ref[:, index : index + 1] * rows_ref[index : index + 1, at]
        first, second = rows_ref[12:13, at], rows_ref[13:14, at]
        number = iota((16, TILE), 0).astype(F32)
        one = jnp.sum(jnp.where(number == first, logits, 0.0), axis=0, keepdims=True)
        two = jnp.sum(jnp.where(number == second, logits, 0.0), axis=0, keepdims=True)
        top = jnp.maximum(one, two)
        one, two = jnp.exp(one - top), jnp.exp(two - top)
        gate_a, gate_b = one / (one + two), two / (one + two)
        mixes = read[MIX_ROW : MIX_ROW + 4]
        shares = []
        for index in range(2):
            left, right = mixes[2 * index : 2 * index + 1], mixes[2 * index + 1 : 2 * index + 2]
            top = jnp.maximum(left, right)
            left, right = jnp.exp(left - top), jnp.exp(right - top)
            shares += [left / (left + right), right / (left + right)]

        def both(value):
            return jnp.where(first == value, gate_a, 0.0) + jnp.where(second == value, gate_b, 0.0)

        gates = jnp.where(number == first, gate_a, 0.0) + jnp.where(number == second, gate_b, 0.0)
        beta_a, beta_b = both(EXPERTS + 2.0), both(EXPERTS + 3.0)
        keep = both(EXPERTS + 1.0) + beta_a * shares[0] + beta_b * shares[2]
        data_ref[0:8, at] = gates[0:8]
        tail = [gate_a, gate_b] + shares + [beta_a, beta_b]
        data_ref[8:16, at] = jnp.concatenate(tail, axis=0)
        yield
        slots = slot_ref[:, at].astype(F32)
        expert = iota((EXPERTS, TILE), 0)
        partner = jnp.bitwise_xor(expert // local, me_ref[0])
        base = ((expert % local) * (group * CAP) + partner * CAP).astype(F32)
        place = jnp.where(slots >= 0, slots + base + 1.0, 0.0)
        expert = expert.astype(F32)
        target_a = jnp.sum(jnp.where(expert == first, place, 0.0), axis=0, keepdims=True) - 1.0
        target_b = jnp.sum(jnp.where(expert == second, place, 0.0), axis=0, keepdims=True) - 1.0
        stack = jnp.concatenate(
            [jnp.zeros((VECTOR_ROW, TILE), F32), beta_a * shares[1], beta_b * shares[3]]
            + [jnp.zeros((2, TILE), F32), target_a, target_b, keep]
            + [jnp.zeros((LANES - KEEP_LANE - 1, TILE), F32)],
            axis=0,
        )
        cols_ref[at] = stack.T

    side_by_side(stages)


def post_call(
    local, group, me, mixed, tokens, weight, acat, bcat, gains, table, mixer, rows, slots
):
    tok_count, width = tokens.shape
    return pl.pallas_call(
        functools.partial(post_body, local, group),
        grid=(tok_count // STEP,),
        in_specs=[
            smem(), tall(width), tall(width), whole(weight.shape), whole(acat.shape),
            pl.BlockSpec((1, LANES, width), lambda i: (3, 0, 0)), whole(gains.shape),
            whole(table.shape), whole(mixer.shape), wide(16), wide(EXPERTS),
        ],
        out_specs=[tall(width), tall(width), tall(LANES), wide(16), tall(LANES)],
        out_shape=[
            shape_of(tok_count, width, dtype=F32), shape_of(tok_count, width),
            shape_of(tok_count, LANES), shape_of(16, tok_count, dtype=F32),
            shape_of(tok_count, LANES, dtype=F32),
        ],
        compiler_params=PARAMS,
        cost_estimate=cost(8),
        name="after_attention",
    )(me, mixed, tokens, weight, acat, bcat, gains, table, mixer, rows, slots)


def expert_body(
    pair, per_owner, group, steps, has_grad, *refs
):
    count = len(pair)
    piece_refs, refs = refs[:count], refs[count:]
    cot_refs, refs = refs[:count], refs[count:]
    wg_ref, wu_ref, wd_ref, dn_ref, up_ref, od_ref, ou_ref = refs[:7]
    refs = refs[7:]
    before_ref = None
    if has_grad:
        before_ref, refs = refs[0], refs[1:]
    back_refs, refs = refs[:count], refs[count:]
    out_refs, refs = refs[:count], refs[count:]
    (
        grad_ref, x_ref, g_ref, gate_ref, pick_ref, dr_ref, zg_ref, zu_ref, dzd_ref, zgt_ref, zut_ref,
        dzdt_ref, racc_ref, xacc_ref, zd_acc, dzg_acc, dzu_acc, h_ref, dg_ref, du_ref,
    ) = refs
    step = pl.program_id(0)
    rows, width = x_ref.shape
    compact = group * RANK
    chosen = pick_ref[...] > 0.0

    def fold(value):
        place = iota((compact, LANES), 0)
        block = per_owner * group
        inner = place // block * per_owner + place % per_owner
        folded = mm_nt(hot(iota((compact, LANES), 1) % RANK == inner), value)
        place = iota((compact, rows), 0)
        owner = place % block // per_owner
        mine = iota((compact, rows), 1) // CAP + pair[0]
        return jnp.where(mine == owner, folded, 0.0).astype(BF)

    def put(start, value):
        span = pl.ds(start, value.shape[1])
        if has_grad:
            value = value + before_ref[:, span].astype(F32)
        grad_ref[:, span] = value.astype(BF)

    @pl.when(step == 0)
    def _():
        for index in range(count):
            span = slice(index * CAP, index * CAP + CAP)
            x_ref[span] = piece_refs[index][0:CAP]
            g_ref[span] = cot_refs[index][...]
            meta = piece_refs[index][CAP:PIECE].astype(F32)
            gate = (meta[0:1] + meta[1:2] + meta[2:3])[:, 0 : 2 * LANES]
            gate_ref[span] = jnp.broadcast_to(gate, (LANES, 2 * LANES)).T[0:CAP]
            lane = (iota((CAP, LANES), 1) // RANK).astype(F32)
            pick_ref[span] = jnp.where(lane == meta[3:4, 0:LANES], 1.0, 0.0)
        picked = pick_ref[...] > 0.0
        dr = (gate_ref[:, 0:1] * g_ref[...].astype(F32)).astype(BF)
        dr_ref[...] = dr
        zg = jnp.where(picked, mm(x_ref[...], dn_ref[0]), 0.0).astype(BF)
        zu = jnp.where(picked, mm(x_ref[...], dn_ref[1]), 0.0).astype(BF)
        dzd = jnp.where(picked, mm_nt(dr, ou_ref[...]), 0.0).astype(BF)
        zg_ref[...] = zg
        zu_ref[...] = zu
        dzd_ref[...] = dzd
        zgt_ref[...] = fold(zg)
        zut_ref[...] = fold(zu)
        dzdt_ref[...] = fold(dzd)
        for ref in (racc_ref, xacc_ref, zd_acc, dzg_acc, dzu_acc):
            ref[...] = jnp.zeros_like(ref)

    gate = mm(x_ref[...], wg_ref[...]) + mm(zg_ref[...], up_ref[0])
    upper = mm(x_ref[...], wu_ref[...]) + mm(zu_ref[...], up_ref[1])
    share = 0.5 * jnp.tanh(0.5 * gate) + 0.5
    silu = gate * share
    active = (silu * upper).astype(BF)
    h_ref[...] = active
    back = mm_nt(dr_ref[...], wd_ref[...]) + mm_nt(dzd_ref[...], od_ref[...])
    du = (back * silu).astype(BF)
    dg = (back * upper * (share + silu * (1.0 - share))).astype(BF)
    du_ref[...] = du
    dg_ref[...] = dg
    racc_ref[...] += mm(active, wd_ref[...])
    zd_acc[...] += mm(active, od_ref[...])
    xacc_ref[...] += mm_nt(dg, wg_ref[...]) + mm_nt(du, wu_ref[...])
    dzg_acc[...] += mm_nt(dg, up_ref[0])
    dzu_acc[...] += mm_nt(du, up_ref[1])
    tile = h_ref.shape[1]
    total = steps * tile
    at = pl.multiple_of(step * tile, tile)
    put(at, mm(zgt_ref[...], dg_ref[...]))
    put(total + at, mm(zut_ref[...], du_ref[...]))
    put(2 * total + at, mm(dzdt_ref[...], h_ref[...]))

    @pl.when(step == steps - 1)
    def _():
        zd = jnp.where(chosen, zd_acc[...], 0.0).astype(BF)
        dzg = jnp.where(chosen, dzg_acc[...], 0.0).astype(BF)
        dzu = jnp.where(chosen, dzu_acc[...], 0.0).astype(BF)
        result = racc_ref[...] + mm(zd, ou_ref[...])
        gated = (gate_ref[:, 0:1] * result).astype(BF)
        product = g_ref[...].astype(F32) * result.astype(BF).astype(F32)
        dots = jnp.broadcast_to(jnp.sum(product, axis=-1, keepdims=True), (rows, LANES))
        back_rows = (xacc_ref[...] + mm_nt(dzg, dn_ref[0]) + mm_nt(dzu, dn_ref[1])).astype(BF)
        for index in range(count):
            span = slice(index * CAP, index * CAP + CAP)
            out_refs[index][...] = gated[span]
            back_refs[index][0:CAP, :] = back_rows[span]
            column = jnp.concatenate(
                [dots[span], jnp.zeros((2 * LANES - CAP, LANES), F32)], axis=0
            ).T[0:1]
            meta = jnp.concatenate(
                [piece.astype(F32) for piece in split3(column)]
                + [jnp.zeros((META - 3, 2 * LANES), F32)],
                axis=0,
            )
            meta = jnp.concatenate([meta, jnp.zeros((META, width - 2 * LANES), F32)], axis=1)
            back_refs[index][CAP:PIECE, :] = meta.astype(BF)
        base = 3 * total
        place = iota((compact, LANES), 0)
        owner = place % (per_owner * group) // per_owner
        ids = jnp.zeros((compact, LANES), F32)
        for index in range(count):
            meta = piece_refs[index][CAP:PIECE, 0:LANES].astype(F32)
            ids = jnp.where(owner == pair[index], meta[3:4], ids)
        put(base + 3 * width, ids)
        put(base, mm(fold(zd), dr_ref[...]))
        put(base + width, mm(fold(dzg), x_ref[...]))
        put(base + 2 * width, mm(fold(dzu), x_ref[...]))


def expert_call(index, pair, group, per_owner, pieces, cots, before, weights):
    gate_w, up_w, down_w, in_down, in_up, out_down, out_up = weights
    width, hidden = gate_w.shape[1:]
    rows = len(pair) * CAP
    steps = hidden // FTILE
    columns = 3 * hidden + 3 * width + LANES
    compact = group * RANK
    has_grad = before is not None
    return pl.pallas_call(
        functools.partial(expert_body, pair, per_owner, group, steps, has_grad),
        grid=(steps,),
        in_specs=[
            pl.BlockSpec((PIECE, width), lambda f, row=piece.shape[0] // PIECE > 1: (index * row, 0))
            for piece in pieces
        ]
        + [pl.BlockSpec((CAP, width), lambda f: (index, 0))] * len(pair)
        + [
            pl.BlockSpec((None, width, FTILE), lambda f: (index, 0, f)),
            pl.BlockSpec((None, width, FTILE), lambda f: (index, 0, f)),
            pl.BlockSpec((None, FTILE, width), lambda f: (index, f, 0)),
            pl.BlockSpec((None, 2, width, LANES), lambda f: (index, 0, 0, 0)),
            pl.BlockSpec((None, 2, LANES, FTILE), lambda f: (index, 0, 0, f)),
            pl.BlockSpec((None, FTILE, LANES), lambda f: (index, f, 0)),
            pl.BlockSpec((None, LANES, width), lambda f: (index, 0, 0)),
        ]
        + [whole((compact, columns))] * has_grad,
        out_specs=[whole((PIECE, width))] * len(pair)
        + [whole((CAP, width))] * len(pair)
        + [whole((compact, columns))],
        out_shape=[shape_of(PIECE, width)] * len(pair)
        + [shape_of(CAP, width)] * len(pair)
        + [shape_of(compact, columns)],
        scratch_shapes=[pltpu.VMEM((rows, width), BF)] * 2
        + [pltpu.VMEM((rows, LANES), F32)] * 2
        + [pltpu.VMEM((rows, width), BF)]
        + [pltpu.VMEM((rows, LANES), BF)] * 3
        + [pltpu.VMEM((compact, rows), BF)] * 3
        + [pltpu.VMEM((rows, width), F32)] * 2
        + [pltpu.VMEM((rows, LANES), F32)] * 3
        + [pltpu.VMEM((rows, FTILE), BF)] * 3,
        compiler_params=PARAMS,
        cost_estimate=cost(18),
        name="expert_layer",
    )(
        *pieces, *cots, gate_w, up_w, down_w, in_down, in_up, out_down, out_up,
        *([before] if has_grad else []),
    )


def spread(cols, index, count):
    return iota((TILE, count), 1).astype(F32) == cols[:, index : index + 1]


def combine_body(
    pieces, len_ref, *refs
):
    back_refs = refs[:pieces]
    (
        rows_ref, data_ref, cols_ref, cot_ref, ei_ref, hidden_ref, gain_ref, wo_ref, acat_ref, bcat_ref,
        table_ref, bh_ref, ba_ref, din_ref, bm_ref, back_all, dots_ref,
    ) = refs[pieces:]
    count = pieces * CAP

    @pl.when(pl.program_id(0) == 0)
    def _():
        for index, back_ref in enumerate(back_refs):
            back_all[index * CAP : index * CAP + CAP, :] = back_ref[0:CAP, :]
        dots = [back_ref[CAP:PIECE, 0:CAP].astype(F32) for back_ref in back_refs]
        dots = jnp.concatenate(dots, axis=1)
        dots_ref[...] = jnp.concatenate([dots, jnp.zeros_like(dots)], axis=0).astype(BF)

    table_high, table_middle, table_low = split3(table_ref[...])
    stack = dots_ref[...]
    ones = jnp.ones((16, cot_ref.shape[1]), BF)

    def stages(at):
        start = pl.program_id(0) * STEP + at.start
        cols = cols_ref[at]
        chosen_a = hot(spread(cols, TARGET_LANE, count))
        chosen_b = hot(spread(cols, TARGET_LANE + 1, count))
        yield
        routed_a = jnp.sum(mm_nt(stack, chosen_a)[0:8], axis=0, keepdims=True)
        routed_b = jnp.sum(mm_nt(stack, chosen_b)[0:8], axis=0, keepdims=True)
        cot = cot_ref[at]
        cot_f = cot.astype(F32)
        yield
        high, low = split2(cot_f * ei_ref[at].astype(F32))
        along_x = (mm_nt(ones, high) + mm_nt(ones, low))[0:1]
        yield
        along_c = mm_nt(table_high, cot) + mm_nt(table_middle, cot) + mm_nt(table_low, cot)
        along_a = along_c[VECTOR_ROW : VECTOR_ROW + 1]
        along_b = along_c[VECTOR_ROW + 1 : VECTOR_ROW + 2]
        yield
        both = chosen_a + chosen_b
        half = count // 2
        back = mm(both[:, :half], back_all[:half]) + mm(both[:, half:], back_all[half:])
        yield
        first, second = rows_ref[12:13, at], rows_ref[13:14, at]
        token = iota((1, TILE), 1) + start
        valid = jnp.where(token < len_ref[0], 1.0, 0.0)
        gate_a, gate_b = data_ref[8:9, at], data_ref[9:10, at]
        share = [data_ref[index : index + 1, at] for index in range(10, 14)]
        beta_a, beta_b = data_ref[14:15, at], data_ref[15:16, at]
        const_a = share[0] * along_x + share[1] * along_a
        const_b = share[2] * along_x + share[3] * along_b

        def here(route):
            return (
                jnp.where(route == EXPERTS + 1.0, along_x, 0.0)
                + jnp.where(route == EXPERTS + 2.0, const_a, 0.0)
                + jnp.where(route == EXPERTS + 3.0, const_b, 0.0)
            )

        dot_a, dot_b = routed_a + here(first), routed_b + here(second)
        mean = gate_a * dot_a + gate_b * dot_b
        chosen_grad_a = valid * gate_a * (dot_a - mean)
        chosen_grad_b = valid * gate_b * (dot_b - mean)
        number = iota((16, TILE), 0).astype(F32)
        logit_grads = jnp.where(number == first, chosen_grad_a, 0.0) + jnp.where(
            number == second, chosen_grad_b, 0.0
        )
        mixes = []
        for index, (beta, along) in enumerate(((beta_a, along_a), (beta_b, along_b))):
            left, right = share[2 * index], share[2 * index + 1]
            weighted = left * along_x + right * along
            mixes += [
                valid * beta * left * (along_x - weighted),
                valid * beta * right * (along - weighted),
            ]
        small = jnp.concatenate(
            [logit_grads] + mixes + [jnp.zeros((LANES - 20, TILE), F32)], axis=0
        ).T
        high, low = split2(small)
        yield
        inside = iota((TILE, 1), 0) + start < len_ref[0]
        grad = jnp.where(inside, cot_f, 0.0)
        back = back + mm(high, table_high) + mm(low, table_high) + mm(high, table_middle)
        back = back + cols[:, KEEP_LANE : KEEP_LANE + 1] * grad
        yield
        hidden = hidden_ref[at]
        scale = lax.rsqrt(jnp.mean(hidden * hidden, axis=-1, keepdims=True) + EPSILON)
        normed = hidden * scale
        back = back * gain_ref[1:2, :]
        back = grad + scale * (back - normed * jnp.mean(back * normed, axis=-1, keepdims=True))
        bh_ref[at] = back
        rounded = back.astype(BF)
        ba_ref[at] = rounded
        yield
        inner = mm_nt(rounded, bcat_ref[0]).astype(BF)
        din_ref[at] = inner
        yield
        bm_ref[at] = (mm_nt(rounded, wo_ref[...]) + mm_nt(inner, acat_ref[...])).astype(BF)

    side_by_side(stages)


def combine_call(
    length, backs, rows, data, cols, cotangent, ei, hidden, gains, weight, acat, bcat, table
):
    tok_count, width = cotangent.shape
    pieces = len(backs)
    return pl.pallas_call(
        functools.partial(combine_body, pieces),
        grid=(tok_count // STEP,),
        in_specs=[smem()] + [whole(back.shape) for back in backs] + [
            wide(16), wide(16), tall(LANES), tall(width), tall(width), tall(width),
            whole(gains.shape), whole(weight.shape), whole(acat.shape),
            pl.BlockSpec((1, LANES, width), lambda i: (3, 0, 0)), whole(table.shape),
        ],
        out_specs=[tall(width), tall(width), tall(LANES), tall(width)],
        out_shape=[
            shape_of(tok_count, width, dtype=F32), shape_of(tok_count, width),
            shape_of(tok_count, LANES), shape_of(tok_count, width),
        ],
        scratch_shapes=[
            pltpu.VMEM((pieces * CAP, width), BF), pltpu.VMEM((2 * META, pieces * CAP), BF)
        ],
        compiler_params=PARAMS,
        cost_estimate=cost(17),
        name="combine_backward",
    )(
        length, *backs, rows, data, cols, cotangent, ei, hidden, gains, weight, acat, bcat, table
    )


def result_body(pieces, len_ref, *refs):
    result_refs = refs[:pieces]
    cols_ref, ei_ref, hidden_ref, table_ref, out_ref, result_all = refs[pieces:]
    count = pieces * CAP

    @pl.when(pl.program_id(0) == 0)
    def _():
        for index, result_ref in enumerate(result_refs):
            result_all[index * CAP : index * CAP + CAP, :] = result_ref[...]

    table_high, table_low = split2(table_ref[...])

    def stages(at):
        cols = cols_ref[at]
        both = hot(spread(cols, TARGET_LANE, count) | spread(cols, TARGET_LANE + 1, count))
        yield
        half = count // 2
        mixture = mm(both[:, :half], result_all[:half]) + mm(both[:, half:], result_all[half:])
        yield
        high, low = split2(cols)
        mixture = mixture + mm(high, table_high) + mm(low, table_high) + mm(high, table_low)
        mixture = mixture + cols[:, KEEP_LANE : KEEP_LANE + 1] * ei_ref[at].astype(F32)
        yield
        inside = iota((TILE, 1), 0) + pl.program_id(0) * STEP + at.start < len_ref[0]
        out_ref[at] = (hidden_ref[at] + jnp.where(inside, mixture, 0.0)).astype(BF)

    side_by_side(stages)


def result_call(length, results, cols, ei, hidden, table):
    tok_count, width = ei.shape
    pieces = len(results)
    return pl.pallas_call(
        functools.partial(result_body, pieces),
        grid=(tok_count // STEP,),
        in_specs=[smem()] + [whole(result.shape) for result in results] + [
            tall(LANES), tall(width), tall(width), whole(table.shape),
        ],
        out_specs=tall(width),
        out_shape=shape_of(tok_count, width),
        scratch_shapes=[pltpu.VMEM((pieces * CAP, width), BF)],
        compiler_params=PARAMS,
        cost_estimate=cost(8),
        name="layer_output",
    )(length, *results, cols, ei, hidden, table)


def adapter_body(
    packed, id_ref, dq_ref, dk_ref, dv_ref, bcat_ref, normed_ref, inner_ref, mixed_ref, inner_o_ref,
    ba_ref, din_ref, back_ref, grad_ref, acc_ref,
):
    step = pl.program_id(0)
    width = dq_ref.shape[1]
    count = 4 * RANK

    @pl.when(step == 0)
    def _():
        acc_ref[...] = jnp.zeros_like(acc_ref)

    inner_t = inner_ref[...].astype(F32).T[0:count].astype(BF)
    outer_t = inner_o_ref[...].astype(F32).T[0:count].astype(BF)
    number = iota((count, width), 0) % 4
    back_inner = din_ref[...].astype(F32)
    values = [ref[...] for ref in (dq_ref, dk_ref, dv_ref)]
    for index, value in enumerate(values):
        back_inner = back_inner + mm_nt(value, bcat_ref[index]).astype(BF).astype(F32)
    upper = mm(outer_t, ba_ref[...])
    for index, value in enumerate(values):
        upper = jnp.where(number == index, mm(inner_t, value), upper)
    own = iota(back_inner.shape, 1) % 4 < 3
    back_ref[...] = jnp.where(own, back_inner, 0.0).astype(BF)
    back_t = back_inner.T[0:count].astype(BF)
    down = jnp.where(number < 3, mm(back_t, normed_ref[...]), mm(back_t, mixed_ref[...]))
    acc_ref[:, 0:width] += down
    acc_ref[:, width:] += upper

    @pl.when(step == pl.num_programs(0) - 1)
    def _():
        if not packed:
            grad_ref[...] = acc_ref[...].astype(BF)
            return
        half = width // 2
        shape = (16 * RANK, count)
        place, row = iota(shape, 0), iota(shape, 1)
        total = None
        for index in range(4):
            kind, part = index // 2, index % 2
            here = (place % 4 == row % 4) & (place // 16 == row // 4)
            here = here & (place // 8 % 2 == part) & (place // 4 % 2 == kind)
            start = kind * width + part * half
            piece = mm(hot(here), acc_ref[:, start : start + half].astype(BF))
            total = piece if total is None else total + piece
        grad_ref[:, 0:half] = total.astype(BF)
        grad_ref[:, half:] = jnp.full((16 * RANK, LANES), id_ref[0].astype(F32), F32).astype(BF)


def adapter_call(
    packed, ids, dq, dk, dv, bcat, normed, inner, mixed, inner_o, ba, din
):
    tok_count, width = dq.shape
    grad_shape = (16 * RANK, width // 2 + LANES) if packed else (4 * RANK, 2 * width)
    return pl.pallas_call(
        functools.partial(adapter_body, packed),
        grid=(tok_count // TILE,),
        in_specs=[
            smem(), tile(width), tile(width), tile(width), whole(bcat.shape), tile(width), tile(LANES),
            tile(width), tile(LANES), tile(width), tile(LANES),
        ],
        out_specs=[tile(LANES), whole(grad_shape)],
        out_shape=[shape_of(tok_count, LANES), shape_of(*grad_shape)],
        scratch_shapes=[pltpu.VMEM((4 * RANK, 2 * width), F32)],
        compiler_params=PARAMS,
        cost_estimate=cost(6),
        name="adapter_gradients",
    )(ids, dq, dk, dv, bcat, normed, inner, mixed, inner_o, ba, din)


def last_body(
    dq_ref, dk_ref, dv_ref, w_ref, acat_ref, back_ref, x_ref, bh_ref, gain_ref, out_ref
):
    def stages(at):
        parts = [mm_nt(back_ref[at], acat_ref[...])]
        for index, ref in enumerate((dq_ref, dk_ref, dv_ref)):
            parts.append(mm_nt(ref[at], w_ref[index]))
            yield
        total = parts[0] + parts[1] + parts[2] + parts[3]
        x = x_ref[at].astype(F32)
        scale = lax.rsqrt(jnp.mean(x * x, axis=-1, keepdims=True) + EPSILON)
        normed = x * scale
        back = total * gain_ref[0:1, :]
        back = scale * (back - normed * jnp.mean(back * normed, axis=-1, keepdims=True))
        out_ref[at] = (bh_ref[at] + back).astype(BF)

    side_by_side(stages)


def last_call(dq, dk, dv, weights, acat, back, tokens, bh, gains):
    tok_count, width = tokens.shape
    return pl.pallas_call(
        last_body,
        grid=(tok_count // STEP,),
        in_specs=[
            tall(width), tall(width), tall(width), whole(weights.shape), whole(acat.shape),
            tall(LANES), tall(width), tall(width), whole(gains.shape),
        ],
        out_specs=tall(width),
        out_shape=shape_of(tok_count, width),
        compiler_params=PARAMS,
        cost_estimate=cost(9),
        name="after_attention_backward",
    )(dq, dk, dv, weights, acat, back, tokens, bh, gains)


def exchange(value, axes):
    return lax.all_to_all(value, axes, split_axis=0, concat_axis=0, tiled=True)


def gather_all(value, axes, count):
    return exchange(jnp.broadcast_to(value[None], (count,) + value.shape), axes)


def swap(value, partner, group):
    if partner == 0:
        return value
    return lax.ppermute(value, "expert", [(index, index ^ partner) for index in range(group)])


def find_adapters(id_rows):
    count = id_rows.shape[0]
    padded = id_rows.astype(F32)
    if count % LANES:
        padded = jnp.concatenate([padded, jnp.zeros((-count % LANES, LANES), F32)], axis=0)
    return padded.T[0:1, 0:count].astype(jnp.int32)


def sum_expert_body(each, adapters, in_ref, out_ref):
    count, columns = in_ref.shape[0], out_ref.shape[1]
    found = find_adapters(in_ref[:, columns:])
    place = iota((adapters * each, count), 0)
    column = iota((adapters * each, count), 1)
    pick = hot((place // each == found) & (place % each == column % each))
    out_ref[...] = mm(pick, in_ref[:, 0:columns]).astype(BF)


def exchange_expert_grads(grads, group, owners):
    split = min(RANK, owners)
    each, parts = RANK // split, owners // split
    columns = (grads.shape[1] - LANES) // parts
    pieces = grads.reshape(split, each * group, grads.shape[1])
    if parts > 1:
        ids = jnp.broadcast_to(pieces[:, None, :, parts * columns :], (split, parts, each * group, LANES))
        pieces = pieces[:, :, : parts * columns].reshape(split, each * group, parts, columns)
        pieces = jnp.concatenate([pieces.transpose(0, 2, 1, 3), ids], axis=-1)
        pieces = pieces.reshape(owners, each * group, columns + LANES)
    return exchange(pieces, "dp").reshape(owners * group * each, columns + LANES)


def sum_expert_grads(got, adapters, owners):
    columns = got.shape[1] - LANES
    each = RANK // min(RANK, owners)
    return pl.pallas_call(
        functools.partial(sum_expert_body, each, adapters),
        out_shape=shape_of(adapters * each, columns),
        compiler_params=PARAMS,
        cost_estimate=cost(2.2),
        name="expert_gradient_part",
    )(got)


def finish_expert_body(split, adapters, hidden, in_ref, *refs):
    down_ref, up_ref, out_down_ref, out_up_ref = refs[-4:]
    each = RANK // split
    rows = adapters * each
    count = split * rows
    width = out_up_ref.shape[1]

    def place(value):
        return value // each % adapters * RANK + value // (adapters * each) * each + value % each

    move = hot(iota((count, count), 0) == place(iota((count, count), 1)))
    back = hot(iota((count, count), 1) == place(iota((count, count), 0)))

    def part(start, size):
        span = slice(start, start + size)
        rows_of = [in_ref[owner, :, span] for owner in range(split)]
        return jnp.concatenate(rows_of, axis=0)

    for index in range(2):
        up_ref[index] = mm(move, part(index * hidden, hidden))
    out_down_ref[...] = mm_tn(part(2 * hidden, hidden), back)
    base = 3 * hidden
    out_up_ref[...] = mm(move, part(base, width))
    for index in range(2):
        base += width
        down_ref[index] = mm_tn(part(base, width), back)


def finish_expert_call(index, local, everything, outs, adapters, width, hidden):
    owners, rows, columns = everything.shape
    total = adapters * RANK
    shapes = [(local, 2, width, total), (local, 2, total, hidden), (local, hidden, total),
              (local, total, width)]
    specs = [
        pl.BlockSpec((None,) + shape[1:], lambda *_, rank=len(shape): (index,) + (0,) * (rank - 1))
        for shape in shapes
    ]
    return pl.pallas_call(
        functools.partial(finish_expert_body, owners, adapters, hidden),
        grid=(1,),
        in_specs=[whole(everything.shape)] + [pl.BlockSpec(memory_space=pl.ANY)] * len(outs),
        out_specs=specs,
        out_shape=[shape_of(*shape, dtype=F32) for shape in shapes],
        input_output_aliases={1 + place: place for place in range(len(outs))},
        compiler_params=PARAMS,
        cost_estimate=cost(4),
        name="expert_gradient_sums",
    )(everything, *outs)


def spread_expert_grads(own, adapters, owners):
    split = min(RANK, owners)
    each, parts = RANK // split, owners // split
    everything = gather_all(own, "dp", owners)
    everything = everything.reshape(split, parts, adapters, each, own.shape[1])
    everything = everything.transpose(2, 0, 3, 1, 4)
    return everything.reshape(adapters * RANK, parts * own.shape[1]).astype(F32)


def expert_sums(owned, adapters, owners, width, hidden):
    sums = [spread_expert_grads(value, adapters, owners) for value in owned]
    base = 3 * hidden
    up = [[value[:, 0:hidden], value[:, hidden : 2 * hidden]] for value in sums]
    down = [
        [value[:, base + width * part : base + width * (part + 1)].T for part in (1, 2)]
        for value in sums
    ]
    return (
        jnp.stack([jnp.stack(value) for value in down]),
        jnp.stack([jnp.stack(value) for value in up]),
        jnp.stack([value[:, 2 * hidden : base].T for value in sums]),
        jnp.stack([value[:, base : base + width] for value in sums]),
    )


def finish_adapter_body(adapters, me_ref, *refs):
    piece_refs, (down_ref, up_ref, in_ref) = refs[:-3], refs[-3:]
    half = in_ref.shape[3]
    owners, group = piece_refs[0].shape[0], len(piece_refs)
    for other in range(group):
        place = jnp.bitwise_xor(me_ref[0], other)
        for owner in range(owners):
            in_ref[owner * (group // 2) + place // 2, place % 2] = piece_refs[other][owner]
    count = RANK * adapters

    def place(value):
        return value % adapters * RANK + value // adapters

    move = hot(iota((count, count), 0) == place(iota((count, count), 1)))
    back = hot(iota((count, count), 1) == place(iota((count, count), 0)))
    for part in range(2):
        span = slice(part * half, part * half + half)
        for kind in range(2):
            for index in range(4):
                first = (kind * 4 + index) * adapters
                rows = in_ref[:, part, first : first + adapters, :].astype(F32)
                rows = rows.reshape(count, half).astype(BF)
                if kind == 0:
                    down_ref[index, span, :] = mm_tn(rows, back)
                else:
                    up_ref[index, :, span] = mm(move, rows)


def sum_adapter_body(kinds, adapters, in_ref, out_ref):
    count, columns = in_ref.shape[0], out_ref.shape[-1]
    found = find_adapters(in_ref[:, columns:])
    place = iota((adapters * kinds, count), 0)
    column = iota((adapters * kinds, count), 1)
    pick = hot((place % adapters == found) & (place // adapters == column % kinds))
    own = mm(pick, in_ref[:, 0:columns]).astype(BF)
    for index in range(out_ref.shape[0]):
        out_ref[index] = own


def adapter_sums(grads, meanwhile, later, ids, adapters, owners, group, width):
    axes, everyone = ("dp", "expert"), owners * group
    if everyone == 2 * RANK and group == 4:
        kinds = 8
        got = exchange(grads.reshape(everyone, kinds, grads.shape[1]), axes)
        got, meanwhile = lax.optimization_barrier((got, meanwhile))
        own = pl.pallas_call(
            functools.partial(sum_adapter_body, kinds, adapters),
            out_shape=shape_of(owners, kinds * adapters, width // 2),
            compiler_params=PARAMS,
            cost_estimate=cost(2.0),
            name="adapter_gradient_part",
        )(got.reshape(everyone * kinds, grads.shape[1]))
        mine = exchange(own, "dp")
        mine, later = lax.optimization_barrier((mine, later))
        across = swap(mine, 2, group)
        full = [mine, swap(mine, 1, group), across, swap(across, 1, group)]
        total = adapters * RANK
        down, upper = pl.pallas_call(
            functools.partial(finish_adapter_body, adapters),
            in_specs=[smem()] + [pl.BlockSpec(memory_space=pltpu.VMEM)] * group,
            out_shape=[shape_of(4, width, total, dtype=F32), shape_of(4, total, width, dtype=F32)],
            scratch_shapes=[pltpu.VMEM((RANK, 2, kinds * adapters, width // 2), BF)],
            compiler_params=PARAMS,
            cost_estimate=cost(3.6),
            name="adapter_gradient_sums",
        )(lax.axis_index("expert").reshape(1).astype(jnp.int32), *full)
        return down, upper, meanwhile, later
    all_ids = exchange(jnp.broadcast_to(ids, (everyone,)), axes)
    pieces = grads.reshape(everyone, RANK * 4 * 2 * width // everyone)
    got = exchange(pieces, axes)
    pick = (jnp.arange(adapters, dtype=jnp.int32)[:, None] == all_ids[None, :]).astype(BF)
    own = jnp.dot(pick, got, preferred_element_type=F32).astype(BF)
    full = gather_all(own, axes, everyone)
    full = full.reshape(RANK, everyone // RANK, adapters, -1).transpose(2, 0, 1, 3)
    full = full.reshape(adapters * RANK, 4, 2, width).astype(F32)
    return full[:, :, 0].transpose(1, 2, 0), full[:, :, 1].transpose(1, 0, 2), meanwhile, later


def body(
    tokens,
    cotangent,
    lengths,
    adapter_ids,
    routes,
    prev_logits,
    norm_gains,
    input_weights,
    output_weight,
    adapter_down,
    adapter_up,
    router,
    residual_mix,
    constant_mix,
    constant_vectors,
    expert_gate,
    expert_up,
    expert_down,
    expert_adapter_down,
    expert_adapter_up,
    output_adapter_down,
    output_adapter_up,
):
    tok_count, width = tokens.shape
    hidden_width = expert_gate.shape[2]
    group, owners = lax.axis_size("expert"), lax.axis_size("dp")
    local = expert_gate.shape[0]
    adapters = adapter_down.shape[-1] // RANK
    cosine, sine = (jnp.asarray(table) for table in turn_tables(tok_count))
    weights = (
        expert_gate, expert_up, expert_down, expert_adapter_down, expert_adapter_up,
        output_adapter_down, output_adapter_up,
    )
    per_owner = RANK // min(RANK, owners)
    everyone = owners * group
    me = lax.axis_index("expert")

    me = me.reshape(1).astype(jnp.int32)

    rows = jnp.concatenate(
        [prev_logits, routes.astype(F32), jnp.zeros((tok_count, 2), F32)], axis=1
    ).T
    slots, *grad_sends = route_call(local, group, lengths, me, rows, cotangent)
    cots = [swap(value, partner, group) for partner, value in enumerate(grad_sends)]
    small = jnp.concatenate(
        [
            router.astype(F32), jnp.zeros((width, MIX_ROW - EXPERTS - 4), F32), constant_mix,
            jnp.zeros((width, LANES - MIX_ROW - 4), F32),
        ],
        axis=1,
    )
    normed, inner, queries, keys, values, acat, bcat, table = pre_call(
        adapter_ids, tokens, norm_gains, input_weights, adapter_down, adapter_up, cosine, sine, small,
        constant_vectors,
    )
    mixed, q2 = attend_call(lengths, queries, keys, values)
    mixed, cots = lax.optimization_barrier((mixed, cots))
    mixer = jnp.pad(residual_mix.T, ((0, 4), (0, 4)))
    hidden, ei, inner_o, data, cols = post_call(
        local, group, me, mixed, tokens, output_weight, acat, bcat, norm_gains, table, mixer, rows,
        slots,
    )
    sends = send_call(local, group, me, adapter_ids, slots, data, ei)
    near, far = tuple(range(group // 2)), tuple(range(group // 2, group))
    sent_near = [swap(sends[partner], partner, group) for partner in near]
    sent_far = []
    for index in range(local):
        pieces = [sends[group // 2 + place * local + index] for place in range(len(far))]
        if index > 0:
            pieces, sent_near = lax.optimization_barrier((pieces, sent_near))
        sent_far.append([swap(piece, partner, group) for piece, partner in zip(pieces, far)])
    backs = [[None] * group for _ in range(local)]
    results = [[None] * group for _ in range(local)]
    grads, last = [], None
    for index in range(local):
        before = None
        for pair in (near, far) if index % 2 == 0 else (far, near):
            pieces = sent_near if pair == near else sent_far[index]
            if last is not None:
                pieces, last = lax.optimization_barrier((pieces, last))
            if index == local - 1 and pair == near:
                pieces, backs[:index] = lax.optimization_barrier((pieces, backs[:index]))
            outs = expert_call(
                index, pair, group, per_owner, pieces, [cots[partner] for partner in pair], before, weights
            )
            before = last = outs[-1]
            for place, partner in enumerate(pair):
                backs[index][partner] = swap(outs[place], partner, group)
                results[index][partner] = outs[len(pair) + place]
        grads.append(before)
    backs = [value for some in backs for value in some]

    parts = [exchange_expert_grads(grad, group, owners) for grad in grads]
    sums = functools.partial(sum_expert_grads, adapters=adapters, owners=owners)
    parts[:-1], last = lax.optimization_barrier((parts[:-1], last))
    owned = [sums(part) for part in parts[:-1]]
    backs[-2:], owned = lax.optimization_barrier((backs[-2:] , owned))
    gather = functools.partial(lax.all_gather, axis_name="dp", axis=0, tiled=False)
    if owners <= RANK:
        owned = [gather(own) for own in owned]
    back_hidden, back_attention, back_inner_o, back_mixed = combine_call(
        lengths, backs, rows, data, cols, cotangent, ei, hidden, norm_gains, output_weight, acat, bcat,
        table,
    )
    flat = [value for some in results for value in some]
    flat, back_mixed = lax.optimization_barrier((flat, back_mixed))
    flat = [swap(value, place % group, group) for place, value in enumerate(flat)]

    dq, dk, dv = attend_back_call(lengths, q2, keys, values, mixed, back_mixed, cosine, sine)
    parts[-1], dq = lax.optimization_barrier((parts[-1], dq))
    own = sums(parts[-1])
    dq, own, owned = lax.optimization_barrier((dq, own, owned))
    owned.append(gather(own) if owners <= RANK else own)
    back_inner, adapter_grads = adapter_call(
        everyone == 2 * RANK and group == 4, adapter_ids, dq, dk, dv, bcat, normed, inner, mixed,
        inner_o, back_attention, back_inner_o,
    )
    (dq, dk, dv, flat), adapter_grads = lax.optimization_barrier(((dq, dk, dv, flat), adapter_grads))
    layer_out = result_call(lengths, flat, cols, ei, hidden, table)
    input_back = last_call(
        dq, dk, dv, input_weights, acat, back_inner, tokens, back_hidden, norm_gains
    )
    outs = []
    if owners <= RANK:
        for index, own in enumerate(owned[:-1]):
            outs = finish_expert_call(index, local, own, outs, adapters, width, hidden_width)
    down_sum, upper_sum, layer_out, (input_back, outs) = adapter_sums(
        adapter_grads, layer_out, (input_back, outs), adapter_ids, adapters, owners, group, width
    )
    if owners <= RANK:
        outs = finish_expert_call(
            local - 1, local, owned[-1], outs, adapters, width, hidden_width
        )
    else:
        outs = expert_sums(owned, adapters, owners, width, hidden_width)
    in_down_sum, in_up_sum, out_down_sum, out_up_sum = outs
    return (
        layer_out,
        input_back,
        down_sum,
        upper_sum,
        in_down_sum,
        in_up_sum,
        out_down_sum,
        out_up_sum,
    )


def solution(mesh):
    tokens_spec, copied = P(("dp", "expert"), None), P()
    owned = P("expert")
    placed = (
        (tokens_spec, tokens_spec, P(("dp", "expert")), P(("dp", "expert")), tokens_spec, tokens_spec)
        + (copied,) * 9
        + (owned,) * 7
    )
    return jax.shard_map(
        body,
        mesh=mesh,
        in_specs=placed,
        out_specs=(tokens_spec, tokens_spec, copied, copied) + (owned,) * 4,
        check_vma=False,
    )
```

```python
import functools
import math

import jax
import jax.numpy as jnp
import numpy as np
from jax import lax
from jax.experimental import pallas as pl
from jax.experimental.pallas import tpu as pltpu
from jax.sharding import PartitionSpec as P

HEADS = 12
HD = 64
EXPERTS = 8
RANK = 16
CAP = 192
EPSILON = 1e-06
F32 = jnp.float32
BF = jnp.bfloat16
NEG = -1e30
LANES = 128
TILE = 256
STEP = 512
FTILE = 512
PAIRS = HEADS // 2
PARAMS = pltpu.CompilerParams(vmem_limit_bytes=67043328)
META = 8
MIX_ROW = 16
VECTOR_ROW = 20
TARGET_LANE = 24
KEEP_LANE = 26
PIECE = CAP + META


def mm(left, right):
    return jnp.dot(left, right, preferred_element_type=F32)


def mm_nt(left, right):
    return lax.dot_general(left, right, (((1,), (1,)), ((), ())), preferred_element_type=F32)


def mm_tn(left, right):
    return lax.dot_general(left, right, (((0,), (0,)), ((), ())), preferred_element_type=F32)


def iota(shape, axis):
    return lax.broadcasted_iota(jnp.int32, shape, axis)


def hot(condition):
    return jnp.where(condition, 1.0, 0.0).astype(BF)


def split2(value):
    high = value.astype(BF)
    return high, (value - high.astype(F32)).astype(BF)


def split3(value):
    high = value.astype(BF)
    rest = value - high.astype(F32)
    middle = rest.astype(BF)
    return high, middle, (rest - middle.astype(F32)).astype(BF)


def whole(shape):
    zeros = (0,) * len(shape)
    return pl.BlockSpec(shape, lambda *_: zeros)


def smem():
    return pl.BlockSpec(memory_space=pltpu.SMEM)


def tall(width):
    return pl.BlockSpec((STEP, width), lambda i: (i, 0))


def wide(height):
    return pl.BlockSpec((height, STEP), lambda i: (0, i))


def tile(width):
    return pl.BlockSpec((TILE, width), lambda i: (i, 0))


def side_by_side(stages):
    running = [stages(slice(start, start + TILE)) for start in range(0, STEP, TILE)]
    while running:
        running = [stage for stage in running if next(stage, True) is None]


def shape_of(*shape, dtype=BF):
    return jax.ShapeDtypeStruct(shape, dtype)


def cost(microseconds):
    return pl.CostEstimate(flops=int(microseconds * 1e+09), bytes_accessed=0, transcendentals=0)


@functools.lru_cache(maxsize=None)
def turn_tables(length_in):
    half = HD // 2
    inverse = np.exp(np.arange(half, dtype=np.float64) * (-2.0 * math.log(10000.0) / HD))

    def table(positions):
        angles = np.tile(positions[:, None] * inverse[None, :], (1, 4))
        return np.stack([np.cos(angles), np.sin(angles)]).astype(np.float32)

    return table(np.arange(0.0, length_in, 32)), table(np.arange(0.0, 32))


def turn_rows(coarse_ref, fine_ref, first, count):
    fine_cos, fine_sin = fine_ref[0], fine_ref[1]
    sign = jnp.where(iota((32, LANES), 1) % HD < HD // 2, -1.0, 1.0)
    signed_cos, signed_sin = fine_cos * sign, fine_sin * sign
    cosines, sines = [], []
    for index in range(count // 32):
        row = first // 32 + index
        coarse_cos, coarse_sin = coarse_ref[0, pl.ds(row, 1), :], coarse_ref[1, pl.ds(row, 1), :]
        cosines.append(coarse_cos * fine_cos - coarse_sin * fine_sin)
        sines.append(coarse_sin * signed_cos + coarse_cos * signed_sin)
    return jnp.concatenate(cosines, axis=0), jnp.concatenate(sines, axis=0)


def rope(value, cosine, sine):
    first = iota(value.shape, 1) % HD < HD // 2
    turned = jnp.where(first, pltpu.roll(value, LANES - HD // 2, 1), pltpu.roll(value, HD // 2, 1))
    return value * cosine + turned * sine


def find_slots(length, routes_ref, slot_ref):
    tok_count = slot_ref.shape[1]
    before = hot(iota((TILE, TILE), 0) < iota((TILE, TILE), 1))
    carry = jnp.zeros((2 * EXPERTS, 1), F32)
    for start in range(0, tok_count, TILE):
        span = slice(start, start + TILE)
        expert = iota((2 * EXPERTS, TILE), 0)
        token = iota((2 * EXPERTS, TILE), 1) + start
        named = (routes_ref[0:1, span] == expert) | (routes_ref[1:2, span] == expert)
        hit = named & (token < length) & (expert < EXPERTS)
        hits = jnp.where(hit, 1.0, 0.0)
        slots = mm(hits.astype(BF), before) + carry
        carry = carry + jnp.sum(hits, axis=1, keepdims=True)
        slot_ref[:, span] = jnp.where(hit, slots, -1.0)[:EXPERTS].astype(jnp.int32)


def pick_rows(slot_ref, step, me, local):
    first = jnp.bitwise_xor(step, me) * local
    place = iota((CAP, slot_ref.shape[1]), 0)
    return first, [hot(place == slot_ref[pl.ds(first + index, 1), :]) for index in range(local)]


def pick_source(chosen, source_ref):
    half = source_ref.shape[0] // 2
    return mm(chosen[:, :half], source_ref[:half]) + mm(chosen[:, half:], source_ref[half:])


def store_piece(out_refs, step, other, index, value, start):
    @pl.when(step == other)
    def _():
        out_refs[index][start : start + value.shape[0], :] = value


def route_body(local, group, len_ref, me_ref, routes_ref, source_ref, slot_ref, *out_refs):
    step = pl.program_id(0)

    @pl.when(step == 0)
    def _():
        find_slots(len_ref[0], routes_ref, slot_ref)

    _, chosen = pick_rows(slot_ref, step, me_ref[0], local)
    rows = pick_source(jnp.concatenate(chosen, axis=0), source_ref).astype(BF)
    for other in range(group):
        store_piece(out_refs, step, other, other, rows, 0)


def route_call(local, group, length, me, routes, source):
    tok_count, width = source.shape
    return pl.pallas_call(
        functools.partial(route_body, local, group),
        grid=(group,),
        in_specs=[smem(), smem(), whole(routes.shape), whole(source.shape)],
        out_specs=[whole((EXPERTS, tok_count))] + [whole((local * CAP, width))] * group,
        out_shape=[shape_of(EXPERTS, tok_count, dtype=jnp.int32)]
        + [shape_of(local * CAP, width)] * group,
        compiler_params=PARAMS,
        cost_estimate=cost(6.5),
        name="route_rows",
    )(length, me, routes, source)


def send_body(local, group, me_ref, id_ref, slot_ref, data_ref, source_ref, *out_refs):
    step = pl.program_id(0)
    width = source_ref.shape[1]
    first, chosen = pick_rows(slot_ref, step, me_ref[0], local)
    rows = pick_source(jnp.concatenate(chosen, axis=0), source_ref).astype(BF)
    for index in range(local):
        pieces = split3(data_ref[pl.ds(first + index, 1), :])
        stack = jnp.concatenate(
            [piece.astype(F32) for piece in pieces]
            + [jnp.zeros((13, chosen[index].shape[1]), F32)],
            axis=0,
        ).astype(BF)
        gates = mm_nt(stack, chosen[index])[0:META]
        gates = jnp.where(iota(gates.shape, 0) == 3, id_ref[0].astype(F32), gates)
        meta = jnp.concatenate([gates, jnp.zeros((META, width - CAP), F32)], axis=1)
        kept = rows[index * CAP : index * CAP + CAP]
        for other in range(group):
            far = other >= group // 2
            place = group // 2 + (other - group // 2) * local + index if far else other
            start = 0 if far else index * PIECE
            store_piece(out_refs, step, other, place, kept, start)
            store_piece(out_refs, step, other, place, meta.astype(BF), start + CAP)


def send_call(local, group, me, ids, slots, data, source):
    tok_count, width = source.shape
    heights = [local * PIECE] * (group // 2) + [PIECE] * ((group - group // 2) * local)
    return pl.pallas_call(
        functools.partial(send_body, local, group),
        grid=(group,),
        in_specs=[smem(), smem(), whole(slots.shape), whole(data.shape), whole(source.shape)],
        out_specs=[whole((height, width)) for height in heights],
        out_shape=[shape_of(height, width) for height in heights],
        compiler_params=PARAMS,
        cost_estimate=cost(8.4),
        name="send_rows",
    )(me, ids, slots, data, source)


def pre_body(
    id_ref, x_ref, gain_ref, w_ref, ad_ref, au_ref, coarse_ref, fine_ref, router_ref, cmix_ref, vec_ref,
    resid_ref, normed_ref, inner_ref, q_ref, k_ref, v_ref, acat_ref, bcat_ref, table_ref, mix_ref,
    square_ref,
):
    @pl.when(pl.program_id(0) == 0)
    def _():
        first = RANK * id_ref[0]
        total = None
        for index in range(4):
            row, column = iota((LANES, LANES), 0), iota((LANES, LANES), 1)
            place = hot((row >= first) & (row < first + RANK) & (column == (row - first) * 4 + index))
            part = mm(ad_ref[index], place)
            total = part if total is None else total + part
            place = hot(
                (column >= first) & (column < first + RANK) & (row == (column - first) * 4 + index)
            )
            bcat_ref[index] = mm(place, au_ref[index]).astype(BF)
        acat_ref[...] = total.astype(BF)
        table_ref[...] = jnp.zeros_like(table_ref)
        table_ref[0 : EXPERTS + 4, :] = router_ref[...].astype(F32)
        table_ref[MIX_ROW : MIX_ROW + 4, :] = cmix_ref[...]
        table_ref[VECTOR_ROW : VECTOR_ROW + 2, :] = vec_ref[...]
        square_ref[...] = jnp.zeros_like(square_ref)
        square_ref[0 : EXPERTS + 4, 0 : EXPERTS + 4] = resid_ref[...]
        mix_ref[...] = square_ref[...].T[0:16]

    def stages(at):
        x = x_ref[at].astype(F32)
        scale = lax.rsqrt(jnp.mean(x * x, axis=-1, keepdims=True) + EPSILON)
        normed = (x * scale * gain_ref[0:1, :]).astype(BF)
        normed_ref[at] = normed
        yield
        inner = mm(normed, acat_ref[...]).astype(BF)
        inner_ref[at] = inner
        yield
        for index, out_ref in enumerate((q_ref, k_ref, v_ref)):
            value = mm(normed, w_ref[index]) + mm(inner, bcat_ref[index])
            yield
            if index == 2:
                out_ref[at] = value.astype(BF)
                continue
            cosine, sine = turn_rows(coarse_ref, fine_ref, pl.program_id(0) * STEP + at.start, TILE)
            for pair in range(PAIRS):
                span = slice(pair * LANES, pair * LANES + LANES)
                turned = rope(value[:, span], cosine, sine).astype(BF)
                if index == 0:
                    turned = (turned.astype(F32) * HD**-0.5).astype(BF)
                out_ref[at, span] = turned
            yield

    side_by_side(stages)


def pre_call(
    ids, tokens, gains, weights, down, upper, coarse, fine, router, constant_mix, vectors, residual_mix
):
    tok_count, width = tokens.shape
    return pl.pallas_call(
        pre_body,
        grid=(tok_count // STEP,),
        in_specs=[
            smem(), tall(width), whole(gains.shape), whole(weights.shape), whole(down.shape),
            whole(upper.shape), whole(coarse.shape), whole(fine.shape), whole(router.shape),
            whole(constant_mix.shape), whole(vectors.shape), whole(residual_mix.shape),
        ],
        out_specs=[
            tall(width), tall(LANES), tall(width), tall(width), tall(width),
            whole((width, LANES)), whole(upper.shape), whole((LANES, width)), whole((16, LANES)),
        ],
        out_shape=[
            shape_of(tok_count, width), shape_of(tok_count, LANES), shape_of(tok_count, width),
            shape_of(tok_count, width), shape_of(tok_count, width), shape_of(width, LANES),
            shape_of(*upper.shape), shape_of(LANES, width, dtype=F32), shape_of(16, LANES, dtype=F32),
        ],
        scratch_shapes=[pltpu.VMEM((LANES, LANES), F32)],
        compiler_params=PARAMS,
        cost_estimate=cost(12.3),
        name="before_attention",
    )(
        ids, tokens, gains, weights, down, upper, coarse, fine, router, constant_mix, vectors,
        residual_mix,
    )


def attend_body(len_ref, q_ref, k_ref, v_ref, mixed_ref, q2_ref):
    tok_count = q_ref.shape[0]
    lane = iota((tok_count, LANES), 1)
    hidden_key = iota((tok_count, LANES), 0) >= len_ref[0]
    row = iota((LANES, tok_count), 0)
    row_tile = row[:, :TILE]
    causal = iota((TILE, TILE), 0) <= iota((TILE, TILE), 1)
    queries_t = q_ref[...].astype(F32).T
    values_t = v_ref[...].astype(F32).T
    keys = k_ref[...].astype(F32)
    heads = []
    for head in range(2):
        spare = HD * (1 - head)
        bias = jnp.where((lane == spare) & hidden_key, NEG, 0.0)
        one = jnp.where(row == spare, 1.0, 0.0)
        own = row // HD == head
        heads.append(
            (
                jnp.where(lane // HD == head, keys, bias).astype(BF),
                jnp.where(own, queries_t, one).astype(BF),
                jnp.where(own, values_t, one).astype(BF),
            )
        )
    units = [(start, head) for start in range(0, tok_count, TILE) for head in range(2)]

    def score(unit):
        start, head = unit
        keys, queries, _ = heads[head]
        part = queries[:, start : start + TILE]
        near = mm(keys[start : start + TILE], part)
        return near, mm(keys[:start], part) if start else None

    outs = {}
    waiting = score(units[0])
    for index, (start, head) in enumerate(units):
        near, far = waiting
        waiting = score(units[index + 1]) if index + 1 < len(units) else None
        spare = HD * (1 - head)
        _, queries, values = heads[head]
        near = jnp.where(causal, near, NEG)
        top = jnp.max(near, axis=0, keepdims=True)
        if start:
            top = jnp.maximum(top, jnp.max(far, axis=0, keepdims=True))
        mixed = mm(values[:, start : start + TILE], jnp.exp(near - top).astype(BF))
        if start:
            mixed = mixed + mm(values[:, :start], jnp.exp(far - top).astype(BF))
        total = mixed[spare : spare + 1]
        outs[head] = mixed * (1.0 / total)
        kept = queries[:, start : start + TILE]
        logs = jnp.zeros((LANES, TILE), F32)
        for offset, piece in enumerate(split3(top + jnp.log(total))):
            logs = jnp.where(row_tile == spare + 1 + offset, piece.astype(F32), logs)
        q2_ref[head * LANES : head * LANES + LANES, start : start + TILE] = kept + logs.astype(BF)
        if head == 1:
            mixed = jnp.where(row_tile < HD, outs[0], outs[1])
            mixed_ref[start : start + TILE] = mixed.T.astype(BF)


def attend_call(length, queries, keys, values):
    tok_count, width = queries.shape
    column = pl.BlockSpec((tok_count, LANES), lambda i: (0, i))
    return pl.pallas_call(
        attend_body,
        grid=(PAIRS,),
        in_specs=[smem(), column, column, column],
        out_specs=[column, pl.BlockSpec((2 * LANES, tok_count), lambda i: (i, 0))],
        out_shape=[shape_of(tok_count, width), shape_of(2 * width, tok_count)],
        compiler_params=PARAMS,
        cost_estimate=cost(15),
        name="attention_forward",
    )(length, queries, keys, values)


def attend_back_body(
    len_ref, q2_ref, k_ref, v_ref, mixed_ref, back_ref, coarse_ref, fine_ref,
    dq_ref, dk_ref, dv_ref, acc_ref, turn_ref,
):
    tok_count = k_ref.shape[0]

    @pl.when(pl.program_id(0) == 0)
    def _():
        turn_ref[0], turn_ref[1] = turn_rows(coarse_ref, fine_ref, 0, tok_count)

    lane = iota((tok_count, LANES), 1)
    position = iota((tok_count, LANES), 0)
    bias = jnp.where(position < len_ref[0], 0.0, NEG)
    causal = iota((TILE, TILE), 0) <= iota((TILE, TILE), 1)
    row = iota((LANES, tok_count), 0)
    back = back_ref[...].astype(F32)
    product_t = (back * mixed_ref[...].astype(F32)).T
    back_t = back.T
    keys, values = k_ref[...].astype(F32), v_ref[...].astype(F32)
    grads = []
    for head in range(2):
        own = lane // HD == head
        spare = HD * (1 - head)
        minus = jnp.where((lane > spare) & (lane < spare + 4), -1.0, 0.0)
        q2 = q2_ref[head * LANES : head * LANES + LANES, :]
        k2f = jnp.where(own, keys, jnp.where(lane == spare, bias, minus))
        k2 = k2f.astype(BF)
        k2t = k2f.T.astype(BF)
        v2 = jnp.where(own, values, minus).astype(BF)
        own_row = row // HD == head
        delta = jnp.sum(jnp.where(own_row, product_t, 0.0), axis=0, keepdims=True)
        back2 = jnp.where(own_row, back_t, 0.0)
        for offset, piece in enumerate(split3(delta)):
            back2 = jnp.where(row == spare + 1 + offset, piece.astype(F32), back2)
        back2 = back2.astype(BF)
        dk_parts, dv_parts = [], []
        for start in range(0, tok_count, TILE):
            stop = start + TILE
            scores = mm(k2[start:stop], q2[:, start:])
            slopes = mm(v2[start:stop], back2[:, start:])
            diagonal = jnp.where(causal, scores[:, :TILE], NEG)
            scores = (
                diagonal
                if stop == tok_count
                else jnp.concatenate([diagonal, scores[:, TILE:]], axis=1)
            )
            weights = jnp.exp(scores)
            turned = (weights * slopes).astype(BF)
            dv_parts.append(mm_nt(weights.astype(BF), back2[:, start:]))
            dk_parts.append(mm_nt(turned, q2[:, start:]))
            update = mm(k2t[:, start:stop], turned)
            if start == 0:
                acc_ref[head] = update
            else:
                acc_ref[head, :, start:] += update
        grads.append((jnp.concatenate(dk_parts, axis=0), jnp.concatenate(dv_parts, axis=0)))
    low_lane = lane < HD
    cosine, sine = turn_ref[0], -turn_ref[1]
    dq = jnp.where(row < HD, acc_ref[0], acc_ref[1]).T * HD**-0.5
    dq_ref[...] = rope(dq, cosine, sine).astype(BF)
    dk = jnp.where(low_lane, grads[0][0], grads[1][0])
    dk_ref[...] = rope(dk, cosine, sine).astype(BF)
    dv_ref[...] = jnp.where(low_lane, grads[0][1], grads[1][1]).astype(BF)


def attend_back_call(length, q2, keys, values, mixed, back, coarse, fine):
    tok_count, width = keys.shape
    column = pl.BlockSpec((tok_count, LANES), lambda i: (0, i))
    return pl.pallas_call(
        attend_back_body,
        grid=(PAIRS,),
        in_specs=[
            smem(), pl.BlockSpec((2 * LANES, tok_count), lambda i: (i, 0)), column, column, column,
            column, whole(coarse.shape), whole(fine.shape),
        ],
        out_specs=[column] * 3,
        out_shape=[shape_of(tok_count, width)] * 3,
        scratch_shapes=[
            pltpu.VMEM((2, LANES, tok_count), F32), pltpu.VMEM((2, tok_count, LANES), F32)
        ],
        compiler_params=PARAMS,
        cost_estimate=cost(12),
        name="attention_backward",
    )(length, q2, keys, values, mixed, back, coarse, fine)


def post_body(
    local, group, me_ref, mixed_ref, x_ref, wo_ref, acat_ref, bcat_ref, gain_ref, table_ref, mix_ref,
    prev_ref, routes_ref, slot_ref, hidden_ref, ei_ref, inner_ref, data_ref, cols_ref,
):
    pieces = split3(table_ref[...])

    def stages(at):
        mixed = mixed_ref[at]
        inner = mm(mixed, acat_ref[...]).astype(BF)
        inner_ref[at] = inner
        yield
        hidden = x_ref[at].astype(F32) + (mm(mixed, wo_ref[...]) + mm(inner, bcat_ref[0]))
        hidden_ref[at] = hidden
        yield
        scale = lax.rsqrt(jnp.mean(hidden * hidden, axis=-1, keepdims=True) + EPSILON)
        ei = (hidden * scale * gain_ref[1:2, :]).astype(BF)
        ei_ref[at] = ei
        yield
        read = None
        for piece in pieces:
            part = mm_nt(piece, ei)
            read = part if read is None else read + part
        yield
        logits = read[0:16]
        for index in range(EXPERTS + 4):
            logits = logits + mix_ref[:, index : index + 1] * prev_ref[index : index + 1, at]
        first, second = routes_ref[0:1, at].astype(F32), routes_ref[1:2, at].astype(F32)
        number = iota((16, TILE), 0).astype(F32)
        one = jnp.sum(jnp.where(number == first, logits, 0.0), axis=0, keepdims=True)
        two = jnp.sum(jnp.where(number == second, logits, 0.0), axis=0, keepdims=True)
        top = jnp.maximum(one, two)
        one, two = jnp.exp(one - top), jnp.exp(two - top)
        gate_a, gate_b = one / (one + two), two / (one + two)
        mixes = read[MIX_ROW : MIX_ROW + 4]
        shares = []
        for index in range(2):
            left, right = mixes[2 * index : 2 * index + 1], mixes[2 * index + 1 : 2 * index + 2]
            top = jnp.maximum(left, right)
            left, right = jnp.exp(left - top), jnp.exp(right - top)
            shares += [left / (left + right), right / (left + right)]

        def both(value):
            return jnp.where(first == value, gate_a, 0.0) + jnp.where(second == value, gate_b, 0.0)

        gates = jnp.where(number == first, gate_a, 0.0) + jnp.where(number == second, gate_b, 0.0)
        beta_a, beta_b = both(EXPERTS + 2.0), both(EXPERTS + 3.0)
        keep = both(EXPERTS + 1.0) + beta_a * shares[0] + beta_b * shares[2]
        data_ref[0:8, at] = gates[0:8]
        tail = [gate_a, gate_b] + shares + [beta_a, beta_b]
        data_ref[8:16, at] = jnp.concatenate(tail, axis=0)
        yield
        slots = slot_ref[:, at].astype(F32)
        expert = iota((EXPERTS, TILE), 0)
        partner = jnp.bitwise_xor(expert // local, me_ref[0])
        base = ((expert % local) * (group * CAP) + partner * CAP).astype(F32)
        place = jnp.where(slots >= 0, slots + base + 1.0, 0.0)
        expert = expert.astype(F32)
        target_a = jnp.sum(jnp.where(expert == first, place, 0.0), axis=0, keepdims=True) - 1.0
        target_b = jnp.sum(jnp.where(expert == second, place, 0.0), axis=0, keepdims=True) - 1.0
        stack = jnp.concatenate(
            [jnp.zeros((VECTOR_ROW, TILE), F32), beta_a * shares[1], beta_b * shares[3]]
            + [jnp.zeros((2, TILE), F32), target_a, target_b, keep]
            + [jnp.zeros((LANES - KEEP_LANE - 1, TILE), F32)],
            axis=0,
        )
        cols_ref[at] = stack.T

    side_by_side(stages)


def post_call(
    local, group, me, mixed, tokens, weight, acat, bcat, gains, table, mixer, prev, routes, slots
):
    tok_count, width = tokens.shape
    return pl.pallas_call(
        functools.partial(post_body, local, group),
        grid=(tok_count // STEP,),
        in_specs=[
            smem(), tall(width), tall(width), whole(weight.shape), whole(acat.shape),
            pl.BlockSpec((1, LANES, width), lambda i: (3, 0, 0)), whole(gains.shape),
            whole(table.shape), whole(mixer.shape), wide(EXPERTS + 4), wide(2), wide(EXPERTS),
        ],
        out_specs=[tall(width), tall(width), tall(LANES), wide(16), tall(LANES)],
        out_shape=[
            shape_of(tok_count, width, dtype=F32), shape_of(tok_count, width),
            shape_of(tok_count, LANES), shape_of(16, tok_count, dtype=F32),
            shape_of(tok_count, LANES, dtype=F32),
        ],
        compiler_params=PARAMS,
        cost_estimate=cost(8),
        name="after_attention",
    )(me, mixed, tokens, weight, acat, bcat, gains, table, mixer, prev, routes, slots)


def expert_body(
    pair, per_owner, group, steps, has_grad, *refs
):
    count = len(pair)
    piece_refs, refs = refs[:count], refs[count:]
    cot_refs, refs = refs[:count], refs[count:]
    wg_ref, wu_ref, wd_ref, dn_ref, up_ref, od_ref, ou_ref = refs[:7]
    refs = refs[7:]
    before_ref = None
    if has_grad:
        before_ref, refs = refs[0], refs[1:]
    back_refs, refs = refs[:count], refs[count:]
    out_refs, refs = refs[:count], refs[count:]
    (
        grad_ref, x_ref, g_ref, gate_ref, pick_ref, dr_ref, zg_ref, zu_ref, dzd_ref, zgt_ref, zut_ref,
        dzdt_ref, racc_ref, xacc_ref, zd_acc, dzg_acc, dzu_acc, h_ref, dg_ref, du_ref,
    ) = refs
    step = pl.program_id(0)
    rows, width = x_ref.shape
    compact = group * RANK
    chosen = pick_ref[...] > 0.0

    def fold(value):
        place = iota((compact, LANES), 0)
        block = per_owner * group
        inner = place // block * per_owner + place % per_owner
        folded = mm_nt(hot(iota((compact, LANES), 1) % RANK == inner), value)
        place = iota((compact, rows), 0)
        owner = place % block // per_owner
        mine = iota((compact, rows), 1) // CAP + pair[0]
        return jnp.where(mine == owner, folded, 0.0).astype(BF)

    def put(start, value):
        span = pl.ds(start, value.shape[1])
        if has_grad:
            value = value + before_ref[:, span].astype(F32)
        grad_ref[:, span] = value.astype(BF)

    @pl.when(step == 0)
    def _():
        for index in range(count):
            span = slice(index * CAP, index * CAP + CAP)
            x_ref[span] = piece_refs[index][0:CAP]
            g_ref[span] = cot_refs[index][...]
            meta = piece_refs[index][CAP:PIECE].astype(F32)
            gate = (meta[0:1] + meta[1:2] + meta[2:3])[:, 0 : 2 * LANES]
            gate_ref[span] = jnp.broadcast_to(gate, (LANES, 2 * LANES)).T[0:CAP]
            lane = (iota((CAP, LANES), 1) // RANK).astype(F32)
            pick_ref[span] = jnp.where(lane == meta[3:4, 0:LANES], 1.0, 0.0)
        picked = pick_ref[...] > 0.0
        dr = (gate_ref[:, 0:1] * g_ref[...].astype(F32)).astype(BF)
        dr_ref[...] = dr
        zg = jnp.where(picked, mm(x_ref[...], dn_ref[0]), 0.0).astype(BF)
        zu = jnp.where(picked, mm(x_ref[...], dn_ref[1]), 0.0).astype(BF)
        dzd = jnp.where(picked, mm_nt(dr, ou_ref[...]), 0.0).astype(BF)
        zg_ref[...] = zg
        zu_ref[...] = zu
        dzd_ref[...] = dzd
        zgt_ref[...] = fold(zg)
        zut_ref[...] = fold(zu)
        dzdt_ref[...] = fold(dzd)
        for ref in (racc_ref, xacc_ref, zd_acc, dzg_acc, dzu_acc):
            ref[...] = jnp.zeros_like(ref)

    gate = mm(x_ref[...], wg_ref[...]) + mm(zg_ref[...], up_ref[0])
    upper = mm(x_ref[...], wu_ref[...]) + mm(zu_ref[...], up_ref[1])
    share = 0.5 * jnp.tanh(0.5 * gate) + 0.5
    silu = gate * share
    active = (silu * upper).astype(BF)
    h_ref[...] = active
    back = mm_nt(dr_ref[...], wd_ref[...]) + mm_nt(dzd_ref[...], od_ref[...])
    du = (back * silu).astype(BF)
    dg = (back * upper * (share + silu * (1.0 - share))).astype(BF)
    du_ref[...] = du
    dg_ref[...] = dg
    racc_ref[...] += mm(active, wd_ref[...])
    zd_acc[...] += mm(active, od_ref[...])
    xacc_ref[...] += mm_nt(dg, wg_ref[...]) + mm_nt(du, wu_ref[...])
    dzg_acc[...] += mm_nt(dg, up_ref[0])
    dzu_acc[...] += mm_nt(du, up_ref[1])
    tile = h_ref.shape[1]
    total = steps * tile
    at = pl.multiple_of(step * tile, tile)
    put(at, mm(zgt_ref[...], dg_ref[...]))
    put(total + at, mm(zut_ref[...], du_ref[...]))
    put(2 * total + at, mm(dzdt_ref[...], h_ref[...]))

    @pl.when(step == steps - 1)
    def _():
        zd = jnp.where(chosen, zd_acc[...], 0.0).astype(BF)
        dzg = jnp.where(chosen, dzg_acc[...], 0.0).astype(BF)
        dzu = jnp.where(chosen, dzu_acc[...], 0.0).astype(BF)
        result = racc_ref[...] + mm(zd, ou_ref[...])
        gated = (gate_ref[:, 0:1] * result).astype(BF)
        product = g_ref[...].astype(F32) * result.astype(BF).astype(F32)
        dots = jnp.broadcast_to(jnp.sum(product, axis=-1, keepdims=True), (rows, LANES))
        back_rows = (xacc_ref[...] + mm_nt(dzg, dn_ref[0]) + mm_nt(dzu, dn_ref[1])).astype(BF)
        for index in range(count):
            span = slice(index * CAP, index * CAP + CAP)
            out_refs[index][...] = gated[span]
            back_refs[index][0:CAP, :] = back_rows[span]
            column = jnp.concatenate(
                [dots[span], jnp.zeros((2 * LANES - CAP, LANES), F32)], axis=0
            ).T[0:1]
            meta = jnp.concatenate(
                [piece.astype(F32) for piece in split3(column)]
                + [jnp.zeros((META - 3, 2 * LANES), F32)],
                axis=0,
            )
            meta = jnp.concatenate([meta, jnp.zeros((META, width - 2 * LANES), F32)], axis=1)
            back_refs[index][CAP:PIECE, :] = meta.astype(BF)
        base = 3 * total
        place = iota((compact, LANES), 0)
        owner = place % (per_owner * group) // per_owner
        ids = jnp.zeros((compact, LANES), F32)
        for index in range(count):
            meta = piece_refs[index][CAP:PIECE, 0:LANES].astype(F32)
            ids = jnp.where(owner == pair[index], meta[3:4], ids)
        put(base + 3 * width, ids)
        put(base, mm(fold(zd), dr_ref[...]))
        put(base + width, mm(fold(dzg), x_ref[...]))
        put(base + 2 * width, mm(fold(dzu), x_ref[...]))


def expert_call(index, pair, group, per_owner, pieces, cots, before, weights):
    gate_w, up_w, down_w, in_down, in_up, out_down, out_up = weights
    width, hidden = gate_w.shape[1:]
    rows = len(pair) * CAP
    steps = hidden // FTILE
    columns = 3 * hidden + 3 * width + LANES
    compact = group * RANK
    has_grad = before is not None
    return pl.pallas_call(
        functools.partial(expert_body, pair, per_owner, group, steps, has_grad),
        grid=(steps,),
        in_specs=[
            pl.BlockSpec((PIECE, width), lambda f, row=piece.shape[0] // PIECE > 1: (index * row, 0))
            for piece in pieces
        ]
        + [pl.BlockSpec((CAP, width), lambda f: (index, 0))] * len(pair)
        + [
            pl.BlockSpec((None, width, FTILE), lambda f: (index, 0, f)),
            pl.BlockSpec((None, width, FTILE), lambda f: (index, 0, f)),
            pl.BlockSpec((None, FTILE, width), lambda f: (index, f, 0)),
            pl.BlockSpec((None, 2, width, LANES), lambda f: (index, 0, 0, 0)),
            pl.BlockSpec((None, 2, LANES, FTILE), lambda f: (index, 0, 0, f)),
            pl.BlockSpec((None, FTILE, LANES), lambda f: (index, f, 0)),
            pl.BlockSpec((None, LANES, width), lambda f: (index, 0, 0)),
        ]
        + [whole((compact, columns))] * has_grad,
        out_specs=[whole((PIECE, width))] * len(pair)
        + [whole((CAP, width))] * len(pair)
        + [whole((compact, columns))],
        out_shape=[shape_of(PIECE, width)] * len(pair)
        + [shape_of(CAP, width)] * len(pair)
        + [shape_of(compact, columns)],
        scratch_shapes=[pltpu.VMEM((rows, width), BF)] * 2
        + [pltpu.VMEM((rows, LANES), F32)] * 2
        + [pltpu.VMEM((rows, width), BF)]
        + [pltpu.VMEM((rows, LANES), BF)] * 3
        + [pltpu.VMEM((compact, rows), BF)] * 3
        + [pltpu.VMEM((rows, width), F32)] * 2
        + [pltpu.VMEM((rows, LANES), F32)] * 3
        + [pltpu.VMEM((rows, FTILE), BF)] * 3,
        compiler_params=PARAMS,
        cost_estimate=cost(18),
        name="expert_layer",
    )(
        *pieces, *cots, gate_w, up_w, down_w, in_down, in_up, out_down, out_up,
        *([before] if has_grad else []),
    )


def spread(cols, index, count):
    return iota((TILE, count), 1).astype(F32) == cols[:, index : index + 1]


def combine_body(
    pieces, len_ref, *refs
):
    back_refs = refs[:pieces]
    (
        routes_ref, data_ref, cols_ref, cot_ref, ei_ref, hidden_ref, gain_ref, wo_ref, acat_ref, bcat_ref,
        table_ref, bh_ref, ba_ref, din_ref, bm_ref, back_all, dots_ref,
    ) = refs[pieces:]
    count = pieces * CAP

    @pl.when(pl.program_id(0) == 0)
    def _():
        for index, back_ref in enumerate(back_refs):
            back_all[index * CAP : index * CAP + CAP, :] = back_ref[0:CAP, :]
        dots = [back_ref[CAP:PIECE, 0:CAP].astype(F32) for back_ref in back_refs]
        dots = jnp.concatenate(dots, axis=1)
        dots_ref[...] = jnp.concatenate([dots, jnp.zeros_like(dots)], axis=0).astype(BF)

    table_high, table_middle, table_low = split3(table_ref[...])
    stack = dots_ref[...]
    ones = jnp.ones((16, cot_ref.shape[1]), BF)

    def stages(at):
        start = pl.program_id(0) * STEP + at.start
        cols = cols_ref[at]
        chosen_a = hot(spread(cols, TARGET_LANE, count))
        chosen_b = hot(spread(cols, TARGET_LANE + 1, count))
        yield
        routed_a = jnp.sum(mm_nt(stack, chosen_a)[0:8], axis=0, keepdims=True)
        routed_b = jnp.sum(mm_nt(stack, chosen_b)[0:8], axis=0, keepdims=True)
        cot = cot_ref[at]
        cot_f = cot.astype(F32)
        yield
        high, low = split2(cot_f * ei_ref[at].astype(F32))
        along_x = (mm_nt(ones, high) + mm_nt(ones, low))[0:1]
        yield
        along_c = mm_nt(table_high, cot) + mm_nt(table_middle, cot) + mm_nt(table_low, cot)
        along_a = along_c[VECTOR_ROW : VECTOR_ROW + 1]
        along_b = along_c[VECTOR_ROW + 1 : VECTOR_ROW + 2]
        yield
        both = chosen_a + chosen_b
        half = count // 2
        back = mm(both[:, :half], back_all[:half]) + mm(both[:, half:], back_all[half:])
        yield
        first, second = routes_ref[0:1, at].astype(F32), routes_ref[1:2, at].astype(F32)
        token = iota((1, TILE), 1) + start
        valid = jnp.where(token < len_ref[0], 1.0, 0.0)
        gate_a, gate_b = data_ref[8:9, at], data_ref[9:10, at]
        share = [data_ref[index : index + 1, at] for index in range(10, 14)]
        beta_a, beta_b = data_ref[14:15, at], data_ref[15:16, at]
        const_a = share[0] * along_x + share[1] * along_a
        const_b = share[2] * along_x + share[3] * along_b

        def here(route):
            return (
                jnp.where(route == EXPERTS + 1.0, along_x, 0.0)
                + jnp.where(route == EXPERTS + 2.0, const_a, 0.0)
                + jnp.where(route == EXPERTS + 3.0, const_b, 0.0)
            )

        dot_a, dot_b = routed_a + here(first), routed_b + here(second)
        mean = gate_a * dot_a + gate_b * dot_b
        chosen_grad_a = valid * gate_a * (dot_a - mean)
        chosen_grad_b = valid * gate_b * (dot_b - mean)
        number = iota((16, TILE), 0).astype(F32)
        logit_grads = jnp.where(number == first, chosen_grad_a, 0.0) + jnp.where(
            number == second, chosen_grad_b, 0.0
        )
        mixes = []
        for index, (beta, along) in enumerate(((beta_a, along_a), (beta_b, along_b))):
            left, right = share[2 * index], share[2 * index + 1]
            weighted = left * along_x + right * along
            mixes += [
                valid * beta * left * (along_x - weighted),
                valid * beta * right * (along - weighted),
            ]
        small = jnp.concatenate(
            [logit_grads] + mixes + [jnp.zeros((LANES - 20, TILE), F32)], axis=0
        ).T
        high, low = split2(small)
        yield
        inside = iota((TILE, 1), 0) + start < len_ref[0]
        grad = jnp.where(inside, cot_f, 0.0)
        back = back + mm(high, table_high) + mm(low, table_high) + mm(high, table_middle)
        back = back + cols[:, KEEP_LANE : KEEP_LANE + 1] * grad
        yield
        hidden = hidden_ref[at]
        scale = lax.rsqrt(jnp.mean(hidden * hidden, axis=-1, keepdims=True) + EPSILON)
        normed = hidden * scale
        back = back * gain_ref[1:2, :]
        back = grad + scale * (back - normed * jnp.mean(back * normed, axis=-1, keepdims=True))
        bh_ref[at] = back
        rounded = back.astype(BF)
        ba_ref[at] = rounded
        yield
        inner = mm_nt(rounded, bcat_ref[0]).astype(BF)
        din_ref[at] = inner
        yield
        bm_ref[at] = (mm_nt(rounded, wo_ref[...]) + mm_nt(inner, acat_ref[...])).astype(BF)

    side_by_side(stages)


def combine_call(
    length, backs, routes, data, cols, cotangent, ei, hidden, gains, weight, acat, bcat, table
):
    tok_count, width = cotangent.shape
    pieces = len(backs)
    return pl.pallas_call(
        functools.partial(combine_body, pieces),
        grid=(tok_count // STEP,),
        in_specs=[smem()] + [whole(back.shape) for back in backs] + [
            wide(2), wide(16), tall(LANES), tall(width), tall(width), tall(width),
            whole(gains.shape), whole(weight.shape), whole(acat.shape),
            pl.BlockSpec((1, LANES, width), lambda i: (3, 0, 0)), whole(table.shape),
        ],
        out_specs=[tall(width), tall(width), tall(LANES), tall(width)],
        out_shape=[
            shape_of(tok_count, width, dtype=F32), shape_of(tok_count, width),
            shape_of(tok_count, LANES), shape_of(tok_count, width),
        ],
        scratch_shapes=[
            pltpu.VMEM((pieces * CAP, width), BF), pltpu.VMEM((2 * META, pieces * CAP), BF)
        ],
        compiler_params=PARAMS,
        cost_estimate=cost(17),
        name="combine_backward",
    )(
        length, *backs, routes, data, cols, cotangent, ei, hidden, gains, weight, acat, bcat, table
    )


def result_body(pieces, len_ref, *refs):
    result_refs = refs[:pieces]
    cols_ref, ei_ref, hidden_ref, table_ref, out_ref, result_all = refs[pieces:]
    count = pieces * CAP

    @pl.when(pl.program_id(0) == 0)
    def _():
        for index, result_ref in enumerate(result_refs):
            result_all[index * CAP : index * CAP + CAP, :] = result_ref[...]

    table_high, table_low = split2(table_ref[...])

    def stages(at):
        cols = cols_ref[at]
        both = hot(spread(cols, TARGET_LANE, count) | spread(cols, TARGET_LANE + 1, count))
        yield
        half = count // 2
        mixture = mm(both[:, :half], result_all[:half]) + mm(both[:, half:], result_all[half:])
        yield
        high, low = split2(cols)
        mixture = mixture + mm(high, table_high) + mm(low, table_high) + mm(high, table_low)
        mixture = mixture + cols[:, KEEP_LANE : KEEP_LANE + 1] * ei_ref[at].astype(F32)
        yield
        inside = iota((TILE, 1), 0) + pl.program_id(0) * STEP + at.start < len_ref[0]
        out_ref[at] = (hidden_ref[at] + jnp.where(inside, mixture, 0.0)).astype(BF)

    side_by_side(stages)


def result_call(length, results, cols, ei, hidden, table):
    tok_count, width = ei.shape
    pieces = len(results)
    return pl.pallas_call(
        functools.partial(result_body, pieces),
        grid=(tok_count // STEP,),
        in_specs=[smem()] + [whole(result.shape) for result in results] + [
            tall(LANES), tall(width), tall(width), whole(table.shape),
        ],
        out_specs=tall(width),
        out_shape=shape_of(tok_count, width),
        scratch_shapes=[pltpu.VMEM((pieces * CAP, width), BF)],
        compiler_params=PARAMS,
        cost_estimate=cost(8),
        name="layer_output",
    )(length, *results, cols, ei, hidden, table)


def adapter_body(
    packed, id_ref, dq_ref, dk_ref, dv_ref, bcat_ref, normed_ref, inner_ref, mixed_ref, inner_o_ref,
    ba_ref, din_ref, back_ref, grad_ref, acc_ref,
):
    step = pl.program_id(0)
    width = dq_ref.shape[1]
    count = 4 * RANK

    @pl.when(step == 0)
    def _():
        acc_ref[...] = jnp.zeros_like(acc_ref)

    inner_t = inner_ref[...].astype(F32).T[0:count].astype(BF)
    outer_t = inner_o_ref[...].astype(F32).T[0:count].astype(BF)
    number = iota((count, width), 0) % 4
    back_inner = din_ref[...].astype(F32)
    values = [ref[...] for ref in (dq_ref, dk_ref, dv_ref)]
    for index, value in enumerate(values):
        back_inner = back_inner + mm_nt(value, bcat_ref[index]).astype(BF).astype(F32)
    upper = mm(outer_t, ba_ref[...])
    for index, value in enumerate(values):
        upper = jnp.where(number == index, mm(inner_t, value), upper)
    own = iota(back_inner.shape, 1) % 4 < 3
    back_ref[...] = jnp.where(own, back_inner, 0.0).astype(BF)
    back_t = back_inner.T[0:count].astype(BF)
    down = jnp.where(number < 3, mm(back_t, normed_ref[...]), mm(back_t, mixed_ref[...]))
    acc_ref[:, 0:width] += down
    acc_ref[:, width:] += upper

    @pl.when(step == pl.num_programs(0) - 1)
    def _():
        if not packed:
            grad_ref[...] = acc_ref[...].astype(BF)
            return
        half = width // 2
        shape = (16 * RANK, count)
        place, row = iota(shape, 0), iota(shape, 1)
        total = None
        for index in range(4):
            kind, part = index // 2, index % 2
            here = (place % 4 == row % 4) & (place // 16 == row // 4)
            here = here & (place // 8 % 2 == part) & (place // 4 % 2 == kind)
            start = kind * width + part * half
            piece = mm(hot(here), acc_ref[:, start : start + half].astype(BF))
            total = piece if total is None else total + piece
        grad_ref[:, 0:half] = total.astype(BF)
        grad_ref[:, half:] = jnp.full((16 * RANK, LANES), id_ref[0].astype(F32), F32).astype(BF)


def adapter_call(
    packed, ids, dq, dk, dv, bcat, normed, inner, mixed, inner_o, ba, din
):
    tok_count, width = dq.shape
    grad_shape = (16 * RANK, width // 2 + LANES) if packed else (4 * RANK, 2 * width)
    return pl.pallas_call(
        functools.partial(adapter_body, packed),
        grid=(tok_count // TILE,),
        in_specs=[
            smem(), tile(width), tile(width), tile(width), whole(bcat.shape), tile(width), tile(LANES),
            tile(width), tile(LANES), tile(width), tile(LANES),
        ],
        out_specs=[tile(LANES), whole(grad_shape)],
        out_shape=[shape_of(tok_count, LANES), shape_of(*grad_shape)],
        scratch_shapes=[pltpu.VMEM((4 * RANK, 2 * width), F32)],
        compiler_params=PARAMS,
        cost_estimate=cost(6),
        name="adapter_gradients",
    )(ids, dq, dk, dv, bcat, normed, inner, mixed, inner_o, ba, din)


def last_body(
    dq_ref, dk_ref, dv_ref, w_ref, acat_ref, back_ref, x_ref, bh_ref, gain_ref, out_ref
):
    def stages(at):
        parts = [mm_nt(back_ref[at], acat_ref[...])]
        for index, ref in enumerate((dq_ref, dk_ref, dv_ref)):
            parts.append(mm_nt(ref[at], w_ref[index]))
            yield
        total = parts[0] + parts[1] + parts[2] + parts[3]
        x = x_ref[at].astype(F32)
        scale = lax.rsqrt(jnp.mean(x * x, axis=-1, keepdims=True) + EPSILON)
        normed = x * scale
        back = total * gain_ref[0:1, :]
        back = scale * (back - normed * jnp.mean(back * normed, axis=-1, keepdims=True))
        out_ref[at] = (bh_ref[at] + back).astype(BF)

    side_by_side(stages)


def last_call(dq, dk, dv, weights, acat, back, tokens, bh, gains):
    tok_count, width = tokens.shape
    return pl.pallas_call(
        last_body,
        grid=(tok_count // STEP,),
        in_specs=[
            tall(width), tall(width), tall(width), whole(weights.shape), whole(acat.shape),
            tall(LANES), tall(width), tall(width), whole(gains.shape),
        ],
        out_specs=tall(width),
        out_shape=shape_of(tok_count, width),
        compiler_params=PARAMS,
        cost_estimate=cost(9),
        name="after_attention_backward",
    )(dq, dk, dv, weights, acat, back, tokens, bh, gains)


def exchange(value, axes):
    return lax.all_to_all(value, axes, split_axis=0, concat_axis=0, tiled=True)


def gather_all(value, axes, count):
    return exchange(jnp.broadcast_to(value[None], (count,) + value.shape), axes)


def swap(value, partner, group):
    if partner == 0:
        return value
    return lax.ppermute(value, "expert", [(index, index ^ partner) for index in range(group)])


def find_adapters(id_rows):
    count = id_rows.shape[0]
    padded = id_rows.astype(F32)
    if count % LANES:
        padded = jnp.concatenate([padded, jnp.zeros((-count % LANES, LANES), F32)], axis=0)
    return padded.T[0:1, 0:count].astype(jnp.int32)


def sum_expert_body(each, adapters, in_ref, out_ref):
    count, columns = in_ref.shape[0], out_ref.shape[1]
    found = find_adapters(in_ref[:, columns:])
    place = iota((adapters * each, count), 0)
    column = iota((adapters * each, count), 1)
    pick = hot((place // each == found) & (place % each == column % each))
    out_ref[...] = mm(pick, in_ref[:, 0:columns]).astype(BF)


def exchange_expert_grads(grads, group, owners):
    split = min(RANK, owners)
    each, parts = RANK // split, owners // split
    columns = (grads.shape[1] - LANES) // parts
    pieces = grads.reshape(split, each * group, grads.shape[1])
    if parts > 1:
        ids = jnp.broadcast_to(pieces[:, None, :, parts * columns :], (split, parts, each * group, LANES))
        pieces = pieces[:, :, : parts * columns].reshape(split, each * group, parts, columns)
        pieces = jnp.concatenate([pieces.transpose(0, 2, 1, 3), ids], axis=-1)
        pieces = pieces.reshape(owners, each * group, columns + LANES)
    return exchange(pieces, "dp").reshape(owners * group * each, columns + LANES)


def sum_expert_grads(got, adapters, owners):
    columns = got.shape[1] - LANES
    each = RANK // min(RANK, owners)
    return pl.pallas_call(
        functools.partial(sum_expert_body, each, adapters),
        out_shape=shape_of(adapters * each, columns),
        compiler_params=PARAMS,
        cost_estimate=cost(2.2),
        name="expert_gradient_part",
    )(got)


def finish_expert_body(split, adapters, hidden, in_ref, *refs):
    down_ref, up_ref, out_down_ref, out_up_ref = refs[-4:]
    each = RANK // split
    rows = adapters * each
    count = split * rows
    width = out_up_ref.shape[1]

    def place(value):
        return value // each % adapters * RANK + value // (adapters * each) * each + value % each

    move = hot(iota((count, count), 0) == place(iota((count, count), 1)))
    back = hot(iota((count, count), 1) == place(iota((count, count), 0)))

    def part(start, size):
        span = slice(start, start + size)
        rows_of = [in_ref[owner, :, span] for owner in range(split)]
        return jnp.concatenate(rows_of, axis=0)

    for index in range(2):
        up_ref[index] = mm(move, part(index * hidden, hidden))
    out_down_ref[...] = mm_tn(part(2 * hidden, hidden), back)
    base = 3 * hidden
    out_up_ref[...] = mm(move, part(base, width))
    for index in range(2):
        base += width
        down_ref[index] = mm_tn(part(base, width), back)


def finish_expert_call(index, local, everything, outs, adapters, width, hidden):
    owners, rows, columns = everything.shape
    total = adapters * RANK
    shapes = [(local, 2, width, total), (local, 2, total, hidden), (local, hidden, total),
              (local, total, width)]
    specs = [
        pl.BlockSpec((None,) + shape[1:], lambda *_, rank=len(shape): (index,) + (0,) * (rank - 1))
        for shape in shapes
    ]
    return pl.pallas_call(
        functools.partial(finish_expert_body, owners, adapters, hidden),
        grid=(1,),
        in_specs=[whole(everything.shape)] + [pl.BlockSpec(memory_space=pl.ANY)] * len(outs),
        out_specs=specs,
        out_shape=[shape_of(*shape, dtype=F32) for shape in shapes],
        input_output_aliases={1 + place: place for place in range(len(outs))},
        compiler_params=PARAMS,
        cost_estimate=cost(4),
        name="expert_gradient_sums",
    )(everything, *outs)


def spread_expert_grads(own, adapters, owners):
    split = min(RANK, owners)
    each, parts = RANK // split, owners // split
    everything = gather_all(own, "dp", owners)
    everything = everything.reshape(split, parts, adapters, each, own.shape[1])
    everything = everything.transpose(2, 0, 3, 1, 4)
    return everything.reshape(adapters * RANK, parts * own.shape[1]).astype(F32)


def expert_sums(owned, adapters, owners, width, hidden):
    sums = [spread_expert_grads(value, adapters, owners) for value in owned]
    base = 3 * hidden
    up = [[value[:, 0:hidden], value[:, hidden : 2 * hidden]] for value in sums]
    down = [
        [value[:, base + width * part : base + width * (part + 1)].T for part in (1, 2)]
        for value in sums
    ]
    return (
        jnp.stack([jnp.stack(value) for value in down]),
        jnp.stack([jnp.stack(value) for value in up]),
        jnp.stack([value[:, 2 * hidden : base].T for value in sums]),
        jnp.stack([value[:, base : base + width] for value in sums]),
    )


def finish_adapter_body(adapters, me_ref, *refs):
    piece_refs, (down_ref, up_ref, in_ref) = refs[:-3], refs[-3:]
    half = in_ref.shape[3]
    owners, group = piece_refs[0].shape[0], len(piece_refs)
    for other in range(group):
        place = jnp.bitwise_xor(me_ref[0], other)
        for owner in range(owners):
            in_ref[owner * (group // 2) + place // 2, place % 2] = piece_refs[other][owner]
    count = RANK * adapters

    def place(value):
        return value % adapters * RANK + value // adapters

    move = hot(iota((count, count), 0) == place(iota((count, count), 1)))
    back = hot(iota((count, count), 1) == place(iota((count, count), 0)))
    for part in range(2):
        span = slice(part * half, part * half + half)
        for kind in range(2):
            for index in range(4):
                first = (kind * 4 + index) * adapters
                rows = in_ref[:, part, first : first + adapters, :].astype(F32)
                rows = rows.reshape(count, half).astype(BF)
                if kind == 0:
                    down_ref[index, span, :] = mm_tn(rows, back)
                else:
                    up_ref[index, :, span] = mm(move, rows)


def sum_adapter_body(kinds, adapters, in_ref, out_ref):
    count, columns = in_ref.shape[0], out_ref.shape[-1]
    found = find_adapters(in_ref[:, columns:])
    place = iota((adapters * kinds, count), 0)
    column = iota((adapters * kinds, count), 1)
    pick = hot((place % adapters == found) & (place // adapters == column % kinds))
    own = mm(pick, in_ref[:, 0:columns]).astype(BF)
    for index in range(out_ref.shape[0]):
        out_ref[index] = own


def adapter_sums(grads, meanwhile, later, ids, adapters, owners, group, width):
    axes, everyone = ("dp", "expert"), owners * group
    if everyone == 2 * RANK and group == 4:
        kinds = 8
        got = exchange(grads.reshape(everyone, kinds, grads.shape[1]), axes)
        got, meanwhile = lax.optimization_barrier((got, meanwhile))
        own = pl.pallas_call(
            functools.partial(sum_adapter_body, kinds, adapters),
            out_shape=shape_of(owners, kinds * adapters, width // 2),
            compiler_params=PARAMS,
            cost_estimate=cost(2.0),
            name="adapter_gradient_part",
        )(got.reshape(everyone * kinds, grads.shape[1]))
        mine = exchange(own, "dp")
        mine, later = lax.optimization_barrier((mine, later))
        across = swap(mine, 2, group)
        full = [mine, swap(mine, 1, group), across, swap(across, 1, group)]
        total = adapters * RANK
        down, upper = pl.pallas_call(
            functools.partial(finish_adapter_body, adapters),
            in_specs=[smem()] + [pl.BlockSpec(memory_space=pltpu.VMEM)] * group,
            out_shape=[shape_of(4, width, total, dtype=F32), shape_of(4, total, width, dtype=F32)],
            scratch_shapes=[pltpu.VMEM((RANK, 2, kinds * adapters, width // 2), BF)],
            compiler_params=PARAMS,
            cost_estimate=cost(3.6),
            name="adapter_gradient_sums",
        )(lax.axis_index("expert").reshape(1).astype(jnp.int32), *full)
        return down, upper, meanwhile, later
    all_ids = exchange(jnp.broadcast_to(ids, (everyone,)), axes)
    pieces = grads.reshape(everyone, RANK * 4 * 2 * width // everyone)
    got = exchange(pieces, axes)
    pick = (jnp.arange(adapters, dtype=jnp.int32)[:, None] == all_ids[None, :]).astype(BF)
    own = jnp.dot(pick, got, preferred_element_type=F32).astype(BF)
    full = gather_all(own, axes, everyone)
    full = full.reshape(RANK, everyone // RANK, adapters, -1).transpose(2, 0, 1, 3)
    full = full.reshape(adapters * RANK, 4, 2, width).astype(F32)
    return full[:, :, 0].transpose(1, 2, 0), full[:, :, 1].transpose(1, 0, 2), meanwhile, later


def body(
    tokens,
    cotangent,
    lengths,
    adapter_ids,
    routes,
    prev_logits,
    norm_gains,
    input_weights,
    output_weight,
    adapter_down,
    adapter_up,
    router,
    residual_mix,
    constant_mix,
    constant_vectors,
    expert_gate,
    expert_up,
    expert_down,
    expert_adapter_down,
    expert_adapter_up,
    output_adapter_down,
    output_adapter_up,
):
    tok_count, width = tokens.shape
    hidden_width = expert_gate.shape[2]
    group, owners = lax.axis_size("expert"), lax.axis_size("dp")
    local = expert_gate.shape[0]
    adapters = adapter_down.shape[-1] // RANK
    angles = [jnp.asarray(table) for table in turn_tables(tok_count)]
    weights = (
        expert_gate, expert_up, expert_down, expert_adapter_down, expert_adapter_up,
        output_adapter_down, output_adapter_up,
    )
    per_owner = RANK // min(RANK, owners)
    everyone = owners * group
    me = lax.axis_index("expert")

    me = me.reshape(1).astype(jnp.int32)

    routes, prev_logits = routes.T, prev_logits.T
    slots, *grad_sends = route_call(local, group, lengths, me, routes, cotangent)
    cots = [swap(value, partner, group) for partner, value in enumerate(grad_sends)]
    normed, inner, queries, keys, values, acat, bcat, table, mixer = pre_call(
        adapter_ids, tokens, norm_gains, input_weights, adapter_down, adapter_up, *angles, router.T,
        constant_mix.T, constant_vectors, residual_mix,
    )
    mixed, q2 = attend_call(lengths, queries, keys, values)
    mixed, cots = lax.optimization_barrier((mixed, cots))
    hidden, ei, inner_o, data, cols = post_call(
        local, group, me, mixed, tokens, output_weight, acat, bcat, norm_gains, table, mixer, prev_logits,
        routes, slots,
    )
    sends = send_call(local, group, me, adapter_ids, slots, data, ei)
    near, far = tuple(range(group // 2)), tuple(range(group // 2, group))
    sent_near = [swap(sends[partner], partner, group) for partner in near]
    sent_far = []
    for index in range(local):
        pieces = [sends[group // 2 + place * local + index] for place in range(len(far))]
        if index > 0:
            pieces, sent_near = lax.optimization_barrier((pieces, sent_near))
        sent_far.append([swap(piece, partner, group) for piece, partner in zip(pieces, far)])
    backs = [[None] * group for _ in range(local)]
    results = [[None] * group for _ in range(local)]
    grads, last = [], None
    for index in range(local):
        before = None
        for pair in (near, far) if index % 2 == 0 else (far, near):
            pieces = sent_near if pair == near else sent_far[index]
            if last is not None:
                pieces, last = lax.optimization_barrier((pieces, last))
            if index == local - 1 and pair == near:
                pieces, backs[:index] = lax.optimization_barrier((pieces, backs[:index]))
            outs = expert_call(
                index, pair, group, per_owner, pieces, [cots[partner] for partner in pair], before, weights
            )
            before = last = outs[-1]
            for place, partner in enumerate(pair):
                backs[index][partner] = swap(outs[place], partner, group)
                results[index][partner] = outs[len(pair) + place]
        grads.append(before)
    backs = [value for some in backs for value in some]

    parts = [exchange_expert_grads(grad, group, owners) for grad in grads[:-1]]
    sums = functools.partial(sum_expert_grads, adapters=adapters, owners=owners)
    parts, last = lax.optimization_barrier((parts, last))
    owned = [sums(part) for part in parts]
    last, owned = lax.optimization_barrier((last, owned))
    parts.append(exchange_expert_grads(last, group, owners))
    backs[-2:], owned = lax.optimization_barrier((backs[-2:] , owned))
    gather = functools.partial(lax.all_gather, axis_name="dp", axis=0, tiled=False)
    if owners <= RANK:
        owned = [gather(own) for own in owned]
    back_hidden, back_attention, back_inner_o, back_mixed = combine_call(
        lengths, backs, routes, data, cols, cotangent, ei, hidden, norm_gains, output_weight, acat, bcat,
        table,
    )
    flat = [value for some in results for value in some]
    flat, back_mixed = lax.optimization_barrier((flat, back_mixed))
    flat = [swap(value, place % group, group) for place, value in enumerate(flat)]

    dq, dk, dv = attend_back_call(lengths, q2, keys, values, mixed, back_mixed, *angles)
    parts[-1], dq, flat = lax.optimization_barrier((parts[-1], dq, flat))
    own = sums(parts[-1])
    dq, own, flat = lax.optimization_barrier((dq, own, flat))
    owned.append(gather(own) if owners <= RANK else own)
    back_inner, adapter_grads = adapter_call(
        everyone == 2 * RANK and group == 4, adapter_ids, dq, dk, dv, bcat, normed, inner, mixed,
        inner_o, back_attention, back_inner_o,
    )
    (dq, dk, dv, flat, owned[:-1]), adapter_grads = lax.optimization_barrier(
        ((dq, dk, dv, flat, owned[:-1]), adapter_grads)
    )
    layer_out = result_call(lengths, flat, cols, ei, hidden, table)
    input_back = last_call(
        dq, dk, dv, input_weights, acat, back_inner, tokens, back_hidden, norm_gains
    )
    outs = []
    if owners <= RANK:
        for index, own in enumerate(owned[:-1]):
            outs = finish_expert_call(index, local, own, outs, adapters, width, hidden_width)
    down_sum, upper_sum, layer_out, (input_back, outs) = adapter_sums(
        adapter_grads, layer_out, (input_back, outs), adapter_ids, adapters, owners, group, width
    )
    if owners <= RANK:
        outs = finish_expert_call(
            local - 1, local, owned[-1], outs, adapters, width, hidden_width
        )
    else:
        outs = expert_sums(owned, adapters, owners, width, hidden_width)
    in_down_sum, in_up_sum, out_down_sum, out_up_sum = outs
    return (
        layer_out,
        input_back,
        down_sum,
        upper_sum,
        in_down_sum,
        in_up_sum,
        out_down_sum,
        out_up_sum,
    )


def solution(mesh):
    tokens_spec, copied = P(("dp", "expert"), None), P()
    owned = P("expert")
    placed = (
        (tokens_spec, tokens_spec, P(("dp", "expert")), P(("dp", "expert")), tokens_spec, tokens_spec)
        + (copied,) * 9
        + (owned,) * 7
    )
    return jax.shard_map(
        body,
        mesh=mesh,
        in_specs=placed,
        out_specs=(tokens_spec, tokens_spec, copied, copied) + (owned,) * 4,
        check_vma=False,
    )
```

```python
import functools
import math

import jax
import jax.numpy as jnp
import numpy as np
from jax import lax
from jax.experimental import pallas as pl
from jax.experimental.pallas import tpu as pltpu
from jax.sharding import PartitionSpec as P

HEADS = 12
HD = 64
EXPERTS = 8
RANK = 16
CAP = 192
EPSILON = 1e-06
F32 = jnp.float32
BF = jnp.bfloat16
NEG = -1e30
LANES = 128
TILE = 256
STEP = 512
FTILE = 512
PAIRS = HEADS // 2
PARAMS = pltpu.CompilerParams(vmem_limit_bytes=67043328)
META = 8
MIX_ROW = 16
VECTOR_ROW = 20
TARGET_LANE = 24
KEEP_LANE = 26
READ_VECTOR = 48
READ_ROWS = 64
PIECE = CAP + META


def mm(left, right):
    return jnp.dot(left, right, preferred_element_type=F32)


def mm_nt(left, right):
    return lax.dot_general(left, right, (((1,), (1,)), ((), ())), preferred_element_type=F32)


def mm_tn(left, right):
    return lax.dot_general(left, right, (((0,), (0,)), ((), ())), preferred_element_type=F32)


def iota(shape, axis):
    return lax.broadcasted_iota(jnp.int32, shape, axis)


def hot(condition):
    return jnp.where(condition, 1.0, 0.0).astype(BF)


def split2(value):
    high = value.astype(BF)
    return high, (value - high.astype(F32)).astype(BF)


def split3(value):
    high = value.astype(BF)
    rest = value - high.astype(F32)
    middle = rest.astype(BF)
    return high, middle, (rest - middle.astype(F32)).astype(BF)


def whole(shape):
    zeros = (0,) * len(shape)
    return pl.BlockSpec(shape, lambda *_: zeros)


def smem():
    return pl.BlockSpec(memory_space=pltpu.SMEM)


def tall(width):
    return pl.BlockSpec((STEP, width), lambda i: (i, 0))


def wide(height):
    return pl.BlockSpec((height, STEP), lambda i: (0, i))


def tile(width):
    return pl.BlockSpec((TILE, width), lambda i: (i, 0))


def side_by_side(stages):
    running = [stages(slice(start, start + TILE)) for start in range(0, STEP, TILE)]
    while running:
        running = [stage for stage in running if next(stage, True) is None]


def shape_of(*shape, dtype=BF):
    return jax.ShapeDtypeStruct(shape, dtype)


def cost(microseconds):
    return pl.CostEstimate(flops=int(microseconds * 1e+09), bytes_accessed=0, transcendentals=0)


@functools.lru_cache(maxsize=None)
def turn_tables(length_in):
    half = HD // 2
    inverse = np.exp(np.arange(half, dtype=np.float64) * (-2.0 * math.log(10000.0) / HD))

    def table(positions):
        angles = np.tile(positions[:, None] * inverse[None, :], (1, 4))
        return np.stack([np.cos(angles), np.sin(angles)]).astype(np.float32)

    return table(np.arange(0.0, length_in, 32)), table(np.arange(0.0, 32))


def turn_rows(coarse_ref, fine_ref, first, count):
    fine_cos, fine_sin = fine_ref[0], fine_ref[1]
    sign = jnp.where(iota((32, LANES), 1) % HD < HD // 2, -1.0, 1.0)
    signed_cos, signed_sin = fine_cos * sign, fine_sin * sign
    cosines, sines = [], []
    for index in range(count // 32):
        row = first // 32 + index
        coarse_cos, coarse_sin = coarse_ref[0, pl.ds(row, 1), :], coarse_ref[1, pl.ds(row, 1), :]
        cosines.append(coarse_cos * fine_cos - coarse_sin * fine_sin)
        sines.append(coarse_sin * signed_cos + coarse_cos * signed_sin)
    return jnp.concatenate(cosines, axis=0), jnp.concatenate(sines, axis=0)


def rope(value, cosine, sine):
    first = iota(value.shape, 1) % HD < HD // 2
    turned = jnp.where(first, pltpu.roll(value, LANES - HD // 2, 1), pltpu.roll(value, HD // 2, 1))
    return value * cosine + turned * sine


def find_slots(length, routes_ref, slot_ref):
    tok_count = slot_ref.shape[1]
    before = hot(iota((TILE, TILE), 0) < iota((TILE, TILE), 1))
    carry = jnp.zeros((2 * EXPERTS, 1), F32)
    for start in range(0, tok_count, TILE):
        span = slice(start, start + TILE)
        expert = iota((2 * EXPERTS, TILE), 0)
        token = iota((2 * EXPERTS, TILE), 1) + start
        named = (routes_ref[0:1, span] == expert) | (routes_ref[1:2, span] == expert)
        hit = named & (token < length) & (expert < EXPERTS)
        hits = jnp.where(hit, 1.0, 0.0)
        slots = mm(hits.astype(BF), before) + carry
        carry = carry + jnp.sum(hits, axis=1, keepdims=True)
        slot_ref[:, span] = jnp.where(hit, slots, -1.0)[:EXPERTS].astype(jnp.int32)


def pick_rows(slot_ref, step, me, local):
    first = jnp.bitwise_xor(step, me) * local
    place = iota((CAP, slot_ref.shape[1]), 0)
    return first, [hot(place == slot_ref[pl.ds(first + index, 1), :]) for index in range(local)]


def pick_source(chosen, source_ref):
    half = source_ref.shape[0] // 2
    return mm(chosen[:, :half], source_ref[:half]) + mm(chosen[:, half:], source_ref[half:])


def store_piece(out_refs, step, other, index, value, start):
    @pl.when(step == other)
    def _():
        out_refs[index][start : start + value.shape[0], :] = value


def route_body(local, group, len_ref, me_ref, routes_ref, source_ref, slot_ref, *out_refs):
    step = pl.program_id(0)

    @pl.when(step == 0)
    def _():
        find_slots(len_ref[0], routes_ref, slot_ref)

    _, chosen = pick_rows(slot_ref, step, me_ref[0], local)
    rows = pick_source(jnp.concatenate(chosen, axis=0), source_ref).astype(BF)
    for other in range(group):
        store_piece(out_refs, step, other, other, rows, 0)


def route_call(local, group, length, me, routes, source):
    tok_count, width = source.shape
    return pl.pallas_call(
        functools.partial(route_body, local, group),
        grid=(group,),
        in_specs=[smem(), smem(), whole(routes.shape), whole(source.shape)],
        out_specs=[whole((EXPERTS, tok_count))] + [whole((local * CAP, width))] * group,
        out_shape=[shape_of(EXPERTS, tok_count, dtype=jnp.int32)]
        + [shape_of(local * CAP, width)] * group,
        compiler_params=PARAMS,
        cost_estimate=cost(6.5),
        name="route_rows",
    )(length, me, routes, source)


def send_body(local, group, me_ref, id_ref, slot_ref, data_ref, source_ref, *out_refs):
    step = pl.program_id(0)
    width = source_ref.shape[1]
    first, chosen = pick_rows(slot_ref, step, me_ref[0], local)
    rows = pick_source(jnp.concatenate(chosen, axis=0), source_ref).astype(BF)
    for index in range(local):
        pieces = split3(data_ref[pl.ds(first + index, 1), :])
        stack = jnp.concatenate(
            [piece.astype(F32) for piece in pieces]
            + [jnp.zeros((13, chosen[index].shape[1]), F32)],
            axis=0,
        ).astype(BF)
        gates = mm_nt(stack, chosen[index])[0:META]
        gates = jnp.where(iota(gates.shape, 0) == 3, id_ref[0].astype(F32), gates)
        meta = jnp.concatenate([gates, jnp.zeros((META, width - CAP), F32)], axis=1)
        kept = rows[index * CAP : index * CAP + CAP]
        for other in range(group):
            far = other >= group // 2
            place = group // 2 + (other - group // 2) * local + index if far else other
            start = 0 if far else index * PIECE
            store_piece(out_refs, step, other, place, kept, start)
            store_piece(out_refs, step, other, place, meta.astype(BF), start + CAP)


def send_call(local, group, me, ids, slots, data, source):
    tok_count, width = source.shape
    heights = [local * PIECE] * (group // 2) + [PIECE] * ((group - group // 2) * local)
    return pl.pallas_call(
        functools.partial(send_body, local, group),
        grid=(group,),
        in_specs=[smem(), smem(), whole(slots.shape), whole(data.shape), whole(source.shape)],
        out_specs=[whole((height, width)) for height in heights],
        out_shape=[shape_of(height, width) for height in heights],
        compiler_params=PARAMS,
        cost_estimate=cost(8.4),
        name="send_rows",
    )(me, ids, slots, data, source)


def pre_body(
    id_ref, x_ref, gain_ref, w_ref, ad_ref, au_ref, coarse_ref, fine_ref, router_ref, cmix_ref, vec_ref,
    resid_ref, normed_ref, inner_ref, q_ref, k_ref, v_ref, acat_ref, bcat_ref, table_ref, mix_ref,
    read_ref, square_ref,
):
    @pl.when(pl.program_id(0) == 0)
    def _():
        first = RANK * id_ref[0]
        total = None
        for index in range(4):
            row, column = iota((LANES, LANES), 0), iota((LANES, LANES), 1)
            place = hot((row >= first) & (row < first + RANK) & (column == (row - first) * 4 + index))
            part = mm(ad_ref[index], place)
            total = part if total is None else total + part
            place = hot(
                (column >= first) & (column < first + RANK) & (row == (column - first) * 4 + index)
            )
            bcat_ref[index] = mm(place, au_ref[index]).astype(BF)
        acat_ref[...] = total.astype(BF)
        table_ref[...] = jnp.zeros_like(table_ref)
        table_ref[0 : EXPERTS + 4, :] = router_ref[...].astype(F32)
        table_ref[MIX_ROW : MIX_ROW + 4, :] = cmix_ref[...]
        table_ref[VECTOR_ROW : VECTOR_ROW + 2, :] = vec_ref[...]
        read_ref[...] = jnp.zeros_like(read_ref)
        read_ref[0 : EXPERTS + 4, :] = router_ref[...].astype(F32)
        for place, piece in enumerate(split3(cmix_ref[...])):
            read_ref[16 + 8 * place : 20 + 8 * place, :] = piece.astype(F32)
        for place, piece in enumerate(split3(vec_ref[...])):
            read_ref[READ_VECTOR + 2 * place : READ_VECTOR + 2 * place + 2, :] = piece.astype(F32)
        square_ref[...] = jnp.zeros_like(square_ref)
        square_ref[0 : EXPERTS + 4, 0 : EXPERTS + 4] = resid_ref[...]
        mix_ref[...] = square_ref[...].T[0:16]

    def stages(at):
        x = x_ref[at].astype(F32)
        scale = lax.rsqrt(jnp.mean(x * x, axis=-1, keepdims=True) + EPSILON)
        normed = (x * scale * gain_ref[0:1, :]).astype(BF)
        normed_ref[at] = normed
        yield
        inner = mm(normed, acat_ref[...]).astype(BF)
        inner_ref[at] = inner
        yield
        for index, out_ref in enumerate((q_ref, k_ref, v_ref)):
            value = mm(normed, w_ref[index]) + mm(inner, bcat_ref[index])
            yield
            if index == 2:
                out_ref[at] = value.astype(BF)
                continue
            cosine, sine = turn_rows(coarse_ref, fine_ref, pl.program_id(0) * STEP + at.start, TILE)
            for pair in range(PAIRS):
                span = slice(pair * LANES, pair * LANES + LANES)
                turned = rope(value[:, span], cosine, sine).astype(BF)
                if index == 0:
                    turned = (turned.astype(F32) * HD**-0.5).astype(BF)
                out_ref[at, span] = turned
            yield

    side_by_side(stages)


def pre_call(
    ids, tokens, gains, weights, down, upper, coarse, fine, router, constant_mix, vectors, residual_mix
):
    tok_count, width = tokens.shape
    return pl.pallas_call(
        pre_body,
        grid=(tok_count // STEP,),
        in_specs=[
            smem(), tall(width), whole(gains.shape), whole(weights.shape), whole(down.shape),
            whole(upper.shape), whole(coarse.shape), whole(fine.shape), whole(router.shape),
            whole(constant_mix.shape), whole(vectors.shape), whole(residual_mix.shape),
        ],
        out_specs=[
            tall(width), tall(LANES), tall(width), tall(width), tall(width),
            whole((width, LANES)), whole(upper.shape), whole((LANES, width)), whole((16, LANES)),
            whole((READ_ROWS, width)),
        ],
        out_shape=[
            shape_of(tok_count, width), shape_of(tok_count, LANES), shape_of(tok_count, width),
            shape_of(tok_count, width), shape_of(tok_count, width), shape_of(width, LANES),
            shape_of(*upper.shape), shape_of(LANES, width, dtype=F32), shape_of(16, LANES, dtype=F32),
            shape_of(READ_ROWS, width, dtype=F32),
        ],
        scratch_shapes=[pltpu.VMEM((LANES, LANES), F32)],
        compiler_params=PARAMS,
        cost_estimate=cost(12.3),
        name="before_attention",
    )(
        ids, tokens, gains, weights, down, upper, coarse, fine, router, constant_mix, vectors,
        residual_mix,
    )


def attend_body(len_ref, q_ref, k_ref, v_ref, mixed_ref, q2_ref):
    tok_count = q_ref.shape[0]
    lane = iota((tok_count, LANES), 1)
    hidden_key = iota((tok_count, LANES), 0) >= len_ref[0]
    row = iota((LANES, tok_count), 0)
    row_tile = row[:, :TILE]
    causal = iota((TILE, TILE), 0) <= iota((TILE, TILE), 1)
    queries_t = q_ref[...].astype(F32).T
    values_t = v_ref[...].astype(F32).T
    keys = k_ref[...].astype(F32)
    heads = []
    for head in range(2):
        spare = HD * (1 - head)
        bias = jnp.where((lane == spare) & hidden_key, NEG, 0.0)
        one = jnp.where(row == spare, 1.0, 0.0)
        own = row // HD == head
        heads.append(
            (
                jnp.where(lane // HD == head, keys, bias).astype(BF),
                jnp.where(own, queries_t, one).astype(BF),
                jnp.where(own, values_t, one).astype(BF),
            )
        )
    units = [(start, head) for start in range(0, tok_count, TILE) for head in range(2)]

    def score(unit):
        start, head = unit
        keys, queries, _ = heads[head]
        part = queries[:, start : start + TILE]
        near = mm(keys[start : start + TILE], part)
        return near, mm(keys[:start], part) if start else None

    outs = {}
    waiting = score(units[0])
    for index, (start, head) in enumerate(units):
        near, far = waiting
        waiting = score(units[index + 1]) if index + 1 < len(units) else None
        spare = HD * (1 - head)
        _, queries, values = heads[head]
        near = jnp.where(causal, near, NEG)
        top = jnp.max(near, axis=0, keepdims=True)
        if start:
            top = jnp.maximum(top, jnp.max(far, axis=0, keepdims=True))
        mixed = mm(values[:, start : start + TILE], jnp.exp(near - top).astype(BF))
        if start:
            mixed = mixed + mm(values[:, :start], jnp.exp(far - top).astype(BF))
        total = mixed[spare : spare + 1]
        outs[head] = mixed * (1.0 / total)
        kept = queries[:, start : start + TILE]
        logs = jnp.zeros((LANES, TILE), F32)
        for offset, piece in enumerate(split3(top + jnp.log(total))):
            logs = jnp.where(row_tile == spare + 1 + offset, piece.astype(F32), logs)
        q2_ref[head * LANES : head * LANES + LANES, start : start + TILE] = kept + logs.astype(BF)
        if head == 1:
            mixed = jnp.where(row_tile < HD, outs[0], outs[1])
            mixed_ref[start : start + TILE] = mixed.T.astype(BF)


def attend_call(length, queries, keys, values):
    tok_count, width = queries.shape
    column = pl.BlockSpec((tok_count, LANES), lambda i: (0, i))
    return pl.pallas_call(
        attend_body,
        grid=(PAIRS,),
        in_specs=[smem(), column, column, column],
        out_specs=[column, pl.BlockSpec((2 * LANES, tok_count), lambda i: (i, 0))],
        out_shape=[shape_of(tok_count, width), shape_of(2 * width, tok_count)],
        compiler_params=PARAMS,
        cost_estimate=cost(15),
        name="attention_forward",
    )(length, queries, keys, values)


def attend_back_body(
    len_ref, q2_ref, k_ref, v_ref, mixed_ref, back_ref, coarse_ref, fine_ref,
    dq_ref, dk_ref, dv_ref, acc_ref, turn_ref,
):
    tok_count = k_ref.shape[0]

    @pl.when(pl.program_id(0) == 0)
    def _():
        turn_ref[0], turn_ref[1] = turn_rows(coarse_ref, fine_ref, 0, tok_count)

    lane = iota((tok_count, LANES), 1)
    position = iota((tok_count, LANES), 0)
    bias = jnp.where(position < len_ref[0], 0.0, NEG)
    causal = iota((TILE, TILE), 0) <= iota((TILE, TILE), 1)
    row = iota((LANES, tok_count), 0)
    back = back_ref[...].astype(F32)
    product_t = (back * mixed_ref[...].astype(F32)).T
    back_t = back.T
    keys, values = k_ref[...].astype(F32), v_ref[...].astype(F32)
    grads = []
    for head in range(2):
        own = lane // HD == head
        spare = HD * (1 - head)
        minus = jnp.where((lane > spare) & (lane < spare + 4), -1.0, 0.0)
        q2 = q2_ref[head * LANES : head * LANES + LANES, :]
        k2f = jnp.where(own, keys, jnp.where(lane == spare, bias, minus))
        k2 = k2f.astype(BF)
        k2t = k2f.T.astype(BF)
        v2 = jnp.where(own, values, minus).astype(BF)
        own_row = row // HD == head
        delta = jnp.sum(jnp.where(own_row, product_t, 0.0), axis=0, keepdims=True)
        back2 = jnp.where(own_row, back_t, 0.0)
        for offset, piece in enumerate(split3(delta)):
            back2 = jnp.where(row == spare + 1 + offset, piece.astype(F32), back2)
        back2 = back2.astype(BF)
        dk_parts, dv_parts = [], []
        for start in range(0, tok_count, TILE):
            stop = start + TILE
            scores = mm(k2[start:stop], q2[:, start:])
            slopes = mm(v2[start:stop], back2[:, start:])
            diagonal = jnp.where(causal, scores[:, :TILE], NEG)
            scores = (
                diagonal
                if stop == tok_count
                else jnp.concatenate([diagonal, scores[:, TILE:]], axis=1)
            )
            weights = jnp.exp(scores)
            turned = (weights * slopes).astype(BF)
            dv_parts.append(mm_nt(weights.astype(BF), back2[:, start:]))
            dk_parts.append(mm_nt(turned, q2[:, start:]))
            update = mm(k2t[:, start:stop], turned)
            if start == 0:
                acc_ref[head] = update
            else:
                acc_ref[head, :, start:] += update
        grads.append((jnp.concatenate(dk_parts, axis=0), jnp.concatenate(dv_parts, axis=0)))
    low_lane = lane < HD
    cosine, sine = turn_ref[0], -turn_ref[1]
    dq = jnp.where(row < HD, acc_ref[0], acc_ref[1]).T * HD**-0.5
    dq_ref[...] = rope(dq, cosine, sine).astype(BF)
    dk = jnp.where(low_lane, grads[0][0], grads[1][0])
    dk_ref[...] = rope(dk, cosine, sine).astype(BF)
    dv_ref[...] = jnp.where(low_lane, grads[0][1], grads[1][1]).astype(BF)


def attend_back_call(length, q2, keys, values, mixed, back, coarse, fine):
    tok_count, width = keys.shape
    column = pl.BlockSpec((tok_count, LANES), lambda i: (0, i))
    return pl.pallas_call(
        attend_back_body,
        grid=(PAIRS,),
        in_specs=[
            smem(), pl.BlockSpec((2 * LANES, tok_count), lambda i: (i, 0)), column, column, column,
            column, whole(coarse.shape), whole(fine.shape),
        ],
        out_specs=[column] * 3,
        out_shape=[shape_of(tok_count, width)] * 3,
        scratch_shapes=[
            pltpu.VMEM((2, LANES, tok_count), F32), pltpu.VMEM((2, tok_count, LANES), F32)
        ],
        compiler_params=PARAMS,
        cost_estimate=cost(12),
        name="attention_backward",
    )(length, q2, keys, values, mixed, back, coarse, fine)


def post_body(
    local, group, me_ref, mixed_ref, x_ref, wo_ref, acat_ref, bcat_ref, gain_ref, read_ref, mix_ref,
    prev_ref, routes_ref, slot_ref, hidden_ref, ei_ref, inner_ref, data_ref, cols_ref,
):
    reader = read_ref[0:READ_VECTOR].astype(BF)

    def stages(at):
        mixed = mixed_ref[at]
        inner = mm(mixed, acat_ref[...]).astype(BF)
        inner_ref[at] = inner
        yield
        hidden = x_ref[at].astype(F32) + (mm(mixed, wo_ref[...]) + mm(inner, bcat_ref[0]))
        hidden_ref[at] = hidden
        yield
        scale = lax.rsqrt(jnp.mean(hidden * hidden, axis=-1, keepdims=True) + EPSILON)
        ei = (hidden * scale * gain_ref[1:2, :]).astype(BF)
        ei_ref[at] = ei
        yield
        read = mm_nt(reader, ei)
        yield
        logits = read[0:16]
        for index in range(EXPERTS + 4):
            logits = logits + mix_ref[:, index : index + 1] * prev_ref[index : index + 1, at]
        first, second = routes_ref[0:1, at].astype(F32), routes_ref[1:2, at].astype(F32)
        number = iota((16, TILE), 0).astype(F32)
        one = jnp.sum(jnp.where(number == first, logits, 0.0), axis=0, keepdims=True)
        two = jnp.sum(jnp.where(number == second, logits, 0.0), axis=0, keepdims=True)
        top = jnp.maximum(one, two)
        one, two = jnp.exp(one - top), jnp.exp(two - top)
        gate_a, gate_b = one / (one + two), two / (one + two)
        mixes = read[16:20] + read[24:28] + read[32:36]
        shares = []
        for index in range(2):
            left, right = mixes[2 * index : 2 * index + 1], mixes[2 * index + 1 : 2 * index + 2]
            top = jnp.maximum(left, right)
            left, right = jnp.exp(left - top), jnp.exp(right - top)
            shares += [left / (left + right), right / (left + right)]

        def both(value):
            return jnp.where(first == value, gate_a, 0.0) + jnp.where(second == value, gate_b, 0.0)

        gates = jnp.where(number == first, gate_a, 0.0) + jnp.where(number == second, gate_b, 0.0)
        beta_a, beta_b = both(EXPERTS + 2.0), both(EXPERTS + 3.0)
        keep = both(EXPERTS + 1.0) + beta_a * shares[0] + beta_b * shares[2]
        data_ref[0:8, at] = gates[0:8]
        tail = [gate_a, gate_b] + shares + [beta_a, beta_b]
        data_ref[8:16, at] = jnp.concatenate(tail, axis=0)
        yield
        slots = slot_ref[:, at].astype(F32)
        expert = iota((EXPERTS, TILE), 0)
        partner = jnp.bitwise_xor(expert // local, me_ref[0])
        base = ((expert % local) * (group * CAP) + partner * CAP).astype(F32)
        place = jnp.where(slots >= 0, slots + base + 1.0, 0.0)
        expert = expert.astype(F32)
        target_a = jnp.sum(jnp.where(expert == first, place, 0.0), axis=0, keepdims=True) - 1.0
        target_b = jnp.sum(jnp.where(expert == second, place, 0.0), axis=0, keepdims=True) - 1.0
        stack = jnp.concatenate(
            [jnp.zeros((VECTOR_ROW, TILE), F32), beta_a * shares[1], beta_b * shares[3]]
            + [jnp.zeros((2, TILE), F32), target_a, target_b, keep]
            + [jnp.zeros((LANES - KEEP_LANE - 1, TILE), F32)],
            axis=0,
        )
        cols_ref[at] = stack.T

    side_by_side(stages)


def post_call(
    local, group, me, mixed, tokens, weight, acat, bcat, gains, reader, mixer, prev, routes, slots
):
    tok_count, width = tokens.shape
    return pl.pallas_call(
        functools.partial(post_body, local, group),
        grid=(tok_count // STEP,),
        in_specs=[
            smem(), tall(width), tall(width), whole(weight.shape), whole(acat.shape),
            pl.BlockSpec((1, LANES, width), lambda i: (3, 0, 0)), whole(gains.shape),
            whole(reader.shape), whole(mixer.shape), wide(EXPERTS + 4), wide(2), wide(EXPERTS),
        ],
        out_specs=[tall(width), tall(width), tall(LANES), wide(16), tall(LANES)],
        out_shape=[
            shape_of(tok_count, width, dtype=F32), shape_of(tok_count, width),
            shape_of(tok_count, LANES), shape_of(16, tok_count, dtype=F32),
            shape_of(tok_count, LANES, dtype=F32),
        ],
        compiler_params=PARAMS,
        cost_estimate=cost(8),
        name="after_attention",
    )(me, mixed, tokens, weight, acat, bcat, gains, reader, mixer, prev, routes, slots)


def expert_body(
    local_index, pair, per_owner, group, steps, has_grad, *refs
):
    count = len(pair)
    piece_refs, refs = refs[:count], refs[count:]
    cot_refs, refs = refs[:count], refs[count:]
    dn_ref, ou_ref, wg_hbm, wu_hbm, wd_hbm, up_hbm, od_hbm = refs[:7]
    refs = refs[7:]
    if has_grad:
        before_hbm, refs = refs[0], refs[1:]
    back_refs, refs = refs[:count], refs[count:]
    out_refs, refs = refs[:count], refs[count:]
    (
        grad_ref, x_ref, g_ref, gate_ref, pick_ref, dr_ref, zg_ref, zu_ref, dzd_ref, zgt_ref, zut_ref,
        dzdt_ref, racc_ref, xacc_ref, zd_acc, dzg_acc, dzu_acc, h_ref, dg_ref, du_ref, wg_all, wu_all,
        wd_all, up_all, od_all, sems, *rest
    ) = refs
    rows, width = x_ref.shape
    compact = group * RANK
    tile = h_ref.shape[1]

    def copies(step):
        span = pl.ds(pl.multiple_of(step * tile, tile), tile)
        pairs = (
            (wg_hbm.at[local_index, :, span], wg_all),
            (wu_hbm.at[local_index, :, span], wu_all),
            (wd_hbm.at[local_index, span, :], wd_all),
            (up_hbm.at[local_index, :, :, span], up_all),
            (od_hbm.at[local_index, span, :], od_all),
        )
        return [
            pltpu.make_async_copy(source, target.at[step], sems.at[step, place])
            for place, (source, target) in enumerate(pairs)
        ]

    def begin(step):
        for copy in copies(step):
            copy.start()

    begin(0)

    def fold(value):
        place = iota((compact, LANES), 0)
        block = per_owner * group
        inner = place // block * per_owner + place % per_owner
        folded = mm_nt(hot(iota((compact, LANES), 1) % RANK == inner), value)
        place = iota((compact, rows), 0)
        owner = place % block // per_owner
        mine = iota((compact, rows), 1) // CAP + pair[0]
        return jnp.where(mine == owner, folded, 0.0).astype(BF)

    def put(start, value):
        grad_ref[:, pl.ds(start, value.shape[1])] = value.astype(BF)

    for index in range(count):
        span = slice(index * CAP, index * CAP + CAP)
        x_ref[span] = piece_refs[index][0:CAP]
        g_ref[span] = cot_refs[index][...]
        meta = piece_refs[index][CAP:PIECE].astype(F32)
        gate = (meta[0:1] + meta[1:2] + meta[2:3])[:, 0 : 2 * LANES]
        gate_ref[span] = jnp.broadcast_to(gate, (LANES, 2 * LANES)).T[0:CAP]
        lane = (iota((CAP, LANES), 1) // RANK).astype(F32)
        pick_ref[span] = jnp.where(lane == meta[3:4, 0:LANES], 1.0, 0.0)
    chosen = pick_ref[...] > 0.0
    dr = (gate_ref[:, 0:1] * g_ref[...].astype(F32)).astype(BF)
    dr_ref[...] = dr
    zg = jnp.where(chosen, mm(x_ref[...], dn_ref[0]), 0.0).astype(BF)
    zu = jnp.where(chosen, mm(x_ref[...], dn_ref[1]), 0.0).astype(BF)
    dzd = jnp.where(chosen, mm_nt(dr, ou_ref[...]), 0.0).astype(BF)
    zg_ref[...] = zg
    zu_ref[...] = zu
    dzd_ref[...] = dzd
    zgt_ref[...] = fold(zg)
    zut_ref[...] = fold(zu)
    dzdt_ref[...] = fold(dzd)
    for ref in (racc_ref, xacc_ref, zd_acc, dzg_acc, dzu_acc):
        ref[...] = jnp.zeros_like(ref)

    total = steps * tile
    begin(1)
    if has_grad:
        before = pltpu.make_async_copy(before_hbm, rest[0], rest[1])
        before.start()

    def run(step, carry):
        for copy in copies(step):
            copy.wait()

        @pl.when(step + 2 < steps)
        def _():
            begin(step + 2)

        wg_ref, wu_ref, wd_ref = wg_all.at[step], wu_all.at[step], wd_all.at[step]
        up_ref, od_ref = up_all.at[step], od_all.at[step]
        gate = mm(x_ref[...], wg_ref[...]) + mm(zg_ref[...], up_ref[0])
        upper = mm(x_ref[...], wu_ref[...]) + mm(zu_ref[...], up_ref[1])
        share = 0.5 * jnp.tanh(0.5 * gate) + 0.5
        silu = gate * share
        active = (silu * upper).astype(BF)
        h_ref[...] = active
        back = mm_nt(dr_ref[...], wd_ref[...]) + mm_nt(dzd_ref[...], od_ref[...])
        du = (back * silu).astype(BF)
        dg = (back * upper * (share + silu * (1.0 - share))).astype(BF)
        du_ref[...] = du
        dg_ref[...] = dg
        racc_ref[...] += mm(active, wd_ref[...])
        zd_acc[...] += mm(active, od_ref[...])
        xacc_ref[...] += mm_nt(dg, wg_ref[...]) + mm_nt(du, wu_ref[...])
        dzg_acc[...] += mm_nt(dg, up_ref[0])
        dzu_acc[...] += mm_nt(du, up_ref[1])
        at = pl.multiple_of(step * tile, tile)
        put(at, mm(zgt_ref[...], dg_ref[...]))
        put(total + at, mm(zut_ref[...], du_ref[...]))
        put(2 * total + at, mm(dzdt_ref[...], h_ref[...]))
        return carry

    lax.fori_loop(0, steps, run, 0)
    chosen = pick_ref[...] > 0.0
    zd = jnp.where(chosen, zd_acc[...], 0.0).astype(BF)
    dzg = jnp.where(chosen, dzg_acc[...], 0.0).astype(BF)
    dzu = jnp.where(chosen, dzu_acc[...], 0.0).astype(BF)
    result = racc_ref[...] + mm(zd, ou_ref[...])
    gated = (gate_ref[:, 0:1] * result).astype(BF)
    product = g_ref[...].astype(F32) * result.astype(BF).astype(F32)
    dots = jnp.broadcast_to(jnp.sum(product, axis=-1, keepdims=True), (rows, LANES))
    back_rows = (xacc_ref[...] + mm_nt(dzg, dn_ref[0]) + mm_nt(dzu, dn_ref[1])).astype(BF)
    for index in range(count):
        span = slice(index * CAP, index * CAP + CAP)
        out_refs[index][...] = gated[span]
        back_refs[index][0:CAP, :] = back_rows[span]
        column = jnp.concatenate(
            [dots[span], jnp.zeros((2 * LANES - CAP, LANES), F32)], axis=0
        ).T[0:1]
        meta = jnp.concatenate(
            [piece.astype(F32) for piece in split3(column)]
            + [jnp.zeros((META - 3, 2 * LANES), F32)],
            axis=0,
        )
        meta = jnp.concatenate([meta, jnp.zeros((META, width - 2 * LANES), F32)], axis=1)
        back_refs[index][CAP:PIECE, :] = meta.astype(BF)
    base = 3 * total
    place = iota((compact, LANES), 0)
    owner = place % (per_owner * group) // per_owner
    ids = jnp.zeros((compact, LANES), F32)
    for index in range(count):
        meta = piece_refs[index][CAP:PIECE, 0:LANES].astype(F32)
        ids = jnp.where(owner == pair[index], meta[3:4], ids)
    put(base + 3 * width, ids)
    put(base, mm(fold(zd), dr_ref[...]))
    put(base + width, mm(fold(dzg), x_ref[...]))
    put(base + 2 * width, mm(fold(dzu), x_ref[...]))
    if has_grad:
        before.wait()
        grad_ref[...] = grad_ref[...] + rest[0][...]


def expert_call(index, pair, group, per_owner, pieces, cots, before, weights):
    gate_w, up_w, down_w, in_down, in_up, out_down, out_up = weights
    width, hidden = gate_w.shape[1:]
    rows = len(pair) * CAP
    steps = hidden // FTILE
    columns = 3 * hidden + 3 * width + LANES
    compact = group * RANK
    has_grad = before is not None
    return pl.pallas_call(
        functools.partial(expert_body, index, pair, per_owner, group, steps, has_grad),
        grid=(1,),
        in_specs=[
            pl.BlockSpec((PIECE, width), lambda f, row=piece.shape[0] // PIECE > 1: (index * row, 0))
            for piece in pieces
        ]
        + [pl.BlockSpec((CAP, width), lambda f: (index, 0))] * len(pair)
        + [
            pl.BlockSpec((None, 2, width, LANES), lambda f: (index, 0, 0, 0)),
            pl.BlockSpec((None, LANES, width), lambda f: (index, 0, 0)),
        ]
        + [pl.BlockSpec(memory_space=pl.ANY)] * 5
        + [pl.BlockSpec(memory_space=pl.ANY)] * has_grad,
        out_specs=[whole((PIECE, width))] * len(pair)
        + [whole((CAP, width))] * len(pair)
        + [whole((compact, columns))],
        out_shape=[shape_of(PIECE, width)] * len(pair)
        + [shape_of(CAP, width)] * len(pair)
        + [shape_of(compact, columns)],
        scratch_shapes=[pltpu.VMEM((rows, width), BF)] * 2
        + [pltpu.VMEM((rows, LANES), F32)] * 2
        + [pltpu.VMEM((rows, width), BF)]
        + [pltpu.VMEM((rows, LANES), BF)] * 3
        + [pltpu.VMEM((compact, rows), BF)] * 3
        + [pltpu.VMEM((rows, width), F32)] * 2
        + [pltpu.VMEM((rows, LANES), F32)] * 3
        + [pltpu.VMEM((rows, FTILE), BF)] * 3
        + [pltpu.VMEM((steps, width, FTILE), BF)] * 2
        + [
            pltpu.VMEM((steps, FTILE, width), BF), pltpu.VMEM((steps, 2, LANES, FTILE), BF),
            pltpu.VMEM((steps, FTILE, LANES), BF), pltpu.SemaphoreType.DMA((steps, 5)),
        ]
        + [pltpu.VMEM((compact, columns), BF), pltpu.SemaphoreType.DMA] * has_grad,
        compiler_params=PARAMS,
        cost_estimate=cost(rows / 21),
        name="expert_layer",
    )(
        *pieces, *cots, in_down, out_up, gate_w, up_w, down_w, in_up, out_down,
        *([before] if has_grad else []),
    )


def spread(cols, index, count):
    return iota((TILE, count), 1).astype(F32) == cols[:, index : index + 1]


def combine_body(
    pieces, len_ref, *refs
):
    back_refs = refs[:pieces]
    (
        routes_ref, data_ref, cols_ref, cot_ref, ei_ref, hidden_ref, gain_ref, wo_ref, acat_ref, bcat_ref,
        table_ref, read_ref, bh_ref, ba_ref, din_ref, bm_ref, back_all, dots_ref,
    ) = refs[pieces:]
    count = pieces * CAP

    @pl.when(pl.program_id(0) == 0)
    def _():
        for index, back_ref in enumerate(back_refs):
            back_all[index * CAP : index * CAP + CAP, :] = back_ref[0:CAP, :]
        dots = [back_ref[CAP:PIECE, 0:CAP].astype(F32) for back_ref in back_refs]
        dots = jnp.concatenate(dots, axis=1)
        dots_ref[...] = jnp.concatenate([dots, jnp.zeros_like(dots)], axis=0).astype(BF)

    table_high, table_low = split2(table_ref[...])
    stack = dots_ref[...]
    vectors = read_ref[READ_VECTOR:READ_ROWS].astype(BF)

    def stages(at):
        start = pl.program_id(0) * STEP + at.start
        cols = cols_ref[at]
        chosen_a = hot(spread(cols, TARGET_LANE, count))
        chosen_b = hot(spread(cols, TARGET_LANE + 1, count))
        yield
        routed_a = jnp.sum(mm_nt(stack, chosen_a)[0:8], axis=0, keepdims=True)
        routed_b = jnp.sum(mm_nt(stack, chosen_b)[0:8], axis=0, keepdims=True)
        cot = cot_ref[at]
        cot_f = cot.astype(F32)
        yield
        along_x = jnp.sum(cot_f * ei_ref[at].astype(F32), axis=-1, keepdims=True)
        along_x = jnp.broadcast_to(along_x, (TILE, LANES)).T[0:1]
        yield
        along_c = mm_nt(vectors, cot)
        along_a = along_c[0:1] + along_c[2:3] + along_c[4:5]
        along_b = along_c[1:2] + along_c[3:4] + along_c[5:6]
        yield
        both = chosen_a + chosen_b
        half = count // 2
        back = mm(both[:, :half], back_all[:half]) + mm(both[:, half:], back_all[half:])
        yield
        first, second = routes_ref[0:1, at].astype(F32), routes_ref[1:2, at].astype(F32)
        token = iota((1, TILE), 1) + start
        valid = jnp.where(token < len_ref[0], 1.0, 0.0)
        gate_a, gate_b = data_ref[8:9, at], data_ref[9:10, at]
        share = [data_ref[index : index + 1, at] for index in range(10, 14)]
        beta_a, beta_b = data_ref[14:15, at], data_ref[15:16, at]
        const_a = share[0] * along_x + share[1] * along_a
        const_b = share[2] * along_x + share[3] * along_b

        def here(route):
            return (
                jnp.where(route == EXPERTS + 1.0, along_x, 0.0)
                + jnp.where(route == EXPERTS + 2.0, const_a, 0.0)
                + jnp.where(route == EXPERTS + 3.0, const_b, 0.0)
            )

        dot_a, dot_b = routed_a + here(first), routed_b + here(second)
        mean = gate_a * dot_a + gate_b * dot_b
        chosen_grad_a = valid * gate_a * (dot_a - mean)
        chosen_grad_b = valid * gate_b * (dot_b - mean)
        number = iota((16, TILE), 0).astype(F32)
        logit_grads = jnp.where(number == first, chosen_grad_a, 0.0) + jnp.where(
            number == second, chosen_grad_b, 0.0
        )
        mixes = []
        for index, (beta, along) in enumerate(((beta_a, along_a), (beta_b, along_b))):
            left, right = share[2 * index], share[2 * index + 1]
            weighted = left * along_x + right * along
            mixes += [
                valid * beta * left * (along_x - weighted),
                valid * beta * right * (along - weighted),
            ]
        small = jnp.concatenate(
            [logit_grads] + mixes + [jnp.zeros((LANES - 20, TILE), F32)], axis=0
        ).T
        high, low = split2(small)
        yield
        inside = iota((TILE, 1), 0) + start < len_ref[0]
        grad = jnp.where(inside, cot_f, 0.0)
        back = back + mm(high, table_high) + mm(low, table_high) + mm(high, table_low)
        back = back + cols[:, KEEP_LANE : KEEP_LANE + 1] * grad
        yield
        hidden = hidden_ref[at]
        scale = lax.rsqrt(jnp.mean(hidden * hidden, axis=-1, keepdims=True) + EPSILON)
        normed = hidden * scale
        back = back * gain_ref[1:2, :]
        back = grad + scale * (back - normed * jnp.mean(back * normed, axis=-1, keepdims=True))
        bh_ref[at] = back
        rounded = back.astype(BF)
        ba_ref[at] = rounded
        yield
        inner = mm_nt(rounded, bcat_ref[0]).astype(BF)
        din_ref[at] = inner
        yield
        bm_ref[at] = (mm_nt(rounded, wo_ref[...]) + mm_nt(inner, acat_ref[...])).astype(BF)

    side_by_side(stages)


def combine_call(
    length, backs, routes, data, cols, cotangent, ei, hidden, gains, weight, acat, bcat, table,
    reader,
):
    tok_count, width = cotangent.shape
    pieces = len(backs)
    return pl.pallas_call(
        functools.partial(combine_body, pieces),
        grid=(tok_count // STEP,),
        in_specs=[smem()] + [whole(back.shape) for back in backs] + [
            wide(2), wide(16), tall(LANES), tall(width), tall(width), tall(width),
            whole(gains.shape), whole(weight.shape), whole(acat.shape),
            pl.BlockSpec((1, LANES, width), lambda i: (3, 0, 0)), whole(table.shape),
            whole(reader.shape),
        ],
        out_specs=[tall(width), tall(width), tall(LANES), tall(width)],
        out_shape=[
            shape_of(tok_count, width, dtype=F32), shape_of(tok_count, width),
            shape_of(tok_count, LANES), shape_of(tok_count, width),
        ],
        scratch_shapes=[
            pltpu.VMEM((pieces * CAP, width), BF), pltpu.VMEM((2 * META, pieces * CAP), BF)
        ],
        compiler_params=PARAMS,
        cost_estimate=cost(17),
        name="combine_backward",
    )(
        length, *backs, routes, data, cols, cotangent, ei, hidden, gains, weight, acat, bcat, table,
        reader,
    )


def result_body(pieces, len_ref, *refs):
    result_refs = refs[:pieces]
    cols_ref, ei_ref, hidden_ref, table_ref, out_ref, result_all = refs[pieces:]
    count = pieces * CAP

    @pl.when(pl.program_id(0) == 0)
    def _():
        for index, result_ref in enumerate(result_refs):
            result_all[index * CAP : index * CAP + CAP, :] = result_ref[...]

    table_high, table_low = split2(table_ref[...])

    def stages(at):
        cols = cols_ref[at]
        both = hot(spread(cols, TARGET_LANE, count) | spread(cols, TARGET_LANE + 1, count))
        yield
        half = count // 2
        mixture = mm(both[:, :half], result_all[:half]) + mm(both[:, half:], result_all[half:])
        yield
        high, low = split2(cols)
        mixture = mixture + mm(high, table_high) + mm(low, table_high) + mm(high, table_low)
        mixture = mixture + cols[:, KEEP_LANE : KEEP_LANE + 1] * ei_ref[at].astype(F32)
        yield
        inside = iota((TILE, 1), 0) + pl.program_id(0) * STEP + at.start < len_ref[0]
        out_ref[at] = (hidden_ref[at] + jnp.where(inside, mixture, 0.0)).astype(BF)

    side_by_side(stages)


def result_call(length, results, cols, ei, hidden, table):
    tok_count, width = ei.shape
    pieces = len(results)
    return pl.pallas_call(
        functools.partial(result_body, pieces),
        grid=(tok_count // STEP,),
        in_specs=[smem()] + [whole(result.shape) for result in results] + [
            tall(LANES), tall(width), tall(width), whole(table.shape),
        ],
        out_specs=tall(width),
        out_shape=shape_of(tok_count, width),
        scratch_shapes=[pltpu.VMEM((pieces * CAP, width), BF)],
        compiler_params=PARAMS,
        cost_estimate=cost(8),
        name="layer_output",
    )(length, *results, cols, ei, hidden, table)


def adapter_body(
    packed, id_ref, dq_ref, dk_ref, dv_ref, bcat_ref, normed_ref, inner_ref, mixed_ref, inner_o_ref,
    ba_ref, din_ref, back_ref, grad_ref, acc_ref,
):
    step = pl.program_id(0)
    width = dq_ref.shape[1]
    count = 4 * RANK

    @pl.when(step == 0)
    def _():
        acc_ref[...] = jnp.zeros_like(acc_ref)

    inner_t = inner_ref[...].astype(F32).T[0:count].astype(BF)
    outer_t = inner_o_ref[...].astype(F32).T[0:count].astype(BF)
    number = iota((count, width), 0) % 4
    back_inner = din_ref[...].astype(F32)
    values = [ref[...] for ref in (dq_ref, dk_ref, dv_ref)]
    for index, value in enumerate(values):
        back_inner = back_inner + mm_nt(value, bcat_ref[index]).astype(BF).astype(F32)
    upper = mm(outer_t, ba_ref[...])
    for index, value in enumerate(values):
        upper = jnp.where(number == index, mm(inner_t, value), upper)
    own = iota(back_inner.shape, 1) % 4 < 3
    back_ref[...] = jnp.where(own, back_inner, 0.0).astype(BF)
    back_t = back_inner.T[0:count].astype(BF)
    down = jnp.where(number < 3, mm(back_t, normed_ref[...]), mm(back_t, mixed_ref[...]))
    acc_ref[:, 0:width] += down
    acc_ref[:, width:] += upper

    @pl.when(step == pl.num_programs(0) - 1)
    def _():
        if not packed:
            grad_ref[...] = acc_ref[...].astype(BF)
            return
        half = width // 2
        shape = (16 * RANK, count)
        place, row = iota(shape, 0), iota(shape, 1)
        total = None
        for index in range(4):
            kind, part = index // 2, index % 2
            here = (place % 4 == row % 4) & (place // 16 == row // 4)
            here = here & (place // 8 % 2 == part) & (place // 4 % 2 == kind)
            start = kind * width + part * half
            piece = mm(hot(here), acc_ref[:, start : start + half].astype(BF))
            total = piece if total is None else total + piece
        grad_ref[:, 0:half] = total.astype(BF)
        grad_ref[:, half:] = jnp.full((16 * RANK, LANES), id_ref[0].astype(F32), F32).astype(BF)


def adapter_call(
    packed, ids, dq, dk, dv, bcat, normed, inner, mixed, inner_o, ba, din
):
    tok_count, width = dq.shape
    grad_shape = (16 * RANK, width // 2 + LANES) if packed else (4 * RANK, 2 * width)
    return pl.pallas_call(
        functools.partial(adapter_body, packed),
        grid=(tok_count // TILE,),
        in_specs=[
            smem(), tile(width), tile(width), tile(width), whole(bcat.shape), tile(width), tile(LANES),
            tile(width), tile(LANES), tile(width), tile(LANES),
        ],
        out_specs=[tile(LANES), whole(grad_shape)],
        out_shape=[shape_of(tok_count, LANES), shape_of(*grad_shape)],
        scratch_shapes=[pltpu.VMEM((4 * RANK, 2 * width), F32)],
        compiler_params=PARAMS,
        cost_estimate=cost(6),
        name="adapter_gradients",
    )(ids, dq, dk, dv, bcat, normed, inner, mixed, inner_o, ba, din)


def last_body(
    dq_ref, dk_ref, dv_ref, w_ref, acat_ref, back_ref, x_ref, bh_ref, gain_ref, out_ref
):
    def stages(at):
        parts = [mm_nt(back_ref[at], acat_ref[...])]
        for index, ref in enumerate((dq_ref, dk_ref, dv_ref)):
            parts.append(mm_nt(ref[at], w_ref[index]))
            yield
        total = parts[0] + parts[1] + parts[2] + parts[3]
        x = x_ref[at].astype(F32)
        scale = lax.rsqrt(jnp.mean(x * x, axis=-1, keepdims=True) + EPSILON)
        normed = x * scale
        back = total * gain_ref[0:1, :]
        back = scale * (back - normed * jnp.mean(back * normed, axis=-1, keepdims=True))
        out_ref[at] = (bh_ref[at] + back).astype(BF)

    side_by_side(stages)


def last_call(dq, dk, dv, weights, acat, back, tokens, bh, gains):
    tok_count, width = tokens.shape
    return pl.pallas_call(
        last_body,
        grid=(tok_count // STEP,),
        in_specs=[
            tall(width), tall(width), tall(width), whole(weights.shape), whole(acat.shape),
            tall(LANES), tall(width), tall(width), whole(gains.shape),
        ],
        out_specs=tall(width),
        out_shape=shape_of(tok_count, width),
        compiler_params=PARAMS,
        cost_estimate=cost(9),
        name="after_attention_backward",
    )(dq, dk, dv, weights, acat, back, tokens, bh, gains)


def exchange(value, axes):
    return lax.all_to_all(value, axes, split_axis=0, concat_axis=0, tiled=True)


def gather_all(value, axes, count):
    return exchange(jnp.broadcast_to(value[None], (count,) + value.shape), axes)


def swap(value, partner, group):
    if partner == 0:
        return value
    return lax.ppermute(value, "expert", [(index, index ^ partner) for index in range(group)])


def find_adapters(id_rows):
    count = id_rows.shape[0]
    padded = id_rows.astype(F32)
    if count % LANES:
        padded = jnp.concatenate([padded, jnp.zeros((-count % LANES, LANES), F32)], axis=0)
    return padded.T[0:1, 0:count].astype(jnp.int32)


def sum_expert_body(each, adapters, in_ref, out_ref):
    count, columns = in_ref.shape[0], out_ref.shape[1]
    found = find_adapters(in_ref[:, columns:])
    place = iota((adapters * each, count), 0)
    column = iota((adapters * each, count), 1)
    pick = hot((place // each == found) & (place % each == column % each))
    out_ref[...] = mm(pick, in_ref[:, 0:columns]).astype(BF)


def exchange_expert_grads(grads, group, owners):
    split = min(RANK, owners)
    each, parts = RANK // split, owners // split
    columns = (grads.shape[1] - LANES) // parts
    pieces = grads.reshape(split, each * group, grads.shape[1])
    if parts > 1:
        ids = jnp.broadcast_to(pieces[:, None, :, parts * columns :], (split, parts, each * group, LANES))
        pieces = pieces[:, :, : parts * columns].reshape(split, each * group, parts, columns)
        pieces = jnp.concatenate([pieces.transpose(0, 2, 1, 3), ids], axis=-1)
        pieces = pieces.reshape(owners, each * group, columns + LANES)
    return exchange(pieces, "dp").reshape(owners * group * each, columns + LANES)


def sum_expert_grads(got, adapters, owners):
    columns = got.shape[1] - LANES
    each = RANK // min(RANK, owners)
    return pl.pallas_call(
        functools.partial(sum_expert_body, each, adapters),
        out_shape=shape_of(adapters * each, columns),
        compiler_params=PARAMS,
        cost_estimate=cost(2.2),
        name="expert_gradient_part",
    )(got)


def finish_expert_body(split, adapters, hidden, in_ref, *refs):
    down_ref, up_ref, out_down_ref, out_up_ref = refs[-4:]
    each = RANK // split
    rows = adapters * each
    count = split * rows
    width = out_up_ref.shape[1]

    def place(value):
        return value // each % adapters * RANK + value // (adapters * each) * each + value % each

    move = hot(iota((count, count), 0) == place(iota((count, count), 1)))
    back = hot(iota((count, count), 1) == place(iota((count, count), 0)))

    def part(start, size):
        span = slice(start, start + size)
        rows_of = [in_ref[owner, :, span] for owner in range(split)]
        return jnp.concatenate(rows_of, axis=0)

    for index in range(2):
        up_ref[index] = mm(move, part(index * hidden, hidden))
    out_down_ref[...] = mm_tn(part(2 * hidden, hidden), back)
    base = 3 * hidden
    out_up_ref[...] = mm(move, part(base, width))
    for index in range(2):
        base += width
        down_ref[index] = mm_tn(part(base, width), back)


def finish_expert_call(index, local, everything, outs, adapters, width, hidden):
    owners, rows, columns = everything.shape
    total = adapters * RANK
    shapes = [(local, 2, width, total), (local, 2, total, hidden), (local, hidden, total),
              (local, total, width)]
    specs = [
        pl.BlockSpec((None,) + shape[1:], lambda *_, rank=len(shape): (index,) + (0,) * (rank - 1))
        for shape in shapes
    ]
    return pl.pallas_call(
        functools.partial(finish_expert_body, owners, adapters, hidden),
        grid=(1,),
        in_specs=[whole(everything.shape)] + [pl.BlockSpec(memory_space=pl.ANY)] * len(outs),
        out_specs=specs,
        out_shape=[shape_of(*shape, dtype=F32) for shape in shapes],
        input_output_aliases={1 + place: place for place in range(len(outs))},
        compiler_params=PARAMS,
        cost_estimate=cost(4),
        name="expert_gradient_sums",
    )(everything, *outs)


def spread_expert_grads(own, adapters, owners):
    split = min(RANK, owners)
    each, parts = RANK // split, owners // split
    everything = gather_all(own, "dp", owners)
    everything = everything.reshape(split, parts, adapters, each, own.shape[1])
    everything = everything.transpose(2, 0, 3, 1, 4)
    return everything.reshape(adapters * RANK, parts * own.shape[1]).astype(F32)


def expert_sums(owned, adapters, owners, width, hidden):
    sums = [spread_expert_grads(value, adapters, owners) for value in owned]
    base = 3 * hidden
    up = [[value[:, 0:hidden], value[:, hidden : 2 * hidden]] for value in sums]
    down = [
        [value[:, base + width * part : base + width * (part + 1)].T for part in (1, 2)]
        for value in sums
    ]
    return (
        jnp.stack([jnp.stack(value) for value in down]),
        jnp.stack([jnp.stack(value) for value in up]),
        jnp.stack([value[:, 2 * hidden : base].T for value in sums]),
        jnp.stack([value[:, base : base + width] for value in sums]),
    )


def finish_adapter_body(adapters, me_ref, *refs):
    piece_refs, (down_ref, up_ref, in_ref) = refs[:-3], refs[-3:]
    half = in_ref.shape[3]
    owners, group = piece_refs[0].shape[0], len(piece_refs)
    for other in range(group):
        place = jnp.bitwise_xor(me_ref[0], other)
        for owner in range(owners):
            in_ref[owner * (group // 2) + place // 2, place % 2] = piece_refs[other][owner]
    count = RANK * adapters

    def place(value):
        return value % adapters * RANK + value // adapters

    move = hot(iota((count, count), 0) == place(iota((count, count), 1)))
    back = hot(iota((count, count), 1) == place(iota((count, count), 0)))
    for part in range(2):
        span = slice(part * half, part * half + half)
        for kind in range(2):
            for index in range(4):
                first = (kind * 4 + index) * adapters
                rows = in_ref[:, part, first : first + adapters, :].astype(F32)
                rows = rows.reshape(count, half).astype(BF)
                if kind == 0:
                    down_ref[index, span, :] = mm_tn(rows, back)
                else:
                    up_ref[index, :, span] = mm(move, rows)


def sum_adapter_body(kinds, adapters, in_ref, out_ref):
    count, columns = in_ref.shape[0], out_ref.shape[-1]
    found = find_adapters(in_ref[:, columns:])
    place = iota((adapters * kinds, count), 0)
    column = iota((adapters * kinds, count), 1)
    pick = hot((place % adapters == found) & (place // adapters == column % kinds))
    own = mm(pick, in_ref[:, 0:columns]).astype(BF)
    for index in range(out_ref.shape[0]):
        out_ref[index] = own


def adapter_sums(grads, meanwhile, later, ids, adapters, owners, group, width):
    axes, everyone = ("dp", "expert"), owners * group
    if everyone == 2 * RANK and group == 4:
        kinds = 8
        got = exchange(grads.reshape(everyone, kinds, grads.shape[1]), axes)
        got, meanwhile = lax.optimization_barrier((got, meanwhile))
        own = pl.pallas_call(
            functools.partial(sum_adapter_body, kinds, adapters),
            out_shape=shape_of(owners, kinds * adapters, width // 2),
            compiler_params=PARAMS,
            cost_estimate=cost(2.0),
            name="adapter_gradient_part",
        )(got.reshape(everyone * kinds, grads.shape[1]))
        mine = exchange(own, "dp")
        mine, later = lax.optimization_barrier((mine, later))
        across = swap(mine, 2, group)
        full = [mine, swap(mine, 1, group), across, swap(across, 1, group)]
        total = adapters * RANK
        down, upper = pl.pallas_call(
            functools.partial(finish_adapter_body, adapters),
            in_specs=[smem()] + [pl.BlockSpec(memory_space=pltpu.VMEM)] * group,
            out_shape=[shape_of(4, width, total, dtype=F32), shape_of(4, total, width, dtype=F32)],
            scratch_shapes=[pltpu.VMEM((RANK, 2, kinds * adapters, width // 2), BF)],
            compiler_params=PARAMS,
            cost_estimate=cost(3.6),
            name="adapter_gradient_sums",
        )(lax.axis_index("expert").reshape(1).astype(jnp.int32), *full)
        return down, upper, meanwhile, later
    all_ids = exchange(jnp.broadcast_to(ids, (everyone,)), axes)
    pieces = grads.reshape(everyone, RANK * 4 * 2 * width // everyone)
    got = exchange(pieces, axes)
    pick = (jnp.arange(adapters, dtype=jnp.int32)[:, None] == all_ids[None, :]).astype(BF)
    own = jnp.dot(pick, got, preferred_element_type=F32).astype(BF)
    full = gather_all(own, axes, everyone)
    full = full.reshape(RANK, everyone // RANK, adapters, -1).transpose(2, 0, 1, 3)
    full = full.reshape(adapters * RANK, 4, 2, width).astype(F32)
    return full[:, :, 0].transpose(1, 2, 0), full[:, :, 1].transpose(1, 0, 2), meanwhile, later


def body(
    tokens,
    cotangent,
    lengths,
    adapter_ids,
    routes,
    prev_logits,
    norm_gains,
    input_weights,
    output_weight,
    adapter_down,
    adapter_up,
    router,
    residual_mix,
    constant_mix,
    constant_vectors,
    expert_gate,
    expert_up,
    expert_down,
    expert_adapter_down,
    expert_adapter_up,
    output_adapter_down,
    output_adapter_up,
):
    tok_count, width = tokens.shape
    hidden_width = expert_gate.shape[2]
    group, owners = lax.axis_size("expert"), lax.axis_size("dp")
    local = expert_gate.shape[0]
    adapters = adapter_down.shape[-1] // RANK
    angles = [jnp.asarray(table) for table in turn_tables(tok_count)]
    weights = (
        expert_gate, expert_up, expert_down, expert_adapter_down, expert_adapter_up,
        output_adapter_down, output_adapter_up,
    )
    per_owner = RANK // min(RANK, owners)
    everyone = owners * group
    me = lax.axis_index("expert")

    me = me.reshape(1).astype(jnp.int32)

    routes, prev_logits = routes.T, prev_logits.T
    slots, *grad_sends = route_call(local, group, lengths, me, routes, cotangent)
    cots = [swap(value, partner, group) for partner, value in enumerate(grad_sends)]
    normed, inner, queries, keys, values, acat, bcat, table, mixer, reader = pre_call(
        adapter_ids, tokens, norm_gains, input_weights, adapter_down, adapter_up, *angles, router.T,
        constant_mix.T, constant_vectors, residual_mix,
    )
    mixed, q2 = attend_call(lengths, queries, keys, values)
    mixed, cots = lax.optimization_barrier((mixed, cots))
    hidden, ei, inner_o, data, cols = post_call(
        local, group, me, mixed, tokens, output_weight, acat, bcat, norm_gains, reader, mixer, prev_logits,
        routes, slots,
    )
    sends = send_call(local, group, me, adapter_ids, slots, data, ei)
    near, far = tuple(range(group // 2)), tuple(range(group // 2, group))
    sent_near = [swap(sends[partner], partner, group) for partner in near]
    sent_far = []
    for index in range(local):
        pieces = [sends[group // 2 + place * local + index] for place in range(len(far))]
        if index > 0:
            pieces, sent_near = lax.optimization_barrier((pieces, sent_near))
        sent_far.append([swap(piece, partner, group) for piece, partner in zip(pieces, far)])
    backs = [[None] * group for _ in range(local)]
    results = [[None] * group for _ in range(local)]
    calls = []
    for index in range(local - 1):
        calls += [(index, near), (index, far)]
    calls += [(local - 1, near[1:] + far), (local - 1, near[:1])]
    grads, owned, parts = [None] * local, [], []
    sums = functools.partial(sum_expert_grads, adapters=adapters, owners=owners)
    last = None
    for index, some in calls:
        pieces = [
            sent_near[partner] if partner in near else sent_far[index][partner - len(near)]
            for partner in some
        ]
        if last is not None:
            pieces, last = lax.optimization_barrier((pieces, last))
        if (index, some) == calls[-1]:
            parts, last = lax.optimization_barrier((parts, last))
            owned = [sums(part) for part in parts]
            pieces, backs[:index], owned = lax.optimization_barrier((pieces, backs[:index], owned))
        outs = expert_call(
            index, some, group, per_owner, pieces, [cots[partner] for partner in some], grads[index], weights
        )
        grads[index] = last = outs[-1]
        for place, partner in enumerate(some):
            backs[index][partner] = swap(outs[place], partner, group)
            results[index][partner] = outs[len(some) + place]
        if index < local - 1 and some == far:
            parts.append(exchange_expert_grads(last, group, owners))
    backs = [value for some in backs for value in some]
    parts.append(exchange_expert_grads(last, group, owners))
    gather = functools.partial(lax.all_gather, axis_name="dp", axis=0, tiled=False)
    if owners <= RANK:
        owned = [gather(own) for own in owned]
    back_hidden, back_attention, back_inner_o, back_mixed = combine_call(
        lengths, backs, routes, data, cols, cotangent, ei, hidden, norm_gains, output_weight, acat, bcat,
        table, reader,
    )
    flat = [value for some in results for value in some]
    flat, back_mixed = lax.optimization_barrier((flat, back_mixed))
    flat = [swap(value, place % group, group) for place, value in enumerate(flat)]

    dq, dk, dv = attend_back_call(lengths, q2, keys, values, mixed, back_mixed, *angles)
    parts[-1], dq, flat, owned = lax.optimization_barrier((parts[-1], dq, flat, owned))
    own = sums(parts[-1])
    dq, own, flat = lax.optimization_barrier((dq, own, flat))
    owned.append(gather(own) if owners <= RANK else own)
    back_inner, adapter_grads = adapter_call(
        everyone == 2 * RANK and group == 4, adapter_ids, dq, dk, dv, bcat, normed, inner, mixed,
        inner_o, back_attention, back_inner_o,
    )
    (dq, dk, dv, flat, owned[:-1]), adapter_grads = lax.optimization_barrier(
        ((dq, dk, dv, flat, owned[:-1]), adapter_grads)
    )
    layer_out = result_call(lengths, flat, cols, ei, hidden, table)
    input_back = last_call(
        dq, dk, dv, input_weights, acat, back_inner, tokens, back_hidden, norm_gains
    )
    outs = []
    if owners <= RANK:
        for index, own in enumerate(owned[:-1]):
            outs = finish_expert_call(index, local, own, outs, adapters, width, hidden_width)
    down_sum, upper_sum, layer_out, (input_back, outs) = adapter_sums(
        adapter_grads, layer_out, (input_back, outs), adapter_ids, adapters, owners, group, width
    )
    if owners <= RANK:
        outs = finish_expert_call(
            local - 1, local, owned[-1], outs, adapters, width, hidden_width
        )
    else:
        outs = expert_sums(owned, adapters, owners, width, hidden_width)
    in_down_sum, in_up_sum, out_down_sum, out_up_sum = outs
    return (
        layer_out,
        input_back,
        down_sum,
        upper_sum,
        in_down_sum,
        in_up_sum,
        out_down_sum,
        out_up_sum,
    )


def solution(mesh):
    tokens_spec, copied = P(("dp", "expert"), None), P()
    owned = P("expert")
    placed = (
        (tokens_spec, tokens_spec, P(("dp", "expert")), P(("dp", "expert")), tokens_spec, tokens_spec)
        + (copied,) * 9
        + (owned,) * 7
    )
    return jax.shard_map(
        body,
        mesh=mesh,
        in_specs=placed,
        out_specs=(tokens_spec, tokens_spec, copied, copied) + (owned,) * 4,
        check_vma=False,
    )
```

```python
import functools
import math

import jax
import jax.numpy as jnp
import numpy as np
from jax import lax
from jax.experimental import pallas as pl
from jax.experimental.pallas import tpu as pltpu
from jax.sharding import PartitionSpec as P

HEADS = 12
HD = 64
EXPERTS = 8
RANK = 16
CAP = 192
EPSILON = 1e-06
F32 = jnp.float32
BF = jnp.bfloat16
NEG = -1e30
LANES = 128
TILE = 256
STEP = 512
FTILE = 512
PAIRS = HEADS // 2
PARAMS = pltpu.CompilerParams(vmem_limit_bytes=67043328)
META = 8
MIX_ROW = 16
VECTOR_ROW = 20
TARGET_LANE = 24
KEEP_LANE = 26
READ_VECTOR = 48
READ_ROWS = 64
PIECE = CAP + META


def mm(left, right):
    return jnp.dot(left, right, preferred_element_type=F32)


def mm_nt(left, right):
    return lax.dot_general(left, right, (((1,), (1,)), ((), ())), preferred_element_type=F32)


def mm_tn(left, right):
    return lax.dot_general(left, right, (((0,), (0,)), ((), ())), preferred_element_type=F32)


def iota(shape, axis):
    return lax.broadcasted_iota(jnp.int32, shape, axis)


def hot(condition):
    return jnp.where(condition, 1.0, 0.0).astype(BF)


def split2(value):
    high = value.astype(BF)
    return high, (value - high.astype(F32)).astype(BF)


def split3(value):
    high = value.astype(BF)
    rest = value - high.astype(F32)
    middle = rest.astype(BF)
    return high, middle, (rest - middle.astype(F32)).astype(BF)


def whole(shape):
    zeros = (0,) * len(shape)
    return pl.BlockSpec(shape, lambda *_: zeros)


def smem():
    return pl.BlockSpec(memory_space=pltpu.SMEM)


def tall(width):
    return pl.BlockSpec((STEP, width), lambda i: (i, 0))


def wide(height):
    return pl.BlockSpec((height, STEP), lambda i: (0, i))


def tile(width):
    return pl.BlockSpec((TILE, width), lambda i: (i, 0))


def side_by_side(stages):
    running = [stages(slice(start, start + TILE)) for start in range(0, STEP, TILE)]
    while running:
        running = [stage for stage in running if next(stage, True) is None]


def shape_of(*shape, dtype=BF):
    return jax.ShapeDtypeStruct(shape, dtype)


def cost(microseconds):
    return pl.CostEstimate(flops=int(microseconds * 1e+09), bytes_accessed=0, transcendentals=0)


@functools.lru_cache(maxsize=None)
def turn_tables(length_in):
    half = HD // 2
    inverse = np.exp(np.arange(half, dtype=np.float64) * (-2.0 * math.log(10000.0) / HD))

    def table(positions):
        angles = np.tile(positions[:, None] * inverse[None, :], (1, 4))
        return np.stack([np.cos(angles), np.sin(angles)]).astype(np.float32)

    return table(np.arange(0.0, length_in, 32)), table(np.arange(0.0, 32))


def turn_rows(coarse_ref, fine_ref, first, count):
    fine_cos, fine_sin = fine_ref[0], fine_ref[1]
    sign = jnp.where(iota((32, LANES), 1) % HD < HD // 2, -1.0, 1.0)
    signed_cos, signed_sin = fine_cos * sign, fine_sin * sign
    cosines, sines = [], []
    for index in range(count // 32):
        row = first // 32 + index
        coarse_cos, coarse_sin = coarse_ref[0, pl.ds(row, 1), :], coarse_ref[1, pl.ds(row, 1), :]
        cosines.append(coarse_cos * fine_cos - coarse_sin * fine_sin)
        sines.append(coarse_sin * signed_cos + coarse_cos * signed_sin)
    return jnp.concatenate(cosines, axis=0), jnp.concatenate(sines, axis=0)


def rope(value, cosine, sine):
    first = iota(value.shape, 1) % HD < HD // 2
    turned = jnp.where(first, pltpu.roll(value, LANES - HD // 2, 1), pltpu.roll(value, HD // 2, 1))
    return value * cosine + turned * sine


def find_slots(length, routes_ref, slot_ref):
    tok_count = slot_ref.shape[1]
    before = hot(iota((TILE, TILE), 0) < iota((TILE, TILE), 1))
    carry = jnp.zeros((2 * EXPERTS, 1), F32)
    for start in range(0, tok_count, TILE):
        span = slice(start, start + TILE)
        expert = iota((2 * EXPERTS, TILE), 0)
        token = iota((2 * EXPERTS, TILE), 1) + start
        named = (routes_ref[0:1, span] == expert) | (routes_ref[1:2, span] == expert)
        hit = named & (token < length) & (expert < EXPERTS)
        hits = jnp.where(hit, 1.0, 0.0)
        slots = mm(hits.astype(BF), before) + carry
        carry = carry + jnp.sum(hits, axis=1, keepdims=True)
        slot_ref[:, span] = jnp.where(hit, slots, -1.0)[:EXPERTS].astype(jnp.int32)


def pick_rows(slot_ref, step, me, local):
    first = jnp.bitwise_xor(step, me) * local
    place = iota((CAP, slot_ref.shape[1]), 0)
    return first, [hot(place == slot_ref[pl.ds(first + index, 1), :]) for index in range(local)]


def pick_source(chosen, source_ref):
    half = source_ref.shape[0] // 2
    return mm(chosen[:, :half], source_ref[:half]) + mm(chosen[:, half:], source_ref[half:])


def store_piece(out_refs, step, other, index, value, start):
    @pl.when(step == other)
    def _():
        out_refs[index][start : start + value.shape[0], :] = value


def route_body(local, group, len_ref, me_ref, routes_ref, source_ref, slot_ref, *out_refs):
    step = pl.program_id(0)

    @pl.when(step == 0)
    def _():
        find_slots(len_ref[0], routes_ref, slot_ref)

    _, chosen = pick_rows(slot_ref, step, me_ref[0], local)
    rows = pick_source(jnp.concatenate(chosen, axis=0), source_ref).astype(BF)
    for other in range(group):
        store_piece(out_refs, step, other, other, rows, 0)


def route_call(local, group, length, me, routes, source):
    tok_count, width = source.shape
    return pl.pallas_call(
        functools.partial(route_body, local, group),
        grid=(group,),
        in_specs=[smem(), smem(), whole(routes.shape), whole(source.shape)],
        out_specs=[whole((EXPERTS, tok_count))] + [whole((local * CAP, width))] * group,
        out_shape=[shape_of(EXPERTS, tok_count, dtype=jnp.int32)]
        + [shape_of(local * CAP, width)] * group,
        compiler_params=PARAMS,
        cost_estimate=cost(6.5),
        name="route_rows",
    )(length, me, routes, source)


def send_rows(local, group, partner, me_ref, id_ref, slot_ref, data_ref, source_ref, out_refs):
    width = source_ref.shape[1]
    first, chosen = pick_rows(slot_ref, partner, me_ref[0], local)
    rows = pick_source(jnp.concatenate(chosen, axis=0), source_ref).astype(BF)
    for index in range(local):
        pieces = split3(data_ref[pl.ds(first + index, 1), :])
        stack = jnp.concatenate(
            [piece.astype(F32) for piece in pieces]
            + [jnp.zeros((13, chosen[index].shape[1]), F32)],
            axis=0,
        ).astype(BF)
        gates = mm_nt(stack, chosen[index])[0:META]
        gates = jnp.where(iota(gates.shape, 0) == 3, id_ref[0].astype(F32), gates)
        meta = jnp.concatenate([gates, jnp.zeros((META, width - CAP), F32)], axis=1)
        kept = rows[index * CAP : index * CAP + CAP]
        for other in range(group):
            far = other >= group // 2
            place = group // 2 + (other - group // 2) * local + index if far else other
            start = 0 if far else index * PIECE
            store_piece(out_refs, partner, other, place, kept, start)
            store_piece(out_refs, partner, other, place, meta.astype(BF), start + CAP)


def pre_body(
    id_ref, x_ref, gain_ref, w_ref, ad_ref, au_ref, coarse_ref, fine_ref, router_ref, cmix_ref, vec_ref,
    resid_ref, normed_ref, inner_ref, acat_ref, bcat_ref, table_ref, mix_ref, read_ref, q_ref, k_ref,
    v_ref, square_ref,
):
    @pl.when(pl.program_id(0) == 0)
    def _():
        first = RANK * id_ref[0]
        total = None
        for index in range(4):
            row, column = iota((LANES, LANES), 0), iota((LANES, LANES), 1)
            place = hot((row >= first) & (row < first + RANK) & (column == (row - first) * 4 + index))
            part = mm(ad_ref[index], place)
            total = part if total is None else total + part
            place = hot(
                (column >= first) & (column < first + RANK) & (row == (column - first) * 4 + index)
            )
            bcat_ref[index] = mm(place, au_ref[index]).astype(BF)
        acat_ref[...] = total.astype(BF)
        table_ref[...] = jnp.zeros_like(table_ref)
        table_ref[0 : EXPERTS + 4, :] = router_ref[...].astype(F32)
        table_ref[MIX_ROW : MIX_ROW + 4, :] = cmix_ref[...]
        table_ref[VECTOR_ROW : VECTOR_ROW + 2, :] = vec_ref[...]
        read_ref[...] = jnp.zeros_like(read_ref)
        read_ref[0 : EXPERTS + 4, :] = router_ref[...].astype(F32)
        for place, piece in enumerate(split3(cmix_ref[...])):
            read_ref[16 + 8 * place : 20 + 8 * place, :] = piece.astype(F32)
        for place, piece in enumerate(split3(vec_ref[...])):
            read_ref[READ_VECTOR + 2 * place : READ_VECTOR + 2 * place + 2, :] = piece.astype(F32)
        square_ref[...] = jnp.zeros_like(square_ref)
        square_ref[0 : EXPERTS + 4, 0 : EXPERTS + 4] = resid_ref[...]
        mix_ref[...] = square_ref[...].T[0:16]

    def stages(at):
        x = x_ref[at].astype(F32)
        scale = lax.rsqrt(jnp.mean(x * x, axis=-1, keepdims=True) + EPSILON)
        normed = (x * scale * gain_ref[0:1, :]).astype(BF)
        normed_ref[at] = normed
        yield
        inner = mm(normed, acat_ref[...]).astype(BF)
        inner_ref[at] = inner
        yield
        for index, out_ref in enumerate((q_ref, k_ref, v_ref)):
            value = mm(normed, w_ref[index]) + mm(inner, bcat_ref[index])
            yield
            rows = pl.ds(pl.multiple_of(pl.program_id(0) * STEP + at.start, TILE), TILE)
            if index == 2:
                for pair in range(PAIRS):
                    span = slice(pair * LANES, pair * LANES + LANES)
                    out_ref[pair, rows] = value[:, span].astype(BF)
                continue
            cosine, sine = turn_rows(coarse_ref, fine_ref, pl.program_id(0) * STEP + at.start, TILE)
            for pair in range(PAIRS):
                span = slice(pair * LANES, pair * LANES + LANES)
                turned = rope(value[:, span], cosine, sine).astype(BF)
                if index == 0:
                    turned = (turned.astype(F32) * HD**-0.5).astype(BF)
                out_ref[pair, rows] = turned
            yield

    side_by_side(stages)


def attend_body(len_ref, q_ref, k_ref, v_ref, mixed_ref, q2_ref):
    tok_count = q_ref.shape[0]
    lane = iota((tok_count, LANES), 1)
    hidden_key = iota((tok_count, LANES), 0) >= len_ref[0]
    row = iota((LANES, tok_count), 0)
    row_tile = row[:, :TILE]
    causal = iota((TILE, TILE), 0) <= iota((TILE, TILE), 1)
    queries_t = q_ref[...].astype(F32).T
    values_t = v_ref[...].astype(F32).T
    keys = k_ref[...].astype(F32)
    heads = []
    for head in range(2):
        spare = HD * (1 - head)
        bias = jnp.where((lane == spare) & hidden_key, NEG, 0.0)
        one = jnp.where(row == spare, 1.0, 0.0)
        own = row // HD == head
        heads.append(
            (
                jnp.where(lane // HD == head, keys, bias).astype(BF),
                jnp.where(own, queries_t, one).astype(BF),
                jnp.where(own, values_t, one).astype(BF),
            )
        )
    units = [(start, head) for start in range(0, tok_count, TILE) for head in range(2)]

    def score(unit):
        start, head = unit
        keys, queries, _ = heads[head]
        part = queries[:, start : start + TILE]
        near = mm(keys[start : start + TILE], part)
        return near, mm(keys[:start], part) if start else None

    outs = {}
    waiting = score(units[0])
    for index, (start, head) in enumerate(units):
        near, far = waiting
        waiting = score(units[index + 1]) if index + 1 < len(units) else None
        spare = HD * (1 - head)
        _, queries, values = heads[head]
        near = jnp.where(causal, near, NEG)
        top = jnp.max(near, axis=0, keepdims=True)
        if start:
            top = jnp.maximum(top, jnp.max(far, axis=0, keepdims=True))
        mixed = mm(values[:, start : start + TILE], jnp.exp(near - top).astype(BF))
        if start:
            mixed = mixed + mm(values[:, :start], jnp.exp(far - top).astype(BF))
        total = mixed[spare : spare + 1]
        outs[head] = mixed * (1.0 / total)
        kept = queries[:, start : start + TILE]
        logs = jnp.zeros((LANES, TILE), F32)
        for offset, piece in enumerate(split3(top + jnp.log(total))):
            logs = jnp.where(row_tile == spare + 1 + offset, piece.astype(F32), logs)
        q2_ref[head * LANES : head * LANES + LANES, start : start + TILE] = kept + logs.astype(BF)
        if head == 1:
            mixed = jnp.where(row_tile < HD, outs[0], outs[1])
            mixed_ref[start : start + TILE] = mixed.T.astype(BF)


def pre_attend_body(steps, len_ref, *refs):
    pre_ins, pre_outs = refs[:12], refs[12:19]
    key_ref, value_ref, mixed_ref, q2_ref, q_all, k_all, v_all, square_ref = refs[19:]
    step = pl.program_id(0)

    @pl.when(step < steps)
    def _():
        pre_body(*pre_ins, *pre_outs, q_all, k_all, v_all, square_ref)

    @pl.when(step >= steps)
    def _():
        pair = step - steps
        key_ref[...] = k_all[pair]
        value_ref[...] = v_all[pair]
        attend_body(len_ref, q_all.at[pair], k_all.at[pair], v_all.at[pair], mixed_ref, q2_ref)


def pre_attend_call(
    length, ids, tokens, gains, weights, down, upper, coarse, fine, router, constant_mix, vectors,
    residual_mix,
):
    tok_count, width = tokens.shape
    steps = tok_count // STEP

    def rows_of(columns):
        return pl.BlockSpec((STEP, columns), lambda i: (jnp.minimum(i, steps - 1), 0))

    column = pl.BlockSpec((tok_count, LANES), lambda i: (0, jnp.maximum(i - steps, 0)))
    return pl.pallas_call(
        functools.partial(pre_attend_body, steps),
        grid=(steps + PAIRS,),
        in_specs=[
            smem(), smem(), rows_of(width), whole(gains.shape), whole(weights.shape), whole(down.shape),
            whole(upper.shape), whole(coarse.shape), whole(fine.shape), whole(router.shape),
            whole(constant_mix.shape), whole(vectors.shape), whole(residual_mix.shape),
        ],
        out_specs=[
            rows_of(width), rows_of(LANES), whole((width, LANES)), whole(upper.shape),
            whole((LANES, width)), whole((16, LANES)), whole((READ_ROWS, width)), column, column,
            column, pl.BlockSpec((2 * LANES, tok_count), lambda i: (jnp.maximum(i - steps, 0), 0)),
        ],
        out_shape=[
            shape_of(tok_count, width), shape_of(tok_count, LANES), shape_of(width, LANES),
            shape_of(*upper.shape), shape_of(LANES, width, dtype=F32), shape_of(16, LANES, dtype=F32),
            shape_of(READ_ROWS, width, dtype=F32), shape_of(tok_count, width),
            shape_of(tok_count, width), shape_of(tok_count, width), shape_of(2 * width, tok_count),
        ],
        scratch_shapes=[pltpu.VMEM((PAIRS, tok_count, LANES), BF)] * 3
        + [pltpu.VMEM((LANES, LANES), F32)],
        compiler_params=PARAMS,
        cost_estimate=cost(25),
        name="attention_forward",
    )(
        length, ids, tokens, gains, weights, down, upper, coarse, fine, router, constant_mix, vectors,
        residual_mix,
    )


def attend_back_body(
    len_ref, q2_ref, k_ref, v_ref, mixed_ref, back_ref, coarse_ref, fine_ref,
    dq_ref, dk_ref, dv_ref, acc_ref, turn_ref,
):
    tok_count = k_ref.shape[0]

    @pl.when(pl.program_id(0) == 0)
    def _():
        turn_ref[0], turn_ref[1] = turn_rows(coarse_ref, fine_ref, 0, tok_count)

    lane = iota((tok_count, LANES), 1)
    position = iota((tok_count, LANES), 0)
    bias = jnp.where(position < len_ref[0], 0.0, NEG)
    causal = iota((TILE, TILE), 0) <= iota((TILE, TILE), 1)
    row = iota((LANES, tok_count), 0)
    back = back_ref[...].astype(F32)
    product_t = (back * mixed_ref[...].astype(F32)).T
    back_t = back.T
    keys, values = k_ref[...].astype(F32), v_ref[...].astype(F32)
    grads = []
    for head in range(2):
        own = lane // HD == head
        spare = HD * (1 - head)
        minus = jnp.where((lane > spare) & (lane < spare + 4), -1.0, 0.0)
        q2 = q2_ref[head * LANES : head * LANES + LANES, :]
        k2f = jnp.where(own, keys, jnp.where(lane == spare, bias, minus))
        k2 = k2f.astype(BF)
        k2t = k2f.T.astype(BF)
        v2 = jnp.where(own, values, minus).astype(BF)
        own_row = row // HD == head
        delta = jnp.sum(jnp.where(own_row, product_t, 0.0), axis=0, keepdims=True)
        back2 = jnp.where(own_row, back_t, 0.0)
        for offset, piece in enumerate(split3(delta)):
            back2 = jnp.where(row == spare + 1 + offset, piece.astype(F32), back2)
        back2 = back2.astype(BF)
        dk_parts, dv_parts = [], []
        for start in range(0, tok_count, TILE):
            stop = start + TILE
            scores = mm(k2[start:stop], q2[:, start:])
            slopes = mm(v2[start:stop], back2[:, start:])
            diagonal = jnp.where(causal, scores[:, :TILE], NEG)
            scores = (
                diagonal
                if stop == tok_count
                else jnp.concatenate([diagonal, scores[:, TILE:]], axis=1)
            )
            weights = jnp.exp(scores)
            turned = (weights * slopes).astype(BF)
            dv_parts.append(mm_nt(weights.astype(BF), back2[:, start:]))
            dk_parts.append(mm_nt(turned, q2[:, start:]))
            update = mm(k2t[:, start:stop], turned)
            if start == 0:
                acc_ref[head] = update
            else:
                acc_ref[head, :, start:] += update
        grads.append((jnp.concatenate(dk_parts, axis=0), jnp.concatenate(dv_parts, axis=0)))
    low_lane = lane < HD
    cosine, sine = turn_ref[0], -turn_ref[1]
    dq = jnp.where(row < HD, acc_ref[0], acc_ref[1]).T * HD**-0.5
    dq_ref[...] = rope(dq, cosine, sine).astype(BF)
    dk = jnp.where(low_lane, grads[0][0], grads[1][0])
    dk_ref[...] = rope(dk, cosine, sine).astype(BF)
    dv_ref[...] = jnp.where(low_lane, grads[0][1], grads[1][1]).astype(BF)


def attend_back_call(length, q2, keys, values, mixed, back, coarse, fine):
    tok_count, width = keys.shape
    column = pl.BlockSpec((tok_count, LANES), lambda i: (0, i))
    return pl.pallas_call(
        attend_back_body,
        grid=(PAIRS,),
        in_specs=[
            smem(), pl.BlockSpec((2 * LANES, tok_count), lambda i: (i, 0)), column, column, column,
            column, whole(coarse.shape), whole(fine.shape),
        ],
        out_specs=[column] * 3,
        out_shape=[shape_of(tok_count, width)] * 3,
        scratch_shapes=[
            pltpu.VMEM((2, LANES, tok_count), F32), pltpu.VMEM((2, tok_count, LANES), F32)
        ],
        compiler_params=PARAMS,
        cost_estimate=cost(12),
        name="attention_backward",
    )(length, q2, keys, values, mixed, back, coarse, fine)


def post_body(
    local, group, me_ref, mixed_ref, x_ref, wo_ref, acat_ref, bcat_ref, gain_ref, read_ref, mix_ref,
    prev_ref, routes_ref, slot_ref, hidden_ref, ei_ref, inner_ref, data_ref, cols_ref,
):
    reader = read_ref[0:READ_VECTOR].astype(BF)

    def stages(at):
        mixed = mixed_ref[at]
        inner = mm(mixed, acat_ref[...]).astype(BF)
        inner_ref[at] = inner
        yield
        hidden = x_ref[at].astype(F32) + (mm(mixed, wo_ref[...]) + mm(inner, bcat_ref[0]))
        hidden_ref[at] = hidden
        yield
        scale = lax.rsqrt(jnp.mean(hidden * hidden, axis=-1, keepdims=True) + EPSILON)
        ei = (hidden * scale * gain_ref[1:2, :]).astype(BF)
        ei_ref[at] = ei
        yield
        read = mm_nt(reader, ei)
        yield
        logits = read[0:16]
        for index in range(EXPERTS + 4):
            logits = logits + mix_ref[:, index : index + 1] * prev_ref[index : index + 1, at]
        first, second = routes_ref[0:1, at].astype(F32), routes_ref[1:2, at].astype(F32)
        number = iota((16, TILE), 0).astype(F32)
        one = jnp.sum(jnp.where(number == first, logits, 0.0), axis=0, keepdims=True)
        two = jnp.sum(jnp.where(number == second, logits, 0.0), axis=0, keepdims=True)
        top = jnp.maximum(one, two)
        one, two = jnp.exp(one - top), jnp.exp(two - top)
        gate_a, gate_b = one / (one + two), two / (one + two)
        mixes = read[16:20] + read[24:28] + read[32:36]
        shares = []
        for index in range(2):
            left, right = mixes[2 * index : 2 * index + 1], mixes[2 * index + 1 : 2 * index + 2]
            top = jnp.maximum(left, right)
            left, right = jnp.exp(left - top), jnp.exp(right - top)
            shares += [left / (left + right), right / (left + right)]

        def both(value):
            return jnp.where(first == value, gate_a, 0.0) + jnp.where(second == value, gate_b, 0.0)

        gates = jnp.where(number == first, gate_a, 0.0) + jnp.where(number == second, gate_b, 0.0)
        beta_a, beta_b = both(EXPERTS + 2.0), both(EXPERTS + 3.0)
        keep = both(EXPERTS + 1.0) + beta_a * shares[0] + beta_b * shares[2]
        data_ref[0:8, at] = gates[0:8]
        tail = [gate_a, gate_b] + shares + [beta_a, beta_b]
        data_ref[8:16, at] = jnp.concatenate(tail, axis=0)
        yield
        slots = slot_ref[:, at].astype(F32)
        expert = iota((EXPERTS, TILE), 0)
        partner = jnp.bitwise_xor(expert // local, me_ref[0])
        base = ((expert % local) * (group * CAP) + partner * CAP).astype(F32)
        place = jnp.where(slots >= 0, slots + base + 1.0, 0.0)
        expert = expert.astype(F32)
        target_a = jnp.sum(jnp.where(expert == first, place, 0.0), axis=0, keepdims=True) - 1.0
        target_b = jnp.sum(jnp.where(expert == second, place, 0.0), axis=0, keepdims=True) - 1.0
        stack = jnp.concatenate(
            [jnp.zeros((VECTOR_ROW, TILE), F32), beta_a * shares[1], beta_b * shares[3]]
            + [jnp.zeros((2, TILE), F32), target_a, target_b, keep]
            + [jnp.zeros((LANES - KEEP_LANE - 1, TILE), F32)],
            axis=0,
        )
        cols_ref[at] = stack.T

    side_by_side(stages)


def post_send_body(local, group, steps, me_ref, id_ref, slot_all_ref, *refs):
    post_refs, out_refs, (ei_all, data_all) = refs[:16], refs[16:-2], refs[-2:]
    step = pl.program_id(0)

    @pl.when(step < steps)
    def _():
        post_body(local, group, me_ref, *post_refs)
        span = pl.ds(pl.multiple_of(step * STEP, STEP), STEP)
        ei_all[span] = post_refs[12][...]
        data_all[:, span] = post_refs[14][...]

    @pl.when(step >= steps)
    def _():
        send_rows(local, group, step - steps, me_ref, id_ref, slot_all_ref, data_all, ei_all, out_refs)


def post_call(
    local, group, me, ids, mixed, tokens, weight, acat, bcat, gains, reader, mixer, prev, routes, slots
):
    tok_count, width = tokens.shape
    steps = tok_count // STEP
    heights = [local * PIECE] * (group // 2) + [PIECE] * ((group - group // 2) * local)

    def rows_of(columns):
        return pl.BlockSpec((STEP, columns), lambda i: (jnp.minimum(i, steps - 1), 0))

    def lanes_of(height):
        return pl.BlockSpec((height, STEP), lambda i: (0, jnp.minimum(i, steps - 1)))

    return pl.pallas_call(
        functools.partial(post_send_body, local, group, steps),
        grid=(steps + group,),
        in_specs=[
            smem(), smem(), whole(slots.shape), rows_of(width), rows_of(width), whole(weight.shape),
            whole(acat.shape), pl.BlockSpec((1, LANES, width), lambda i: (3, 0, 0)), whole(gains.shape),
            whole(reader.shape), whole(mixer.shape), lanes_of(EXPERTS + 4), lanes_of(2),
            lanes_of(EXPERTS),
        ],
        out_specs=[
            rows_of(width), rows_of(width), rows_of(LANES), lanes_of(16), rows_of(LANES)
        ] + [whole((height, width)) for height in heights],
        out_shape=[
            shape_of(tok_count, width, dtype=F32), shape_of(tok_count, width),
            shape_of(tok_count, LANES), shape_of(16, tok_count, dtype=F32),
            shape_of(tok_count, LANES, dtype=F32),
        ] + [shape_of(height, width) for height in heights],
        scratch_shapes=[pltpu.VMEM((tok_count, width), BF), pltpu.VMEM((16, tok_count), F32)],
        compiler_params=PARAMS,
        cost_estimate=cost(14),
        name="after_attention",
    )(
        me, ids, slots, mixed, tokens, weight, acat, bcat, gains, reader, mixer, prev, routes, slots
    )


def expert_body(
    local_index, pair, per_owner, group, steps, has_grad, *refs
):
    count = len(pair)
    piece_refs, refs = refs[:count], refs[count:]
    cot_refs, refs = refs[:count], refs[count:]
    dn_ref, ou_ref, wg_hbm, wu_hbm, wd_hbm, up_hbm, od_hbm = refs[:7]
    refs = refs[7:]
    if has_grad:
        before_hbm, refs = refs[0], refs[1:]
    back_refs, refs = refs[:count], refs[count:]
    out_refs, refs = refs[:count], refs[count:]
    (
        grad_ref, x_ref, g_ref, gate_ref, pick_ref, dr_ref, zg_ref, zu_ref, dzd_ref, zgt_ref, zut_ref,
        dzdt_ref, racc_ref, xacc_ref, zd_acc, dzg_acc, dzu_acc, h_ref, dg_ref, du_ref, wg_all, wu_all,
        wd_all, up_all, od_all, sems, *rest
    ) = refs
    rows, width = x_ref.shape
    compact = group * RANK
    tile = h_ref.shape[1]

    def copies(step):
        span = pl.ds(pl.multiple_of(step * tile, tile), tile)
        pairs = (
            (wg_hbm.at[local_index, :, span], wg_all),
            (wu_hbm.at[local_index, :, span], wu_all),
            (wd_hbm.at[local_index, span, :], wd_all),
            (up_hbm.at[local_index, :, :, span], up_all),
            (od_hbm.at[local_index, span, :], od_all),
        )
        return [
            pltpu.make_async_copy(source, target.at[step], sems.at[step, place])
            for place, (source, target) in enumerate(pairs)
        ]

    def begin(step):
        for copy in copies(step):
            copy.start()

    begin(0)

    def fold(value):
        place = iota((compact, LANES), 0)
        block = per_owner * group
        inner = place // block * per_owner + place % per_owner
        folded = mm_nt(hot(iota((compact, LANES), 1) % RANK == inner), value)
        place = iota((compact, rows), 0)
        owner = place % block // per_owner
        mine = iota((compact, rows), 1) // CAP + pair[0]
        return jnp.where(mine == owner, folded, 0.0).astype(BF)

    def put(start, value):
        grad_ref[:, pl.ds(start, value.shape[1])] = value.astype(BF)

    for index in range(count):
        span = slice(index * CAP, index * CAP + CAP)
        x_ref[span] = piece_refs[index][0:CAP]
        g_ref[span] = cot_refs[index][...]
        meta = piece_refs[index][CAP:PIECE].astype(F32)
        gate = (meta[0:1] + meta[1:2] + meta[2:3])[:, 0 : 2 * LANES]
        gate_ref[span] = jnp.broadcast_to(gate, (LANES, 2 * LANES)).T[0:CAP]
        lane = (iota((CAP, LANES), 1) // RANK).astype(F32)
        pick_ref[span] = jnp.where(lane == meta[3:4, 0:LANES], 1.0, 0.0)
    chosen = pick_ref[...] > 0.0
    dr = (gate_ref[:, 0:1] * g_ref[...].astype(F32)).astype(BF)
    dr_ref[...] = dr
    zg = jnp.where(chosen, mm(x_ref[...], dn_ref[0]), 0.0).astype(BF)
    zu = jnp.where(chosen, mm(x_ref[...], dn_ref[1]), 0.0).astype(BF)
    dzd = jnp.where(chosen, mm_nt(dr, ou_ref[...]), 0.0).astype(BF)
    zg_ref[...] = zg
    zu_ref[...] = zu
    dzd_ref[...] = dzd
    zgt_ref[...] = fold(zg)
    zut_ref[...] = fold(zu)
    dzdt_ref[...] = fold(dzd)
    for ref in (racc_ref, xacc_ref, zd_acc, dzg_acc, dzu_acc):
        ref[...] = jnp.zeros_like(ref)

    total = steps * tile
    begin(1)
    if has_grad:
        before = pltpu.make_async_copy(before_hbm, rest[0], rest[1])
        before.start()

    def run(step, carry):
        for copy in copies(step):
            copy.wait()

        @pl.when(step + 2 < steps)
        def _():
            begin(step + 2)

        wg_ref, wu_ref, wd_ref = wg_all.at[step], wu_all.at[step], wd_all.at[step]
        up_ref, od_ref = up_all.at[step], od_all.at[step]
        gate = mm(x_ref[...], wg_ref[...]) + mm(zg_ref[...], up_ref[0])
        upper = mm(x_ref[...], wu_ref[...]) + mm(zu_ref[...], up_ref[1])
        share = 0.5 * jnp.tanh(0.5 * gate) + 0.5
        silu = gate * share
        active = (silu * upper).astype(BF)
        h_ref[...] = active
        back = mm_nt(dr_ref[...], wd_ref[...]) + mm_nt(dzd_ref[...], od_ref[...])
        du = (back * silu).astype(BF)
        dg = (back * upper * (share + silu * (1.0 - share))).astype(BF)
        du_ref[...] = du
        dg_ref[...] = dg
        racc_ref[...] += mm(active, wd_ref[...])
        zd_acc[...] += mm(active, od_ref[...])
        xacc_ref[...] += mm_nt(dg, wg_ref[...]) + mm_nt(du, wu_ref[...])
        dzg_acc[...] += mm_nt(dg, up_ref[0])
        dzu_acc[...] += mm_nt(du, up_ref[1])
        at = pl.multiple_of(step * tile, tile)
        put(at, mm(zgt_ref[...], dg_ref[...]))
        put(total + at, mm(zut_ref[...], du_ref[...]))
        put(2 * total + at, mm(dzdt_ref[...], h_ref[...]))
        return carry

    lax.fori_loop(0, steps, run, 0)
    chosen = pick_ref[...] > 0.0
    zd = jnp.where(chosen, zd_acc[...], 0.0).astype(BF)
    dzg = jnp.where(chosen, dzg_acc[...], 0.0).astype(BF)
    dzu = jnp.where(chosen, dzu_acc[...], 0.0).astype(BF)
    result = racc_ref[...] + mm(zd, ou_ref[...])
    gated = (gate_ref[:, 0:1] * result).astype(BF)
    product = g_ref[...].astype(F32) * result.astype(BF).astype(F32)
    dots = jnp.broadcast_to(jnp.sum(product, axis=-1, keepdims=True), (rows, LANES))
    back_rows = (xacc_ref[...] + mm_nt(dzg, dn_ref[0]) + mm_nt(dzu, dn_ref[1])).astype(BF)
    for index in range(count):
        span = slice(index * CAP, index * CAP + CAP)
        out_refs[index][...] = gated[span]
        back_refs[index][0:CAP, :] = back_rows[span]
        column = jnp.concatenate(
            [dots[span], jnp.zeros((2 * LANES - CAP, LANES), F32)], axis=0
        ).T[0:1]
        meta = jnp.concatenate(
            [piece.astype(F32) for piece in split3(column)]
            + [jnp.zeros((META - 3, 2 * LANES), F32)],
            axis=0,
        )
        meta = jnp.concatenate([meta, jnp.zeros((META, width - 2 * LANES), F32)], axis=1)
        back_refs[index][CAP:PIECE, :] = meta.astype(BF)
    base = 3 * total
    place = iota((compact, LANES), 0)
    owner = place % (per_owner * group) // per_owner
    ids = jnp.zeros((compact, LANES), F32)
    for index in range(count):
        meta = piece_refs[index][CAP:PIECE, 0:LANES].astype(F32)
        ids = jnp.where(owner == pair[index], meta[3:4], ids)
    put(base + 3 * width, ids)
    put(base, mm(fold(zd), dr_ref[...]))
    put(base + width, mm(fold(dzg), x_ref[...]))
    put(base + 2 * width, mm(fold(dzu), x_ref[...]))
    if has_grad:
        before.wait()
        grad_ref[...] = grad_ref[...] + rest[0][...]


def expert_call(index, pair, group, per_owner, pieces, cots, before, weights):
    gate_w, up_w, down_w, in_down, in_up, out_down, out_up = weights
    width, hidden = gate_w.shape[1:]
    rows = len(pair) * CAP
    steps = hidden // FTILE
    columns = 3 * hidden + 3 * width + LANES
    compact = group * RANK
    has_grad = before is not None
    return pl.pallas_call(
        functools.partial(expert_body, index, pair, per_owner, group, steps, has_grad),
        grid=(1,),
        in_specs=[
            pl.BlockSpec((PIECE, width), lambda f, row=piece.shape[0] // PIECE > 1: (index * row, 0))
            for piece in pieces
        ]
        + [pl.BlockSpec((CAP, width), lambda f: (index, 0))] * len(pair)
        + [
            pl.BlockSpec((None, 2, width, LANES), lambda f: (index, 0, 0, 0)),
            pl.BlockSpec((None, LANES, width), lambda f: (index, 0, 0)),
        ]
        + [pl.BlockSpec(memory_space=pl.ANY)] * 5
        + [pl.BlockSpec(memory_space=pl.ANY)] * has_grad,
        out_specs=[whole((PIECE, width))] * len(pair)
        + [whole((CAP, width))] * len(pair)
        + [whole((compact, columns))],
        out_shape=[shape_of(PIECE, width)] * len(pair)
        + [shape_of(CAP, width)] * len(pair)
        + [shape_of(compact, columns)],
        scratch_shapes=[pltpu.VMEM((rows, width), BF)] * 2
        + [pltpu.VMEM((rows, LANES), F32)] * 2
        + [pltpu.VMEM((rows, width), BF)]
        + [pltpu.VMEM((rows, LANES), BF)] * 3
        + [pltpu.VMEM((compact, rows), BF)] * 3
        + [pltpu.VMEM((rows, width), F32)] * 2
        + [pltpu.VMEM((rows, LANES), F32)] * 3
        + [pltpu.VMEM((rows, FTILE), BF)] * 3
        + [pltpu.VMEM((steps, width, FTILE), BF)] * 2
        + [
            pltpu.VMEM((steps, FTILE, width), BF), pltpu.VMEM((steps, 2, LANES, FTILE), BF),
            pltpu.VMEM((steps, FTILE, LANES), BF), pltpu.SemaphoreType.DMA((steps, 5)),
        ]
        + [pltpu.VMEM((compact, columns), BF), pltpu.SemaphoreType.DMA] * has_grad,
        compiler_params=PARAMS,
        cost_estimate=cost(rows / 21),
        name="expert_layer",
    )(
        *pieces, *cots, in_down, out_up, gate_w, up_w, down_w, in_up, out_down,
        *([before] if has_grad else []),
    )


def spread(cols, index, count):
    return iota((TILE, count), 1).astype(F32) == cols[:, index : index + 1]


def combine_body(
    pieces, len_ref, *refs
):
    back_refs = refs[:pieces]
    (
        routes_ref, data_ref, cols_ref, cot_ref, ei_ref, hidden_ref, gain_ref, wo_ref, acat_ref, bcat_ref,
        table_ref, read_ref, bh_ref, ba_ref, din_ref, bm_ref, back_all, dots_ref,
    ) = refs[pieces:]
    count = pieces * CAP

    @pl.when(pl.program_id(0) == 0)
    def _():
        for index, back_ref in enumerate(back_refs):
            back_all[index * CAP : index * CAP + CAP, :] = back_ref[0:CAP, :]
        dots = [back_ref[CAP:PIECE, 0:CAP].astype(F32) for back_ref in back_refs]
        dots = jnp.concatenate(dots, axis=1)
        dots_ref[...] = jnp.concatenate([dots, jnp.zeros_like(dots)], axis=0).astype(BF)

    table_high, table_low = split2(table_ref[...])
    stack = dots_ref[...]
    vectors = read_ref[READ_VECTOR:READ_ROWS].astype(BF)

    def stages(at):
        start = pl.program_id(0) * STEP + at.start
        cols = cols_ref[at]
        chosen_a = hot(spread(cols, TARGET_LANE, count))
        chosen_b = hot(spread(cols, TARGET_LANE + 1, count))
        yield
        routed_a = jnp.sum(mm_nt(stack, chosen_a)[0:8], axis=0, keepdims=True)
        routed_b = jnp.sum(mm_nt(stack, chosen_b)[0:8], axis=0, keepdims=True)
        cot = cot_ref[at]
        cot_f = cot.astype(F32)
        yield
        along_x = jnp.sum(cot_f * ei_ref[at].astype(F32), axis=-1, keepdims=True)
        along_x = jnp.broadcast_to(along_x, (TILE, LANES)).T[0:1]
        yield
        along_c = mm_nt(vectors, cot)
        along_a = along_c[0:1] + along_c[2:3] + along_c[4:5]
        along_b = along_c[1:2] + along_c[3:4] + along_c[5:6]
        yield
        both = chosen_a + chosen_b
        half = count // 2
        back = mm(both[:, :half], back_all[:half]) + mm(both[:, half:], back_all[half:])
        yield
        first, second = routes_ref[0:1, at].astype(F32), routes_ref[1:2, at].astype(F32)
        token = iota((1, TILE), 1) + start
        valid = jnp.where(token < len_ref[0], 1.0, 0.0)
        gate_a, gate_b = data_ref[8:9, at], data_ref[9:10, at]
        share = [data_ref[index : index + 1, at] for index in range(10, 14)]
        beta_a, beta_b = data_ref[14:15, at], data_ref[15:16, at]
        const_a = share[0] * along_x + share[1] * along_a
        const_b = share[2] * along_x + share[3] * along_b

        def here(route):
            return (
                jnp.where(route == EXPERTS + 1.0, along_x, 0.0)
                + jnp.where(route == EXPERTS + 2.0, const_a, 0.0)
                + jnp.where(route == EXPERTS + 3.0, const_b, 0.0)
            )

        dot_a, dot_b = routed_a + here(first), routed_b + here(second)
        mean = gate_a * dot_a + gate_b * dot_b
        chosen_grad_a = valid * gate_a * (dot_a - mean)
        chosen_grad_b = valid * gate_b * (dot_b - mean)
        number = iota((16, TILE), 0).astype(F32)
        logit_grads = jnp.where(number == first, chosen_grad_a, 0.0) + jnp.where(
            number == second, chosen_grad_b, 0.0
        )
        mixes = []
        for index, (beta, along) in enumerate(((beta_a, along_a), (beta_b, along_b))):
            left, right = share[2 * index], share[2 * index + 1]
            weighted = left * along_x + right * along
            mixes += [
                valid * beta * left * (along_x - weighted),
                valid * beta * right * (along - weighted),
            ]
        small = jnp.concatenate(
            [logit_grads] + mixes + [jnp.zeros((LANES - 20, TILE), F32)], axis=0
        ).T
        high, low = split2(small)
        yield
        inside = iota((TILE, 1), 0) + start < len_ref[0]
        grad = jnp.where(inside, cot_f, 0.0)
        back = back + mm(high, table_high) + mm(low, table_high) + mm(high, table_low)
        back = back + cols[:, KEEP_LANE : KEEP_LANE + 1] * grad
        yield
        hidden = hidden_ref[at]
        scale = lax.rsqrt(jnp.mean(hidden * hidden, axis=-1, keepdims=True) + EPSILON)
        normed = hidden * scale
        back = back * gain_ref[1:2, :]
        back = grad + scale * (back - normed * jnp.mean(back * normed, axis=-1, keepdims=True))
        bh_ref[at] = back
        rounded = back.astype(BF)
        ba_ref[at] = rounded
        yield
        inner = mm_nt(rounded, bcat_ref[0]).astype(BF)
        din_ref[at] = inner
        yield
        bm_ref[at] = (mm_nt(rounded, wo_ref[...]) + mm_nt(inner, acat_ref[...])).astype(BF)

    side_by_side(stages)


def combine_call(
    length, backs, routes, data, cols, cotangent, ei, hidden, gains, weight, acat, bcat, table,
    reader,
):
    tok_count, width = cotangent.shape
    pieces = len(backs)
    return pl.pallas_call(
        functools.partial(combine_body, pieces),
        grid=(tok_count // STEP,),
        in_specs=[smem()] + [whole(back.shape) for back in backs] + [
            wide(2), wide(16), tall(LANES), tall(width), tall(width), tall(width),
            whole(gains.shape), whole(weight.shape), whole(acat.shape),
            pl.BlockSpec((1, LANES, width), lambda i: (3, 0, 0)), whole(table.shape),
            whole(reader.shape),
        ],
        out_specs=[tall(width), tall(width), tall(LANES), tall(width)],
        out_shape=[
            shape_of(tok_count, width, dtype=F32), shape_of(tok_count, width),
            shape_of(tok_count, LANES), shape_of(tok_count, width),
        ],
        scratch_shapes=[
            pltpu.VMEM((pieces * CAP, width), BF), pltpu.VMEM((2 * META, pieces * CAP), BF)
        ],
        compiler_params=PARAMS,
        cost_estimate=cost(17),
        name="combine_backward",
    )(
        length, *backs, routes, data, cols, cotangent, ei, hidden, gains, weight, acat, bcat, table,
        reader,
    )


def result_body(pieces, len_ref, *refs):
    result_refs = refs[:pieces]
    cols_ref, ei_ref, hidden_ref, table_ref, out_ref, result_all = refs[pieces:]
    count = pieces * CAP

    @pl.when(pl.program_id(0) == 0)
    def _():
        for index, result_ref in enumerate(result_refs):
            result_all[index * CAP : index * CAP + CAP, :] = result_ref[...]

    table_high, table_low = split2(table_ref[...])

    def stages(at):
        cols = cols_ref[at]
        both = hot(spread(cols, TARGET_LANE, count) | spread(cols, TARGET_LANE + 1, count))
        yield
        half = count // 2
        mixture = mm(both[:, :half], result_all[:half]) + mm(both[:, half:], result_all[half:])
        yield
        high, low = split2(cols)
        mixture = mixture + mm(high, table_high) + mm(low, table_high) + mm(high, table_low)
        mixture = mixture + cols[:, KEEP_LANE : KEEP_LANE + 1] * ei_ref[at].astype(F32)
        yield
        inside = iota((TILE, 1), 0) + pl.program_id(0) * STEP + at.start < len_ref[0]
        out_ref[at] = (hidden_ref[at] + jnp.where(inside, mixture, 0.0)).astype(BF)

    side_by_side(stages)


def result_call(length, results, cols, ei, hidden, table):
    tok_count, width = ei.shape
    pieces = len(results)
    return pl.pallas_call(
        functools.partial(result_body, pieces),
        grid=(tok_count // STEP,),
        in_specs=[smem()] + [whole(result.shape) for result in results] + [
            tall(LANES), tall(width), tall(width), whole(table.shape),
        ],
        out_specs=tall(width),
        out_shape=shape_of(tok_count, width),
        scratch_shapes=[pltpu.VMEM((pieces * CAP, width), BF)],
        compiler_params=PARAMS,
        cost_estimate=cost(8),
        name="layer_output",
    )(length, *results, cols, ei, hidden, table)


def adapter_body(
    packed, id_ref, dq_ref, dk_ref, dv_ref, bcat_ref, normed_ref, inner_ref, mixed_ref, inner_o_ref,
    ba_ref, din_ref, back_ref, grad_ref, acc_ref,
):
    step = pl.program_id(0)
    width = dq_ref.shape[1]
    count = 4 * RANK

    @pl.when(step == 0)
    def _():
        acc_ref[...] = jnp.zeros_like(acc_ref)

    inner_t = inner_ref[...].astype(F32).T[0:count].astype(BF)
    outer_t = inner_o_ref[...].astype(F32).T[0:count].astype(BF)
    number = iota((count, width), 0) % 4
    back_inner = din_ref[...].astype(F32)
    values = [ref[...] for ref in (dq_ref, dk_ref, dv_ref)]
    for index, value in enumerate(values):
        back_inner = back_inner + mm_nt(value, bcat_ref[index]).astype(BF).astype(F32)
    upper = mm(outer_t, ba_ref[...])
    for index, value in enumerate(values):
        upper = jnp.where(number == index, mm(inner_t, value), upper)
    own = iota(back_inner.shape, 1) % 4 < 3
    back_ref[...] = jnp.where(own, back_inner, 0.0).astype(BF)
    back_t = back_inner.T[0:count].astype(BF)
    down = jnp.where(number < 3, mm(back_t, normed_ref[...]), mm(back_t, mixed_ref[...]))
    acc_ref[:, 0:width] += down
    acc_ref[:, width:] += upper

    @pl.when(step == pl.num_programs(0) - 1)
    def _():
        if not packed:
            grad_ref[...] = acc_ref[...].astype(BF)
            return
        half = width // 2
        shape = (16 * RANK, count)
        place, row = iota(shape, 0), iota(shape, 1)
        total = None
        for index in range(4):
            kind, part = index // 2, index % 2
            here = (place % 4 == row % 4) & (place // 16 == row // 4)
            here = here & (place // 8 % 2 == part) & (place // 4 % 2 == kind)
            start = kind * width + part * half
            piece = mm(hot(here), acc_ref[:, start : start + half].astype(BF))
            total = piece if total is None else total + piece
        grad_ref[:, 0:half] = total.astype(BF)
        grad_ref[:, half:] = jnp.full((16 * RANK, LANES), id_ref[0].astype(F32), F32).astype(BF)


def adapter_call(
    packed, ids, dq, dk, dv, bcat, normed, inner, mixed, inner_o, ba, din
):
    tok_count, width = dq.shape
    grad_shape = (16 * RANK, width // 2 + LANES) if packed else (4 * RANK, 2 * width)
    return pl.pallas_call(
        functools.partial(adapter_body, packed),
        grid=(tok_count // TILE,),
        in_specs=[
            smem(), tile(width), tile(width), tile(width), whole(bcat.shape), tile(width), tile(LANES),
            tile(width), tile(LANES), tile(width), tile(LANES),
        ],
        out_specs=[tile(LANES), whole(grad_shape)],
        out_shape=[shape_of(tok_count, LANES), shape_of(*grad_shape)],
        scratch_shapes=[pltpu.VMEM((4 * RANK, 2 * width), F32)],
        compiler_params=PARAMS,
        cost_estimate=cost(6),
        name="adapter_gradients",
    )(ids, dq, dk, dv, bcat, normed, inner, mixed, inner_o, ba, din)


def last_body(
    dq_ref, dk_ref, dv_ref, w_ref, acat_ref, back_ref, x_ref, bh_ref, gain_ref, out_ref
):
    def stages(at):
        parts = [mm_nt(back_ref[at], acat_ref[...])]
        for index, ref in enumerate((dq_ref, dk_ref, dv_ref)):
            parts.append(mm_nt(ref[at], w_ref[index]))
            yield
        total = parts[0] + parts[1] + parts[2] + parts[3]
        x = x_ref[at].astype(F32)
        scale = lax.rsqrt(jnp.mean(x * x, axis=-1, keepdims=True) + EPSILON)
        normed = x * scale
        back = total * gain_ref[0:1, :]
        back = scale * (back - normed * jnp.mean(back * normed, axis=-1, keepdims=True))
        out_ref[at] = (bh_ref[at] + back).astype(BF)

    side_by_side(stages)


def last_call(dq, dk, dv, weights, acat, back, tokens, bh, gains):
    tok_count, width = tokens.shape
    return pl.pallas_call(
        last_body,
        grid=(tok_count // STEP,),
        in_specs=[
            tall(width), tall(width), tall(width), whole(weights.shape), whole(acat.shape),
            tall(LANES), tall(width), tall(width), whole(gains.shape),
        ],
        out_specs=tall(width),
        out_shape=shape_of(tok_count, width),
        compiler_params=PARAMS,
        cost_estimate=cost(9),
        name="after_attention_backward",
    )(dq, dk, dv, weights, acat, back, tokens, bh, gains)


def exchange(value, axes):
    return lax.all_to_all(value, axes, split_axis=0, concat_axis=0, tiled=True)


def gather_all(value, axes, count):
    return exchange(jnp.broadcast_to(value[None], (count,) + value.shape), axes)


def swap(value, partner, group):
    if partner == 0:
        return value
    return lax.ppermute(value, "expert", [(index, index ^ partner) for index in range(group)])


def find_adapters(id_rows):
    count = id_rows.shape[0]
    padded = id_rows.astype(F32)
    if count % LANES:
        padded = jnp.concatenate([padded, jnp.zeros((-count % LANES, LANES), F32)], axis=0)
    return padded.T[0:1, 0:count].astype(jnp.int32)


def sum_expert_body(each, adapters, in_ref, out_ref):
    count, columns = in_ref.shape[0], out_ref.shape[1]
    found = find_adapters(in_ref[:, columns:])
    place = iota((adapters * each, count), 0)
    column = iota((adapters * each, count), 1)
    pick = hot((place // each == found) & (place % each == column % each))
    out_ref[...] = mm(pick, in_ref[:, 0:columns]).astype(BF)


def exchange_expert_grads(grads, group, owners):
    split = min(RANK, owners)
    each, parts = RANK // split, owners // split
    columns = (grads.shape[1] - LANES) // parts
    pieces = grads.reshape(split, each * group, grads.shape[1])
    if parts > 1:
        ids = jnp.broadcast_to(pieces[:, None, :, parts * columns :], (split, parts, each * group, LANES))
        pieces = pieces[:, :, : parts * columns].reshape(split, each * group, parts, columns)
        pieces = jnp.concatenate([pieces.transpose(0, 2, 1, 3), ids], axis=-1)
        pieces = pieces.reshape(owners, each * group, columns + LANES)
    return exchange(pieces, "dp").reshape(owners * group * each, columns + LANES)


def sum_expert_grads(got, adapters, owners):
    columns = got.shape[1] - LANES
    each = RANK // min(RANK, owners)
    return pl.pallas_call(
        functools.partial(sum_expert_body, each, adapters),
        out_shape=shape_of(adapters * each, columns),
        compiler_params=PARAMS,
        cost_estimate=cost(2.2),
        name="expert_gradient_part",
    )(got)


def finish_expert_body(split, adapters, hidden, in_ref, *refs):
    down_ref, up_ref, out_down_ref, out_up_ref = refs[-4:]
    each = RANK // split
    rows = adapters * each
    count = split * rows
    width = out_up_ref.shape[1]

    def place(value):
        return value // each % adapters * RANK + value // (adapters * each) * each + value % each

    move = hot(iota((count, count), 0) == place(iota((count, count), 1)))
    back = hot(iota((count, count), 1) == place(iota((count, count), 0)))

    def part(start, size):
        span = slice(start, start + size)
        rows_of = [in_ref[owner, :, span] for owner in range(split)]
        return jnp.concatenate(rows_of, axis=0)

    for index in range(2):
        up_ref[index] = mm(move, part(index * hidden, hidden))
    out_down_ref[...] = mm_tn(part(2 * hidden, hidden), back)
    base = 3 * hidden
    out_up_ref[...] = mm(move, part(base, width))
    for index in range(2):
        base += width
        down_ref[index] = mm_tn(part(base, width), back)


def finish_expert_call(index, local, everything, outs, adapters, width, hidden):
    owners, rows, columns = everything.shape
    total = adapters * RANK
    shapes = [(local, 2, width, total), (local, 2, total, hidden), (local, hidden, total),
              (local, total, width)]
    specs = [
        pl.BlockSpec((None,) + shape[1:], lambda *_, rank=len(shape): (index,) + (0,) * (rank - 1))
        for shape in shapes
    ]
    return pl.pallas_call(
        functools.partial(finish_expert_body, owners, adapters, hidden),
        grid=(1,),
        in_specs=[whole(everything.shape)] + [pl.BlockSpec(memory_space=pl.ANY)] * len(outs),
        out_specs=specs,
        out_shape=[shape_of(*shape, dtype=F32) for shape in shapes],
        input_output_aliases={1 + place: place for place in range(len(outs))},
        compiler_params=PARAMS,
        cost_estimate=cost(4),
        name="expert_gradient_sums",
    )(everything, *outs)


def spread_expert_grads(own, adapters, owners):
    split = min(RANK, owners)
    each, parts = RANK // split, owners // split
    everything = gather_all(own, "dp", owners)
    everything = everything.reshape(split, parts, adapters, each, own.shape[1])
    everything = everything.transpose(2, 0, 3, 1, 4)
    return everything.reshape(adapters * RANK, parts * own.shape[1]).astype(F32)


def expert_sums(owned, adapters, owners, width, hidden):
    sums = [spread_expert_grads(value, adapters, owners) for value in owned]
    base = 3 * hidden
    up = [[value[:, 0:hidden], value[:, hidden : 2 * hidden]] for value in sums]
    down = [
        [value[:, base + width * part : base + width * (part + 1)].T for part in (1, 2)]
        for value in sums
    ]
    return (
        jnp.stack([jnp.stack(value) for value in down]),
        jnp.stack([jnp.stack(value) for value in up]),
        jnp.stack([value[:, 2 * hidden : base].T for value in sums]),
        jnp.stack([value[:, base : base + width] for value in sums]),
    )


def finish_adapter_body(adapters, me_ref, *refs):
    piece_refs, (down_ref, up_ref, in_ref) = refs[:-3], refs[-3:]
    half = in_ref.shape[3]
    owners, group = piece_refs[0].shape[0], len(piece_refs)
    for other in range(group):
        place = jnp.bitwise_xor(me_ref[0], other)
        for owner in range(owners):
            in_ref[owner * (group // 2) + place // 2, place % 2] = piece_refs[other][owner]
    count = RANK * adapters

    def place(value):
        return value % adapters * RANK + value // adapters

    move = hot(iota((count, count), 0) == place(iota((count, count), 1)))
    back = hot(iota((count, count), 1) == place(iota((count, count), 0)))
    for part in range(2):
        span = slice(part * half, part * half + half)
        for kind in range(2):
            for index in range(4):
                first = (kind * 4 + index) * adapters
                rows = in_ref[:, part, first : first + adapters, :].astype(F32)
                rows = rows.reshape(count, half).astype(BF)
                if kind == 0:
                    down_ref[index, span, :] = mm_tn(rows, back)
                else:
                    up_ref[index, :, span] = mm(move, rows)


def sum_adapter_body(kinds, adapters, in_ref, out_ref):
    count, columns = in_ref.shape[0], out_ref.shape[-1]
    found = find_adapters(in_ref[:, columns:])
    place = iota((adapters * kinds, count), 0)
    column = iota((adapters * kinds, count), 1)
    pick = hot((place % adapters == found) & (place // adapters == column % kinds))
    own = mm(pick, in_ref[:, 0:columns]).astype(BF)
    for index in range(out_ref.shape[0]):
        out_ref[index] = own


def adapter_sums(grads, meanwhile, later, finish, ids, adapters, owners, group, width):
    axes, everyone = ("dp", "expert"), owners * group
    if everyone == 2 * RANK and group == 4:
        kinds = 8
        got = exchange(grads.reshape(everyone, kinds, grads.shape[1]), axes)
        got, meanwhile = lax.optimization_barrier((got, meanwhile))
        own = pl.pallas_call(
            functools.partial(sum_adapter_body, kinds, adapters),
            out_shape=shape_of(owners, kinds * adapters, width // 2),
            compiler_params=PARAMS,
            cost_estimate=cost(2.0),
            name="adapter_gradient_part",
        )(got.reshape(everyone * kinds, grads.shape[1]))
        mine = exchange(own, "dp")
        mine, later = lax.optimization_barrier((mine, later))
        across = swap(mine, 2, group)
        full = [mine, swap(mine, 1, group), across, swap(across, 1, group)]
        full, later = lax.optimization_barrier((full, finish(later)))
        total = adapters * RANK
        down, upper = pl.pallas_call(
            functools.partial(finish_adapter_body, adapters),
            in_specs=[smem()] + [pl.BlockSpec(memory_space=pltpu.VMEM)] * group,
            out_shape=[shape_of(4, width, total, dtype=F32), shape_of(4, total, width, dtype=F32)],
            scratch_shapes=[pltpu.VMEM((RANK, 2, kinds * adapters, width // 2), BF)],
            compiler_params=PARAMS,
            cost_estimate=cost(3.6),
            name="adapter_gradient_sums",
        )(lax.axis_index("expert").reshape(1).astype(jnp.int32), *full)
        return down, upper, meanwhile, later
    later = finish(later)
    all_ids = exchange(jnp.broadcast_to(ids, (everyone,)), axes)
    pieces = grads.reshape(everyone, RANK * 4 * 2 * width // everyone)
    got = exchange(pieces, axes)
    pick = (jnp.arange(adapters, dtype=jnp.int32)[:, None] == all_ids[None, :]).astype(BF)
    own = jnp.dot(pick, got, preferred_element_type=F32).astype(BF)
    full = gather_all(own, axes, everyone)
    full = full.reshape(RANK, everyone // RANK, adapters, -1).transpose(2, 0, 1, 3)
    full = full.reshape(adapters * RANK, 4, 2, width).astype(F32)
    return full[:, :, 0].transpose(1, 2, 0), full[:, :, 1].transpose(1, 0, 2), meanwhile, later


def body(
    tokens,
    cotangent,
    lengths,
    adapter_ids,
    routes,
    prev_logits,
    norm_gains,
    input_weights,
    output_weight,
    adapter_down,
    adapter_up,
    router,
    residual_mix,
    constant_mix,
    constant_vectors,
    expert_gate,
    expert_up,
    expert_down,
    expert_adapter_down,
    expert_adapter_up,
    output_adapter_down,
    output_adapter_up,
):
    tok_count, width = tokens.shape
    hidden_width = expert_gate.shape[2]
    group, owners = lax.axis_size("expert"), lax.axis_size("dp")
    local = expert_gate.shape[0]
    adapters = adapter_down.shape[-1] // RANK
    angles = [jnp.asarray(table) for table in turn_tables(tok_count)]
    weights = (
        expert_gate, expert_up, expert_down, expert_adapter_down, expert_adapter_up,
        output_adapter_down, output_adapter_up,
    )
    per_owner = RANK // min(RANK, owners)
    everyone = owners * group
    me = lax.axis_index("expert")

    me = me.reshape(1).astype(jnp.int32)

    routes, prev_logits = routes.T, prev_logits.T
    slots, *grad_sends = route_call(local, group, lengths, me, routes, cotangent)
    cots = [swap(value, partner, group) for partner, value in enumerate(grad_sends)]
    normed, inner, acat, bcat, table, mixer, reader, keys, values, mixed, q2 = pre_attend_call(
        lengths, adapter_ids, tokens, norm_gains, input_weights, adapter_down, adapter_up, *angles,
        router.T, constant_mix.T, constant_vectors, residual_mix,
    )
    mixed, cots = lax.optimization_barrier((mixed, cots))
    hidden, ei, inner_o, data, cols, *sends = post_call(
        local, group, me, adapter_ids, mixed, tokens, output_weight, acat, bcat, norm_gains, reader, mixer, prev_logits,
        routes, slots,
    )
    near, far = tuple(range(group // 2)), tuple(range(group // 2, group))
    sent_near = [swap(sends[partner], partner, group) for partner in near]
    sent_far = []
    for index in range(local):
        pieces = [sends[group // 2 + place * local + index] for place in range(len(far))]
        if index > 0:
            pieces, sent_near = lax.optimization_barrier((pieces, sent_near))
        sent_far.append([swap(piece, partner, group) for piece, partner in zip(pieces, far)])
    backs = [[None] * group for _ in range(local)]
    results = [[None] * group for _ in range(local)]
    calls = []
    for index in range(local - 1):
        calls += [(index, near), (index, far)]
    calls += [(local - 1, near[1:] + far), (local - 1, near[:1])]
    grads, owned, parts = [None] * local, [], []
    sums = functools.partial(sum_expert_grads, adapters=adapters, owners=owners)
    last = None
    for index, some in calls:
        pieces = [
            sent_near[partner] if partner in near else sent_far[index][partner - len(near)]
            for partner in some
        ]
        if last is not None:
            pieces, last = lax.optimization_barrier((pieces, last))
        if (index, some) == calls[-1]:
            parts, last = lax.optimization_barrier((parts, last))
            owned = [sums(part) for part in parts]
            pieces, backs[:index], owned = lax.optimization_barrier((pieces, backs[:index], owned))
        outs = expert_call(
            index, some, group, per_owner, pieces, [cots[partner] for partner in some], grads[index], weights
        )
        grads[index] = last = outs[-1]
        for place, partner in enumerate(some):
            backs[index][partner] = swap(outs[place], partner, group)
            results[index][partner] = outs[len(some) + place]
        if index < local - 1 and some == far:
            parts.append(exchange_expert_grads(last, group, owners))
    backs = [value for some in backs for value in some]
    parts.append(exchange_expert_grads(last, group, owners))
    gather = functools.partial(lax.all_gather, axis_name="dp", axis=0, tiled=False)
    if owners <= RANK:
        owned = [gather(own) for own in owned]
    back_hidden, back_attention, back_inner_o, back_mixed = combine_call(
        lengths, backs, routes, data, cols, cotangent, ei, hidden, norm_gains, output_weight, acat, bcat,
        table, reader,
    )
    flat = [value for some in results for value in some]
    flat, back_mixed = lax.optimization_barrier((flat, back_mixed))
    flat = [swap(value, place % group, group) for place, value in enumerate(flat)]

    dq, dk, dv = attend_back_call(lengths, q2, keys, values, mixed, back_mixed, *angles)
    parts[-1], dq, flat, owned = lax.optimization_barrier((parts[-1], dq, flat, owned))
    own = sums(parts[-1])
    dq, own, flat = lax.optimization_barrier((dq, own, flat))
    owned.append(gather(own) if owners <= RANK else own)
    back_inner, adapter_grads = adapter_call(
        everyone == 2 * RANK and group == 4, adapter_ids, dq, dk, dv, bcat, normed, inner, mixed,
        inner_o, back_attention, back_inner_o,
    )
    (dq, dk, dv, flat, owned[:-1]), adapter_grads = lax.optimization_barrier(
        ((dq, dk, dv, flat, owned[:-1]), adapter_grads)
    )
    layer_out = result_call(lengths, flat, cols, ei, hidden, table)
    input_back = last_call(
        dq, dk, dv, input_weights, acat, back_inner, tokens, back_hidden, norm_gains
    )
    outs = []
    if owners <= RANK:
        for index, own in enumerate(owned[:-1]):
            outs = finish_expert_call(index, local, own, outs, adapters, width, hidden_width)
    def finish(later):
        input_back, outs = later
        if owners <= RANK:
            return input_back, finish_expert_call(
                local - 1, local, owned[-1], outs, adapters, width, hidden_width
            )
        return input_back, expert_sums(owned, adapters, owners, width, hidden_width)

    down_sum, upper_sum, layer_out, (input_back, outs) = adapter_sums(
        adapter_grads, layer_out, (input_back, outs), finish, adapter_ids, adapters, owners, group, width
    )
    in_down_sum, in_up_sum, out_down_sum, out_up_sum = outs
    return (
        layer_out,
        input_back,
        down_sum,
        upper_sum,
        in_down_sum,
        in_up_sum,
        out_down_sum,
        out_up_sum,
    )


def solution(mesh):
    tokens_spec, copied = P(("dp", "expert"), None), P()
    owned = P("expert")
    placed = (
        (tokens_spec, tokens_spec, P(("dp", "expert")), P(("dp", "expert")), tokens_spec, tokens_spec)
        + (copied,) * 9
        + (owned,) * 7
    )
    return jax.shard_map(
        body,
        mesh=mesh,
        in_specs=placed,
        out_specs=(tokens_spec, tokens_spec, copied, copied) + (owned,) * 4,
        check_vma=False,
    )
```

```python
import functools
import math

import jax
import jax.numpy as jnp
import numpy as np
from jax import lax
from jax.experimental import pallas as pl
from jax.experimental.pallas import tpu as pltpu
from jax.sharding import PartitionSpec as P

HEADS = 12
HD = 64
EXPERTS = 8
RANK = 16
CAP = 192
EPSILON = 1e-06
F32 = jnp.float32
BF = jnp.bfloat16
NEG = -1e30
LANES = 128
TILE = 256
STEP = 512
FTILE = 512
PAIRS = HEADS // 2
PARAMS = pltpu.CompilerParams(vmem_limit_bytes=67043328)
META = 8
MIX_ROW = 16
VECTOR_ROW = 20
TARGET_LANE = 24
KEEP_LANE = 26
READ_VECTOR = 48
READ_ROWS = 64
PIECE = CAP + META


def mm(left, right):
    return jnp.dot(left, right, preferred_element_type=F32)


def mm_nt(left, right):
    return lax.dot_general(left, right, (((1,), (1,)), ((), ())), preferred_element_type=F32)


def mm_tn(left, right):
    return lax.dot_general(left, right, (((0,), (0,)), ((), ())), preferred_element_type=F32)


def iota(shape, axis):
    return lax.broadcasted_iota(jnp.int32, shape, axis)


def hot(condition):
    return jnp.where(condition, 1.0, 0.0).astype(BF)


def split2(value):
    high = value.astype(BF)
    return high, (value - high.astype(F32)).astype(BF)


def split3(value):
    high = value.astype(BF)
    rest = value - high.astype(F32)
    middle = rest.astype(BF)
    return high, middle, (rest - middle.astype(F32)).astype(BF)


def whole(shape):
    zeros = (0,) * len(shape)
    return pl.BlockSpec(shape, lambda *_: zeros)


def smem():
    return pl.BlockSpec(memory_space=pltpu.SMEM)


def tall(width):
    return pl.BlockSpec((STEP, width), lambda i: (i, 0))


def wide(height):
    return pl.BlockSpec((height, STEP), lambda i: (0, i))


def tile(width):
    return pl.BlockSpec((TILE, width), lambda i: (i, 0))


def side_by_side(stages):
    running = [stages(slice(start, start + TILE)) for start in range(0, STEP, TILE)]
    while running:
        running = [stage for stage in running if next(stage, True) is None]


def shape_of(*shape, dtype=BF):
    return jax.ShapeDtypeStruct(shape, dtype)


def cost(microseconds):
    return pl.CostEstimate(flops=int(microseconds * 1e+09), bytes_accessed=0, transcendentals=0)


@functools.lru_cache(maxsize=None)
def turn_tables(length_in):
    half = HD // 2
    inverse = np.exp(np.arange(half, dtype=np.float64) * (-2.0 * math.log(10000.0) / HD))

    def table(positions):
        angles = np.tile(positions[:, None] * inverse[None, :], (1, 4))
        return np.stack([np.cos(angles), np.sin(angles)]).astype(np.float32)

    return table(np.arange(0.0, length_in, 32)), table(np.arange(0.0, 32))


def turn_rows(coarse_ref, fine_ref, first, count):
    fine_cos, fine_sin = fine_ref[0], fine_ref[1]
    sign = jnp.where(iota((32, LANES), 1) % HD < HD // 2, -1.0, 1.0)
    signed_cos, signed_sin = fine_cos * sign, fine_sin * sign
    cosines, sines = [], []
    for index in range(count // 32):
        row = first // 32 + index
        coarse_cos, coarse_sin = coarse_ref[0, pl.ds(row, 1), :], coarse_ref[1, pl.ds(row, 1), :]
        cosines.append(coarse_cos * fine_cos - coarse_sin * fine_sin)
        sines.append(coarse_sin * signed_cos + coarse_cos * signed_sin)
    return jnp.concatenate(cosines, axis=0), jnp.concatenate(sines, axis=0)


def rope(value, cosine, sine):
    first = iota(value.shape, 1) % HD < HD // 2
    turned = jnp.where(first, pltpu.roll(value, LANES - HD // 2, 1), pltpu.roll(value, HD // 2, 1))
    return value * cosine + turned * sine


def find_slots(length, routes_ref, slot_ref):
    tok_count = slot_ref.shape[1]
    before = hot(iota((TILE, TILE), 0) < iota((TILE, TILE), 1))
    carry = jnp.zeros((2 * EXPERTS, 1), F32)
    for start in range(0, tok_count, TILE):
        span = slice(start, start + TILE)
        expert = iota((2 * EXPERTS, TILE), 0)
        token = iota((2 * EXPERTS, TILE), 1) + start
        named = (routes_ref[0:1, span] == expert) | (routes_ref[1:2, span] == expert)
        hit = named & (token < length) & (expert < EXPERTS)
        hits = jnp.where(hit, 1.0, 0.0)
        slots = mm(hits.astype(BF), before) + carry
        carry = carry + jnp.sum(hits, axis=1, keepdims=True)
        slot_ref[:, span] = jnp.where(hit, slots, -1.0)[:EXPERTS].astype(jnp.int32)


def pick_rows(slot_ref, step, me, local):
    first = jnp.bitwise_xor(step, me) * local
    place = iota((CAP, slot_ref.shape[1]), 0)
    return first, [hot(place == slot_ref[pl.ds(first + index, 1), :]) for index in range(local)]


def pick_source(chosen, source_ref):
    half = source_ref.shape[0] // 2
    return mm(chosen[:, :half], source_ref[:half]) + mm(chosen[:, half:], source_ref[half:])


def store_piece(out_refs, step, other, index, value, start):
    @pl.when(step == other)
    def _():
        out_refs[index][start : start + value.shape[0], :] = value


def route_body(local, group, len_ref, me_ref, routes_ref, source_ref, slot_ref, *out_refs):
    step = pl.program_id(0)

    @pl.when(step == 0)
    def _():
        find_slots(len_ref[0], routes_ref, slot_ref)

    _, chosen = pick_rows(slot_ref, step, me_ref[0], local)
    rows = pick_source(jnp.concatenate(chosen, axis=0), source_ref).astype(BF)
    for other in range(group):
        store_piece(out_refs, step, other, other, rows, 0)


def route_call(local, group, length, me, routes, source):
    tok_count, width = source.shape
    return pl.pallas_call(
        functools.partial(route_body, local, group),
        grid=(group,),
        in_specs=[smem(), smem(), whole(routes.shape), whole(source.shape)],
        out_specs=[whole((EXPERTS, tok_count))] + [whole((local * CAP, width))] * group,
        out_shape=[shape_of(EXPERTS, tok_count, dtype=jnp.int32)]
        + [shape_of(local * CAP, width)] * group,
        compiler_params=PARAMS,
        cost_estimate=cost(6.5),
        name="route_rows",
    )(length, me, routes, source)


def send_rows(local, group, partner, me_ref, id_ref, slot_ref, data_ref, source_ref, out_refs):
    width = source_ref.shape[1]
    first, chosen = pick_rows(slot_ref, partner, me_ref[0], local)
    rows = pick_source(jnp.concatenate(chosen, axis=0), source_ref).astype(BF)
    for index in range(local):
        pieces = split3(data_ref[pl.ds(first + index, 1), :])
        stack = jnp.concatenate(
            [piece.astype(F32) for piece in pieces]
            + [jnp.zeros((13, chosen[index].shape[1]), F32)],
            axis=0,
        ).astype(BF)
        gates = mm_nt(stack, chosen[index])[0:META]
        gates = jnp.where(iota(gates.shape, 0) == 3, id_ref[0].astype(F32), gates)
        meta = jnp.concatenate([gates, jnp.zeros((META, width - CAP), F32)], axis=1)
        kept = rows[index * CAP : index * CAP + CAP]
        for other in range(group):
            far = other >= group // 2
            place = group // 2 + (other - group // 2) * local + index if far else other
            start = 0 if far else index * PIECE
            store_piece(out_refs, partner, other, place, kept, start)
            store_piece(out_refs, partner, other, place, meta.astype(BF), start + CAP)


def pre_body(
    id_ref, x_ref, gain_ref, w_ref, ad_ref, au_ref, coarse_ref, fine_ref, router_ref, cmix_ref, vec_ref,
    resid_ref, normed_ref, inner_ref, acat_ref, bcat_ref, table_ref, mix_ref, read_ref, q_ref, k_ref,
    v_ref, square_ref,
):
    @pl.when(pl.program_id(0) == 0)
    def _():
        first = RANK * id_ref[0]
        total = None
        for index in range(4):
            row, column = iota((LANES, LANES), 0), iota((LANES, LANES), 1)
            place = hot((row >= first) & (row < first + RANK) & (column == (row - first) * 4 + index))
            part = mm(ad_ref[index], place)
            total = part if total is None else total + part
            place = hot(
                (column >= first) & (column < first + RANK) & (row == (column - first) * 4 + index)
            )
            bcat_ref[index] = mm(place, au_ref[index]).astype(BF)
        acat_ref[...] = total.astype(BF)
        table_ref[...] = jnp.zeros_like(table_ref)
        table_ref[0 : EXPERTS + 4, :] = router_ref[...].astype(F32)
        table_ref[MIX_ROW : MIX_ROW + 4, :] = cmix_ref[...]
        table_ref[VECTOR_ROW : VECTOR_ROW + 2, :] = vec_ref[...]
        read_ref[...] = jnp.zeros_like(read_ref)
        read_ref[0 : EXPERTS + 4, :] = router_ref[...].astype(F32)
        for place, piece in enumerate(split3(cmix_ref[...])):
            read_ref[16 + 8 * place : 20 + 8 * place, :] = piece.astype(F32)
        for place, piece in enumerate(split3(vec_ref[...])):
            read_ref[READ_VECTOR + 2 * place : READ_VECTOR + 2 * place + 2, :] = piece.astype(F32)
        square_ref[...] = jnp.zeros_like(square_ref)
        square_ref[0 : EXPERTS + 4, 0 : EXPERTS + 4] = resid_ref[...]
        mix_ref[...] = square_ref[...].T[0:16]

    def stages(at):
        x = x_ref[at].astype(F32)
        scale = lax.rsqrt(jnp.mean(x * x, axis=-1, keepdims=True) + EPSILON)
        normed = (x * scale * gain_ref[0:1, :]).astype(BF)
        normed_ref[at] = normed
        yield
        inner = mm(normed, acat_ref[...]).astype(BF)
        inner_ref[at] = inner
        yield
        for index, out_ref in enumerate((q_ref, k_ref, v_ref)):
            value = mm(normed, w_ref[index]) + mm(inner, bcat_ref[index])
            yield
            rows = pl.ds(pl.multiple_of(pl.program_id(0) * STEP + at.start, TILE), TILE)
            if index == 2:
                for pair in range(PAIRS):
                    span = slice(pair * LANES, pair * LANES + LANES)
                    out_ref[pair, rows] = value[:, span].astype(BF)
                continue
            cosine, sine = turn_rows(coarse_ref, fine_ref, pl.program_id(0) * STEP + at.start, TILE)
            for pair in range(PAIRS):
                span = slice(pair * LANES, pair * LANES + LANES)
                turned = rope(value[:, span], cosine, sine).astype(BF)
                if index == 0:
                    turned = (turned.astype(F32) * HD**-0.5).astype(BF)
                out_ref[pair, rows] = turned
            yield

    side_by_side(stages)


def attend_body(len_ref, q_ref, k_ref, v_ref, mixed_ref, q2_ref):
    tok_count = q_ref.shape[0]
    lane = iota((tok_count, LANES), 1)
    hidden_key = iota((tok_count, LANES), 0) >= len_ref[0]
    row = iota((LANES, tok_count), 0)
    row_tile = row[:, :TILE]
    causal = iota((TILE, TILE), 0) <= iota((TILE, TILE), 1)
    queries_t = q_ref[...].astype(F32).T
    values_t = v_ref[...].astype(F32).T
    keys = k_ref[...].astype(F32)
    heads = []
    for head in range(2):
        spare = HD * (1 - head)
        bias = jnp.where((lane == spare) & hidden_key, NEG, 0.0)
        one = jnp.where(row == spare, 1.0, 0.0)
        own = row // HD == head
        heads.append(
            (
                jnp.where(lane // HD == head, keys, bias).astype(BF),
                jnp.where(own, queries_t, one).astype(BF),
                jnp.where(own, values_t, one).astype(BF),
            )
        )
    units = [(start, head) for start in range(0, tok_count, TILE) for head in range(2)]

    def score(unit):
        start, head = unit
        keys, queries, _ = heads[head]
        part = queries[:, start : start + TILE]
        near = mm(keys[start : start + TILE], part)
        return near, mm(keys[:start], part) if start else None

    outs = {}
    waiting = score(units[0])
    for index, (start, head) in enumerate(units):
        near, far = waiting
        waiting = score(units[index + 1]) if index + 1 < len(units) else None
        spare = HD * (1 - head)
        _, queries, values = heads[head]
        near = jnp.where(causal, near, NEG)
        top = jnp.max(near, axis=0, keepdims=True)
        if start:
            top = jnp.maximum(top, jnp.max(far, axis=0, keepdims=True))
        mixed = mm(values[:, start : start + TILE], jnp.exp(near - top).astype(BF))
        if start:
            mixed = mixed + mm(values[:, :start], jnp.exp(far - top).astype(BF))
        total = mixed[spare : spare + 1]
        outs[head] = mixed * (1.0 / total)
        kept = queries[:, start : start + TILE]
        logs = jnp.zeros((LANES, TILE), F32)
        for offset, piece in enumerate(split3(top + jnp.log(total))):
            logs = jnp.where(row_tile == spare + 1 + offset, piece.astype(F32), logs)
        q2_ref[head * LANES : head * LANES + LANES, start : start + TILE] = kept + logs.astype(BF)
        if head == 1:
            mixed = jnp.where(row_tile < HD, outs[0], outs[1])
            mixed_ref[start : start + TILE] = mixed.T.astype(BF)


def pre_attend_body(steps, len_ref, *refs):
    pre_ins, pre_outs = refs[:12], refs[12:19]
    key_ref, value_ref, mixed_ref, q2_ref, q_all, k_all, v_all, square_ref = refs[19:]
    step = pl.program_id(0)

    @pl.when(step < steps)
    def _():
        pre_body(*pre_ins, *pre_outs, q_all, k_all, v_all, square_ref)

    @pl.when(step >= steps)
    def _():
        pair = step - steps
        key_ref[...] = k_all[pair]
        value_ref[...] = v_all[pair]
        attend_body(len_ref, q_all.at[pair], k_all.at[pair], v_all.at[pair], mixed_ref, q2_ref)


def pre_attend_call(
    length, ids, tokens, gains, weights, down, upper, coarse, fine, router, constant_mix, vectors,
    residual_mix,
):
    tok_count, width = tokens.shape
    steps = tok_count // STEP

    def rows_of(columns):
        return pl.BlockSpec((STEP, columns), lambda i: (jnp.minimum(i, steps - 1), 0))

    column = pl.BlockSpec((tok_count, LANES), lambda i: (0, jnp.maximum(i - steps, 0)))
    return pl.pallas_call(
        functools.partial(pre_attend_body, steps),
        grid=(steps + PAIRS,),
        in_specs=[
            smem(), smem(), rows_of(width), whole(gains.shape), whole(weights.shape), whole(down.shape),
            whole(upper.shape), whole(coarse.shape), whole(fine.shape), whole(router.shape),
            whole(constant_mix.shape), whole(vectors.shape), whole(residual_mix.shape),
        ],
        out_specs=[
            rows_of(width), rows_of(LANES), whole((width, LANES)), whole(upper.shape),
            whole((LANES, width)), whole((16, LANES)), whole((READ_ROWS, width)), column, column,
            column, pl.BlockSpec((2 * LANES, tok_count), lambda i: (jnp.maximum(i - steps, 0), 0)),
        ],
        out_shape=[
            shape_of(tok_count, width), shape_of(tok_count, LANES), shape_of(width, LANES),
            shape_of(*upper.shape), shape_of(LANES, width, dtype=F32), shape_of(16, LANES, dtype=F32),
            shape_of(READ_ROWS, width, dtype=F32), shape_of(tok_count, width),
            shape_of(tok_count, width), shape_of(tok_count, width), shape_of(2 * width, tok_count),
        ],
        scratch_shapes=[pltpu.VMEM((PAIRS, tok_count, LANES), BF)] * 3
        + [pltpu.VMEM((LANES, LANES), F32)],
        compiler_params=PARAMS,
        cost_estimate=cost(25),
        name="attention_forward",
    )(
        length, ids, tokens, gains, weights, down, upper, coarse, fine, router, constant_mix, vectors,
        residual_mix,
    )


def attend_back_body(
    len_ref, q2_ref, k_ref, v_ref, mixed_ref, back_ref, coarse_ref, fine_ref,
    dq_ref, dk_ref, dv_ref, acc_ref, turn_ref,
):
    tok_count = k_ref.shape[0]

    @pl.when(pl.program_id(0) == 0)
    def _():
        turn_ref[0], turn_ref[1] = turn_rows(coarse_ref, fine_ref, 0, tok_count)

    lane = iota((tok_count, LANES), 1)
    position = iota((tok_count, LANES), 0)
    bias = jnp.where(position < len_ref[0], 0.0, NEG)
    causal = iota((TILE, TILE), 0) <= iota((TILE, TILE), 1)
    row = iota((LANES, tok_count), 0)
    back = back_ref[...].astype(F32)
    product_t = (back * mixed_ref[...].astype(F32)).T
    back_t = back.T
    keys, values = k_ref[...].astype(F32), v_ref[...].astype(F32)
    grads = []
    for head in range(2):
        own = lane // HD == head
        spare = HD * (1 - head)
        minus = jnp.where((lane > spare) & (lane < spare + 4), -1.0, 0.0)
        q2 = q2_ref[head * LANES : head * LANES + LANES, :]
        k2f = jnp.where(own, keys, jnp.where(lane == spare, bias, minus))
        k2 = k2f.astype(BF)
        k2t = k2f.T.astype(BF)
        v2 = jnp.where(own, values, minus).astype(BF)
        own_row = row // HD == head
        delta = jnp.sum(jnp.where(own_row, product_t, 0.0), axis=0, keepdims=True)
        back2 = jnp.where(own_row, back_t, 0.0)
        for offset, piece in enumerate(split3(delta)):
            back2 = jnp.where(row == spare + 1 + offset, piece.astype(F32), back2)
        back2 = back2.astype(BF)
        dk_parts, dv_parts = [], []
        for start in range(0, tok_count, TILE):
            stop = start + TILE
            scores = mm(k2[start:stop], q2[:, start:])
            slopes = mm(v2[start:stop], back2[:, start:])
            diagonal = jnp.where(causal, scores[:, :TILE], NEG)
            scores = (
                diagonal
                if stop == tok_count
                else jnp.concatenate([diagonal, scores[:, TILE:]], axis=1)
            )
            weights = jnp.exp(scores)
            turned = (weights * slopes).astype(BF)
            dv_parts.append(mm_nt(weights.astype(BF), back2[:, start:]))
            dk_parts.append(mm_nt(turned, q2[:, start:]))
            update = mm(k2t[:, start:stop], turned)
            if start == 0:
                acc_ref[head] = update
            else:
                acc_ref[head, :, start:] += update
        grads.append((jnp.concatenate(dk_parts, axis=0), jnp.concatenate(dv_parts, axis=0)))
    low_lane = lane < HD
    cosine, sine = turn_ref[0], -turn_ref[1]
    dq = jnp.where(row < HD, acc_ref[0], acc_ref[1]).T * HD**-0.5
    dq_ref[...] = rope(dq, cosine, sine).astype(BF)
    dk = jnp.where(low_lane, grads[0][0], grads[1][0])
    dk_ref[...] = rope(dk, cosine, sine).astype(BF)
    dv_ref[...] = jnp.where(low_lane, grads[0][1], grads[1][1]).astype(BF)


def pack_grads(packed, id_ref, acc_ref, grad_ref):
    count, width = acc_ref.shape[0], acc_ref.shape[1] // 2
    if not packed:
        grad_ref[...] = acc_ref[...].astype(BF)
        return
    half = width // 2
    shape = (16 * RANK, count)
    place, row = iota(shape, 0), iota(shape, 1)
    total = None
    for index in range(4):
        kind, part = index // 2, index % 2
        here = (place % 4 == row % 4) & (place // 16 == row // 4)
        here = here & (place // 8 % 2 == part) & (place // 4 % 2 == kind)
        start = kind * width + part * half
        piece = mm(hot(here), acc_ref[:, start : start + half].astype(BF))
        total = piece if total is None else total + piece
    grad_ref[:, 0:half] = total.astype(BF)
    grad_ref[:, half:] = jnp.full((16 * RANK, LANES), id_ref[0].astype(F32), F32).astype(BF)


def attend_back_all_body(packed, len_ref, id_ref, *refs):
    ins, refs = refs[:7], refs[7:]
    bcat_ref, inner_ref, inner_o_ref, din_ref, ba_ref, normed_hbm, mixed_hbm = refs[:7]
    dq_ref, dk_ref, dv_ref, back_ref, grad_ref = refs[7:12]
    scratch, (inner_all, back_all, acc_ref, normed_all, mixed_all, sems) = refs[12:14], refs[14:]
    step = pl.program_id(0)
    count = inner_all.shape[1]
    width = normed_all.shape[1]
    copies = [
        pltpu.make_async_copy(normed_hbm, normed_all, sems.at[0]),
        pltpu.make_async_copy(mixed_hbm, mixed_all, sems.at[1]),
    ]

    @pl.when(step == 0)
    def _():
        for copy in copies:
            copy.start()
        inner_all[0] = inner_ref[...].astype(F32).T[0:count].astype(BF)
        inner_all[1] = inner_o_ref[...].astype(F32).T[0:count].astype(BF)
        back_all[...] = jnp.zeros_like(back_all)

    @pl.when(step < PAIRS)
    def _():
        attend_back_body(len_ref, *ins, dq_ref, dk_ref, dv_ref, *scratch)
        number = iota((count, LANES), 0) % 4
        upper = mm(inner_all[1], ba_ref[...])
        total = back_all[...]
        for index, ref in enumerate((dq_ref, dk_ref, dv_ref)):
            value = ref[...]
            upper = jnp.where(number == index, mm(inner_all[0], value), upper)
            total = total + mm_nt(value, bcat_ref[index])
        back_all[...] = total
        at = width + step * LANES
        acc_ref[:, pl.ds(pl.multiple_of(at, LANES), LANES)] = upper

    @pl.when(step == PAIRS)
    def _():
        back = back_all[...].astype(BF)
        back_ref[...] = back
        back_t = (back.astype(F32) + din_ref[...].astype(F32)).T[0:count].astype(BF)
        for copy in copies:
            copy.wait()
        number = iota((count, width), 0) % 4
        half = back_t.shape[1] // 2

        def down(rows_ref):
            return mm(back_t[:, :half], rows_ref[:half]) + mm(back_t[:, half:], rows_ref[half:])

        acc_ref[:, 0:width] = jnp.where(number < 3, down(normed_all), down(mixed_all))
        pack_grads(packed, id_ref, acc_ref, grad_ref)


def attend_back_call(
    packed, length, ids, q2, keys, values, mixed, back, coarse, fine, bcat, inner, inner_o, din, ba,
    normed,
):
    tok_count, width = keys.shape
    column = pl.BlockSpec((tok_count, LANES), lambda i: (0, jnp.minimum(i, PAIRS - 1)))
    grad_shape = (16 * RANK, width // 2 + LANES) if packed else (4 * RANK, 2 * width)
    return pl.pallas_call(
        functools.partial(attend_back_all_body, packed),
        grid=(PAIRS + 1,),
        in_specs=[
            smem(), smem(),
            pl.BlockSpec((2 * LANES, tok_count), lambda i: (jnp.minimum(i, PAIRS - 1), 0)), column,
            column, column, column, whole(coarse.shape), whole(fine.shape),
            pl.BlockSpec((4, LANES, LANES), lambda i: (0, 0, jnp.minimum(i, PAIRS - 1))),
            whole(inner.shape), whole(inner_o.shape), whole(din.shape), column,
            pl.BlockSpec(memory_space=pl.ANY), pl.BlockSpec(memory_space=pl.ANY),
        ],
        out_specs=[column] * 3 + [whole((tok_count, LANES)), whole(grad_shape)],
        out_shape=[shape_of(tok_count, width)] * 3
        + [shape_of(tok_count, LANES), shape_of(*grad_shape)],
        scratch_shapes=[
            pltpu.VMEM((2, LANES, tok_count), F32), pltpu.VMEM((2, tok_count, LANES), F32),
            pltpu.VMEM((2, 4 * RANK, tok_count), BF), pltpu.VMEM((tok_count, LANES), F32),
            pltpu.VMEM((4 * RANK, 2 * width), F32), pltpu.VMEM((tok_count, width), BF),
            pltpu.VMEM((tok_count, width), BF), pltpu.SemaphoreType.DMA((2,)),
        ],
        compiler_params=PARAMS,
        cost_estimate=cost(12),
        name="attention_backward",
    )(
        length, ids, q2, keys, values, mixed, back, coarse, fine, bcat, inner, inner_o, din, ba,
        normed, mixed,
    )


def post_body(
    local, group, me_ref, mixed_ref, x_ref, wo_ref, acat_ref, bcat_ref, gain_ref, read_ref, mix_ref,
    prev_ref, routes_ref, slot_ref, hidden_ref, ei_ref, inner_ref, data_ref, cols_ref,
):
    reader = read_ref[0:READ_VECTOR].astype(BF)

    def stages(at):
        mixed = mixed_ref[at]
        inner = mm(mixed, acat_ref[...]).astype(BF)
        inner_ref[at] = inner
        yield
        hidden = x_ref[at].astype(F32) + (mm(mixed, wo_ref[...]) + mm(inner, bcat_ref[0]))
        hidden_ref[at] = hidden
        yield
        scale = lax.rsqrt(jnp.mean(hidden * hidden, axis=-1, keepdims=True) + EPSILON)
        ei = (hidden * scale * gain_ref[1:2, :]).astype(BF)
        ei_ref[at] = ei
        yield
        read = mm_nt(reader, ei)
        yield
        logits = read[0:16]
        for index in range(EXPERTS + 4):
            logits = logits + mix_ref[:, index : index + 1] * prev_ref[index : index + 1, at]
        first, second = routes_ref[0:1, at].astype(F32), routes_ref[1:2, at].astype(F32)
        number = iota((16, TILE), 0).astype(F32)
        one = jnp.sum(jnp.where(number == first, logits, 0.0), axis=0, keepdims=True)
        two = jnp.sum(jnp.where(number == second, logits, 0.0), axis=0, keepdims=True)
        top = jnp.maximum(one, two)
        one, two = jnp.exp(one - top), jnp.exp(two - top)
        gate_a, gate_b = one / (one + two), two / (one + two)
        mixes = read[16:20] + read[24:28] + read[32:36]
        shares = []
        for index in range(2):
            left, right = mixes[2 * index : 2 * index + 1], mixes[2 * index + 1 : 2 * index + 2]
            top = jnp.maximum(left, right)
            left, right = jnp.exp(left - top), jnp.exp(right - top)
            shares += [left / (left + right), right / (left + right)]

        def both(value):
            return jnp.where(first == value, gate_a, 0.0) + jnp.where(second == value, gate_b, 0.0)

        gates = jnp.where(number == first, gate_a, 0.0) + jnp.where(number == second, gate_b, 0.0)
        beta_a, beta_b = both(EXPERTS + 2.0), both(EXPERTS + 3.0)
        keep = both(EXPERTS + 1.0) + beta_a * shares[0] + beta_b * shares[2]
        data_ref[0:8, at] = gates[0:8]
        tail = [gate_a, gate_b] + shares + [beta_a, beta_b]
        data_ref[8:16, at] = jnp.concatenate(tail, axis=0)
        yield
        slots = slot_ref[:, at].astype(F32)
        expert = iota((EXPERTS, TILE), 0)
        partner = jnp.bitwise_xor(expert // local, me_ref[0])
        base = ((expert % local) * (group * CAP) + partner * CAP).astype(F32)
        place = jnp.where(slots >= 0, slots + base + 1.0, 0.0)
        expert = expert.astype(F32)
        target_a = jnp.sum(jnp.where(expert == first, place, 0.0), axis=0, keepdims=True) - 1.0
        target_b = jnp.sum(jnp.where(expert == second, place, 0.0), axis=0, keepdims=True) - 1.0
        stack = jnp.concatenate(
            [jnp.zeros((VECTOR_ROW, TILE), F32), beta_a * shares[1], beta_b * shares[3]]
            + [jnp.zeros((2, TILE), F32), target_a, target_b, keep]
            + [jnp.zeros((LANES - KEEP_LANE - 1, TILE), F32)],
            axis=0,
        )
        cols_ref[at] = stack.T

    side_by_side(stages)


def post_send_body(local, group, steps, me_ref, id_ref, slot_all_ref, *refs):
    post_refs, out_refs, (ei_all, data_all) = refs[:16], refs[16:-2], refs[-2:]
    step = pl.program_id(0)

    @pl.when(step < steps)
    def _():
        post_body(local, group, me_ref, *post_refs)
        span = pl.ds(pl.multiple_of(step * STEP, STEP), STEP)
        ei_all[span] = post_refs[12][...]
        data_all[:, span] = post_refs[14][...]

    @pl.when(step >= steps)
    def _():
        send_rows(local, group, step - steps, me_ref, id_ref, slot_all_ref, data_all, ei_all, out_refs)


def post_call(
    local, group, me, ids, mixed, tokens, weight, acat, bcat, gains, reader, mixer, prev, routes, slots
):
    tok_count, width = tokens.shape
    steps = tok_count // STEP
    heights = [local * PIECE] * (group // 2) + [PIECE] * ((group - group // 2) * local)

    def rows_of(columns):
        return pl.BlockSpec((STEP, columns), lambda i: (jnp.minimum(i, steps - 1), 0))

    def lanes_of(height):
        return pl.BlockSpec((height, STEP), lambda i: (0, jnp.minimum(i, steps - 1)))

    return pl.pallas_call(
        functools.partial(post_send_body, local, group, steps),
        grid=(steps + group,),
        in_specs=[
            smem(), smem(), whole(slots.shape), rows_of(width), rows_of(width), whole(weight.shape),
            whole(acat.shape), pl.BlockSpec((1, LANES, width), lambda i: (3, 0, 0)), whole(gains.shape),
            whole(reader.shape), whole(mixer.shape), lanes_of(EXPERTS + 4), lanes_of(2),
            lanes_of(EXPERTS),
        ],
        out_specs=[
            rows_of(width), rows_of(width), rows_of(LANES), lanes_of(16), rows_of(LANES)
        ] + [whole((height, width)) for height in heights],
        out_shape=[
            shape_of(tok_count, width, dtype=F32), shape_of(tok_count, width),
            shape_of(tok_count, LANES), shape_of(16, tok_count, dtype=F32),
            shape_of(tok_count, LANES, dtype=F32),
        ] + [shape_of(height, width) for height in heights],
        scratch_shapes=[pltpu.VMEM((tok_count, width), BF), pltpu.VMEM((16, tok_count), F32)],
        compiler_params=PARAMS,
        cost_estimate=cost(14),
        name="after_attention",
    )(
        me, ids, slots, mixed, tokens, weight, acat, bcat, gains, reader, mixer, prev, routes, slots
    )


def expert_body(
    local_index, pair, per_owner, group, steps, has_grad, *refs
):
    count = len(pair)
    piece_refs, refs = refs[:count], refs[count:]
    cot_refs, refs = refs[:count], refs[count:]
    dn_ref, ou_ref, wg_hbm, wu_hbm, wd_hbm, up_hbm, od_hbm = refs[:7]
    refs = refs[7:]
    if has_grad:
        before_hbm, refs = refs[0], refs[1:]
    back_refs, refs = refs[:count], refs[count:]
    out_refs, refs = refs[:count], refs[count:]
    (
        grad_ref, x_ref, g_ref, gate_ref, pick_ref, dr_ref, zg_ref, zu_ref, dzd_ref, zgt_ref, zut_ref,
        dzdt_ref, racc_ref, xacc_ref, zd_acc, dzg_acc, dzu_acc, h_ref, dg_ref, du_ref, wg_all, wu_all,
        wd_all, up_all, od_all, sems, *rest
    ) = refs
    rows, width = x_ref.shape
    compact = group * RANK
    tile = h_ref.shape[1]

    def copies(step):
        span = pl.ds(pl.multiple_of(step * tile, tile), tile)
        pairs = (
            (wg_hbm.at[local_index, :, span], wg_all),
            (wu_hbm.at[local_index, :, span], wu_all),
            (wd_hbm.at[local_index, span, :], wd_all),
            (up_hbm.at[local_index, :, :, span], up_all),
            (od_hbm.at[local_index, span, :], od_all),
        )
        return [
            pltpu.make_async_copy(source, target.at[step], sems.at[step, place])
            for place, (source, target) in enumerate(pairs)
        ]

    def begin(step):
        for copy in copies(step):
            copy.start()

    begin(0)

    def fold(value):
        place = iota((compact, LANES), 0)
        block = per_owner * group
        inner = place // block * per_owner + place % per_owner
        folded = mm_nt(hot(iota((compact, LANES), 1) % RANK == inner), value)
        place = iota((compact, rows), 0)
        owner = place % block // per_owner
        mine = iota((compact, rows), 1) // CAP + pair[0]
        return jnp.where(mine == owner, folded, 0.0).astype(BF)

    def put(start, value):
        grad_ref[:, pl.ds(start, value.shape[1])] = value.astype(BF)

    for index in range(count):
        span = slice(index * CAP, index * CAP + CAP)
        x_ref[span] = piece_refs[index][0:CAP]
        g_ref[span] = cot_refs[index][...]
        meta = piece_refs[index][CAP:PIECE].astype(F32)
        gate = (meta[0:1] + meta[1:2] + meta[2:3])[:, 0 : 2 * LANES]
        gate_ref[span] = jnp.broadcast_to(gate, (LANES, 2 * LANES)).T[0:CAP]
        lane = (iota((CAP, LANES), 1) // RANK).astype(F32)
        pick_ref[span] = jnp.where(lane == meta[3:4, 0:LANES], 1.0, 0.0)
    chosen = pick_ref[...] > 0.0
    dr = (gate_ref[:, 0:1] * g_ref[...].astype(F32)).astype(BF)
    dr_ref[...] = dr
    zg = jnp.where(chosen, mm(x_ref[...], dn_ref[0]), 0.0).astype(BF)
    zu = jnp.where(chosen, mm(x_ref[...], dn_ref[1]), 0.0).astype(BF)
    dzd = jnp.where(chosen, mm_nt(dr, ou_ref[...]), 0.0).astype(BF)
    zg_ref[...] = zg
    zu_ref[...] = zu
    dzd_ref[...] = dzd
    zgt_ref[...] = fold(zg)
    zut_ref[...] = fold(zu)
    dzdt_ref[...] = fold(dzd)
    for ref in (racc_ref, xacc_ref, zd_acc, dzg_acc, dzu_acc):
        ref[...] = jnp.zeros_like(ref)

    total = steps * tile
    begin(1)
    if has_grad:
        before = pltpu.make_async_copy(before_hbm, rest[0], rest[1])
        before.start()

    def run(step, carry):
        for copy in copies(step):
            copy.wait()

        @pl.when(step + 2 < steps)
        def _():
            begin(step + 2)

        wg_ref, wu_ref, wd_ref = wg_all.at[step], wu_all.at[step], wd_all.at[step]
        up_ref, od_ref = up_all.at[step], od_all.at[step]
        gate = mm(x_ref[...], wg_ref[...]) + mm(zg_ref[...], up_ref[0])
        upper = mm(x_ref[...], wu_ref[...]) + mm(zu_ref[...], up_ref[1])
        share = 0.5 * jnp.tanh(0.5 * gate) + 0.5
        silu = gate * share
        active = (silu * upper).astype(BF)
        h_ref[...] = active
        back = mm_nt(dr_ref[...], wd_ref[...]) + mm_nt(dzd_ref[...], od_ref[...])
        du = (back * silu).astype(BF)
        dg = (back * upper * (share + silu * (1.0 - share))).astype(BF)
        du_ref[...] = du
        dg_ref[...] = dg
        racc_ref[...] += mm(active, wd_ref[...])
        zd_acc[...] += mm(active, od_ref[...])
        xacc_ref[...] += mm_nt(dg, wg_ref[...]) + mm_nt(du, wu_ref[...])
        dzg_acc[...] += mm_nt(dg, up_ref[0])
        dzu_acc[...] += mm_nt(du, up_ref[1])
        at = pl.multiple_of(step * tile, tile)
        put(at, mm(zgt_ref[...], dg_ref[...]))
        put(total + at, mm(zut_ref[...], du_ref[...]))
        put(2 * total + at, mm(dzdt_ref[...], h_ref[...]))
        return carry

    lax.fori_loop(0, steps, run, 0)
    chosen = pick_ref[...] > 0.0
    zd = jnp.where(chosen, zd_acc[...], 0.0).astype(BF)
    dzg = jnp.where(chosen, dzg_acc[...], 0.0).astype(BF)
    dzu = jnp.where(chosen, dzu_acc[...], 0.0).astype(BF)
    result = racc_ref[...] + mm(zd, ou_ref[...])
    gated = (gate_ref[:, 0:1] * result).astype(BF)
    product = g_ref[...].astype(F32) * result.astype(BF).astype(F32)
    dots = jnp.broadcast_to(jnp.sum(product, axis=-1, keepdims=True), (rows, LANES))
    back_rows = (xacc_ref[...] + mm_nt(dzg, dn_ref[0]) + mm_nt(dzu, dn_ref[1])).astype(BF)
    for index in range(count):
        span = slice(index * CAP, index * CAP + CAP)
        out_refs[index][...] = gated[span]
        back_refs[index][0:CAP, :] = back_rows[span]
        column = jnp.concatenate(
            [dots[span], jnp.zeros((2 * LANES - CAP, LANES), F32)], axis=0
        ).T[0:1]
        meta = jnp.concatenate(
            [piece.astype(F32) for piece in split3(column)]
            + [jnp.zeros((META - 3, 2 * LANES), F32)],
            axis=0,
        )
        meta = jnp.concatenate([meta, jnp.zeros((META, width - 2 * LANES), F32)], axis=1)
        back_refs[index][CAP:PIECE, :] = meta.astype(BF)
    base = 3 * total
    place = iota((compact, LANES), 0)
    owner = place % (per_owner * group) // per_owner
    ids = jnp.zeros((compact, LANES), F32)
    for index in range(count):
        meta = piece_refs[index][CAP:PIECE, 0:LANES].astype(F32)
        ids = jnp.where(owner == pair[index], meta[3:4], ids)
    put(base + 3 * width, ids)
    put(base, mm(fold(zd), dr_ref[...]))
    put(base + width, mm(fold(dzg), x_ref[...]))
    put(base + 2 * width, mm(fold(dzu), x_ref[...]))
    if has_grad:
        before.wait()
        grad_ref[...] = grad_ref[...] + rest[0][...]


def expert_call(index, pair, group, per_owner, pieces, cots, before, weights):
    gate_w, up_w, down_w, in_down, in_up, out_down, out_up = weights
    width, hidden = gate_w.shape[1:]
    rows = len(pair) * CAP
    steps = hidden // FTILE
    columns = 3 * hidden + 3 * width + LANES
    compact = group * RANK
    has_grad = before is not None
    return pl.pallas_call(
        functools.partial(expert_body, index, pair, per_owner, group, steps, has_grad),
        grid=(1,),
        in_specs=[
            pl.BlockSpec((PIECE, width), lambda f, row=piece.shape[0] // PIECE > 1: (index * row, 0))
            for piece in pieces
        ]
        + [pl.BlockSpec((CAP, width), lambda f: (index, 0))] * len(pair)
        + [
            pl.BlockSpec((None, 2, width, LANES), lambda f: (index, 0, 0, 0)),
            pl.BlockSpec((None, LANES, width), lambda f: (index, 0, 0)),
        ]
        + [pl.BlockSpec(memory_space=pl.ANY)] * 5
        + [pl.BlockSpec(memory_space=pl.ANY)] * has_grad,
        out_specs=[whole((PIECE, width))] * len(pair)
        + [whole((CAP, width))] * len(pair)
        + [whole((compact, columns))],
        out_shape=[shape_of(PIECE, width)] * len(pair)
        + [shape_of(CAP, width)] * len(pair)
        + [shape_of(compact, columns)],
        scratch_shapes=[pltpu.VMEM((rows, width), BF)] * 2
        + [pltpu.VMEM((rows, LANES), F32)] * 2
        + [pltpu.VMEM((rows, width), BF)]
        + [pltpu.VMEM((rows, LANES), BF)] * 3
        + [pltpu.VMEM((compact, rows), BF)] * 3
        + [pltpu.VMEM((rows, width), F32)] * 2
        + [pltpu.VMEM((rows, LANES), F32)] * 3
        + [pltpu.VMEM((rows, FTILE), BF)] * 3
        + [pltpu.VMEM((steps, width, FTILE), BF)] * 2
        + [
            pltpu.VMEM((steps, FTILE, width), BF), pltpu.VMEM((steps, 2, LANES, FTILE), BF),
            pltpu.VMEM((steps, FTILE, LANES), BF), pltpu.SemaphoreType.DMA((steps, 5)),
        ]
        + [pltpu.VMEM((compact, columns), BF), pltpu.SemaphoreType.DMA] * has_grad,
        compiler_params=PARAMS,
        cost_estimate=cost(rows / 21),
        name="expert_layer",
    )(
        *pieces, *cots, in_down, out_up, gate_w, up_w, down_w, in_up, out_down,
        *([before] if has_grad else []),
    )


def spread(cols, index, count):
    return iota((TILE, count), 1).astype(F32) == cols[:, index : index + 1]


def combine_body(
    pieces, len_ref, *refs
):
    back_refs = refs[:pieces]
    (
        routes_ref, data_ref, cols_ref, cot_ref, ei_ref, hidden_ref, gain_ref, wo_ref, acat_ref, bcat_ref,
        table_ref, read_ref, bh_ref, ba_ref, din_ref, bm_ref, back_all, dots_ref,
    ) = refs[pieces:]
    count = pieces * CAP

    @pl.when(pl.program_id(0) == 0)
    def _():
        for index, back_ref in enumerate(back_refs):
            back_all[index * CAP : index * CAP + CAP, :] = back_ref[0:CAP, :]
        dots = [back_ref[CAP:PIECE, 0:CAP].astype(F32) for back_ref in back_refs]
        dots = jnp.concatenate(dots, axis=1)
        dots_ref[...] = jnp.concatenate([dots, jnp.zeros_like(dots)], axis=0).astype(BF)

    table_high, table_low = split2(table_ref[...])
    stack = dots_ref[...]
    vectors = read_ref[READ_VECTOR:READ_ROWS].astype(BF)

    def stages(at):
        start = pl.program_id(0) * STEP + at.start
        cols = cols_ref[at]
        chosen_a = hot(spread(cols, TARGET_LANE, count))
        chosen_b = hot(spread(cols, TARGET_LANE + 1, count))
        yield
        routed_a = jnp.sum(mm_nt(stack, chosen_a)[0:8], axis=0, keepdims=True)
        routed_b = jnp.sum(mm_nt(stack, chosen_b)[0:8], axis=0, keepdims=True)
        cot = cot_ref[at]
        cot_f = cot.astype(F32)
        yield
        along_x = jnp.sum(cot_f * ei_ref[at].astype(F32), axis=-1, keepdims=True)
        along_x = jnp.broadcast_to(along_x, (TILE, LANES)).T[0:1]
        yield
        along_c = mm_nt(vectors, cot)
        along_a = along_c[0:1] + along_c[2:3] + along_c[4:5]
        along_b = along_c[1:2] + along_c[3:4] + along_c[5:6]
        yield
        both = chosen_a + chosen_b
        half = count // 2
        back = mm(both[:, :half], back_all[:half]) + mm(both[:, half:], back_all[half:])
        yield
        first, second = routes_ref[0:1, at].astype(F32), routes_ref[1:2, at].astype(F32)
        token = iota((1, TILE), 1) + start
        valid = jnp.where(token < len_ref[0], 1.0, 0.0)
        gate_a, gate_b = data_ref[8:9, at], data_ref[9:10, at]
        share = [data_ref[index : index + 1, at] for index in range(10, 14)]
        beta_a, beta_b = data_ref[14:15, at], data_ref[15:16, at]
        const_a = share[0] * along_x + share[1] * along_a
        const_b = share[2] * along_x + share[3] * along_b

        def here(route):
            return (
                jnp.where(route == EXPERTS + 1.0, along_x, 0.0)
                + jnp.where(route == EXPERTS + 2.0, const_a, 0.0)
                + jnp.where(route == EXPERTS + 3.0, const_b, 0.0)
            )

        dot_a, dot_b = routed_a + here(first), routed_b + here(second)
        mean = gate_a * dot_a + gate_b * dot_b
        chosen_grad_a = valid * gate_a * (dot_a - mean)
        chosen_grad_b = valid * gate_b * (dot_b - mean)
        number = iota((16, TILE), 0).astype(F32)
        logit_grads = jnp.where(number == first, chosen_grad_a, 0.0) + jnp.where(
            number == second, chosen_grad_b, 0.0
        )
        mixes = []
        for index, (beta, along) in enumerate(((beta_a, along_a), (beta_b, along_b))):
            left, right = share[2 * index], share[2 * index + 1]
            weighted = left * along_x + right * along
            mixes += [
                valid * beta * left * (along_x - weighted),
                valid * beta * right * (along - weighted),
            ]
        small = jnp.concatenate(
            [logit_grads] + mixes + [jnp.zeros((LANES - 20, TILE), F32)], axis=0
        ).T
        high, low = split2(small)
        yield
        inside = iota((TILE, 1), 0) + start < len_ref[0]
        grad = jnp.where(inside, cot_f, 0.0)
        back = back + mm(high, table_high) + mm(low, table_high) + mm(high, table_low)
        back = back + cols[:, KEEP_LANE : KEEP_LANE + 1] * grad
        yield
        hidden = hidden_ref[at]
        scale = lax.rsqrt(jnp.mean(hidden * hidden, axis=-1, keepdims=True) + EPSILON)
        normed = hidden * scale
        back = back * gain_ref[1:2, :]
        back = grad + scale * (back - normed * jnp.mean(back * normed, axis=-1, keepdims=True))
        bh_ref[at] = back
        rounded = back.astype(BF)
        ba_ref[at] = rounded
        yield
        inner = mm_nt(rounded, bcat_ref[0]).astype(BF)
        din_ref[at] = inner
        yield
        bm_ref[at] = (mm_nt(rounded, wo_ref[...]) + mm_nt(inner, acat_ref[...])).astype(BF)

    side_by_side(stages)


def combine_call(
    length, backs, routes, data, cols, cotangent, ei, hidden, gains, weight, acat, bcat, table,
    reader,
):
    tok_count, width = cotangent.shape
    pieces = len(backs)
    return pl.pallas_call(
        functools.partial(combine_body, pieces),
        grid=(tok_count // STEP,),
        in_specs=[smem()] + [whole(back.shape) for back in backs] + [
            wide(2), wide(16), tall(LANES), tall(width), tall(width), tall(width),
            whole(gains.shape), whole(weight.shape), whole(acat.shape),
            pl.BlockSpec((1, LANES, width), lambda i: (3, 0, 0)), whole(table.shape),
            whole(reader.shape),
        ],
        out_specs=[tall(width), tall(width), tall(LANES), tall(width)],
        out_shape=[
            shape_of(tok_count, width, dtype=F32), shape_of(tok_count, width),
            shape_of(tok_count, LANES), shape_of(tok_count, width),
        ],
        scratch_shapes=[
            pltpu.VMEM((pieces * CAP, width), BF), pltpu.VMEM((2 * META, pieces * CAP), BF)
        ],
        compiler_params=PARAMS,
        cost_estimate=cost(17),
        name="combine_backward",
    )(
        length, *backs, routes, data, cols, cotangent, ei, hidden, gains, weight, acat, bcat, table,
        reader,
    )


def result_body(pieces, len_ref, *refs):
    result_refs = refs[:pieces]
    cols_ref, ei_ref, hidden_ref, table_ref, out_ref, result_all = refs[pieces:]
    count = pieces * CAP

    @pl.when(pl.program_id(0) == 0)
    def _():
        for index, result_ref in enumerate(result_refs):
            result_all[index * CAP : index * CAP + CAP, :] = result_ref[...]

    table_high, table_low = split2(table_ref[...])

    def stages(at):
        cols = cols_ref[at]
        both = hot(spread(cols, TARGET_LANE, count) | spread(cols, TARGET_LANE + 1, count))
        yield
        half = count // 2
        mixture = mm(both[:, :half], result_all[:half]) + mm(both[:, half:], result_all[half:])
        yield
        high, low = split2(cols)
        mixture = mixture + mm(high, table_high) + mm(low, table_high) + mm(high, table_low)
        mixture = mixture + cols[:, KEEP_LANE : KEEP_LANE + 1] * ei_ref[at].astype(F32)
        yield
        inside = iota((TILE, 1), 0) + pl.program_id(0) * STEP + at.start < len_ref[0]
        out_ref[at] = (hidden_ref[at] + jnp.where(inside, mixture, 0.0)).astype(BF)

    side_by_side(stages)


def result_call(length, results, cols, ei, hidden, table):
    tok_count, width = ei.shape
    pieces = len(results)
    return pl.pallas_call(
        functools.partial(result_body, pieces),
        grid=(tok_count // STEP,),
        in_specs=[smem()] + [whole(result.shape) for result in results] + [
            tall(LANES), tall(width), tall(width), whole(table.shape),
        ],
        out_specs=tall(width),
        out_shape=shape_of(tok_count, width),
        scratch_shapes=[pltpu.VMEM((pieces * CAP, width), BF)],
        compiler_params=PARAMS,
        cost_estimate=cost(8),
        name="layer_output",
    )(length, *results, cols, ei, hidden, table)


def last_body(
    dq_ref, dk_ref, dv_ref, w_ref, acat_ref, back_ref, x_ref, bh_ref, gain_ref, out_ref
):
    def stages(at):
        parts = [mm_nt(back_ref[at], acat_ref[...])]
        for index, ref in enumerate((dq_ref, dk_ref, dv_ref)):
            parts.append(mm_nt(ref[at], w_ref[index]))
            yield
        total = parts[0] + parts[1] + parts[2] + parts[3]
        x = x_ref[at].astype(F32)
        scale = lax.rsqrt(jnp.mean(x * x, axis=-1, keepdims=True) + EPSILON)
        normed = x * scale
        back = total * gain_ref[0:1, :]
        back = scale * (back - normed * jnp.mean(back * normed, axis=-1, keepdims=True))
        out_ref[at] = (bh_ref[at] + back).astype(BF)

    side_by_side(stages)


def last_call(dq, dk, dv, weights, acat, back, tokens, bh, gains):
    tok_count, width = tokens.shape
    return pl.pallas_call(
        last_body,
        grid=(tok_count // STEP,),
        in_specs=[
            tall(width), tall(width), tall(width), whole(weights.shape), whole(acat.shape),
            tall(LANES), tall(width), tall(width), whole(gains.shape),
        ],
        out_specs=tall(width),
        out_shape=shape_of(tok_count, width),
        compiler_params=PARAMS,
        cost_estimate=cost(9),
        name="after_attention_backward",
    )(dq, dk, dv, weights, acat, back, tokens, bh, gains)


def exchange(value, axes):
    return lax.all_to_all(value, axes, split_axis=0, concat_axis=0, tiled=True)


def gather_all(value, axes, count):
    return exchange(jnp.broadcast_to(value[None], (count,) + value.shape), axes)


def swap(value, partner, group):
    if partner == 0:
        return value
    return lax.ppermute(value, "expert", [(index, index ^ partner) for index in range(group)])


def find_adapters(id_rows):
    count = id_rows.shape[0]
    padded = id_rows.astype(F32)
    if count % LANES:
        padded = jnp.concatenate([padded, jnp.zeros((-count % LANES, LANES), F32)], axis=0)
    return padded.T[0:1, 0:count].astype(jnp.int32)


def sum_expert_body(each, adapters, in_ref, out_ref):
    count, columns = in_ref.shape[0], out_ref.shape[1]
    found = find_adapters(in_ref[:, columns:])
    place = iota((adapters * each, count), 0)
    column = iota((adapters * each, count), 1)
    pick = hot((place // each == found) & (place % each == column % each))
    out_ref[...] = mm(pick, in_ref[:, 0:columns]).astype(BF)


def exchange_expert_grads(grads, group, owners):
    split = min(RANK, owners)
    each, parts = RANK // split, owners // split
    columns = (grads.shape[1] - LANES) // parts
    pieces = grads.reshape(split, each * group, grads.shape[1])
    if parts > 1:
        ids = jnp.broadcast_to(pieces[:, None, :, parts * columns :], (split, parts, each * group, LANES))
        pieces = pieces[:, :, : parts * columns].reshape(split, each * group, parts, columns)
        pieces = jnp.concatenate([pieces.transpose(0, 2, 1, 3), ids], axis=-1)
        pieces = pieces.reshape(owners, each * group, columns + LANES)
    return exchange(pieces, "dp").reshape(owners * group * each, columns + LANES)


def sum_expert_grads(got, adapters, owners):
    columns = got.shape[1] - LANES
    each = RANK // min(RANK, owners)
    return pl.pallas_call(
        functools.partial(sum_expert_body, each, adapters),
        out_shape=shape_of(adapters * each, columns),
        compiler_params=PARAMS,
        cost_estimate=cost(2.2),
        name="expert_gradient_part",
    )(got)


def finish_expert_body(split, adapters, hidden, in_ref, *refs):
    down_ref, up_ref, out_down_ref, out_up_ref = refs[-4:]
    each = RANK // split
    rows = adapters * each
    count = split * rows
    width = out_up_ref.shape[1]

    def place(value):
        return value // each % adapters * RANK + value // (adapters * each) * each + value % each

    move = hot(iota((count, count), 0) == place(iota((count, count), 1)))
    back = hot(iota((count, count), 1) == place(iota((count, count), 0)))

    def part(start, size):
        span = slice(start, start + size)
        rows_of = [in_ref[owner, :, span] for owner in range(split)]
        return jnp.concatenate(rows_of, axis=0)

    for index in range(2):
        up_ref[index] = mm(move, part(index * hidden, hidden))
    out_down_ref[...] = mm_tn(part(2 * hidden, hidden), back)
    base = 3 * hidden
    out_up_ref[...] = mm(move, part(base, width))
    for index in range(2):
        base += width
        down_ref[index] = mm_tn(part(base, width), back)


def finish_expert_call(index, local, everything, outs, adapters, width, hidden):
    owners, rows, columns = everything.shape
    total = adapters * RANK
    shapes = [(local, 2, width, total), (local, 2, total, hidden), (local, hidden, total),
              (local, total, width)]
    specs = [
        pl.BlockSpec((None,) + shape[1:], lambda *_, rank=len(shape): (index,) + (0,) * (rank - 1))
        for shape in shapes
    ]
    return pl.pallas_call(
        functools.partial(finish_expert_body, owners, adapters, hidden),
        grid=(1,),
        in_specs=[whole(everything.shape)] + [pl.BlockSpec(memory_space=pl.ANY)] * len(outs),
        out_specs=specs,
        out_shape=[shape_of(*shape, dtype=F32) for shape in shapes],
        input_output_aliases={1 + place: place for place in range(len(outs))},
        compiler_params=PARAMS,
        cost_estimate=cost(4),
        name="expert_gradient_sums",
    )(everything, *outs)


def spread_expert_grads(own, adapters, owners):
    split = min(RANK, owners)
    each, parts = RANK // split, owners // split
    everything = gather_all(own, "dp", owners)
    everything = everything.reshape(split, parts, adapters, each, own.shape[1])
    everything = everything.transpose(2, 0, 3, 1, 4)
    return everything.reshape(adapters * RANK, parts * own.shape[1]).astype(F32)


def expert_sums(owned, adapters, owners, width, hidden):
    sums = [spread_expert_grads(value, adapters, owners) for value in owned]
    base = 3 * hidden
    up = [[value[:, 0:hidden], value[:, hidden : 2 * hidden]] for value in sums]
    down = [
        [value[:, base + width * part : base + width * (part + 1)].T for part in (1, 2)]
        for value in sums
    ]
    return (
        jnp.stack([jnp.stack(value) for value in down]),
        jnp.stack([jnp.stack(value) for value in up]),
        jnp.stack([value[:, 2 * hidden : base].T for value in sums]),
        jnp.stack([value[:, base : base + width] for value in sums]),
    )


def finish_adapter_body(adapters, me_ref, *refs):
    piece_refs, (down_ref, up_ref, in_ref) = refs[:-3], refs[-3:]
    half = in_ref.shape[3]
    owners, group = piece_refs[0].shape[0], len(piece_refs)
    for other in range(group):
        place = jnp.bitwise_xor(me_ref[0], other)
        for owner in range(owners):
            in_ref[owner * (group // 2) + place // 2, place % 2] = piece_refs[other][owner]
    count = RANK * adapters

    def place(value):
        return value % adapters * RANK + value // adapters

    move = hot(iota((count, count), 0) == place(iota((count, count), 1)))
    back = hot(iota((count, count), 1) == place(iota((count, count), 0)))
    for part in range(2):
        span = slice(part * half, part * half + half)
        for kind in range(2):
            for index in range(4):
                first = (kind * 4 + index) * adapters
                rows = in_ref[:, part, first : first + adapters, :].astype(F32)
                rows = rows.reshape(count, half).astype(BF)
                if kind == 0:
                    down_ref[index, span, :] = mm_tn(rows, back)
                else:
                    up_ref[index, :, span] = mm(move, rows)


def sum_adapter_body(kinds, adapters, in_ref, out_ref):
    count, columns = in_ref.shape[0], out_ref.shape[-1]
    found = find_adapters(in_ref[:, columns:])
    place = iota((adapters * kinds, count), 0)
    column = iota((adapters * kinds, count), 1)
    pick = hot((place % adapters == found) & (place // adapters == column % kinds))
    own = mm(pick, in_ref[:, 0:columns]).astype(BF)
    for index in range(out_ref.shape[0]):
        out_ref[index] = own


def adapter_sums(grads, meanwhile, later, finish, ids, adapters, owners, group, width):
    axes, everyone = ("dp", "expert"), owners * group
    if everyone == 2 * RANK and group == 4:
        kinds = 8
        got = exchange(grads.reshape(everyone, kinds, grads.shape[1]), axes)
        got, meanwhile = lax.optimization_barrier((got, meanwhile))
        own = pl.pallas_call(
            functools.partial(sum_adapter_body, kinds, adapters),
            out_shape=shape_of(owners, kinds * adapters, width // 2),
            compiler_params=PARAMS,
            cost_estimate=cost(2.0),
            name="adapter_gradient_part",
        )(got.reshape(everyone * kinds, grads.shape[1]))
        mine = exchange(own, "dp")
        mine, later = lax.optimization_barrier((mine, later))
        across = swap(mine, 2, group)
        full = [mine, swap(mine, 1, group), across, swap(across, 1, group)]
        full, later = lax.optimization_barrier((full, finish(later)))
        total = adapters * RANK
        down, upper = pl.pallas_call(
            functools.partial(finish_adapter_body, adapters),
            in_specs=[smem()] + [pl.BlockSpec(memory_space=pltpu.VMEM)] * group,
            out_shape=[shape_of(4, width, total, dtype=F32), shape_of(4, total, width, dtype=F32)],
            scratch_shapes=[pltpu.VMEM((RANK, 2, kinds * adapters, width // 2), BF)],
            compiler_params=PARAMS,
            cost_estimate=cost(3.6),
            name="adapter_gradient_sums",
        )(lax.axis_index("expert").reshape(1).astype(jnp.int32), *full)
        return down, upper, meanwhile, later
    later = finish(later)
    all_ids = exchange(jnp.broadcast_to(ids, (everyone,)), axes)
    pieces = grads.reshape(everyone, RANK * 4 * 2 * width // everyone)
    got = exchange(pieces, axes)
    pick = (jnp.arange(adapters, dtype=jnp.int32)[:, None] == all_ids[None, :]).astype(BF)
    own = jnp.dot(pick, got, preferred_element_type=F32).astype(BF)
    full = gather_all(own, axes, everyone)
    full = full.reshape(RANK, everyone // RANK, adapters, -1).transpose(2, 0, 1, 3)
    full = full.reshape(adapters * RANK, 4, 2, width).astype(F32)
    return full[:, :, 0].transpose(1, 2, 0), full[:, :, 1].transpose(1, 0, 2), meanwhile, later


def body(
    tokens,
    cotangent,
    lengths,
    adapter_ids,
    routes,
    prev_logits,
    norm_gains,
    input_weights,
    output_weight,
    adapter_down,
    adapter_up,
    router,
    residual_mix,
    constant_mix,
    constant_vectors,
    expert_gate,
    expert_up,
    expert_down,
    expert_adapter_down,
    expert_adapter_up,
    output_adapter_down,
    output_adapter_up,
):
    tok_count, width = tokens.shape
    hidden_width = expert_gate.shape[2]
    group, owners = lax.axis_size("expert"), lax.axis_size("dp")
    local = expert_gate.shape[0]
    adapters = adapter_down.shape[-1] // RANK
    angles = [jnp.asarray(table) for table in turn_tables(tok_count)]
    weights = (
        expert_gate, expert_up, expert_down, expert_adapter_down, expert_adapter_up,
        output_adapter_down, output_adapter_up,
    )
    per_owner = RANK // min(RANK, owners)
    everyone = owners * group
    me = lax.axis_index("expert")

    me = me.reshape(1).astype(jnp.int32)

    routes, prev_logits = routes.T, prev_logits.T
    slots, *grad_sends = route_call(local, group, lengths, me, routes, cotangent)
    cots = [swap(value, partner, group) for partner, value in enumerate(grad_sends)]
    normed, inner, acat, bcat, table, mixer, reader, keys, values, mixed, q2 = pre_attend_call(
        lengths, adapter_ids, tokens, norm_gains, input_weights, adapter_down, adapter_up, *angles,
        router.T, constant_mix.T, constant_vectors, residual_mix,
    )
    mixed, cots = lax.optimization_barrier((mixed, cots))
    hidden, ei, inner_o, data, cols, *sends = post_call(
        local, group, me, adapter_ids, mixed, tokens, output_weight, acat, bcat, norm_gains, reader, mixer, prev_logits,
        routes, slots,
    )
    near, far = tuple(range(group // 2)), tuple(range(group // 2, group))
    sent_near = [swap(sends[partner], partner, group) for partner in near]
    sent_far = []
    for index in range(local):
        pieces = [sends[group // 2 + place * local + index] for place in range(len(far))]
        if index > 0:
            pieces, sent_near = lax.optimization_barrier((pieces, sent_near))
        sent_far.append([swap(piece, partner, group) for piece, partner in zip(pieces, far)])
    backs = [[None] * group for _ in range(local)]
    results = [[None] * group for _ in range(local)]
    calls = []
    for index in range(local - 1):
        calls += [(index, near), (index, far)]
    calls += [(local - 1, near[1:] + far), (local - 1, near[:1])]
    grads, owned, parts = [None] * local, [], []
    sums = functools.partial(sum_expert_grads, adapters=adapters, owners=owners)
    last = None
    for index, some in calls:
        pieces = [
            sent_near[partner] if partner in near else sent_far[index][partner - len(near)]
            for partner in some
        ]
        if last is not None:
            pieces, last = lax.optimization_barrier((pieces, last))
        if (index, some) == calls[-1]:
            parts, last = lax.optimization_barrier((parts, last))
            owned = [sums(part) for part in parts]
            pieces, backs[:index], owned = lax.optimization_barrier((pieces, backs[:index], owned))
        outs = expert_call(
            index, some, group, per_owner, pieces, [cots[partner] for partner in some], grads[index], weights
        )
        grads[index] = last = outs[-1]
        for place, partner in enumerate(some):
            backs[index][partner] = swap(outs[place], partner, group)
            results[index][partner] = outs[len(some) + place]
        if index < local - 1 and some == far:
            parts.append(exchange_expert_grads(last, group, owners))
    backs = [value for some in backs for value in some]
    parts.append(exchange_expert_grads(last, group, owners))
    gather = functools.partial(lax.all_gather, axis_name="dp", axis=0, tiled=False)
    if owners <= RANK:
        owned = [gather(own) for own in owned]
    back_hidden, back_attention, back_inner_o, back_mixed = combine_call(
        lengths, backs, routes, data, cols, cotangent, ei, hidden, norm_gains, output_weight, acat, bcat,
        table, reader,
    )
    flat = [value for some in results for value in some]
    flat, back_mixed = lax.optimization_barrier((flat, back_mixed))
    flat = [swap(value, place % group, group) for place, value in enumerate(flat)]

    packed = everyone == 2 * RANK and group == 4
    dq, dk, dv, back_inner, adapter_grads = attend_back_call(
        packed, lengths, adapter_ids, q2, keys, values, mixed, back_mixed, *angles, bcat, inner, inner_o,
        back_inner_o, back_attention, normed,
    )
    parts[-1], adapter_grads, flat, owned = lax.optimization_barrier(
        (parts[-1], adapter_grads, flat, owned)
    )
    own = sums(parts[-1])
    adapter_grads, own, flat = lax.optimization_barrier((adapter_grads, own, flat))
    owned.append(gather(own) if owners <= RANK else own)
    layer_out = result_call(lengths, flat, cols, ei, hidden, table)
    input_back = last_call(
        dq, dk, dv, input_weights, acat, back_inner, tokens, back_hidden, norm_gains
    )
    outs = []
    if owners <= RANK:
        for index, own in enumerate(owned[:-1]):
            outs = finish_expert_call(index, local, own, outs, adapters, width, hidden_width)
    def finish(later):
        input_back, outs = later
        if owners <= RANK:
            return input_back, finish_expert_call(
                local - 1, local, owned[-1], outs, adapters, width, hidden_width
            )
        return input_back, expert_sums(owned, adapters, owners, width, hidden_width)

    down_sum, upper_sum, layer_out, (input_back, outs) = adapter_sums(
        adapter_grads, layer_out, (input_back, outs), finish, adapter_ids, adapters, owners, group, width
    )
    in_down_sum, in_up_sum, out_down_sum, out_up_sum = outs
    return (
        layer_out,
        input_back,
        down_sum,
        upper_sum,
        in_down_sum,
        in_up_sum,
        out_down_sum,
        out_up_sum,
    )


def solution(mesh):
    tokens_spec, copied = P(("dp", "expert"), None), P()
    owned = P("expert")
    placed = (
        (tokens_spec, tokens_spec, P(("dp", "expert")), P(("dp", "expert")), tokens_spec, tokens_spec)
        + (copied,) * 9
        + (owned,) * 7
    )
    return jax.shard_map(
        body,
        mesh=mesh,
        in_specs=placed,
        out_specs=(tokens_spec, tokens_spec, copied, copied) + (owned,) * 4,
        check_vma=False,
    )
```

```python
import functools
import math

import jax
import jax.numpy as jnp
import numpy as np
from jax import lax
from jax.experimental import pallas as pl
from jax.experimental.pallas import tpu as pltpu
from jax.sharding import PartitionSpec as P

HEADS = 12
HD = 64
EXPERTS = 8
RANK = 16
CAP = 192
EPSILON = 1e-06
F32 = jnp.float32
BF = jnp.bfloat16
NEG = -1e30
LANES = 128
TILE = 256
STEP = 512
FTILE = 512
PAIRS = HEADS // 2
PARAMS = pltpu.CompilerParams(vmem_limit_bytes=67043328)
META = 8
MIX_ROW = 16
VECTOR_ROW = 20
TARGET_LANE = 24
KEEP_LANE = 26
READ_VECTOR = 48
READ_ROWS = 64
PIECE = CAP + META


def mm(left, right):
    return jnp.dot(left, right, preferred_element_type=F32)


def mm_nt(left, right):
    return lax.dot_general(left, right, (((1,), (1,)), ((), ())), preferred_element_type=F32)


def mm_tn(left, right):
    return lax.dot_general(left, right, (((0,), (0,)), ((), ())), preferred_element_type=F32)


def iota(shape, axis):
    return lax.broadcasted_iota(jnp.int32, shape, axis)


def hot(condition):
    return jnp.where(condition, 1.0, 0.0).astype(BF)


def split2(value):
    high = value.astype(BF)
    return high, (value - high.astype(F32)).astype(BF)


def split3(value):
    high = value.astype(BF)
    rest = value - high.astype(F32)
    middle = rest.astype(BF)
    return high, middle, (rest - middle.astype(F32)).astype(BF)


def whole(shape):
    zeros = (0,) * len(shape)
    return pl.BlockSpec(shape, lambda *_: zeros)


def smem():
    return pl.BlockSpec(memory_space=pltpu.SMEM)


def tall(width):
    return pl.BlockSpec((STEP, width), lambda i: (i, 0))


def wide(height):
    return pl.BlockSpec((height, STEP), lambda i: (0, i))


def tile(width):
    return pl.BlockSpec((TILE, width), lambda i: (i, 0))


def side_by_side(stages):
    running = [stages(slice(start, start + TILE)) for start in range(0, STEP, TILE)]
    while running:
        running = [stage for stage in running if next(stage, True) is None]


def shape_of(*shape, dtype=BF):
    return jax.ShapeDtypeStruct(shape, dtype)


def cost(microseconds):
    return pl.CostEstimate(flops=int(microseconds * 1e+09), bytes_accessed=0, transcendentals=0)


@functools.lru_cache(maxsize=None)
def turn_tables(length_in):
    half = HD // 2
    inverse = np.exp(np.arange(half, dtype=np.float64) * (-2.0 * math.log(10000.0) / HD))

    def table(positions):
        angles = np.tile(positions[:, None] * inverse[None, :], (1, 4))
        return np.stack([np.cos(angles), np.sin(angles)]).astype(np.float32)

    return table(np.arange(0.0, length_in, 32)), table(np.arange(0.0, 32))


def turn_rows(coarse_ref, fine_ref, first, count):
    fine_cos, fine_sin = fine_ref[0], fine_ref[1]
    sign = jnp.where(iota((32, LANES), 1) % HD < HD // 2, -1.0, 1.0)
    signed_cos, signed_sin = fine_cos * sign, fine_sin * sign
    cosines, sines = [], []
    for index in range(count // 32):
        row = first // 32 + index
        coarse_cos, coarse_sin = coarse_ref[0, pl.ds(row, 1), :], coarse_ref[1, pl.ds(row, 1), :]
        cosines.append(coarse_cos * fine_cos - coarse_sin * fine_sin)
        sines.append(coarse_sin * signed_cos + coarse_cos * signed_sin)
    return jnp.concatenate(cosines, axis=0), jnp.concatenate(sines, axis=0)


def rope(value, cosine, sine):
    first = iota(value.shape, 1) % HD < HD // 2
    turned = jnp.where(first, pltpu.roll(value, LANES - HD // 2, 1), pltpu.roll(value, HD // 2, 1))
    return value * cosine + turned * sine


def find_slots(length, routes_ref, slot_ref):
    tok_count = slot_ref.shape[1]
    before = hot(iota((TILE, TILE), 0) < iota((TILE, TILE), 1))
    carry = jnp.zeros((2 * EXPERTS, 1), F32)
    for start in range(0, tok_count, TILE):
        span = slice(start, start + TILE)
        expert = iota((2 * EXPERTS, TILE), 0)
        token = iota((2 * EXPERTS, TILE), 1) + start
        named = (routes_ref[0:1, span] == expert) | (routes_ref[1:2, span] == expert)
        hit = named & (token < length) & (expert < EXPERTS)
        hits = jnp.where(hit, 1.0, 0.0)
        slots = mm(hits.astype(BF), before) + carry
        carry = carry + jnp.sum(hits, axis=1, keepdims=True)
        slot_ref[:, span] = jnp.where(hit, slots, -1.0)[:EXPERTS].astype(jnp.int32)


def pick_rows(slot_ref, step, me, local):
    first = jnp.bitwise_xor(step, me) * local
    place = iota((CAP, slot_ref.shape[1]), 0)
    return first, [hot(place == slot_ref[pl.ds(first + index, 1), :]) for index in range(local)]


def pick_source(chosen, source_ref):
    half = source_ref.shape[0] // 2
    return mm(chosen[:, :half], source_ref[:half]) + mm(chosen[:, half:], source_ref[half:])


def store_piece(out_refs, step, other, index, value, start):
    @pl.when(step == other)
    def _():
        out_refs[index][start : start + value.shape[0], :] = value


def route_body(local, group, len_ref, me_ref, routes_ref, source_ref, slot_ref, *out_refs):
    step = pl.program_id(0)

    @pl.when(step == 0)
    def _():
        find_slots(len_ref[0], routes_ref, slot_ref)

    _, chosen = pick_rows(slot_ref, step, me_ref[0], local)
    rows = pick_source(jnp.concatenate(chosen, axis=0), source_ref).astype(BF)
    for other in range(group):
        store_piece(out_refs, step, other, other, rows, 0)


def route_call(local, group, length, me, routes, source):
    tok_count, width = source.shape
    return pl.pallas_call(
        functools.partial(route_body, local, group),
        grid=(group,),
        in_specs=[smem(), smem(), whole(routes.shape), whole(source.shape)],
        out_specs=[whole((EXPERTS, tok_count))] + [whole((local * CAP, width))] * group,
        out_shape=[shape_of(EXPERTS, tok_count, dtype=jnp.int32)]
        + [shape_of(local * CAP, width)] * group,
        compiler_params=PARAMS,
        cost_estimate=cost(6.5),
        name="route_rows",
    )(length, me, routes, source)


def send_rows(local, group, partner, me_ref, id_ref, slot_ref, data_ref, source_ref, out_refs):
    width = source_ref.shape[1]
    first, chosen = pick_rows(slot_ref, partner, me_ref[0], local)
    rows = pick_source(jnp.concatenate(chosen, axis=0), source_ref).astype(BF)
    for index in range(local):
        pieces = split3(data_ref[pl.ds(first + index, 1), :])
        stack = jnp.concatenate(
            [piece.astype(F32) for piece in pieces]
            + [jnp.zeros((13, chosen[index].shape[1]), F32)],
            axis=0,
        ).astype(BF)
        gates = mm_nt(stack, chosen[index])[0:META]
        gates = jnp.where(iota(gates.shape, 0) == 3, id_ref[0].astype(F32), gates)
        meta = jnp.concatenate([gates, jnp.zeros((META, width - CAP), F32)], axis=1)
        kept = rows[index * CAP : index * CAP + CAP]
        for other in range(group):
            far = other >= group // 2
            place = group // 2 + (other - group // 2) * local + index if far else other
            start = 0 if far else index * PIECE
            store_piece(out_refs, partner, other, place, kept, start)
            store_piece(out_refs, partner, other, place, meta.astype(BF), start + CAP)


def pre_body(
    id_ref, x_ref, gain_ref, w_ref, ad_ref, au_ref, coarse_ref, fine_ref, router_ref, cmix_ref, vec_ref,
    resid_ref, normed_ref, inner_ref, acat_ref, bcat_ref, table_ref, mix_ref, read_ref, q_ref, k_ref,
    v_ref, square_ref,
):
    @pl.when(pl.program_id(0) == 0)
    def _():
        first = RANK * id_ref[0]
        total = None
        for index in range(4):
            row, column = iota((LANES, LANES), 0), iota((LANES, LANES), 1)
            place = hot((row >= first) & (row < first + RANK) & (column == (row - first) * 4 + index))
            part = mm(ad_ref[index], place)
            total = part if total is None else total + part
            place = hot(
                (column >= first) & (column < first + RANK) & (row == (column - first) * 4 + index)
            )
            bcat_ref[index] = mm(place, au_ref[index]).astype(BF)
        acat_ref[...] = total.astype(BF)
        table_ref[...] = jnp.zeros_like(table_ref)
        table_ref[0 : EXPERTS + 4, :] = router_ref[...].astype(F32)
        table_ref[MIX_ROW : MIX_ROW + 4, :] = cmix_ref[...]
        table_ref[VECTOR_ROW : VECTOR_ROW + 2, :] = vec_ref[...]
        read_ref[...] = jnp.zeros_like(read_ref)
        read_ref[0 : EXPERTS + 4, :] = router_ref[...].astype(F32)
        for place, piece in enumerate(split3(cmix_ref[...])):
            read_ref[16 + 8 * place : 20 + 8 * place, :] = piece.astype(F32)
        for place, piece in enumerate(split3(vec_ref[...])):
            read_ref[READ_VECTOR + 2 * place : READ_VECTOR + 2 * place + 2, :] = piece.astype(F32)
        square_ref[...] = jnp.zeros_like(square_ref)
        square_ref[0 : EXPERTS + 4, 0 : EXPERTS + 4] = resid_ref[...]
        mix_ref[...] = square_ref[...].T[0:16]

    def stages(at):
        x = x_ref[at].astype(F32)
        scale = lax.rsqrt(jnp.mean(x * x, axis=-1, keepdims=True) + EPSILON)
        normed = (x * scale * gain_ref[0:1, :]).astype(BF)
        normed_ref[at] = normed
        yield
        inner = mm(normed, acat_ref[...]).astype(BF)
        inner_ref[at] = inner
        yield
        for index, out_ref in enumerate((q_ref, k_ref, v_ref)):
            value = mm(normed, w_ref[index]) + mm(inner, bcat_ref[index])
            yield
            rows = pl.ds(pl.multiple_of(pl.program_id(0) * STEP + at.start, TILE), TILE)
            if index == 2:
                for pair in range(PAIRS):
                    span = slice(pair * LANES, pair * LANES + LANES)
                    out_ref[pair, rows] = value[:, span].astype(BF)
                continue
            cosine, sine = turn_rows(coarse_ref, fine_ref, pl.program_id(0) * STEP + at.start, TILE)
            for pair in range(PAIRS):
                span = slice(pair * LANES, pair * LANES + LANES)
                turned = rope(value[:, span], cosine, sine).astype(BF)
                if index == 0:
                    turned = (turned.astype(F32) * HD**-0.5).astype(BF)
                out_ref[pair, rows] = turned
            yield

    side_by_side(stages)


def attend_body(len_ref, q_ref, k_ref, v_ref, mixed_ref, q2_ref):
    tok_count = q_ref.shape[0]
    lane = iota((tok_count, LANES), 1)
    hidden_key = iota((tok_count, LANES), 0) >= len_ref[0]
    row = iota((LANES, tok_count), 0)
    row_tile = row[:, :TILE]
    causal = iota((TILE, TILE), 0) <= iota((TILE, TILE), 1)
    queries_t = q_ref[...].astype(F32).T
    values_t = v_ref[...].astype(F32).T
    keys = k_ref[...].astype(F32)
    heads = []
    for head in range(2):
        spare = HD * (1 - head)
        bias = jnp.where((lane == spare) & hidden_key, NEG, 0.0)
        one = jnp.where(row == spare, 1.0, 0.0)
        own = row // HD == head
        heads.append(
            (
                jnp.where(lane // HD == head, keys, bias).astype(BF),
                jnp.where(own, queries_t, one).astype(BF),
                jnp.where(own, values_t, one).astype(BF),
            )
        )
    units = [(start, head) for start in range(0, tok_count, TILE) for head in range(2)]

    def score(unit):
        start, head = unit
        keys, queries, _ = heads[head]
        part = queries[:, start : start + TILE]
        near = mm(keys[start : start + TILE], part)
        return near, mm(keys[:start], part) if start else None

    outs = {}
    waiting = score(units[0])
    for index, (start, head) in enumerate(units):
        near, far = waiting
        waiting = score(units[index + 1]) if index + 1 < len(units) else None
        spare = HD * (1 - head)
        _, queries, values = heads[head]
        near = jnp.where(causal, near, NEG)
        top = jnp.max(near, axis=0, keepdims=True)
        if start:
            top = jnp.maximum(top, jnp.max(far, axis=0, keepdims=True))
        mixed = mm(values[:, start : start + TILE], jnp.exp(near - top).astype(BF))
        if start:
            mixed = mixed + mm(values[:, :start], jnp.exp(far - top).astype(BF))
        total = mixed[spare : spare + 1]
        outs[head] = mixed * (1.0 / total)
        kept = queries[:, start : start + TILE]
        logs = jnp.zeros((LANES, TILE), F32)
        for offset, piece in enumerate(split3(top + jnp.log(total))):
            logs = jnp.where(row_tile == spare + 1 + offset, piece.astype(F32), logs)
        q2_ref[head * LANES : head * LANES + LANES, start : start + TILE] = kept + logs.astype(BF)
        if head == 1:
            mixed = jnp.where(row_tile < HD, outs[0], outs[1])
            mixed_ref[start : start + TILE] = mixed.T.astype(BF)


def pre_attend_body(steps, len_ref, *refs):
    pre_ins, pre_outs = refs[:12], refs[12:19]
    key_ref, value_ref, mixed_ref, q2_ref, q_all, k_all, v_all, square_ref = refs[19:]
    step = pl.program_id(0)

    @pl.when(step < steps)
    def _():
        pre_body(*pre_ins, *pre_outs, q_all, k_all, v_all, square_ref)

    @pl.when(step >= steps)
    def _():
        pair = step - steps
        key_ref[...] = k_all[pair]
        value_ref[...] = v_all[pair]
        attend_body(len_ref, q_all.at[pair], k_all.at[pair], v_all.at[pair], mixed_ref, q2_ref)


def pre_attend_call(
    length, ids, tokens, gains, weights, down, upper, coarse, fine, router, constant_mix, vectors,
    residual_mix,
):
    tok_count, width = tokens.shape
    steps = tok_count // STEP

    def rows_of(columns):
        return pl.BlockSpec((STEP, columns), lambda i: (jnp.minimum(i, steps - 1), 0))

    column = pl.BlockSpec((tok_count, LANES), lambda i: (0, jnp.maximum(i - steps, 0)))
    return pl.pallas_call(
        functools.partial(pre_attend_body, steps),
        grid=(steps + PAIRS,),
        in_specs=[
            smem(), smem(), rows_of(width), whole(gains.shape), whole(weights.shape), whole(down.shape),
            whole(upper.shape), whole(coarse.shape), whole(fine.shape), whole(router.shape),
            whole(constant_mix.shape), whole(vectors.shape), whole(residual_mix.shape),
        ],
        out_specs=[
            rows_of(width), rows_of(LANES), whole((width, LANES)), whole(upper.shape),
            whole((LANES, width)), whole((16, LANES)), whole((READ_ROWS, width)), column, column,
            column, pl.BlockSpec((2 * LANES, tok_count), lambda i: (jnp.maximum(i - steps, 0), 0)),
        ],
        out_shape=[
            shape_of(tok_count, width), shape_of(tok_count, LANES), shape_of(width, LANES),
            shape_of(*upper.shape), shape_of(LANES, width, dtype=F32), shape_of(16, LANES, dtype=F32),
            shape_of(READ_ROWS, width, dtype=F32), shape_of(tok_count, width),
            shape_of(tok_count, width), shape_of(tok_count, width), shape_of(2 * width, tok_count),
        ],
        scratch_shapes=[pltpu.VMEM((PAIRS, tok_count, LANES), BF)] * 3
        + [pltpu.VMEM((LANES, LANES), F32)],
        compiler_params=PARAMS,
        cost_estimate=cost(25),
        name="attention_forward",
    )(
        length, ids, tokens, gains, weights, down, upper, coarse, fine, router, constant_mix, vectors,
        residual_mix,
    )


def attend_back_body(
    len_ref, q2_ref, k_ref, v_ref, mixed_ref, back_ref, coarse_ref, fine_ref,
    dq_ref, dk_ref, dv_ref, acc_ref, turn_ref,
):
    tok_count = k_ref.shape[0]

    @pl.when(pl.program_id(0) == 0)
    def _():
        turn_ref[0], turn_ref[1] = turn_rows(coarse_ref, fine_ref, 0, tok_count)

    lane = iota((tok_count, LANES), 1)
    position = iota((tok_count, LANES), 0)
    bias = jnp.where(position < len_ref[0], 0.0, NEG)
    causal = iota((TILE, TILE), 0) <= iota((TILE, TILE), 1)
    row = iota((LANES, tok_count), 0)
    back = back_ref[...].astype(F32)
    product_t = (back * mixed_ref[...].astype(F32)).T
    back_t = back.T
    keys, values = k_ref[...].astype(F32), v_ref[...].astype(F32)
    grads = []
    for head in range(2):
        own = lane // HD == head
        spare = HD * (1 - head)
        minus = jnp.where((lane > spare) & (lane < spare + 4), -1.0, 0.0)
        q2 = q2_ref[head * LANES : head * LANES + LANES, :]
        k2f = jnp.where(own, keys, jnp.where(lane == spare, bias, minus))
        k2 = k2f.astype(BF)
        k2t = k2f.T.astype(BF)
        v2 = jnp.where(own, values, minus).astype(BF)
        own_row = row // HD == head
        delta = jnp.sum(jnp.where(own_row, product_t, 0.0), axis=0, keepdims=True)
        back2 = jnp.where(own_row, back_t, 0.0)
        for offset, piece in enumerate(split3(delta)):
            back2 = jnp.where(row == spare + 1 + offset, piece.astype(F32), back2)
        back2 = back2.astype(BF)
        dk_parts, dv_parts = [], []
        for start in range(0, tok_count, TILE):
            stop = start + TILE
            scores = mm(k2[start:stop], q2[:, start:])
            slopes = mm(v2[start:stop], back2[:, start:])
            diagonal = jnp.where(causal, scores[:, :TILE], NEG)
            scores = (
                diagonal
                if stop == tok_count
                else jnp.concatenate([diagonal, scores[:, TILE:]], axis=1)
            )
            weights = jnp.exp(scores)
            turned = (weights * slopes).astype(BF)
            dv_parts.append(mm_nt(weights.astype(BF), back2[:, start:]))
            dk_parts.append(mm_nt(turned, q2[:, start:]))
            update = mm(k2t[:, start:stop], turned)
            if start == 0:
                acc_ref[head] = update
            else:
                acc_ref[head, :, start:] += update
        grads.append((jnp.concatenate(dk_parts, axis=0), jnp.concatenate(dv_parts, axis=0)))
    low_lane = lane < HD
    cosine, sine = turn_ref[0], -turn_ref[1]
    dq = jnp.where(row < HD, acc_ref[0], acc_ref[1]).T * HD**-0.5
    dq_ref[...] = rope(dq, cosine, sine).astype(BF)
    dk = jnp.where(low_lane, grads[0][0], grads[1][0])
    dk_ref[...] = rope(dk, cosine, sine).astype(BF)
    dv_ref[...] = jnp.where(low_lane, grads[0][1], grads[1][1]).astype(BF)


def pack_grads(packed, id_ref, acc_ref, grad_ref):
    count, width = acc_ref.shape[0], acc_ref.shape[1] // 2
    if not packed:
        grad_ref[...] = acc_ref[...].astype(BF)
        return
    half = width // 2
    shape = (16 * RANK, count)
    place, row = iota(shape, 0), iota(shape, 1)
    total = None
    for index in range(4):
        kind, part = index // 2, index % 2
        here = (place % 4 == row % 4) & (place // 16 == row // 4)
        here = here & (place // 8 % 2 == part) & (place // 4 % 2 == kind)
        start = kind * width + part * half
        piece = mm(hot(here), acc_ref[:, start : start + half].astype(BF))
        total = piece if total is None else total + piece
    grad_ref[:, 0:half] = total.astype(BF)
    grad_ref[:, half:] = jnp.full((16 * RANK, LANES), id_ref[0].astype(F32), F32).astype(BF)


def attend_back_all_body(packed, len_ref, id_ref, *refs):
    ins, refs = refs[:7], refs[7:]
    bcat_ref, inner_ref, inner_o_ref, din_ref, ba_ref, normed_hbm, mixed_hbm = refs[:7]
    dq_ref, dk_ref, dv_ref, back_ref, grad_ref = refs[7:12]
    scratch, (inner_all, back_all, acc_ref, normed_all, mixed_all, sems) = refs[12:14], refs[14:]
    step = pl.program_id(0)
    count = inner_all.shape[1]
    width = normed_all.shape[1]
    copies = [
        pltpu.make_async_copy(normed_hbm, normed_all, sems.at[0]),
        pltpu.make_async_copy(mixed_hbm, mixed_all, sems.at[1]),
    ]

    @pl.when(step == 0)
    def _():
        for copy in copies:
            copy.start()
        inner_all[0] = inner_ref[...].astype(F32).T[0:count].astype(BF)
        inner_all[1] = inner_o_ref[...].astype(F32).T[0:count].astype(BF)
        back_all[...] = jnp.zeros_like(back_all)

    @pl.when(step < PAIRS)
    def _():
        attend_back_body(len_ref, *ins, dq_ref, dk_ref, dv_ref, *scratch)
        number = iota((count, LANES), 0) % 4
        upper = mm(inner_all[1], ba_ref[...])
        total = back_all[...]
        for index, ref in enumerate((dq_ref, dk_ref, dv_ref)):
            value = ref[...]
            upper = jnp.where(number == index, mm(inner_all[0], value), upper)
            total = total + mm_nt(value, bcat_ref[index])
        back_all[...] = total
        at = width + step * LANES
        acc_ref[:, pl.ds(pl.multiple_of(at, LANES), LANES)] = upper

    @pl.when(step == PAIRS)
    def _():
        back = back_all[...].astype(BF)
        back_ref[...] = back
        back_t = (back.astype(F32) + din_ref[...].astype(F32)).T[0:count].astype(BF)
        for copy in copies:
            copy.wait()
        number = iota((count, width), 0) % 4
        half = back_t.shape[1] // 2

        def down(rows_ref):
            return mm(back_t[:, :half], rows_ref[:half]) + mm(back_t[:, half:], rows_ref[half:])

        acc_ref[:, 0:width] = jnp.where(number < 3, down(normed_all), down(mixed_all))
        pack_grads(packed, id_ref, acc_ref, grad_ref)


def attend_back_call(
    packed, length, ids, q2, keys, values, mixed, back, coarse, fine, bcat, inner, inner_o, din, ba,
    normed,
):
    tok_count, width = keys.shape
    column = pl.BlockSpec((tok_count, LANES), lambda i: (0, jnp.minimum(i, PAIRS - 1)))
    grad_shape = (16 * RANK, width // 2 + LANES) if packed else (4 * RANK, 2 * width)
    return pl.pallas_call(
        functools.partial(attend_back_all_body, packed),
        grid=(PAIRS + 1,),
        in_specs=[
            smem(), smem(),
            pl.BlockSpec((2 * LANES, tok_count), lambda i: (jnp.minimum(i, PAIRS - 1), 0)), column,
            column, column, column, whole(coarse.shape), whole(fine.shape),
            pl.BlockSpec((4, LANES, LANES), lambda i: (0, 0, jnp.minimum(i, PAIRS - 1))),
            whole(inner.shape), whole(inner_o.shape), whole(din.shape), column,
            pl.BlockSpec(memory_space=pl.ANY), pl.BlockSpec(memory_space=pl.ANY),
        ],
        out_specs=[column] * 3 + [whole((tok_count, LANES)), whole(grad_shape)],
        out_shape=[shape_of(tok_count, width)] * 3
        + [shape_of(tok_count, LANES), shape_of(*grad_shape)],
        scratch_shapes=[
            pltpu.VMEM((2, LANES, tok_count), F32), pltpu.VMEM((2, tok_count, LANES), F32),
            pltpu.VMEM((2, 4 * RANK, tok_count), BF), pltpu.VMEM((tok_count, LANES), F32),
            pltpu.VMEM((4 * RANK, 2 * width), F32), pltpu.VMEM((tok_count, width), BF),
            pltpu.VMEM((tok_count, width), BF), pltpu.SemaphoreType.DMA((2,)),
        ],
        compiler_params=PARAMS,
        cost_estimate=cost(12),
        name="attention_backward",
    )(
        length, ids, q2, keys, values, mixed, back, coarse, fine, bcat, inner, inner_o, din, ba,
        normed, mixed,
    )


def post_body(
    local, group, me_ref, mixed_ref, x_ref, wo_ref, acat_ref, bcat_ref, gain_ref, read_ref, mix_ref,
    prev_ref, routes_ref, slot_ref, hidden_ref, ei_ref, inner_ref, data_ref, cols_ref,
):
    reader = read_ref[0:READ_VECTOR].astype(BF)

    def stages(at):
        mixed = mixed_ref[at]
        inner = mm(mixed, acat_ref[...]).astype(BF)
        inner_ref[at] = inner
        yield
        hidden = x_ref[at].astype(F32) + (mm(mixed, wo_ref[...]) + mm(inner, bcat_ref[0]))
        hidden_ref[at] = hidden
        yield
        scale = lax.rsqrt(jnp.mean(hidden * hidden, axis=-1, keepdims=True) + EPSILON)
        ei = (hidden * scale * gain_ref[1:2, :]).astype(BF)
        ei_ref[at] = ei
        yield
        read = mm_nt(reader, ei)
        yield
        logits = read[0:16]
        for index in range(EXPERTS + 4):
            logits = logits + mix_ref[:, index : index + 1] * prev_ref[index : index + 1, at]
        first, second = routes_ref[0:1, at].astype(F32), routes_ref[1:2, at].astype(F32)
        number = iota((16, TILE), 0).astype(F32)
        one = jnp.sum(jnp.where(number == first, logits, 0.0), axis=0, keepdims=True)
        two = jnp.sum(jnp.where(number == second, logits, 0.0), axis=0, keepdims=True)
        top = jnp.maximum(one, two)
        one, two = jnp.exp(one - top), jnp.exp(two - top)
        gate_a, gate_b = one / (one + two), two / (one + two)
        mixes = read[16:20] + read[24:28] + read[32:36]
        shares = []
        for index in range(2):
            left, right = mixes[2 * index : 2 * index + 1], mixes[2 * index + 1 : 2 * index + 2]
            top = jnp.maximum(left, right)
            left, right = jnp.exp(left - top), jnp.exp(right - top)
            shares += [left / (left + right), right / (left + right)]

        def both(value):
            return jnp.where(first == value, gate_a, 0.0) + jnp.where(second == value, gate_b, 0.0)

        gates = jnp.where(number == first, gate_a, 0.0) + jnp.where(number == second, gate_b, 0.0)
        beta_a, beta_b = both(EXPERTS + 2.0), both(EXPERTS + 3.0)
        keep = both(EXPERTS + 1.0) + beta_a * shares[0] + beta_b * shares[2]
        data_ref[0:8, at] = gates[0:8]
        tail = [gate_a, gate_b] + shares + [beta_a, beta_b]
        data_ref[8:16, at] = jnp.concatenate(tail, axis=0)
        yield
        slots = slot_ref[:, at].astype(F32)
        expert = iota((EXPERTS, TILE), 0)
        partner = jnp.bitwise_xor(expert // local, me_ref[0])
        base = ((expert % local) * (group * CAP) + partner * CAP).astype(F32)
        place = jnp.where(slots >= 0, slots + base + 1.0, 0.0)
        expert = expert.astype(F32)
        target_a = jnp.sum(jnp.where(expert == first, place, 0.0), axis=0, keepdims=True) - 1.0
        target_b = jnp.sum(jnp.where(expert == second, place, 0.0), axis=0, keepdims=True) - 1.0
        stack = jnp.concatenate(
            [jnp.zeros((VECTOR_ROW, TILE), F32), beta_a * shares[1], beta_b * shares[3]]
            + [jnp.zeros((2, TILE), F32), target_a, target_b, keep]
            + [jnp.zeros((LANES - KEEP_LANE - 1, TILE), F32)],
            axis=0,
        )
        cols_ref[at] = stack.T

    side_by_side(stages)


def post_send_body(local, group, steps, me_ref, id_ref, slot_all_ref, *refs):
    post_refs, out_refs, (ei_all, data_all) = refs[:16], refs[16:-2], refs[-2:]
    step = pl.program_id(0)

    @pl.when(step < steps)
    def _():
        post_body(local, group, me_ref, *post_refs)
        span = pl.ds(pl.multiple_of(step * STEP, STEP), STEP)
        ei_all[span] = post_refs[12][...]
        data_all[:, span] = post_refs[14][...]

    @pl.when(step >= steps)
    def _():
        send_rows(local, group, step - steps, me_ref, id_ref, slot_all_ref, data_all, ei_all, out_refs)


def post_call(
    local, group, me, ids, mixed, tokens, weight, acat, bcat, gains, reader, mixer, prev, routes, slots
):
    tok_count, width = tokens.shape
    steps = tok_count // STEP
    heights = [local * PIECE] * (group // 2) + [PIECE] * ((group - group // 2) * local)

    def rows_of(columns):
        return pl.BlockSpec((STEP, columns), lambda i: (jnp.minimum(i, steps - 1), 0))

    def lanes_of(height):
        return pl.BlockSpec((height, STEP), lambda i: (0, jnp.minimum(i, steps - 1)))

    return pl.pallas_call(
        functools.partial(post_send_body, local, group, steps),
        grid=(steps + group,),
        in_specs=[
            smem(), smem(), whole(slots.shape), rows_of(width), rows_of(width), whole(weight.shape),
            whole(acat.shape), pl.BlockSpec((1, LANES, width), lambda i: (3, 0, 0)), whole(gains.shape),
            whole(reader.shape), whole(mixer.shape), lanes_of(EXPERTS + 4), lanes_of(2),
            lanes_of(EXPERTS),
        ],
        out_specs=[
            rows_of(width), rows_of(width), rows_of(LANES), lanes_of(16), rows_of(LANES)
        ] + [whole((height, width)) for height in heights],
        out_shape=[
            shape_of(tok_count, width, dtype=F32), shape_of(tok_count, width),
            shape_of(tok_count, LANES), shape_of(16, tok_count, dtype=F32),
            shape_of(tok_count, LANES, dtype=F32),
        ] + [shape_of(height, width) for height in heights],
        scratch_shapes=[pltpu.VMEM((tok_count, width), BF), pltpu.VMEM((16, tok_count), F32)],
        compiler_params=PARAMS,
        cost_estimate=cost(14),
        name="after_attention",
    )(
        me, ids, slots, mixed, tokens, weight, acat, bcat, gains, reader, mixer, prev, routes, slots
    )


def expert_body(
    local_index, pair, per_owner, group, steps, has_grad, kept, *refs
):
    count = len(pair)
    piece_refs, refs = refs[:count], refs[count:]
    cot_refs, refs = refs[:count], refs[count:]
    dn_ref, ou_ref, wg_hbm, wu_hbm, wd_hbm, up_hbm, od_hbm = refs[:7]
    refs = refs[7:]
    if has_grad:
        before_hbm, refs = refs[0], refs[1:]
    refs = refs[kept:]
    back_refs, refs = refs[:count], refs[count:]
    out_refs, refs = refs[:count], refs[count:]
    (
        grad_ref, x_ref, g_ref, gate_ref, pick_ref, dr_ref, zg_ref, zu_ref, dzd_ref, zgt_ref, zut_ref,
        dzdt_ref, racc_ref, xacc_ref, zd_acc, dzg_acc, dzu_acc, h_ref, dg_ref, du_ref, wg_all, wu_all,
        wd_all, up_all, od_all, sems, *rest
    ) = refs
    rows, width = x_ref.shape
    compact = group * RANK
    tile = h_ref.shape[1]

    def copies(step):
        span = pl.ds(pl.multiple_of(step * tile, tile), tile)
        pairs = (
            (wg_hbm.at[local_index, :, span], wg_all),
            (wu_hbm.at[local_index, :, span], wu_all),
            (wd_hbm.at[local_index, span, :], wd_all),
            (up_hbm.at[local_index, :, :, span], up_all),
            (od_hbm.at[local_index, span, :], od_all),
        )
        return [
            pltpu.make_async_copy(source, target.at[step], sems.at[step, place])
            for place, (source, target) in enumerate(pairs)
        ]

    def begin(step):
        for copy in copies(step):
            copy.start()

    begin(0)

    def fold(value):
        place = iota((compact, LANES), 0)
        block = per_owner * group
        inner = place // block * per_owner + place % per_owner
        folded = mm_nt(hot(iota((compact, LANES), 1) % RANK == inner), value)
        place = iota((compact, rows), 0)
        owner = place % block // per_owner
        mine = iota((compact, rows), 1) // CAP + pair[0]
        return jnp.where(mine == owner, folded, 0.0).astype(BF)

    def put(start, value):
        grad_ref[:, pl.ds(start, value.shape[1])] = value.astype(BF)

    for index in range(count):
        span = slice(index * CAP, index * CAP + CAP)
        x_ref[span] = piece_refs[index][0:CAP]
        g_ref[span] = cot_refs[index][...]
        meta = piece_refs[index][CAP:PIECE].astype(F32)
        gate = (meta[0:1] + meta[1:2] + meta[2:3])[:, 0 : 2 * LANES]
        gate_ref[span] = jnp.broadcast_to(gate, (LANES, 2 * LANES)).T[0:CAP]
        lane = (iota((CAP, LANES), 1) // RANK).astype(F32)
        pick_ref[span] = jnp.where(lane == meta[3:4, 0:LANES], 1.0, 0.0)
    chosen = pick_ref[...] > 0.0
    dr = (gate_ref[:, 0:1] * g_ref[...].astype(F32)).astype(BF)
    dr_ref[...] = dr
    zg = jnp.where(chosen, mm(x_ref[...], dn_ref[0]), 0.0).astype(BF)
    zu = jnp.where(chosen, mm(x_ref[...], dn_ref[1]), 0.0).astype(BF)
    dzd = jnp.where(chosen, mm_nt(dr, ou_ref[...]), 0.0).astype(BF)
    zg_ref[...] = zg
    zu_ref[...] = zu
    dzd_ref[...] = dzd
    zgt_ref[...] = fold(zg)
    zut_ref[...] = fold(zu)
    dzdt_ref[...] = fold(dzd)
    for ref in (racc_ref, xacc_ref, zd_acc, dzg_acc, dzu_acc):
        ref[...] = jnp.zeros_like(ref)

    total = steps * tile
    begin(1)
    if has_grad:
        before = pltpu.make_async_copy(before_hbm, rest[0], rest[1])
        before.start()

    def run(step, carry):
        for copy in copies(step):
            copy.wait()

        @pl.when(step + 2 < steps)
        def _():
            begin(step + 2)

        wg_ref, wu_ref, wd_ref = wg_all.at[step], wu_all.at[step], wd_all.at[step]
        up_ref, od_ref = up_all.at[step], od_all.at[step]
        gate = mm(x_ref[...], wg_ref[...]) + mm(zg_ref[...], up_ref[0])
        upper = mm(x_ref[...], wu_ref[...]) + mm(zu_ref[...], up_ref[1])
        share = 0.5 * jnp.tanh(0.5 * gate) + 0.5
        silu = gate * share
        active = (silu * upper).astype(BF)
        h_ref[...] = active
        back = mm_nt(dr_ref[...], wd_ref[...]) + mm_nt(dzd_ref[...], od_ref[...])
        du = (back * silu).astype(BF)
        dg = (back * upper * (share + silu * (1.0 - share))).astype(BF)
        du_ref[...] = du
        dg_ref[...] = dg
        racc_ref[...] += mm(active, wd_ref[...])
        zd_acc[...] += mm(active, od_ref[...])
        xacc_ref[...] += mm_nt(dg, wg_ref[...]) + mm_nt(du, wu_ref[...])
        dzg_acc[...] += mm_nt(dg, up_ref[0])
        dzu_acc[...] += mm_nt(du, up_ref[1])
        at = pl.multiple_of(step * tile, tile)
        put(at, mm(zgt_ref[...], dg_ref[...]))
        put(total + at, mm(zut_ref[...], du_ref[...]))
        put(2 * total + at, mm(dzdt_ref[...], h_ref[...]))
        return carry

    lax.fori_loop(0, steps, run, 0)
    chosen = pick_ref[...] > 0.0
    zd = jnp.where(chosen, zd_acc[...], 0.0).astype(BF)
    dzg = jnp.where(chosen, dzg_acc[...], 0.0).astype(BF)
    dzu = jnp.where(chosen, dzu_acc[...], 0.0).astype(BF)
    result = racc_ref[...] + mm(zd, ou_ref[...])
    gated = (gate_ref[:, 0:1] * result).astype(BF)
    product = g_ref[...].astype(F32) * result.astype(BF).astype(F32)
    dots = jnp.broadcast_to(jnp.sum(product, axis=-1, keepdims=True), (rows, LANES))
    back_rows = (xacc_ref[...] + mm_nt(dzg, dn_ref[0]) + mm_nt(dzu, dn_ref[1])).astype(BF)
    for index in range(count):
        span = slice(index * CAP, index * CAP + CAP)
        out_refs[index][...] = gated[span]
        back_refs[index][0:CAP, :] = back_rows[span]
        column = jnp.concatenate(
            [dots[span], jnp.zeros((2 * LANES - CAP, LANES), F32)], axis=0
        ).T[0:1]
        meta = jnp.concatenate(
            [piece.astype(F32) for piece in split3(column)]
            + [jnp.zeros((META - 3, 2 * LANES), F32)],
            axis=0,
        )
        meta = jnp.concatenate([meta, jnp.zeros((META, width - 2 * LANES), F32)], axis=1)
        back_refs[index][CAP:PIECE, :] = meta.astype(BF)
    base = 3 * total
    place = iota((compact, LANES), 0)
    owner = place % (per_owner * group) // per_owner
    ids = jnp.zeros((compact, LANES), F32)
    for index in range(count):
        meta = piece_refs[index][CAP:PIECE, 0:LANES].astype(F32)
        ids = jnp.where(owner == pair[index], meta[3:4], ids)
    put(base + 3 * width, ids)
    put(base, mm(fold(zd), dr_ref[...]))
    put(base + width, mm(fold(dzg), x_ref[...]))
    put(base + 2 * width, mm(fold(dzu), x_ref[...]))
    if has_grad:
        before.wait()
        grad_ref[...] = grad_ref[...] + rest[0][...]


def expert_call(index, pair, group, per_owner, pieces, cots, before, results, weights):
    gate_w, up_w, down_w, in_down, in_up, out_down, out_up = weights
    width, hidden = gate_w.shape[1:]
    rows = len(pair) * CAP
    steps = hidden // FTILE
    columns = 3 * hidden + 3 * width + LANES
    compact = group * RANK
    has_grad = before is not None
    return pl.pallas_call(
        functools.partial(
            expert_body, index, pair, per_owner, group, steps, has_grad, len(results)
        ),
        grid=(1,),
        in_specs=[
            pl.BlockSpec((PIECE, width), lambda f, row=piece.shape[0] // PIECE > 1: (index * row, 0))
            for piece in pieces
        ]
        + [pl.BlockSpec((CAP, width), lambda f: (index, 0))] * len(pair)
        + [
            pl.BlockSpec((None, 2, width, LANES), lambda f: (index, 0, 0, 0)),
            pl.BlockSpec((None, LANES, width), lambda f: (index, 0, 0)),
        ]
        + [pl.BlockSpec(memory_space=pl.ANY)] * 5
        + [pl.BlockSpec(memory_space=pl.ANY)] * (has_grad + len(results)),
        out_specs=[whole((PIECE, width))] * len(pair)
        + [pl.BlockSpec((CAP, width), lambda f: (index, 0))] * len(pair)
        + [whole((compact, columns))],
        out_shape=[shape_of(PIECE, width)] * len(pair)
        + [shape_of(gate_w.shape[0] * CAP, width)] * len(pair)
        + [shape_of(compact, columns)],
        input_output_aliases={
            2 * len(pair) + 7 + has_grad + place: len(pair) + place for place in range(len(results))
        },
        scratch_shapes=[pltpu.VMEM((rows, width), BF)] * 2
        + [pltpu.VMEM((rows, LANES), F32)] * 2
        + [pltpu.VMEM((rows, width), BF)]
        + [pltpu.VMEM((rows, LANES), BF)] * 3
        + [pltpu.VMEM((compact, rows), BF)] * 3
        + [pltpu.VMEM((rows, width), F32)] * 2
        + [pltpu.VMEM((rows, LANES), F32)] * 3
        + [pltpu.VMEM((rows, FTILE), BF)] * 3
        + [pltpu.VMEM((steps, width, FTILE), BF)] * 2
        + [
            pltpu.VMEM((steps, FTILE, width), BF), pltpu.VMEM((steps, 2, LANES, FTILE), BF),
            pltpu.VMEM((steps, FTILE, LANES), BF), pltpu.SemaphoreType.DMA((steps, 5)),
        ]
        + [pltpu.VMEM((compact, columns), BF), pltpu.SemaphoreType.DMA] * has_grad,
        compiler_params=PARAMS,
        cost_estimate=cost(rows / 21),
        name="expert_layer",
    )(
        *pieces, *cots, in_down, out_up, gate_w, up_w, down_w, in_up, out_down,
        *([before] if has_grad else []), *results,
    )


def spread(cols, index, count):
    return iota((TILE, count), 1).astype(F32) == cols[:, index : index + 1]


def combine_body(
    pieces, len_ref, *refs
):
    back_refs = refs[:pieces]
    (
        routes_ref, data_ref, cols_ref, cot_ref, ei_ref, hidden_ref, gain_ref, wo_ref, acat_ref, bcat_ref,
        table_ref, read_ref, bh_ref, ba_ref, din_ref, bm_ref, back_all, dots_ref,
    ) = refs[pieces:]
    count = pieces * CAP

    @pl.when(pl.program_id(0) == 0)
    def _():
        for index, back_ref in enumerate(back_refs):
            back_all[index * CAP : index * CAP + CAP, :] = back_ref[0:CAP, :]
        dots = [back_ref[CAP:PIECE, 0:CAP].astype(F32) for back_ref in back_refs]
        dots = jnp.concatenate(dots, axis=1)
        dots_ref[...] = jnp.concatenate([dots, jnp.zeros_like(dots)], axis=0).astype(BF)

    table_high, table_low = split2(table_ref[...])
    stack = dots_ref[...]
    vectors = read_ref[READ_VECTOR:READ_ROWS].astype(BF)

    def stages(at):
        start = pl.program_id(0) * STEP + at.start
        cols = cols_ref[at]
        chosen_a = hot(spread(cols, TARGET_LANE, count))
        chosen_b = hot(spread(cols, TARGET_LANE + 1, count))
        yield
        routed_a = jnp.sum(mm_nt(stack, chosen_a)[0:8], axis=0, keepdims=True)
        routed_b = jnp.sum(mm_nt(stack, chosen_b)[0:8], axis=0, keepdims=True)
        cot = cot_ref[at]
        cot_f = cot.astype(F32)
        yield
        along_x = jnp.sum(cot_f * ei_ref[at].astype(F32), axis=-1, keepdims=True)
        along_x = jnp.broadcast_to(along_x, (TILE, LANES)).T[0:1]
        yield
        along_c = mm_nt(vectors, cot)
        along_a = along_c[0:1] + along_c[2:3] + along_c[4:5]
        along_b = along_c[1:2] + along_c[3:4] + along_c[5:6]
        yield
        both = chosen_a + chosen_b
        half = count // 2
        back = mm(both[:, :half], back_all[:half]) + mm(both[:, half:], back_all[half:])
        yield
        first, second = routes_ref[0:1, at].astype(F32), routes_ref[1:2, at].astype(F32)
        token = iota((1, TILE), 1) + start
        valid = jnp.where(token < len_ref[0], 1.0, 0.0)
        gate_a, gate_b = data_ref[8:9, at], data_ref[9:10, at]
        share = [data_ref[index : index + 1, at] for index in range(10, 14)]
        beta_a, beta_b = data_ref[14:15, at], data_ref[15:16, at]
        const_a = share[0] * along_x + share[1] * along_a
        const_b = share[2] * along_x + share[3] * along_b

        def here(route):
            return (
                jnp.where(route == EXPERTS + 1.0, along_x, 0.0)
                + jnp.where(route == EXPERTS + 2.0, const_a, 0.0)
                + jnp.where(route == EXPERTS + 3.0, const_b, 0.0)
            )

        dot_a, dot_b = routed_a + here(first), routed_b + here(second)
        mean = gate_a * dot_a + gate_b * dot_b
        chosen_grad_a = valid * gate_a * (dot_a - mean)
        chosen_grad_b = valid * gate_b * (dot_b - mean)
        number = iota((16, TILE), 0).astype(F32)
        logit_grads = jnp.where(number == first, chosen_grad_a, 0.0) + jnp.where(
            number == second, chosen_grad_b, 0.0
        )
        mixes = []
        for index, (beta, along) in enumerate(((beta_a, along_a), (beta_b, along_b))):
            left, right = share[2 * index], share[2 * index + 1]
            weighted = left * along_x + right * along
            mixes += [
                valid * beta * left * (along_x - weighted),
                valid * beta * right * (along - weighted),
            ]
        small = jnp.concatenate(
            [logit_grads] + mixes + [jnp.zeros((LANES - 20, TILE), F32)], axis=0
        ).T
        high, low = split2(small)
        yield
        inside = iota((TILE, 1), 0) + start < len_ref[0]
        grad = jnp.where(inside, cot_f, 0.0)
        back = back + mm(high, table_high) + mm(low, table_high) + mm(high, table_low)
        back = back + cols[:, KEEP_LANE : KEEP_LANE + 1] * grad
        yield
        hidden = hidden_ref[at]
        scale = lax.rsqrt(jnp.mean(hidden * hidden, axis=-1, keepdims=True) + EPSILON)
        normed = hidden * scale
        back = back * gain_ref[1:2, :]
        back = grad + scale * (back - normed * jnp.mean(back * normed, axis=-1, keepdims=True))
        bh_ref[at] = back
        rounded = back.astype(BF)
        ba_ref[at] = rounded
        yield
        inner = mm_nt(rounded, bcat_ref[0]).astype(BF)
        din_ref[at] = inner
        yield
        bm_ref[at] = (mm_nt(rounded, wo_ref[...]) + mm_nt(inner, acat_ref[...])).astype(BF)

    side_by_side(stages)


def combine_call(
    length, backs, routes, data, cols, cotangent, ei, hidden, gains, weight, acat, bcat, table,
    reader,
):
    tok_count, width = cotangent.shape
    pieces = len(backs)
    return pl.pallas_call(
        functools.partial(combine_body, pieces),
        grid=(tok_count // STEP,),
        in_specs=[smem()] + [whole(back.shape) for back in backs] + [
            wide(2), wide(16), tall(LANES), tall(width), tall(width), tall(width),
            whole(gains.shape), whole(weight.shape), whole(acat.shape),
            pl.BlockSpec((1, LANES, width), lambda i: (3, 0, 0)), whole(table.shape),
            whole(reader.shape),
        ],
        out_specs=[tall(width), tall(width), tall(LANES), tall(width)],
        out_shape=[
            shape_of(tok_count, width, dtype=F32), shape_of(tok_count, width),
            shape_of(tok_count, LANES), shape_of(tok_count, width),
        ],
        scratch_shapes=[
            pltpu.VMEM((pieces * CAP, width), BF), pltpu.VMEM((2 * META, pieces * CAP), BF)
        ],
        compiler_params=PARAMS,
        cost_estimate=cost(17),
        name="combine_backward",
    )(
        length, *backs, routes, data, cols, cotangent, ei, hidden, gains, weight, acat, bcat, table,
        reader,
    )


def result_body(pieces, len_ref, *refs):
    result_refs = refs[:pieces]
    cols_ref, ei_ref, hidden_ref, table_ref, out_ref, result_all = refs[pieces:]
    count = result_all.shape[0]

    @pl.when(pl.program_id(0) == 0)
    def _():
        for index in range(count // CAP):
            start = index // pieces * CAP
            result_all[index * CAP : index * CAP + CAP] = result_refs[index % pieces][start : start + CAP]

    table_high, table_low = split2(table_ref[...])

    def stages(at):
        cols = cols_ref[at]
        both = hot(spread(cols, TARGET_LANE, count) | spread(cols, TARGET_LANE + 1, count))
        yield
        half = count // 2
        mixture = mm(both[:, :half], result_all[:half]) + mm(both[:, half:], result_all[half:])
        yield
        high, low = split2(cols)
        mixture = mixture + mm(high, table_high) + mm(low, table_high) + mm(high, table_low)
        mixture = mixture + cols[:, KEEP_LANE : KEEP_LANE + 1] * ei_ref[at].astype(F32)
        yield
        inside = iota((TILE, 1), 0) + pl.program_id(0) * STEP + at.start < len_ref[0]
        out_ref[at] = (hidden_ref[at] + jnp.where(inside, mixture, 0.0)).astype(BF)

    side_by_side(stages)


def result_call(length, results, cols, ei, hidden, table):
    tok_count, width = ei.shape
    pieces = len(results)
    return pl.pallas_call(
        functools.partial(result_body, pieces),
        grid=(tok_count // STEP,),
        in_specs=[smem()] + [whole(result.shape) for result in results] + [
            tall(LANES), tall(width), tall(width), whole(table.shape),
        ],
        out_specs=tall(width),
        out_shape=shape_of(tok_count, width),
        scratch_shapes=[pltpu.VMEM((pieces * results[0].shape[0], width), BF)],
        compiler_params=PARAMS,
        cost_estimate=cost(8),
        name="layer_output",
    )(length, *results, cols, ei, hidden, table)


def last_body(
    dq_ref, dk_ref, dv_ref, w_ref, acat_ref, back_ref, x_ref, bh_ref, gain_ref, out_ref
):
    def stages(at):
        parts = [mm_nt(back_ref[at], acat_ref[...])]
        for index, ref in enumerate((dq_ref, dk_ref, dv_ref)):
            parts.append(mm_nt(ref[at], w_ref[index]))
            yield
        total = parts[0] + parts[1] + parts[2] + parts[3]
        x = x_ref[at].astype(F32)
        scale = lax.rsqrt(jnp.mean(x * x, axis=-1, keepdims=True) + EPSILON)
        normed = x * scale
        back = total * gain_ref[0:1, :]
        back = scale * (back - normed * jnp.mean(back * normed, axis=-1, keepdims=True))
        out_ref[at] = (bh_ref[at] + back).astype(BF)

    side_by_side(stages)


def last_call(dq, dk, dv, weights, acat, back, tokens, bh, gains):
    tok_count, width = tokens.shape
    return pl.pallas_call(
        last_body,
        grid=(tok_count // STEP,),
        in_specs=[
            tall(width), tall(width), tall(width), whole(weights.shape), whole(acat.shape),
            tall(LANES), tall(width), tall(width), whole(gains.shape),
        ],
        out_specs=tall(width),
        out_shape=shape_of(tok_count, width),
        compiler_params=PARAMS,
        cost_estimate=cost(9),
        name="after_attention_backward",
    )(dq, dk, dv, weights, acat, back, tokens, bh, gains)


def exchange(value, axes):
    return lax.all_to_all(value, axes, split_axis=0, concat_axis=0, tiled=True)


def gather_all(value, axes, count):
    return exchange(jnp.broadcast_to(value[None], (count,) + value.shape), axes)


def swap(value, partner, group):
    if partner == 0:
        return value
    return lax.ppermute(value, "expert", [(index, index ^ partner) for index in range(group)])


def find_adapters(id_rows):
    count = id_rows.shape[0]
    padded = id_rows.astype(F32)
    if count % LANES:
        padded = jnp.concatenate([padded, jnp.zeros((-count % LANES, LANES), F32)], axis=0)
    return padded.T[0:1, 0:count].astype(jnp.int32)


def sum_expert_body(each, adapters, in_ref, out_ref):
    count, columns = in_ref.shape[0], out_ref.shape[1]
    found = find_adapters(in_ref[:, columns:])
    place = iota((adapters * each, count), 0)
    column = iota((adapters * each, count), 1)
    pick = hot((place // each == found) & (place % each == column % each))
    out_ref[...] = mm(pick, in_ref[:, 0:columns]).astype(BF)


def exchange_expert_grads(grads, group, owners):
    split = min(RANK, owners)
    each, parts = RANK // split, owners // split
    columns = (grads.shape[1] - LANES) // parts
    pieces = grads.reshape(split, each * group, grads.shape[1])
    if parts > 1:
        ids = jnp.broadcast_to(pieces[:, None, :, parts * columns :], (split, parts, each * group, LANES))
        pieces = pieces[:, :, : parts * columns].reshape(split, each * group, parts, columns)
        pieces = jnp.concatenate([pieces.transpose(0, 2, 1, 3), ids], axis=-1)
        pieces = pieces.reshape(owners, each * group, columns + LANES)
    return exchange(pieces, "dp").reshape(owners * group * each, columns + LANES)


def sum_expert_grads(got, adapters, owners):
    columns = got.shape[1] - LANES
    each = RANK // min(RANK, owners)
    return pl.pallas_call(
        functools.partial(sum_expert_body, each, adapters),
        out_shape=shape_of(adapters * each, columns),
        compiler_params=PARAMS,
        cost_estimate=cost(2.2),
        name="expert_gradient_part",
    )(got)


def finish_expert_body(split, adapters, hidden, in_ref, *refs):
    down_ref, up_ref, out_down_ref, out_up_ref = refs[-4:]
    each = RANK // split
    rows = adapters * each
    count = split * rows
    width = out_up_ref.shape[1]

    def place(value):
        return value // each % adapters * RANK + value // (adapters * each) * each + value % each

    move = hot(iota((count, count), 0) == place(iota((count, count), 1)))
    back = hot(iota((count, count), 1) == place(iota((count, count), 0)))

    def part(start, size):
        span = slice(start, start + size)
        rows_of = [in_ref[owner, :, span] for owner in range(split)]
        return jnp.concatenate(rows_of, axis=0)

    for index in range(2):
        up_ref[index] = mm(move, part(index * hidden, hidden))
    out_down_ref[...] = mm_tn(part(2 * hidden, hidden), back)
    base = 3 * hidden
    out_up_ref[...] = mm(move, part(base, width))
    for index in range(2):
        base += width
        down_ref[index] = mm_tn(part(base, width), back)


def finish_expert_call(index, local, everything, outs, adapters, width, hidden):
    owners, rows, columns = everything.shape
    total = adapters * RANK
    shapes = [(local, 2, width, total), (local, 2, total, hidden), (local, hidden, total),
              (local, total, width)]
    specs = [
        pl.BlockSpec((None,) + shape[1:], lambda *_, rank=len(shape): (index,) + (0,) * (rank - 1))
        for shape in shapes
    ]
    return pl.pallas_call(
        functools.partial(finish_expert_body, owners, adapters, hidden),
        grid=(1,),
        in_specs=[whole(everything.shape)] + [pl.BlockSpec(memory_space=pl.ANY)] * len(outs),
        out_specs=specs,
        out_shape=[shape_of(*shape, dtype=F32) for shape in shapes],
        input_output_aliases={1 + place: place for place in range(len(outs))},
        compiler_params=PARAMS,
        cost_estimate=cost(4),
        name="expert_gradient_sums",
    )(everything, *outs)


def spread_expert_grads(own, adapters, owners):
    split = min(RANK, owners)
    each, parts = RANK // split, owners // split
    everything = gather_all(own, "dp", owners)
    everything = everything.reshape(split, parts, adapters, each, own.shape[1])
    everything = everything.transpose(2, 0, 3, 1, 4)
    return everything.reshape(adapters * RANK, parts * own.shape[1]).astype(F32)


def expert_sums(owned, adapters, owners, width, hidden):
    sums = [spread_expert_grads(value, adapters, owners) for value in owned]
    base = 3 * hidden
    up = [[value[:, 0:hidden], value[:, hidden : 2 * hidden]] for value in sums]
    down = [
        [value[:, base + width * part : base + width * (part + 1)].T for part in (1, 2)]
        for value in sums
    ]
    return (
        jnp.stack([jnp.stack(value) for value in down]),
        jnp.stack([jnp.stack(value) for value in up]),
        jnp.stack([value[:, 2 * hidden : base].T for value in sums]),
        jnp.stack([value[:, base : base + width] for value in sums]),
    )


def finish_adapter_body(adapters, me_ref, *refs):
    piece_refs, (down_ref, up_ref, in_ref) = refs[:-3], refs[-3:]
    half = in_ref.shape[3]
    owners, group = piece_refs[0].shape[0], len(piece_refs)
    for other in range(group):
        place = jnp.bitwise_xor(me_ref[0], other)
        for owner in range(owners):
            in_ref[owner * (group // 2) + place // 2, place % 2] = piece_refs[other][owner]
    count = RANK * adapters

    def place(value):
        return value % adapters * RANK + value // adapters

    move = hot(iota((count, count), 0) == place(iota((count, count), 1)))
    back = hot(iota((count, count), 1) == place(iota((count, count), 0)))
    for part in range(2):
        span = slice(part * half, part * half + half)
        for kind in range(2):
            for index in range(4):
                first = (kind * 4 + index) * adapters
                rows = in_ref[:, part, first : first + adapters, :].astype(F32)
                rows = rows.reshape(count, half).astype(BF)
                if kind == 0:
                    down_ref[index, span, :] = mm_tn(rows, back)
                else:
                    up_ref[index, :, span] = mm(move, rows)


def sum_adapter_body(kinds, adapters, in_ref, out_ref):
    count, columns = in_ref.shape[0], out_ref.shape[-1]
    found = find_adapters(in_ref[:, columns:])
    place = iota((adapters * kinds, count), 0)
    column = iota((adapters * kinds, count), 1)
    pick = hot((place % adapters == found) & (place // adapters == column % kinds))
    own = mm(pick, in_ref[:, 0:columns]).astype(BF)
    for index in range(out_ref.shape[0]):
        out_ref[index] = own


def adapter_sums(grads, meanwhile, later, finish, parts, ids, adapters, owners, group, width):
    axes, everyone = ("dp", "expert"), owners * group
    if everyone == 2 * RANK and group == 4:
        kinds = 8
        got = exchange(grads.reshape(everyone, kinds, grads.shape[1]), axes)
        got, meanwhile = lax.optimization_barrier((got, meanwhile))
        own = pl.pallas_call(
            functools.partial(sum_adapter_body, kinds, adapters),
            out_shape=shape_of(owners, kinds * adapters, width // 2),
            compiler_params=PARAMS,
            cost_estimate=cost(2.0),
            name="adapter_gradient_part",
        )(got.reshape(everyone * kinds, grads.shape[1]))
        mine = exchange(own, "dp")
        mine, later = lax.optimization_barrier((mine, later))
        across = swap(mine, 2, group)
        full = [mine, swap(mine, 1, group), across, swap(across, 1, group)]
        total = adapters * RANK
        down, upper = pl.pallas_call(
            functools.partial(finish_adapter_body, adapters),
            in_specs=[smem()] + [pl.BlockSpec(memory_space=pltpu.VMEM)] * group,
            out_shape=[shape_of(4, width, total, dtype=F32), shape_of(4, total, width, dtype=F32)],
            scratch_shapes=[pltpu.VMEM((RANK, 2, kinds * adapters, width // 2), BF)],
            compiler_params=PARAMS,
            cost_estimate=cost(3.6),
            name="adapter_gradient_sums",
        )(lax.axis_index("expert").reshape(1).astype(jnp.int32), *full)
        (down, upper), later, parts = lax.optimization_barrier(((down, upper), later, parts))
        return down, upper, meanwhile, finish(later, parts)
    later = finish(later, parts)
    all_ids = exchange(jnp.broadcast_to(ids, (everyone,)), axes)
    pieces = grads.reshape(everyone, RANK * 4 * 2 * width // everyone)
    got = exchange(pieces, axes)
    pick = (jnp.arange(adapters, dtype=jnp.int32)[:, None] == all_ids[None, :]).astype(BF)
    own = jnp.dot(pick, got, preferred_element_type=F32).astype(BF)
    full = gather_all(own, axes, everyone)
    full = full.reshape(RANK, everyone // RANK, adapters, -1).transpose(2, 0, 1, 3)
    full = full.reshape(adapters * RANK, 4, 2, width).astype(F32)
    return full[:, :, 0].transpose(1, 2, 0), full[:, :, 1].transpose(1, 0, 2), meanwhile, later


def body(
    tokens,
    cotangent,
    lengths,
    adapter_ids,
    routes,
    prev_logits,
    norm_gains,
    input_weights,
    output_weight,
    adapter_down,
    adapter_up,
    router,
    residual_mix,
    constant_mix,
    constant_vectors,
    expert_gate,
    expert_up,
    expert_down,
    expert_adapter_down,
    expert_adapter_up,
    output_adapter_down,
    output_adapter_up,
):
    tok_count, width = tokens.shape
    hidden_width = expert_gate.shape[2]
    group, owners = lax.axis_size("expert"), lax.axis_size("dp")
    local = expert_gate.shape[0]
    adapters = adapter_down.shape[-1] // RANK
    angles = [jnp.asarray(table) for table in turn_tables(tok_count)]
    weights = (
        expert_gate, expert_up, expert_down, expert_adapter_down, expert_adapter_up,
        output_adapter_down, output_adapter_up,
    )
    per_owner = RANK // min(RANK, owners)
    everyone = owners * group
    me = lax.axis_index("expert")

    me = me.reshape(1).astype(jnp.int32)

    routes, prev_logits = routes.T, prev_logits.T
    slots, *grad_sends = route_call(local, group, lengths, me, routes, cotangent)
    cots = [swap(value, partner, group) for partner, value in enumerate(grad_sends)]
    normed, inner, acat, bcat, table, mixer, reader, keys, values, mixed, q2 = pre_attend_call(
        lengths, adapter_ids, tokens, norm_gains, input_weights, adapter_down, adapter_up, *angles,
        router.T, constant_mix.T, constant_vectors, residual_mix,
    )
    mixed, cots = lax.optimization_barrier((mixed, cots))
    hidden, ei, inner_o, data, cols, *sends = post_call(
        local, group, me, adapter_ids, mixed, tokens, output_weight, acat, bcat, norm_gains, reader, mixer, prev_logits,
        routes, slots,
    )
    near, far = tuple(range(group // 2)), tuple(range(group // 2, group))
    sent_near = [swap(sends[partner], partner, group) for partner in near]
    sent_far = []
    for index in range(local):
        pieces = [sends[group // 2 + place * local + index] for place in range(len(far))]
        if index > 0:
            pieces, sent_near = lax.optimization_barrier((pieces, sent_near))
        sent_far.append([swap(piece, partner, group) for piece, partner in zip(pieces, far)])
    backs = [[None] * group for _ in range(local)]
    results = [None] * group
    calls = []
    for index in range(local - 1):
        calls += [(index, near), (index, far)]
    calls += [(local - 1, near[1:] + far), (local - 1, near[:1])]
    grads, owned, parts = [None] * local, [], []
    sums = functools.partial(sum_expert_grads, adapters=adapters, owners=owners)
    last = None
    for index, some in calls:
        pieces = [
            sent_near[partner] if partner in near else sent_far[index][partner - len(near)]
            for partner in some
        ]
        if last is not None:
            pieces, last = lax.optimization_barrier((pieces, last))
        if (index, some) == calls[-1]:
            parts, last = lax.optimization_barrier((parts, last))
            owned = [sums(part) for part in parts]
            pieces, backs[:index], owned = lax.optimization_barrier((pieces, backs[:index], owned))
        outs = expert_call(
            index, some, group, per_owner, pieces, [cots[partner] for partner in some], grads[index],
            [results[partner] for partner in some] if index else [], weights,
        )
        grads[index] = last = outs[-1]
        for place, partner in enumerate(some):
            backs[index][partner] = swap(outs[place], partner, group)
            results[partner] = outs[len(some) + place]
        if index < local - 1 and some == far:
            parts.append(exchange_expert_grads(last, group, owners))
    backs = [value for some in backs for value in some]
    parts.append(exchange_expert_grads(last, group, owners))
    gather = functools.partial(lax.all_gather, axis_name="dp", axis=0, tiled=False)
    if owners <= RANK:
        owned = [gather(own) for own in owned]
    back_hidden, back_attention, back_inner_o, back_mixed = combine_call(
        lengths, backs, routes, data, cols, cotangent, ei, hidden, norm_gains, output_weight, acat, bcat,
        table, reader,
    )
    flat, back_mixed = lax.optimization_barrier((results, back_mixed))
    flat = [swap(value, partner, group) for partner, value in enumerate(flat)]

    packed = everyone == 2 * RANK and group == 4
    dq, dk, dv, back_inner, adapter_grads = attend_back_call(
        packed, lengths, adapter_ids, q2, keys, values, mixed, back_mixed, *angles, bcat, inner, inner_o,
        back_inner_o, back_attention, normed,
    )
    parts[-1], adapter_grads, flat, owned = lax.optimization_barrier(
        (parts[-1], adapter_grads, flat, owned)
    )
    own = sums(parts[-1])
    adapter_grads, own, flat = lax.optimization_barrier((adapter_grads, own, flat))
    owned.append(gather(own) if owners <= RANK else own)
    layer_out = result_call(lengths, flat, cols, ei, hidden, table)
    input_back = last_call(
        dq, dk, dv, input_weights, acat, back_inner, tokens, back_hidden, norm_gains
    )
    outs = []
    if owners <= RANK:
        for index, own in enumerate(owned[:-1]):
            outs = finish_expert_call(index, local, own, outs, adapters, width, hidden_width)
    def finish(later, part):
        input_back, outs = later
        if owners <= RANK:
            return input_back, finish_expert_call(
                local - 1, local, part, outs, adapters, width, hidden_width
            )
        return input_back, expert_sums(owned, adapters, owners, width, hidden_width)

    down_sum, upper_sum, layer_out, (input_back, outs) = adapter_sums(
        adapter_grads, layer_out, (input_back, outs), finish, owned[-1], adapter_ids, adapters, owners, group, width
    )
    in_down_sum, in_up_sum, out_down_sum, out_up_sum = outs
    return (
        layer_out,
        input_back,
        down_sum,
        upper_sum,
        in_down_sum,
        in_up_sum,
        out_down_sum,
        out_up_sum,
    )


def solution(mesh):
    tokens_spec, copied = P(("dp", "expert"), None), P()
    owned = P("expert")
    placed = (
        (tokens_spec, tokens_spec, P(("dp", "expert")), P(("dp", "expert")), tokens_spec, tokens_spec)
        + (copied,) * 9
        + (owned,) * 7
    )
    return jax.shard_map(
        body,
        mesh=mesh,
        in_specs=placed,
        out_specs=(tokens_spec, tokens_spec, copied, copied) + (owned,) * 4,
        check_vma=False,
    )
```

```python
import functools
import math

import jax
import jax.numpy as jnp
import numpy as np
from jax import lax
from jax.experimental import pallas as pl
from jax.experimental.pallas import tpu as pltpu
from jax.sharding import PartitionSpec as P

HEADS = 12
HD = 64
EXPERTS = 8
RANK = 16
CAP = 192
EPSILON = 1e-06
F32 = jnp.float32
BF = jnp.bfloat16
NEG = -1e30
LANES = 128
TILE = 256
STEP = 512
FTILE = 512
PAIRS = HEADS // 2
AHEAD = 1
PARAMS = pltpu.CompilerParams(vmem_limit_bytes=67043328)
META = 8
MIX_ROW = 16
VECTOR_ROW = 20
TARGET_LANE = 24
KEEP_LANE = 26
READ_VECTOR = 48
READ_ROWS = 64
PIECE = CAP + META


def mm(left, right):
    return jnp.dot(left, right, preferred_element_type=F32)


def mm_nt(left, right):
    return lax.dot_general(left, right, (((1,), (1,)), ((), ())), preferred_element_type=F32)


def mm_tn(left, right):
    return lax.dot_general(left, right, (((0,), (0,)), ((), ())), preferred_element_type=F32)


def iota(shape, axis):
    return lax.broadcasted_iota(jnp.int32, shape, axis)


def hot(condition):
    return jnp.where(condition, 1.0, 0.0).astype(BF)


def split2(value):
    high = value.astype(BF)
    return high, (value - high.astype(F32)).astype(BF)


def split3(value):
    high = value.astype(BF)
    rest = value - high.astype(F32)
    middle = rest.astype(BF)
    return high, middle, (rest - middle.astype(F32)).astype(BF)


def whole(shape):
    zeros = (0,) * len(shape)
    return pl.BlockSpec(shape, lambda *_: zeros)


def smem():
    return pl.BlockSpec(memory_space=pltpu.SMEM)


def tall(width):
    return pl.BlockSpec((STEP, width), lambda i: (i, 0))


def wide(height):
    return pl.BlockSpec((height, STEP), lambda i: (0, i))


def tile(width):
    return pl.BlockSpec((TILE, width), lambda i: (i, 0))


def side_by_side(stages):
    running = [stages(slice(start, start + TILE)) for start in range(0, STEP, TILE)]
    while running:
        running = [stage for stage in running if next(stage, True) is None]


def shape_of(*shape, dtype=BF):
    return jax.ShapeDtypeStruct(shape, dtype)


def cost(microseconds):
    return pl.CostEstimate(flops=int(microseconds * 1e+09), bytes_accessed=0, transcendentals=0)


@functools.lru_cache(maxsize=None)
def turn_tables(length_in):
    half = HD // 2
    inverse = np.exp(np.arange(half, dtype=np.float64) * (-2.0 * math.log(10000.0) / HD))

    def table(positions):
        angles = np.tile(positions[:, None] * inverse[None, :], (1, 4))
        return np.stack([np.cos(angles), np.sin(angles)]).astype(np.float32)

    return table(np.arange(0.0, length_in, 32)), table(np.arange(0.0, 32))


def turn_rows(coarse_ref, fine_ref, first, count):
    fine_cos, fine_sin = fine_ref[0], fine_ref[1]
    sign = jnp.where(iota((32, LANES), 1) % HD < HD // 2, -1.0, 1.0)
    signed_cos, signed_sin = fine_cos * sign, fine_sin * sign
    cosines, sines = [], []
    for index in range(count // 32):
        row = first // 32 + index
        coarse_cos, coarse_sin = coarse_ref[0, pl.ds(row, 1), :], coarse_ref[1, pl.ds(row, 1), :]
        cosines.append(coarse_cos * fine_cos - coarse_sin * fine_sin)
        sines.append(coarse_sin * signed_cos + coarse_cos * signed_sin)
    return jnp.concatenate(cosines, axis=0), jnp.concatenate(sines, axis=0)


def rope(value, cosine, sine):
    first = iota(value.shape, 1) % HD < HD // 2
    turned = jnp.where(first, pltpu.roll(value, LANES - HD // 2, 1), pltpu.roll(value, HD // 2, 1))
    return value * cosine + turned * sine


def find_slots(length, routes_ref, slot_ref):
    tok_count = slot_ref.shape[1]
    before = hot(iota((TILE, TILE), 0) < iota((TILE, TILE), 1))
    carry = jnp.zeros((2 * EXPERTS, 1), F32)
    for start in range(0, tok_count, TILE):
        span = slice(start, start + TILE)
        expert = iota((2 * EXPERTS, TILE), 0)
        token = iota((2 * EXPERTS, TILE), 1) + start
        named = (routes_ref[0:1, span] == expert) | (routes_ref[1:2, span] == expert)
        hit = named & (token < length) & (expert < EXPERTS)
        hits = jnp.where(hit, 1.0, 0.0)
        slots = mm(hits.astype(BF), before) + carry
        carry = carry + jnp.sum(hits, axis=1, keepdims=True)
        slot_ref[:, span] = jnp.where(hit, slots, -1.0)[:EXPERTS].astype(jnp.int32)


def pick_rows(slot_ref, step, me, local):
    first = jnp.bitwise_xor(step, me) * local
    place = iota((CAP, slot_ref.shape[1]), 0)
    return first, [hot(place == slot_ref[pl.ds(first + index, 1), :]) for index in range(local)]


def pick_source(chosen, source_ref):
    half = source_ref.shape[0] // 2
    return mm(chosen[:, :half], source_ref[:half]) + mm(chosen[:, half:], source_ref[half:])


def store_piece(out_refs, step, other, index, value, start):
    @pl.when(step == other)
    def _():
        out_refs[index][start : start + value.shape[0], :] = value


def route_body(local, group, len_ref, me_ref, routes_ref, source_ref, slot_ref, *out_refs):
    step = pl.program_id(0)

    @pl.when(step == 0)
    def _():
        find_slots(len_ref[0], routes_ref, slot_ref)

    _, chosen = pick_rows(slot_ref, step, me_ref[0], local)
    rows = pick_source(jnp.concatenate(chosen, axis=0), source_ref).astype(BF)
    for other in range(group):
        store_piece(out_refs, step, other, other, rows, 0)


def route_call(local, group, length, me, routes, source):
    tok_count, width = source.shape
    return pl.pallas_call(
        functools.partial(route_body, local, group),
        grid=(group,),
        in_specs=[smem(), smem(), whole(routes.shape), whole(source.shape)],
        out_specs=[whole((EXPERTS, tok_count))] + [whole((local * CAP, width))] * group,
        out_shape=[shape_of(EXPERTS, tok_count, dtype=jnp.int32)]
        + [shape_of(local * CAP, width)] * group,
        compiler_params=PARAMS,
        cost_estimate=cost(6.5),
        name="route_rows",
    )(length, me, routes, source)


def send_rows(local, group, partner, me_ref, id_ref, slot_ref, data_ref, source_ref, out_refs):
    width = source_ref.shape[1]
    first, chosen = pick_rows(slot_ref, partner, me_ref[0], local)
    rows = pick_source(jnp.concatenate(chosen, axis=0), source_ref).astype(BF)
    for index in range(local):
        pieces = split3(data_ref[pl.ds(first + index, 1), :])
        stack = jnp.concatenate(
            [piece.astype(F32) for piece in pieces]
            + [jnp.zeros((13, chosen[index].shape[1]), F32)],
            axis=0,
        ).astype(BF)
        gates = mm_nt(stack, chosen[index])[0:META]
        gates = jnp.where(iota(gates.shape, 0) == 3, id_ref[0].astype(F32), gates)
        meta = jnp.concatenate([gates, jnp.zeros((META, width - CAP), F32)], axis=1)
        kept = rows[index * CAP : index * CAP + CAP]
        for other in range(group):
            far = other >= group // 2
            place = group // 2 + (other - group // 2) * local + index if far else other
            start = 0 if far else index * PIECE
            store_piece(out_refs, partner, other, place, kept, start)
            store_piece(out_refs, partner, other, place, meta.astype(BF), start + CAP)


def pre_body(
    id_ref, x_ref, gain_ref, w_ref, ad_ref, au_ref, coarse_ref, fine_ref, router_ref, cmix_ref, vec_ref,
    resid_ref, normed_ref, inner_ref, acat_ref, bcat_ref, table_ref, mix_ref, read_ref, q_ref, k_ref,
    v_ref, square_ref,
):
    @pl.when(pl.program_id(0) == 0)
    def _():
        first = RANK * id_ref[0]
        total = None
        for index in range(4):
            row, column = iota((LANES, LANES), 0), iota((LANES, LANES), 1)
            place = hot((row >= first) & (row < first + RANK) & (column == (row - first) * 4 + index))
            part = mm(ad_ref[index], place)
            total = part if total is None else total + part
            place = hot(
                (column >= first) & (column < first + RANK) & (row == (column - first) * 4 + index)
            )
            bcat_ref[index] = mm(place, au_ref[index]).astype(BF)
        acat_ref[...] = total.astype(BF)
        table_ref[...] = jnp.zeros_like(table_ref)
        table_ref[0 : EXPERTS + 4, :] = router_ref[...].astype(F32)
        table_ref[MIX_ROW : MIX_ROW + 4, :] = cmix_ref[...]
        table_ref[VECTOR_ROW : VECTOR_ROW + 2, :] = vec_ref[...]
        read_ref[...] = jnp.zeros_like(read_ref)
        read_ref[0 : EXPERTS + 4, :] = router_ref[...].astype(F32)
        for place, piece in enumerate(split3(cmix_ref[...])):
            read_ref[16 + 8 * place : 20 + 8 * place, :] = piece.astype(F32)
        for place, piece in enumerate(split3(vec_ref[...])):
            read_ref[READ_VECTOR + 2 * place : READ_VECTOR + 2 * place + 2, :] = piece.astype(F32)
        square_ref[...] = jnp.zeros_like(square_ref)
        square_ref[0 : EXPERTS + 4, 0 : EXPERTS + 4] = resid_ref[...]
        mix_ref[...] = square_ref[...].T[0:16]

    def stages(at):
        x = x_ref[at].astype(F32)
        scale = lax.rsqrt(jnp.mean(x * x, axis=-1, keepdims=True) + EPSILON)
        normed = (x * scale * gain_ref[0:1, :]).astype(BF)
        normed_ref[at] = normed
        yield
        inner = mm(normed, acat_ref[...]).astype(BF)
        inner_ref[at] = inner
        yield
        for index, out_ref in enumerate((q_ref, k_ref, v_ref)):
            value = mm(normed, w_ref[index]) + mm(inner, bcat_ref[index])
            yield
            rows = pl.ds(pl.multiple_of(pl.program_id(0) * STEP + at.start, TILE), TILE)
            if index == 2:
                for pair in range(PAIRS):
                    span = slice(pair * LANES, pair * LANES + LANES)
                    out_ref[pair, rows] = value[:, span].astype(BF)
                continue
            cosine, sine = turn_rows(coarse_ref, fine_ref, pl.program_id(0) * STEP + at.start, TILE)
            for pair in range(PAIRS):
                span = slice(pair * LANES, pair * LANES + LANES)
                turned = rope(value[:, span], cosine, sine).astype(BF)
                if index == 0:
                    turned = (turned.astype(F32) * HD**-0.5).astype(BF)
                out_ref[pair, rows] = turned
            yield

    side_by_side(stages)


def attend_body(len_ref, q_ref, k_ref, v_ref, mixed_ref, q2_ref):
    tok_count = q_ref.shape[0]
    lane = iota((tok_count, LANES), 1)
    hidden_key = iota((tok_count, LANES), 0) >= len_ref[0]
    row = iota((LANES, tok_count), 0)
    row_tile = row[:, :TILE]
    causal = iota((TILE, TILE), 0) <= iota((TILE, TILE), 1)
    queries_t = q_ref[...].astype(F32).T
    values_t = v_ref[...].astype(F32).T
    keys = k_ref[...].astype(F32)
    heads = []
    for head in range(2):
        spare = HD * (1 - head)
        bias = jnp.where((lane == spare) & hidden_key, NEG, 0.0)
        one = jnp.where(row == spare, 1.0, 0.0)
        own = row // HD == head
        heads.append(
            (
                jnp.where(lane // HD == head, keys, bias).astype(BF),
                jnp.where(own, queries_t, one).astype(BF),
                jnp.where(own, values_t, one).astype(BF),
            )
        )
    units = [(start, head) for start in range(0, tok_count, TILE) for head in range(2)]

    def score(unit):
        start, head = unit
        keys, queries, _ = heads[head]
        part = queries[:, start : start + TILE]
        near = mm(keys[start : start + TILE], part)
        return near, mm(keys[:start], part) if start else None

    outs = {}
    waiting = [score(unit) for unit in units[:3]]
    for index, (start, head) in enumerate(units):
        near, far = waiting.pop(0)
        if index + 3 < len(units):
            waiting.append(score(units[index + 3]))
        spare = HD * (1 - head)
        _, queries, values = heads[head]
        near = jnp.where(causal, near, NEG)
        top = jnp.max(near, axis=0, keepdims=True)
        if start:
            top = jnp.maximum(top, jnp.max(far, axis=0, keepdims=True))
        mixed = mm(values[:, start : start + TILE], jnp.exp(near - top).astype(BF))
        if start:
            mixed = mixed + mm(values[:, :start], jnp.exp(far - top).astype(BF))
        total = mixed[spare : spare + 1]
        outs[head] = mixed * (1.0 / total)
        kept = queries[:, start : start + TILE]
        logs = jnp.zeros((LANES, TILE), F32)
        for offset, piece in enumerate(split3(top + jnp.log(total))):
            logs = jnp.where(row_tile == spare + 1 + offset, piece.astype(F32), logs)
        q2_ref[head * LANES : head * LANES + LANES, start : start + TILE] = kept + logs.astype(BF)
        if head == 1:
            mixed = jnp.where(row_tile < HD, outs[0], outs[1])
            mixed_ref[start : start + TILE] = mixed.T.astype(BF)


def pre_attend_body(steps, len_ref, *refs):
    pre_ins, pre_outs = refs[:12], refs[12:19]
    key_ref, value_ref, mixed_ref, q2_ref, q_all, k_all, v_all, square_ref = refs[19:]
    step = pl.program_id(0)

    @pl.when(step < steps)
    def _():
        pre_body(*pre_ins, *pre_outs, q_all, k_all, v_all, square_ref)

    @pl.when(step >= steps)
    def _():
        pair = step - steps
        key_ref[...] = k_all[pair]
        value_ref[...] = v_all[pair]
        attend_body(len_ref, q_all.at[pair], k_all.at[pair], v_all.at[pair], mixed_ref, q2_ref)


def pre_attend_call(
    length, ids, tokens, gains, weights, down, upper, coarse, fine, router, constant_mix, vectors,
    residual_mix,
):
    tok_count, width = tokens.shape
    steps = tok_count // STEP

    def rows_of(columns):
        return pl.BlockSpec((STEP, columns), lambda i: (jnp.minimum(i, steps - 1), 0))

    column = pl.BlockSpec((tok_count, LANES), lambda i: (0, jnp.maximum(i - steps, 0)))
    return pl.pallas_call(
        functools.partial(pre_attend_body, steps),
        grid=(steps + PAIRS,),
        in_specs=[
            smem(), smem(), rows_of(width), whole(gains.shape), whole(weights.shape), whole(down.shape),
            whole(upper.shape), whole(coarse.shape), whole(fine.shape), whole(router.shape),
            whole(constant_mix.shape), whole(vectors.shape), whole(residual_mix.shape),
        ],
        out_specs=[
            rows_of(width), rows_of(LANES), whole((width, LANES)), whole(upper.shape),
            whole((LANES, width)), whole((16, LANES)), whole((READ_ROWS, width)), column, column,
            column, pl.BlockSpec((2 * LANES, tok_count), lambda i: (jnp.maximum(i - steps, 0), 0)),
        ],
        out_shape=[
            shape_of(tok_count, width), shape_of(tok_count, LANES), shape_of(width, LANES),
            shape_of(*upper.shape), shape_of(LANES, width, dtype=F32), shape_of(16, LANES, dtype=F32),
            shape_of(READ_ROWS, width, dtype=F32), shape_of(tok_count, width),
            shape_of(tok_count, width), shape_of(tok_count, width), shape_of(2 * width, tok_count),
        ],
        scratch_shapes=[pltpu.VMEM((PAIRS, tok_count, LANES), BF)] * 3
        + [pltpu.VMEM((LANES, LANES), F32)],
        compiler_params=PARAMS,
        cost_estimate=cost(25),
        name="attention_forward",
    )(
        length, ids, tokens, gains, weights, down, upper, coarse, fine, router, constant_mix, vectors,
        residual_mix,
    )


def attend_back_body(
    len_ref, q2_ref, k_ref, v_ref, mixed_ref, back_ref, coarse_ref, fine_ref,
    dq_ref, dk_ref, dv_ref, acc_ref, turn_ref,
):
    tok_count = k_ref.shape[0]

    @pl.when(pl.program_id(0) == 0)
    def _():
        turn_ref[0], turn_ref[1] = turn_rows(coarse_ref, fine_ref, 0, tok_count)

    lane = iota((tok_count, LANES), 1)
    position = iota((tok_count, LANES), 0)
    bias = jnp.where(position < len_ref[0], 0.0, NEG)
    causal = iota((TILE, TILE), 0) <= iota((TILE, TILE), 1)
    row = iota((LANES, tok_count), 0)
    back = back_ref[...].astype(F32)
    product_t = (back * mixed_ref[...].astype(F32)).T
    back_t = back.T
    keys, values = k_ref[...].astype(F32), v_ref[...].astype(F32)
    heads = []
    for head in range(2):
        own = lane // HD == head
        spare = HD * (1 - head)
        minus = jnp.where((lane > spare) & (lane < spare + 4), -1.0, 0.0)
        q2 = q2_ref[head * LANES : head * LANES + LANES, :]
        k2f = jnp.where(own, keys, jnp.where(lane == spare, bias, minus))
        k2 = k2f.astype(BF)
        k2t = k2f.T.astype(BF)
        v2 = jnp.where(own, values, minus).astype(BF)
        own_row = row // HD == head
        delta = jnp.sum(jnp.where(own_row, product_t, 0.0), axis=0, keepdims=True)
        back2 = jnp.where(own_row, back_t, 0.0)
        for offset, piece in enumerate(split3(delta)):
            back2 = jnp.where(row == spare + 1 + offset, piece.astype(F32), back2)
        back2 = back2.astype(BF)
        heads.append((k2, k2t, v2, q2, back2))
    units = [(start, head) for start in range(0, tok_count, TILE) for head in range(2)]

    def score(unit):
        start, head = unit
        k2, _, v2, q2, back2 = heads[head]
        stop = start + TILE
        return mm(k2[start:stop], q2[:, start:]), mm(v2[start:stop], back2[:, start:])

    grads = [([], []), ([], [])]
    waiting = [score(unit) for unit in units[:AHEAD]]
    for index, (start, head) in enumerate(units):
        scores, slopes = waiting.pop(0)
        if index + AHEAD < len(units):
            waiting.append(score(units[index + AHEAD]))
        _, k2t, _, q2, back2 = heads[head]
        stop = start + TILE
        diagonal = jnp.where(causal, scores[:, :TILE], NEG)
        if stop < tok_count:
            diagonal = jnp.concatenate([diagonal, scores[:, TILE:]], axis=1)
        weights = jnp.exp(diagonal)
        turned = (weights * slopes).astype(BF)
        grads[head][1].append(mm_nt(weights.astype(BF), back2[:, start:]))
        grads[head][0].append(mm_nt(turned, q2[:, start:]))
        update = mm(k2t[:, start:stop], turned)
        if start == 0:
            acc_ref[head] = update
        else:
            acc_ref[head, :, start:] += update
    grads = [
        (jnp.concatenate(keys, axis=0), jnp.concatenate(values, axis=0)) for keys, values in grads
    ]
    low_lane = lane < HD
    cosine, sine = turn_ref[0], -turn_ref[1]
    dq = jnp.where(row < HD, acc_ref[0], acc_ref[1]).T * HD**-0.5
    dq_ref[...] = rope(dq, cosine, sine).astype(BF)
    dk = jnp.where(low_lane, grads[0][0], grads[1][0])
    dk_ref[...] = rope(dk, cosine, sine).astype(BF)
    dv_ref[...] = jnp.where(low_lane, grads[0][1], grads[1][1]).astype(BF)


def pack_grads(packed, id_ref, acc_ref, grad_ref):
    count, width = acc_ref.shape[0], acc_ref.shape[1] // 2
    if not packed:
        grad_ref[...] = acc_ref[...].astype(BF)
        return
    half = width // 2
    shape = (16 * RANK, count)
    place, row = iota(shape, 0), iota(shape, 1)
    total = None
    for index in range(4):
        kind, part = index // 2, index % 2
        here = (place % 4 == row % 4) & (place // 16 == row // 4)
        here = here & (place // 8 % 2 == part) & (place // 4 % 2 == kind)
        start = kind * width + part * half
        piece = mm(hot(here), acc_ref[:, start : start + half].astype(BF))
        total = piece if total is None else total + piece
    grad_ref[:, 0:half] = total.astype(BF)
    grad_ref[:, half:] = jnp.full((16 * RANK, LANES), id_ref[0].astype(F32), F32).astype(BF)


def attend_back_all_body(packed, len_ref, id_ref, *refs):
    ins, refs = refs[:7], refs[7:]
    bcat_ref, inner_ref, inner_o_ref, din_ref, ba_ref, normed_hbm, mixed_hbm = refs[:7]
    dq_ref, dk_ref, dv_ref, back_ref, grad_ref = refs[7:12]
    scratch, (inner_all, back_all, acc_ref, normed_all, mixed_all, sems) = refs[12:14], refs[14:]
    step = pl.program_id(0)
    count = inner_all.shape[1]
    width = normed_all.shape[1]
    copies = [
        pltpu.make_async_copy(normed_hbm, normed_all, sems.at[0]),
        pltpu.make_async_copy(mixed_hbm, mixed_all, sems.at[1]),
    ]

    @pl.when(step == 0)
    def _():
        for copy in copies:
            copy.start()
        inner_all[0] = inner_ref[...].astype(F32).T[0:count].astype(BF)
        inner_all[1] = inner_o_ref[...].astype(F32).T[0:count].astype(BF)
        back_all[...] = jnp.zeros_like(back_all)

    @pl.when(step < PAIRS)
    def _():
        attend_back_body(len_ref, *ins, dq_ref, dk_ref, dv_ref, *scratch)
        number = iota((count, LANES), 0) % 4
        upper = mm(inner_all[1], ba_ref[...])
        total = back_all[...]
        for index, ref in enumerate((dq_ref, dk_ref, dv_ref)):
            value = ref[...]
            upper = jnp.where(number == index, mm(inner_all[0], value), upper)
            total = total + mm_nt(value, bcat_ref[index])
        back_all[...] = total
        at = width + step * LANES
        acc_ref[:, pl.ds(pl.multiple_of(at, LANES), LANES)] = upper

    @pl.when(step == PAIRS)
    def _():
        back = back_all[...].astype(BF)
        back_ref[...] = back
        back_t = (back.astype(F32) + din_ref[...].astype(F32)).T[0:count].astype(BF)
        for copy in copies:
            copy.wait()
        number = iota((count, width), 0) % 4
        half = back_t.shape[1] // 2

        def down(rows_ref):
            return mm(back_t[:, :half], rows_ref[:half]) + mm(back_t[:, half:], rows_ref[half:])

        acc_ref[:, 0:width] = jnp.where(number < 3, down(normed_all), down(mixed_all))
        pack_grads(packed, id_ref, acc_ref, grad_ref)


def attend_back_call(
    packed, length, ids, q2, keys, values, mixed, back, coarse, fine, bcat, inner, inner_o, din, ba,
    normed,
):
    tok_count, width = keys.shape
    column = pl.BlockSpec((tok_count, LANES), lambda i: (0, jnp.minimum(i, PAIRS - 1)))
    grad_shape = (16 * RANK, width // 2 + LANES) if packed else (4 * RANK, 2 * width)
    return pl.pallas_call(
        functools.partial(attend_back_all_body, packed),
        grid=(PAIRS + 1,),
        in_specs=[
            smem(), smem(),
            pl.BlockSpec((2 * LANES, tok_count), lambda i: (jnp.minimum(i, PAIRS - 1), 0)), column,
            column, column, column, whole(coarse.shape), whole(fine.shape),
            pl.BlockSpec((4, LANES, LANES), lambda i: (0, 0, jnp.minimum(i, PAIRS - 1))),
            whole(inner.shape), whole(inner_o.shape), whole(din.shape), column,
            pl.BlockSpec(memory_space=pl.ANY), pl.BlockSpec(memory_space=pl.ANY),
        ],
        out_specs=[column] * 3 + [whole((tok_count, LANES)), whole(grad_shape)],
        out_shape=[shape_of(tok_count, width)] * 3
        + [shape_of(tok_count, LANES), shape_of(*grad_shape)],
        scratch_shapes=[
            pltpu.VMEM((2, LANES, tok_count), F32), pltpu.VMEM((2, tok_count, LANES), F32),
            pltpu.VMEM((2, 4 * RANK, tok_count), BF), pltpu.VMEM((tok_count, LANES), F32),
            pltpu.VMEM((4 * RANK, 2 * width), F32), pltpu.VMEM((tok_count, width), BF),
            pltpu.VMEM((tok_count, width), BF), pltpu.SemaphoreType.DMA((2,)),
        ],
        compiler_params=PARAMS,
        cost_estimate=cost(12),
        name="attention_backward",
    )(
        length, ids, q2, keys, values, mixed, back, coarse, fine, bcat, inner, inner_o, din, ba,
        normed, mixed,
    )


def post_body(
    local, group, me_ref, mixed_ref, x_ref, wo_ref, acat_ref, bcat_ref, gain_ref, read_ref, mix_ref,
    prev_ref, routes_ref, slot_ref, hidden_ref, ei_ref, inner_ref, data_ref, cols_ref,
):
    reader = read_ref[0:READ_VECTOR].astype(BF)

    def stages(at):
        mixed = mixed_ref[at]
        inner = mm(mixed, acat_ref[...]).astype(BF)
        inner_ref[at] = inner
        yield
        hidden = x_ref[at].astype(F32) + (mm(mixed, wo_ref[...]) + mm(inner, bcat_ref[0]))
        hidden_ref[at] = hidden
        yield
        scale = lax.rsqrt(jnp.mean(hidden * hidden, axis=-1, keepdims=True) + EPSILON)
        ei = (hidden * scale * gain_ref[1:2, :]).astype(BF)
        ei_ref[at] = ei
        yield
        read = mm_nt(reader, ei)
        yield
        logits = read[0:16]
        for index in range(EXPERTS + 4):
            logits = logits + mix_ref[:, index : index + 1] * prev_ref[index : index + 1, at]
        first, second = routes_ref[0:1, at].astype(F32), routes_ref[1:2, at].astype(F32)
        number = iota((16, TILE), 0).astype(F32)
        one = jnp.sum(jnp.where(number == first, logits, 0.0), axis=0, keepdims=True)
        two = jnp.sum(jnp.where(number == second, logits, 0.0), axis=0, keepdims=True)
        top = jnp.maximum(one, two)
        one, two = jnp.exp(one - top), jnp.exp(two - top)
        gate_a, gate_b = one / (one + two), two / (one + two)
        mixes = read[16:20] + read[24:28] + read[32:36]
        shares = []
        for index in range(2):
            left, right = mixes[2 * index : 2 * index + 1], mixes[2 * index + 1 : 2 * index + 2]
            top = jnp.maximum(left, right)
            left, right = jnp.exp(left - top), jnp.exp(right - top)
            shares += [left / (left + right), right / (left + right)]

        def both(value):
            return jnp.where(first == value, gate_a, 0.0) + jnp.where(second == value, gate_b, 0.0)

        gates = jnp.where(number == first, gate_a, 0.0) + jnp.where(number == second, gate_b, 0.0)
        beta_a, beta_b = both(EXPERTS + 2.0), both(EXPERTS + 3.0)
        keep = both(EXPERTS + 1.0) + beta_a * shares[0] + beta_b * shares[2]
        data_ref[0:8, at] = gates[0:8]
        tail = [gate_a, gate_b] + shares + [beta_a, beta_b]
        data_ref[8:16, at] = jnp.concatenate(tail, axis=0)
        yield
        slots = slot_ref[:, at].astype(F32)
        expert = iota((EXPERTS, TILE), 0)
        partner = jnp.bitwise_xor(expert // local, me_ref[0])
        base = ((expert % local) * (group * CAP) + partner * CAP).astype(F32)
        place = jnp.where(slots >= 0, slots + base + 1.0, 0.0)
        expert = expert.astype(F32)
        target_a = jnp.sum(jnp.where(expert == first, place, 0.0), axis=0, keepdims=True) - 1.0
        target_b = jnp.sum(jnp.where(expert == second, place, 0.0), axis=0, keepdims=True) - 1.0
        stack = jnp.concatenate(
            [jnp.zeros((VECTOR_ROW, TILE), F32), beta_a * shares[1], beta_b * shares[3]]
            + [jnp.zeros((2, TILE), F32), target_a, target_b, keep]
            + [jnp.zeros((LANES - KEEP_LANE - 1, TILE), F32)],
            axis=0,
        )
        cols_ref[at] = stack.T

    side_by_side(stages)


def post_send_body(local, group, steps, me_ref, id_ref, slot_all_ref, *refs):
    post_refs, out_refs, (ei_all, data_all) = refs[:16], refs[16:-2], refs[-2:]
    step = pl.program_id(0)

    @pl.when(step < steps)
    def _():
        post_body(local, group, me_ref, *post_refs)
        span = pl.ds(pl.multiple_of(step * STEP, STEP), STEP)
        ei_all[span] = post_refs[12][...]
        data_all[:, span] = post_refs[14][...]

    @pl.when(step >= steps)
    def _():
        send_rows(local, group, step - steps, me_ref, id_ref, slot_all_ref, data_all, ei_all, out_refs)


def post_call(
    local, group, me, ids, mixed, tokens, weight, acat, bcat, gains, reader, mixer, prev, routes, slots
):
    tok_count, width = tokens.shape
    steps = tok_count // STEP
    heights = [local * PIECE] * (group // 2) + [PIECE] * ((group - group // 2) * local)

    def rows_of(columns):
        return pl.BlockSpec((STEP, columns), lambda i: (jnp.minimum(i, steps - 1), 0))

    def lanes_of(height):
        return pl.BlockSpec((height, STEP), lambda i: (0, jnp.minimum(i, steps - 1)))

    return pl.pallas_call(
        functools.partial(post_send_body, local, group, steps),
        grid=(steps + group,),
        in_specs=[
            smem(), smem(), whole(slots.shape), rows_of(width), rows_of(width), whole(weight.shape),
            whole(acat.shape), pl.BlockSpec((1, LANES, width), lambda i: (3, 0, 0)), whole(gains.shape),
            whole(reader.shape), whole(mixer.shape), lanes_of(EXPERTS + 4), lanes_of(2),
            lanes_of(EXPERTS),
        ],
        out_specs=[
            rows_of(width), rows_of(width), rows_of(LANES), lanes_of(16), rows_of(LANES)
        ] + [whole((height, width)) for height in heights],
        out_shape=[
            shape_of(tok_count, width, dtype=F32), shape_of(tok_count, width),
            shape_of(tok_count, LANES), shape_of(16, tok_count, dtype=F32),
            shape_of(tok_count, LANES, dtype=F32),
        ] + [shape_of(height, width) for height in heights],
        scratch_shapes=[pltpu.VMEM((tok_count, width), BF), pltpu.VMEM((16, tok_count), F32)],
        compiler_params=PARAMS,
        cost_estimate=cost(14),
        name="after_attention",
    )(
        me, ids, slots, mixed, tokens, weight, acat, bcat, gains, reader, mixer, prev, routes, slots
    )


def expert_body(
    local_index, pair, per_owner, group, steps, has_grad, kept, *refs
):
    count = len(pair)
    piece_refs, refs = refs[:count], refs[count:]
    cot_refs, refs = refs[:count], refs[count:]
    dn_ref, ou_ref, wg_hbm, wu_hbm, wd_hbm, up_hbm, od_hbm = refs[:7]
    refs = refs[7:]
    if has_grad:
        before_hbm, refs = refs[0], refs[1:]
    refs = refs[kept:]
    back_refs, refs = refs[:count], refs[count:]
    out_refs, refs = refs[:count], refs[count:]
    (
        grad_ref, x_ref, g_ref, gate_ref, pick_ref, dr_ref, zg_ref, zu_ref, dzd_ref, zgt_ref, zut_ref,
        dzdt_ref, racc_ref, xacc_ref, zd_acc, dzg_acc, dzu_acc, h_ref, dg_ref, du_ref, wg_all, wu_all,
        wd_all, up_all, od_all, sems, *rest
    ) = refs
    rows, width = x_ref.shape
    compact = group * RANK
    tile = h_ref.shape[1]

    def copies(step):
        span = pl.ds(pl.multiple_of(step * tile, tile), tile)
        pairs = (
            (wg_hbm.at[local_index, :, span], wg_all),
            (wu_hbm.at[local_index, :, span], wu_all),
            (wd_hbm.at[local_index, span, :], wd_all),
            (up_hbm.at[local_index, :, :, span], up_all),
            (od_hbm.at[local_index, span, :], od_all),
        )
        return [
            pltpu.make_async_copy(source, target.at[step], sems.at[step, place])
            for place, (source, target) in enumerate(pairs)
        ]

    def begin(step):
        for copy in copies(step):
            copy.start()

    begin(0)

    def fold(value):
        place = iota((compact, LANES), 0)
        block = per_owner * group
        inner = place // block * per_owner + place % per_owner
        folded = mm_nt(hot(iota((compact, LANES), 1) % RANK == inner), value)
        place = iota((compact, rows), 0)
        owner = place % block // per_owner
        mine = iota((compact, rows), 1) // CAP + pair[0]
        return jnp.where(mine == owner, folded, 0.0).astype(BF)

    def put(start, value):
        grad_ref[:, pl.ds(start, value.shape[1])] = value.astype(BF)

    for index in range(count):
        span = slice(index * CAP, index * CAP + CAP)
        x_ref[span] = piece_refs[index][0:CAP]
        g_ref[span] = cot_refs[index][...]
        meta = piece_refs[index][CAP:PIECE].astype(F32)
        gate = (meta[0:1] + meta[1:2] + meta[2:3])[:, 0 : 2 * LANES]
        gate_ref[span] = jnp.broadcast_to(gate, (LANES, 2 * LANES)).T[0:CAP]
        lane = (iota((CAP, LANES), 1) // RANK).astype(F32)
        pick_ref[span] = jnp.where(lane == meta[3:4, 0:LANES], 1.0, 0.0)
    chosen = pick_ref[...] > 0.0
    dr = (gate_ref[:, 0:1] * g_ref[...].astype(F32)).astype(BF)
    dr_ref[...] = dr
    zg = jnp.where(chosen, mm(x_ref[...], dn_ref[0]), 0.0).astype(BF)
    zu = jnp.where(chosen, mm(x_ref[...], dn_ref[1]), 0.0).astype(BF)
    dzd = jnp.where(chosen, mm_nt(dr, ou_ref[...]), 0.0).astype(BF)
    zg_ref[...] = zg
    zu_ref[...] = zu
    dzd_ref[...] = dzd
    zgt_ref[...] = fold(zg)
    zut_ref[...] = fold(zu)
    dzdt_ref[...] = fold(dzd)
    for ref in (racc_ref, xacc_ref, zd_acc, dzg_acc, dzu_acc):
        ref[...] = jnp.zeros_like(ref)

    total = steps * tile
    begin(1)
    if has_grad:
        before = pltpu.make_async_copy(before_hbm, rest[0], rest[1])
        before.start()

    def run(step, carry):
        for copy in copies(step):
            copy.wait()

        @pl.when(step + 2 < steps)
        def _():
            begin(step + 2)

        wg_ref, wu_ref, wd_ref = wg_all.at[step], wu_all.at[step], wd_all.at[step]
        up_ref, od_ref = up_all.at[step], od_all.at[step]
        gate = mm(x_ref[...], wg_ref[...]) + mm(zg_ref[...], up_ref[0])
        upper = mm(x_ref[...], wu_ref[...]) + mm(zu_ref[...], up_ref[1])
        share = 0.5 * jnp.tanh(0.5 * gate) + 0.5
        silu = gate * share
        active = (silu * upper).astype(BF)
        h_ref[...] = active
        back = mm_nt(dr_ref[...], wd_ref[...]) + mm_nt(dzd_ref[...], od_ref[...])
        du = (back * silu).astype(BF)
        dg = (back * upper * (share + silu * (1.0 - share))).astype(BF)
        du_ref[...] = du
        dg_ref[...] = dg
        racc_ref[...] += mm(active, wd_ref[...])
        zd_acc[...] += mm(active, od_ref[...])
        xacc_ref[...] += mm_nt(dg, wg_ref[...]) + mm_nt(du, wu_ref[...])
        dzg_acc[...] += mm_nt(dg, up_ref[0])
        dzu_acc[...] += mm_nt(du, up_ref[1])
        at = pl.multiple_of(step * tile, tile)
        put(at, mm(zgt_ref[...], dg_ref[...]))
        put(total + at, mm(zut_ref[...], du_ref[...]))
        put(2 * total + at, mm(dzdt_ref[...], h_ref[...]))
        return carry

    lax.fori_loop(0, steps, run, 0)
    chosen = pick_ref[...] > 0.0
    zd = jnp.where(chosen, zd_acc[...], 0.0).astype(BF)
    dzg = jnp.where(chosen, dzg_acc[...], 0.0).astype(BF)
    dzu = jnp.where(chosen, dzu_acc[...], 0.0).astype(BF)
    result = racc_ref[...] + mm(zd, ou_ref[...])
    gated = (gate_ref[:, 0:1] * result).astype(BF)
    product = g_ref[...].astype(F32) * result.astype(BF).astype(F32)
    dots = jnp.broadcast_to(jnp.sum(product, axis=-1, keepdims=True), (rows, LANES))
    back_rows = (xacc_ref[...] + mm_nt(dzg, dn_ref[0]) + mm_nt(dzu, dn_ref[1])).astype(BF)
    for index in range(count):
        span = slice(index * CAP, index * CAP + CAP)
        out_refs[index][...] = gated[span]
        back_refs[index][0:CAP, :] = back_rows[span]
        column = jnp.concatenate(
            [dots[span], jnp.zeros((2 * LANES - CAP, LANES), F32)], axis=0
        ).T[0:1]
        meta = jnp.concatenate(
            [piece.astype(F32) for piece in split3(column)]
            + [jnp.zeros((META - 3, 2 * LANES), F32)],
            axis=0,
        )
        meta = jnp.concatenate([meta, jnp.zeros((META, width - 2 * LANES), F32)], axis=1)
        back_refs[index][CAP:PIECE, :] = meta.astype(BF)
    base = 3 * total
    place = iota((compact, LANES), 0)
    owner = place % (per_owner * group) // per_owner
    ids = jnp.zeros((compact, LANES), F32)
    for index in range(count):
        meta = piece_refs[index][CAP:PIECE, 0:LANES].astype(F32)
        ids = jnp.where(owner == pair[index], meta[3:4], ids)
    put(base + 3 * width, ids)
    put(base, mm(fold(zd), dr_ref[...]))
    put(base + width, mm(fold(dzg), x_ref[...]))
    put(base + 2 * width, mm(fold(dzu), x_ref[...]))
    if has_grad:
        before.wait()
        grad_ref[...] = grad_ref[...] + rest[0][...]


def expert_call(index, pair, group, per_owner, pieces, cots, before, results, weights):
    gate_w, up_w, down_w, in_down, in_up, out_down, out_up = weights
    width, hidden = gate_w.shape[1:]
    rows = len(pair) * CAP
    steps = hidden // FTILE
    columns = 3 * hidden + 3 * width + LANES
    compact = group * RANK
    has_grad = before is not None
    return pl.pallas_call(
        functools.partial(
            expert_body, index, pair, per_owner, group, steps, has_grad, len(results)
        ),
        grid=(1,),
        in_specs=[
            pl.BlockSpec((PIECE, width), lambda f, row=piece.shape[0] // PIECE > 1: (index * row, 0))
            for piece in pieces
        ]
        + [pl.BlockSpec((CAP, width), lambda f: (index, 0))] * len(pair)
        + [
            pl.BlockSpec((None, 2, width, LANES), lambda f: (index, 0, 0, 0)),
            pl.BlockSpec((None, LANES, width), lambda f: (index, 0, 0)),
        ]
        + [pl.BlockSpec(memory_space=pl.ANY)] * 5
        + [pl.BlockSpec(memory_space=pl.ANY)] * (has_grad + len(results)),
        out_specs=[whole((PIECE, width))] * len(pair)
        + [pl.BlockSpec((CAP, width), lambda f: (index, 0))] * len(pair)
        + [whole((compact, columns))],
        out_shape=[shape_of(PIECE, width)] * len(pair)
        + [shape_of(gate_w.shape[0] * CAP, width)] * len(pair)
        + [shape_of(compact, columns)],
        input_output_aliases={
            2 * len(pair) + 7 + has_grad + place: len(pair) + place for place in range(len(results))
        },
        scratch_shapes=[pltpu.VMEM((rows, width), BF)] * 2
        + [pltpu.VMEM((rows, LANES), F32)] * 2
        + [pltpu.VMEM((rows, width), BF)]
        + [pltpu.VMEM((rows, LANES), BF)] * 3
        + [pltpu.VMEM((compact, rows), BF)] * 3
        + [pltpu.VMEM((rows, width), F32)] * 2
        + [pltpu.VMEM((rows, LANES), F32)] * 3
        + [pltpu.VMEM((rows, FTILE), BF)] * 3
        + [pltpu.VMEM((steps, width, FTILE), BF)] * 2
        + [
            pltpu.VMEM((steps, FTILE, width), BF), pltpu.VMEM((steps, 2, LANES, FTILE), BF),
            pltpu.VMEM((steps, FTILE, LANES), BF), pltpu.SemaphoreType.DMA((steps, 5)),
        ]
        + [pltpu.VMEM((compact, columns), BF), pltpu.SemaphoreType.DMA] * has_grad,
        compiler_params=PARAMS,
        cost_estimate=cost(rows / 21),
        name="expert_layer",
    )(
        *pieces, *cots, in_down, out_up, gate_w, up_w, down_w, in_up, out_down,
        *([before] if has_grad else []), *results,
    )


def spread(cols, index, count):
    return iota((TILE, count), 1).astype(F32) == cols[:, index : index + 1]


def combine_body(
    pieces, len_ref, *refs
):
    back_refs = refs[:pieces]
    (
        routes_ref, data_ref, cols_ref, cot_ref, ei_ref, hidden_ref, gain_ref, wo_ref, acat_ref, bcat_ref,
        table_ref, read_ref, bh_ref, ba_ref, din_ref, bm_ref, back_all, dots_ref,
    ) = refs[pieces:]
    count = pieces * CAP

    @pl.when(pl.program_id(0) == 0)
    def _():
        for index, back_ref in enumerate(back_refs):
            back_all[index * CAP : index * CAP + CAP, :] = back_ref[0:CAP, :]
        dots = [back_ref[CAP:PIECE, 0:CAP].astype(F32) for back_ref in back_refs]
        dots = jnp.concatenate(dots, axis=1)
        dots_ref[...] = jnp.concatenate([dots, jnp.zeros_like(dots)], axis=0).astype(BF)

    table_high, table_low = split2(table_ref[...])
    stack = dots_ref[...]
    vectors = read_ref[READ_VECTOR:READ_ROWS].astype(BF)

    def stages(at):
        start = pl.program_id(0) * STEP + at.start
        cols = cols_ref[at]
        chosen_a = hot(spread(cols, TARGET_LANE, count))
        chosen_b = hot(spread(cols, TARGET_LANE + 1, count))
        yield
        routed_a = jnp.sum(mm_nt(stack, chosen_a)[0:8], axis=0, keepdims=True)
        routed_b = jnp.sum(mm_nt(stack, chosen_b)[0:8], axis=0, keepdims=True)
        cot = cot_ref[at]
        cot_f = cot.astype(F32)
        yield
        along_x = jnp.sum(cot_f * ei_ref[at].astype(F32), axis=-1, keepdims=True)
        along_x = jnp.broadcast_to(along_x, (TILE, LANES)).T[0:1]
        yield
        along_c = mm_nt(vectors, cot)
        along_a = along_c[0:1] + along_c[2:3] + along_c[4:5]
        along_b = along_c[1:2] + along_c[3:4] + along_c[5:6]
        yield
        both = chosen_a + chosen_b
        half = count // 2
        back = mm(both[:, :half], back_all[:half]) + mm(both[:, half:], back_all[half:])
        yield
        first, second = routes_ref[0:1, at].astype(F32), routes_ref[1:2, at].astype(F32)
        token = iota((1, TILE), 1) + start
        valid = jnp.where(token < len_ref[0], 1.0, 0.0)
        gate_a, gate_b = data_ref[8:9, at], data_ref[9:10, at]
        share = [data_ref[index : index + 1, at] for index in range(10, 14)]
        beta_a, beta_b = data_ref[14:15, at], data_ref[15:16, at]
        const_a = share[0] * along_x + share[1] * along_a
        const_b = share[2] * along_x + share[3] * along_b

        def here(route):
            return (
                jnp.where(route == EXPERTS + 1.0, along_x, 0.0)
                + jnp.where(route == EXPERTS + 2.0, const_a, 0.0)
                + jnp.where(route == EXPERTS + 3.0, const_b, 0.0)
            )

        dot_a, dot_b = routed_a + here(first), routed_b + here(second)
        mean = gate_a * dot_a + gate_b * dot_b
        chosen_grad_a = valid * gate_a * (dot_a - mean)
        chosen_grad_b = valid * gate_b * (dot_b - mean)
        number = iota((16, TILE), 0).astype(F32)
        logit_grads = jnp.where(number == first, chosen_grad_a, 0.0) + jnp.where(
            number == second, chosen_grad_b, 0.0
        )
        mixes = []
        for index, (beta, along) in enumerate(((beta_a, along_a), (beta_b, along_b))):
            left, right = share[2 * index], share[2 * index + 1]
            weighted = left * along_x + right * along
            mixes += [
                valid * beta * left * (along_x - weighted),
                valid * beta * right * (along - weighted),
            ]
        small = jnp.concatenate(
            [logit_grads] + mixes + [jnp.zeros((LANES - 20, TILE), F32)], axis=0
        ).T
        high, low = split2(small)
        yield
        inside = iota((TILE, 1), 0) + start < len_ref[0]
        grad = jnp.where(inside, cot_f, 0.0)
        back = back + mm(high, table_high) + mm(low, table_high) + mm(high, table_low)
        back = back + cols[:, KEEP_LANE : KEEP_LANE + 1] * grad
        yield
        hidden = hidden_ref[at]
        scale = lax.rsqrt(jnp.mean(hidden * hidden, axis=-1, keepdims=True) + EPSILON)
        normed = hidden * scale
        back = back * gain_ref[1:2, :]
        back = grad + scale * (back - normed * jnp.mean(back * normed, axis=-1, keepdims=True))
        bh_ref[at] = back
        rounded = back.astype(BF)
        ba_ref[at] = rounded
        yield
        inner = mm_nt(rounded, bcat_ref[0]).astype(BF)
        din_ref[at] = inner
        yield
        bm_ref[at] = (mm_nt(rounded, wo_ref[...]) + mm_nt(inner, acat_ref[...])).astype(BF)

    side_by_side(stages)


def combine_call(
    length, backs, routes, data, cols, cotangent, ei, hidden, gains, weight, acat, bcat, table,
    reader,
):
    tok_count, width = cotangent.shape
    pieces = len(backs)
    return pl.pallas_call(
        functools.partial(combine_body, pieces),
        grid=(tok_count // STEP,),
        in_specs=[smem()] + [whole(back.shape) for back in backs] + [
            wide(2), wide(16), tall(LANES), tall(width), tall(width), tall(width),
            whole(gains.shape), whole(weight.shape), whole(acat.shape),
            pl.BlockSpec((1, LANES, width), lambda i: (3, 0, 0)), whole(table.shape),
            whole(reader.shape),
        ],
        out_specs=[tall(width), tall(width), tall(LANES), tall(width)],
        out_shape=[
            shape_of(tok_count, width, dtype=F32), shape_of(tok_count, width),
            shape_of(tok_count, LANES), shape_of(tok_count, width),
        ],
        scratch_shapes=[
            pltpu.VMEM((pieces * CAP, width), BF), pltpu.VMEM((2 * META, pieces * CAP), BF)
        ],
        compiler_params=PARAMS,
        cost_estimate=cost(17),
        name="combine_backward",
    )(
        length, *backs, routes, data, cols, cotangent, ei, hidden, gains, weight, acat, bcat, table,
        reader,
    )


def result_body(pieces, len_ref, *refs):
    result_refs = refs[:pieces]
    cols_ref, ei_ref, hidden_ref, table_ref, out_ref, result_all = refs[pieces:]
    count = result_all.shape[0]

    @pl.when(pl.program_id(0) == 0)
    def _():
        for index in range(count // CAP):
            start = index // pieces * CAP
            result_all[index * CAP : index * CAP + CAP] = result_refs[index % pieces][start : start + CAP]

    table_high, table_low = split2(table_ref[...])

    def stages(at):
        cols = cols_ref[at]
        both = hot(spread(cols, TARGET_LANE, count) | spread(cols, TARGET_LANE + 1, count))
        yield
        half = count // 2
        mixture = mm(both[:, :half], result_all[:half]) + mm(both[:, half:], result_all[half:])
        yield
        high, low = split2(cols)
        mixture = mixture + mm(high, table_high) + mm(low, table_high) + mm(high, table_low)
        mixture = mixture + cols[:, KEEP_LANE : KEEP_LANE + 1] * ei_ref[at].astype(F32)
        yield
        inside = iota((TILE, 1), 0) + pl.program_id(0) * STEP + at.start < len_ref[0]
        out_ref[at] = (hidden_ref[at] + jnp.where(inside, mixture, 0.0)).astype(BF)

    side_by_side(stages)


def result_call(length, results, cols, ei, hidden, table):
    tok_count, width = ei.shape
    pieces = len(results)
    return pl.pallas_call(
        functools.partial(result_body, pieces),
        grid=(tok_count // STEP,),
        in_specs=[smem()] + [whole(result.shape) for result in results] + [
            tall(LANES), tall(width), tall(width), whole(table.shape),
        ],
        out_specs=tall(width),
        out_shape=shape_of(tok_count, width),
        scratch_shapes=[pltpu.VMEM((pieces * results[0].shape[0], width), BF)],
        compiler_params=PARAMS,
        cost_estimate=cost(8),
        name="layer_output",
    )(length, *results, cols, ei, hidden, table)


def last_body(
    dq_ref, dk_ref, dv_ref, w_ref, acat_ref, back_ref, x_ref, bh_ref, gain_ref, out_ref
):
    def stages(at):
        parts = [mm_nt(back_ref[at], acat_ref[...])]
        for index, ref in enumerate((dq_ref, dk_ref, dv_ref)):
            parts.append(mm_nt(ref[at], w_ref[index]))
            yield
        total = parts[0] + parts[1] + parts[2] + parts[3]
        x = x_ref[at].astype(F32)
        scale = lax.rsqrt(jnp.mean(x * x, axis=-1, keepdims=True) + EPSILON)
        normed = x * scale
        back = total * gain_ref[0:1, :]
        back = scale * (back - normed * jnp.mean(back * normed, axis=-1, keepdims=True))
        out_ref[at] = (bh_ref[at] + back).astype(BF)

    side_by_side(stages)


def last_call(dq, dk, dv, weights, acat, back, tokens, bh, gains):
    tok_count, width = tokens.shape
    return pl.pallas_call(
        last_body,
        grid=(tok_count // STEP,),
        in_specs=[
            tall(width), tall(width), tall(width), whole(weights.shape), whole(acat.shape),
            tall(LANES), tall(width), tall(width), whole(gains.shape),
        ],
        out_specs=tall(width),
        out_shape=shape_of(tok_count, width),
        compiler_params=PARAMS,
        cost_estimate=cost(9),
        name="after_attention_backward",
    )(dq, dk, dv, weights, acat, back, tokens, bh, gains)


def exchange(value, axes):
    return lax.all_to_all(value, axes, split_axis=0, concat_axis=0, tiled=True)


def gather_all(value, axes, count):
    return exchange(jnp.broadcast_to(value[None], (count,) + value.shape), axes)


def swap(value, partner, group):
    if partner == 0:
        return value
    return lax.ppermute(value, "expert", [(index, index ^ partner) for index in range(group)])


def find_adapters(id_rows):
    count = id_rows.shape[0]
    padded = id_rows.astype(F32)
    if count % LANES:
        padded = jnp.concatenate([padded, jnp.zeros((-count % LANES, LANES), F32)], axis=0)
    return padded.T[0:1, 0:count].astype(jnp.int32)


def sum_expert_body(each, adapters, in_ref, out_ref):
    count, columns = in_ref.shape[0], out_ref.shape[1]
    found = find_adapters(in_ref[:, columns:])
    place = iota((adapters * each, count), 0)
    column = iota((adapters * each, count), 1)
    pick = hot((place // each == found) & (place % each == column % each))
    out_ref[...] = mm(pick, in_ref[:, 0:columns]).astype(BF)


def exchange_expert_grads(grads, group, owners):
    split = min(RANK, owners)
    each, parts = RANK // split, owners // split
    columns = (grads.shape[1] - LANES) // parts
    pieces = grads.reshape(split, each * group, grads.shape[1])
    if parts > 1:
        ids = jnp.broadcast_to(pieces[:, None, :, parts * columns :], (split, parts, each * group, LANES))
        pieces = pieces[:, :, : parts * columns].reshape(split, each * group, parts, columns)
        pieces = jnp.concatenate([pieces.transpose(0, 2, 1, 3), ids], axis=-1)
        pieces = pieces.reshape(owners, each * group, columns + LANES)
    return exchange(pieces, "dp").reshape(owners * group * each, columns + LANES)


def sum_expert_grads(got, adapters, owners):
    columns = got.shape[1] - LANES
    each = RANK // min(RANK, owners)
    return pl.pallas_call(
        functools.partial(sum_expert_body, each, adapters),
        out_shape=shape_of(adapters * each, columns),
        compiler_params=PARAMS,
        cost_estimate=cost(2.2),
        name="expert_gradient_part",
    )(got)


def finish_expert_body(split, adapters, hidden, in_ref, *refs):
    down_ref, up_ref, out_down_ref, out_up_ref = refs[-4:]
    each = RANK // split
    rows = adapters * each
    count = split * rows
    width = out_up_ref.shape[1]

    def place(value):
        return value // each % adapters * RANK + value // (adapters * each) * each + value % each

    move = hot(iota((count, count), 0) == place(iota((count, count), 1)))
    back = hot(iota((count, count), 1) == place(iota((count, count), 0)))

    def part(start, size):
        span = slice(start, start + size)
        rows_of = [in_ref[owner, :, span] for owner in range(split)]
        return jnp.concatenate(rows_of, axis=0)

    for index in range(2):
        up_ref[index] = mm(move, part(index * hidden, hidden))
    out_down_ref[...] = mm_tn(part(2 * hidden, hidden), back)
    base = 3 * hidden
    out_up_ref[...] = mm(move, part(base, width))
    for index in range(2):
        base += width
        down_ref[index] = mm_tn(part(base, width), back)


def finish_expert_call(index, local, everything, outs, adapters, width, hidden):
    owners, rows, columns = everything.shape
    total = adapters * RANK
    shapes = [(local, 2, width, total), (local, 2, total, hidden), (local, hidden, total),
              (local, total, width)]
    specs = [
        pl.BlockSpec((None,) + shape[1:], lambda *_, rank=len(shape): (index,) + (0,) * (rank - 1))
        for shape in shapes
    ]
    return pl.pallas_call(
        functools.partial(finish_expert_body, owners, adapters, hidden),
        grid=(1,),
        in_specs=[whole(everything.shape)] + [pl.BlockSpec(memory_space=pl.ANY)] * len(outs),
        out_specs=specs,
        out_shape=[shape_of(*shape, dtype=F32) for shape in shapes],
        input_output_aliases={1 + place: place for place in range(len(outs))},
        compiler_params=PARAMS,
        cost_estimate=cost(4),
        name="expert_gradient_sums",
    )(everything, *outs)


def spread_expert_grads(own, adapters, owners):
    split = min(RANK, owners)
    each, parts = RANK // split, owners // split
    everything = gather_all(own, "dp", owners)
    everything = everything.reshape(split, parts, adapters, each, own.shape[1])
    everything = everything.transpose(2, 0, 3, 1, 4)
    return everything.reshape(adapters * RANK, parts * own.shape[1]).astype(F32)


def expert_sums(owned, adapters, owners, width, hidden):
    sums = [spread_expert_grads(value, adapters, owners) for value in owned]
    base = 3 * hidden
    up = [[value[:, 0:hidden], value[:, hidden : 2 * hidden]] for value in sums]
    down = [
        [value[:, base + width * part : base + width * (part + 1)].T for part in (1, 2)]
        for value in sums
    ]
    return (
        jnp.stack([jnp.stack(value) for value in down]),
        jnp.stack([jnp.stack(value) for value in up]),
        jnp.stack([value[:, 2 * hidden : base].T for value in sums]),
        jnp.stack([value[:, base : base + width] for value in sums]),
    )


def finish_adapter_body(adapters, me_ref, *refs):
    piece_refs, (down_ref, up_ref, in_ref) = refs[:-3], refs[-3:]
    half = in_ref.shape[3]
    owners, group = piece_refs[0].shape[0], len(piece_refs)
    for other in range(group):
        place = jnp.bitwise_xor(me_ref[0], other)
        for owner in range(owners):
            in_ref[owner * (group // 2) + place // 2, place % 2] = piece_refs[other][owner]
    count = RANK * adapters

    def place(value):
        return value % adapters * RANK + value // adapters

    move = hot(iota((count, count), 0) == place(iota((count, count), 1)))
    back = hot(iota((count, count), 1) == place(iota((count, count), 0)))
    for part in range(2):
        span = slice(part * half, part * half + half)
        for kind in range(2):
            for index in range(4):
                first = (kind * 4 + index) * adapters
                rows = in_ref[:, part, first : first + adapters, :].astype(F32)
                rows = rows.reshape(count, half).astype(BF)
                if kind == 0:
                    down_ref[index, span, :] = mm_tn(rows, back)
                else:
                    up_ref[index, :, span] = mm(move, rows)


def sum_adapter_body(kinds, adapters, in_ref, out_ref):
    count, columns = in_ref.shape[0], out_ref.shape[-1]
    found = find_adapters(in_ref[:, columns:])
    place = iota((adapters * kinds, count), 0)
    column = iota((adapters * kinds, count), 1)
    pick = hot((place % adapters == found) & (place // adapters == column % kinds))
    own = mm(pick, in_ref[:, 0:columns]).astype(BF)
    for index in range(out_ref.shape[0]):
        out_ref[index] = own


def adapter_sums(grads, meanwhile, later, finish, parts, ids, adapters, owners, group, width):
    axes, everyone = ("dp", "expert"), owners * group
    if everyone == 2 * RANK and group == 4:
        kinds = 8
        got = exchange(grads.reshape(everyone, kinds, grads.shape[1]), axes)
        got, meanwhile = lax.optimization_barrier((got, meanwhile))
        own = pl.pallas_call(
            functools.partial(sum_adapter_body, kinds, adapters),
            out_shape=shape_of(owners, kinds * adapters, width // 2),
            compiler_params=PARAMS,
            cost_estimate=cost(2.0),
            name="adapter_gradient_part",
        )(got.reshape(everyone * kinds, grads.shape[1]))
        mine = exchange(own, "dp")
        mine, later = lax.optimization_barrier((mine, later))
        across = swap(mine, 2, group)
        full = [mine, swap(mine, 1, group), across, swap(across, 1, group)]
        total = adapters * RANK
        down, upper = pl.pallas_call(
            functools.partial(finish_adapter_body, adapters),
            in_specs=[smem()] + [pl.BlockSpec(memory_space=pltpu.VMEM)] * group,
            out_shape=[shape_of(4, width, total, dtype=F32), shape_of(4, total, width, dtype=F32)],
            scratch_shapes=[pltpu.VMEM((RANK, 2, kinds * adapters, width // 2), BF)],
            compiler_params=PARAMS,
            cost_estimate=cost(3.6),
            name="adapter_gradient_sums",
        )(lax.axis_index("expert").reshape(1).astype(jnp.int32), *full)
        (down, upper), later, parts = lax.optimization_barrier(((down, upper), later, parts))
        return down, upper, meanwhile, finish(later, parts)
    later = finish(later, parts)
    all_ids = exchange(jnp.broadcast_to(ids, (everyone,)), axes)
    pieces = grads.reshape(everyone, RANK * 4 * 2 * width // everyone)
    got = exchange(pieces, axes)
    pick = (jnp.arange(adapters, dtype=jnp.int32)[:, None] == all_ids[None, :]).astype(BF)
    own = jnp.dot(pick, got, preferred_element_type=F32).astype(BF)
    full = gather_all(own, axes, everyone)
    full = full.reshape(RANK, everyone // RANK, adapters, -1).transpose(2, 0, 1, 3)
    full = full.reshape(adapters * RANK, 4, 2, width).astype(F32)
    return full[:, :, 0].transpose(1, 2, 0), full[:, :, 1].transpose(1, 0, 2), meanwhile, later


def body(
    tokens,
    cotangent,
    lengths,
    adapter_ids,
    routes,
    prev_logits,
    norm_gains,
    input_weights,
    output_weight,
    adapter_down,
    adapter_up,
    router,
    residual_mix,
    constant_mix,
    constant_vectors,
    expert_gate,
    expert_up,
    expert_down,
    expert_adapter_down,
    expert_adapter_up,
    output_adapter_down,
    output_adapter_up,
):
    tok_count, width = tokens.shape
    hidden_width = expert_gate.shape[2]
    group, owners = lax.axis_size("expert"), lax.axis_size("dp")
    local = expert_gate.shape[0]
    adapters = adapter_down.shape[-1] // RANK
    angles = [jnp.asarray(table) for table in turn_tables(tok_count)]
    weights = (
        expert_gate, expert_up, expert_down, expert_adapter_down, expert_adapter_up,
        output_adapter_down, output_adapter_up,
    )
    per_owner = RANK // min(RANK, owners)
    everyone = owners * group
    me = lax.axis_index("expert")

    me = me.reshape(1).astype(jnp.int32)

    routes, prev_logits = routes.T, prev_logits.T
    slots, *grad_sends = route_call(local, group, lengths, me, routes, cotangent)
    cots = [swap(value, partner, group) for partner, value in enumerate(grad_sends)]
    normed, inner, acat, bcat, table, mixer, reader, keys, values, mixed, q2 = pre_attend_call(
        lengths, adapter_ids, tokens, norm_gains, input_weights, adapter_down, adapter_up, *angles,
        router.T, constant_mix.T, constant_vectors, residual_mix,
    )
    mixed, cots = lax.optimization_barrier((mixed, cots))
    hidden, ei, inner_o, data, cols, *sends = post_call(
        local, group, me, adapter_ids, mixed, tokens, output_weight, acat, bcat, norm_gains, reader, mixer, prev_logits,
        routes, slots,
    )
    near, far = tuple(range(group // 2)), tuple(range(group // 2, group))
    sent_near = [swap(sends[partner], partner, group) for partner in near]
    sent_far = []
    for index in range(local):
        pieces = [sends[group // 2 + place * local + index] for place in range(len(far))]
        if index > 0:
            pieces, sent_near = lax.optimization_barrier((pieces, sent_near))
        sent_far.append([swap(piece, partner, group) for piece, partner in zip(pieces, far)])
    backs = [[None] * group for _ in range(local)]
    results = [None] * group
    calls = []
    for index in range(local - 1):
        calls += [(index, near), (index, far)]
    calls += [(local - 1, near[1:] + far), (local - 1, near[:1])]
    grads, owned, parts = [None] * local, [], []
    sums = functools.partial(sum_expert_grads, adapters=adapters, owners=owners)
    last = None
    for index, some in calls:
        pieces = [
            sent_near[partner] if partner in near else sent_far[index][partner - len(near)]
            for partner in some
        ]
        if last is not None:
            pieces, last = lax.optimization_barrier((pieces, last))
        if (index, some) == calls[-1]:
            parts, last = lax.optimization_barrier((parts, last))
            owned = [sums(part) for part in parts]
            pieces, backs[:index], owned = lax.optimization_barrier((pieces, backs[:index], owned))
        outs = expert_call(
            index, some, group, per_owner, pieces, [cots[partner] for partner in some], grads[index],
            [results[partner] for partner in some] if index else [], weights,
        )
        grads[index] = last = outs[-1]
        for place, partner in enumerate(some):
            backs[index][partner] = swap(outs[place], partner, group)
            results[partner] = outs[len(some) + place]
        if index < local - 1 and some == far:
            parts.append(exchange_expert_grads(last, group, owners))
    backs = [value for some in backs for value in some]
    parts.append(exchange_expert_grads(last, group, owners))
    gather = functools.partial(lax.all_gather, axis_name="dp", axis=0, tiled=False)
    if owners <= RANK:
        owned = [gather(own) for own in owned]
    back_hidden, back_attention, back_inner_o, back_mixed = combine_call(
        lengths, backs, routes, data, cols, cotangent, ei, hidden, norm_gains, output_weight, acat, bcat,
        table, reader,
    )
    flat, back_mixed = lax.optimization_barrier((results, back_mixed))
    flat = [swap(value, partner, group) for partner, value in enumerate(flat)]

    packed = everyone == 2 * RANK and group == 4
    dq, dk, dv, back_inner, adapter_grads = attend_back_call(
        packed, lengths, adapter_ids, q2, keys, values, mixed, back_mixed, *angles, bcat, inner, inner_o,
        back_inner_o, back_attention, normed,
    )
    parts[-1], adapter_grads, flat, owned = lax.optimization_barrier(
        (parts[-1], adapter_grads, flat, owned)
    )
    own = sums(parts[-1])
    adapter_grads, own, flat = lax.optimization_barrier((adapter_grads, own, flat))
    owned.append(gather(own) if owners <= RANK else own)
    layer_out = result_call(lengths, flat, cols, ei, hidden, table)
    input_back = last_call(
        dq, dk, dv, input_weights, acat, back_inner, tokens, back_hidden, norm_gains
    )
    outs = []
    if owners <= RANK:
        for index, own in enumerate(owned[:-1]):
            outs = finish_expert_call(index, local, own, outs, adapters, width, hidden_width)
    def finish(later, part):
        input_back, outs = later
        if owners <= RANK:
            return input_back, finish_expert_call(
                local - 1, local, part, outs, adapters, width, hidden_width
            )
        return input_back, expert_sums(owned, adapters, owners, width, hidden_width)

    down_sum, upper_sum, layer_out, (input_back, outs) = adapter_sums(
        adapter_grads, layer_out, (input_back, outs), finish, owned[-1], adapter_ids, adapters, owners, group, width
    )
    in_down_sum, in_up_sum, out_down_sum, out_up_sum = outs
    return (
        layer_out,
        input_back,
        down_sum,
        upper_sum,
        in_down_sum,
        in_up_sum,
        out_down_sum,
        out_up_sum,
    )


def solution(mesh):
    tokens_spec, copied = P(("dp", "expert"), None), P()
    owned = P("expert")
    placed = (
        (tokens_spec, tokens_spec, P(("dp", "expert")), P(("dp", "expert")), tokens_spec, tokens_spec)
        + (copied,) * 9
        + (owned,) * 7
    )
    return jax.shard_map(
        body,
        mesh=mesh,
        in_specs=placed,
        out_specs=(tokens_spec, tokens_spec, copied, copied) + (owned,) * 4,
        check_vma=False,
    )
```

```python
import functools
import math

import jax
import jax.numpy as jnp
import numpy as np
from jax import lax
from jax.experimental import pallas as pl
from jax.experimental.pallas import tpu as pltpu
from jax.sharding import PartitionSpec as P

HEADS = 12
HD = 64
EXPERTS = 8
RANK = 16
CAP = 192
EPSILON = 1e-06
F32 = jnp.float32
BF = jnp.bfloat16
NEG = -1e30
LANES = 128
TILE = 256
STEP = 512
FTILE = 512
PAIRS = HEADS // 2
AHEAD = 1
PARAMS = pltpu.CompilerParams(vmem_limit_bytes=67043328)
META = 8
MIX_ROW = 16
VECTOR_ROW = 20
TARGET_LANE = 24
KEEP_LANE = 26
READ_VECTOR = 48
READ_ROWS = 64
PIECE = CAP + META


def mm(left, right):
    return jnp.dot(left, right, preferred_element_type=F32)


def mm_nt(left, right):
    return lax.dot_general(left, right, (((1,), (1,)), ((), ())), preferred_element_type=F32)


def mm_tn(left, right):
    return lax.dot_general(left, right, (((0,), (0,)), ((), ())), preferred_element_type=F32)


def iota(shape, axis):
    return lax.broadcasted_iota(jnp.int32, shape, axis)


def hot(condition):
    return jnp.where(condition, 1.0, 0.0).astype(BF)


def split2(value):
    high = value.astype(BF)
    return high, (value - high.astype(F32)).astype(BF)


def split3(value):
    high = value.astype(BF)
    rest = value - high.astype(F32)
    middle = rest.astype(BF)
    return high, middle, (rest - middle.astype(F32)).astype(BF)


def whole(shape):
    zeros = (0,) * len(shape)
    return pl.BlockSpec(shape, lambda *_: zeros)


def smem():
    return pl.BlockSpec(memory_space=pltpu.SMEM)


def tall(width):
    return pl.BlockSpec((STEP, width), lambda i: (i, 0))


def wide(height):
    return pl.BlockSpec((height, STEP), lambda i: (0, i))


def tile(width):
    return pl.BlockSpec((TILE, width), lambda i: (i, 0))


def side_by_side(stages):
    running = [stages(slice(start, start + TILE)) for start in range(0, STEP, TILE)]
    while running:
        running = [stage for stage in running if next(stage, True) is None]


def shape_of(*shape, dtype=BF):
    return jax.ShapeDtypeStruct(shape, dtype)


def cost(microseconds):
    return pl.CostEstimate(flops=int(microseconds * 1e+09), bytes_accessed=0, transcendentals=0)


@functools.lru_cache(maxsize=None)
def turn_tables(length_in):
    half = HD // 2
    inverse = np.exp(np.arange(half, dtype=np.float64) * (-2.0 * math.log(10000.0) / HD))

    def table(positions):
        angles = np.tile(positions[:, None] * inverse[None, :], (1, 4))
        return np.stack([np.cos(angles), np.sin(angles)]).astype(np.float32)

    return table(np.arange(0.0, length_in, 32)), table(np.arange(0.0, 32))


def turn_rows(coarse_ref, fine_ref, first, count):
    fine_cos, fine_sin = fine_ref[0], fine_ref[1]
    sign = jnp.where(iota((32, LANES), 1) % HD < HD // 2, -1.0, 1.0)
    signed_cos, signed_sin = fine_cos * sign, fine_sin * sign
    cosines, sines = [], []
    for index in range(count // 32):
        row = first // 32 + index
        coarse_cos, coarse_sin = coarse_ref[0, pl.ds(row, 1), :], coarse_ref[1, pl.ds(row, 1), :]
        cosines.append(coarse_cos * fine_cos - coarse_sin * fine_sin)
        sines.append(coarse_sin * signed_cos + coarse_cos * signed_sin)
    return jnp.concatenate(cosines, axis=0), jnp.concatenate(sines, axis=0)


def rope(value, cosine, sine):
    first = iota(value.shape, 1) % HD < HD // 2
    turned = jnp.where(first, pltpu.roll(value, LANES - HD // 2, 1), pltpu.roll(value, HD // 2, 1))
    return value * cosine + turned * sine


def find_slots(length, routes_ref, slot_ref):
    tok_count = slot_ref.shape[1]
    before = hot(iota((TILE, TILE), 0) < iota((TILE, TILE), 1))
    carry = jnp.zeros((2 * EXPERTS, 1), F32)
    for start in range(0, tok_count, TILE):
        span = slice(start, start + TILE)
        expert = iota((2 * EXPERTS, TILE), 0)
        token = iota((2 * EXPERTS, TILE), 1) + start
        named = (routes_ref[0:1, span] == expert) | (routes_ref[1:2, span] == expert)
        hit = named & (token < length) & (expert < EXPERTS)
        hits = jnp.where(hit, 1.0, 0.0)
        slots = mm(hits.astype(BF), before) + carry
        carry = carry + jnp.sum(hits, axis=1, keepdims=True)
        slot_ref[:, span] = jnp.where(hit, slots, -1.0)[:EXPERTS].astype(jnp.int32)


def pick_rows(slot_ref, step, me, local):
    first = jnp.bitwise_xor(step, me) * local
    place = iota((CAP, slot_ref.shape[1]), 0)
    return first, [hot(place == slot_ref[pl.ds(first + index, 1), :]) for index in range(local)]


def pick_source(chosen, source_ref):
    half = source_ref.shape[0] // 2
    return mm(chosen[:, :half], source_ref[:half]) + mm(chosen[:, half:], source_ref[half:])


def store_piece(out_refs, step, other, index, value, start):
    @pl.when(step == other)
    def _():
        out_refs[index][start : start + value.shape[0], :] = value


def route_body(local, group, len_ref, me_ref, routes_ref, source_ref, slot_ref, *out_refs):
    step = pl.program_id(0)

    @pl.when(step == 0)
    def _():
        find_slots(len_ref[0], routes_ref, slot_ref)

    _, chosen = pick_rows(slot_ref, step, me_ref[0], local)
    rows = pick_source(jnp.concatenate(chosen, axis=0), source_ref).astype(BF)
    for other in range(group):
        store_piece(out_refs, step, other, other, rows, 0)


def route_call(local, group, length, me, routes, source):
    tok_count, width = source.shape
    return pl.pallas_call(
        functools.partial(route_body, local, group),
        grid=(group,),
        in_specs=[smem(), smem(), whole(routes.shape), whole(source.shape)],
        out_specs=[whole((EXPERTS, tok_count))] + [whole((local * CAP, width))] * group,
        out_shape=[shape_of(EXPERTS, tok_count, dtype=jnp.int32)]
        + [shape_of(local * CAP, width)] * group,
        compiler_params=PARAMS,
        cost_estimate=cost(6.5),
        name="route_rows",
    )(length, me, routes, source)


def send_rows(local, group, partner, me_ref, id_ref, slot_ref, data_ref, source_ref, out_refs):
    width = source_ref.shape[1]
    first, chosen = pick_rows(slot_ref, partner, me_ref[0], local)
    rows = pick_source(jnp.concatenate(chosen, axis=0), source_ref).astype(BF)
    for index in range(local):
        pieces = split3(data_ref[pl.ds(first + index, 1), :])
        stack = jnp.concatenate(
            [piece.astype(F32) for piece in pieces]
            + [jnp.zeros((13, chosen[index].shape[1]), F32)],
            axis=0,
        ).astype(BF)
        gates = mm_nt(stack, chosen[index])[0:META]
        gates = jnp.where(iota(gates.shape, 0) == 3, id_ref[0].astype(F32), gates)
        meta = jnp.concatenate([gates, jnp.zeros((META, width - CAP), F32)], axis=1)
        kept = rows[index * CAP : index * CAP + CAP]
        for other in range(group):
            far = other >= group // 2
            place = group // 2 + (other - group // 2) * local + index if far else other
            start = 0 if far else index * PIECE
            store_piece(out_refs, partner, other, place, kept, start)
            store_piece(out_refs, partner, other, place, meta.astype(BF), start + CAP)


def pre_body(
    id_ref, x_ref, gain_ref, w_ref, ad_ref, au_ref, coarse_ref, fine_ref, router_ref, cmix_ref, vec_ref,
    resid_ref, normed_ref, inner_ref, acat_ref, bcat_ref, table_ref, mix_ref, read_ref, q_ref, k_ref,
    v_ref, square_ref,
):
    @pl.when(pl.program_id(0) == 0)
    def _():
        first = RANK * id_ref[0]
        total = None
        for index in range(4):
            row, column = iota((LANES, LANES), 0), iota((LANES, LANES), 1)
            place = hot((row >= first) & (row < first + RANK) & (column == (row - first) * 4 + index))
            part = mm(ad_ref[index], place)
            total = part if total is None else total + part
            place = hot(
                (column >= first) & (column < first + RANK) & (row == (column - first) * 4 + index)
            )
            bcat_ref[index] = mm(place, au_ref[index]).astype(BF)
        acat_ref[...] = total.astype(BF)
        table_ref[...] = jnp.zeros_like(table_ref)
        table_ref[0 : EXPERTS + 4, :] = router_ref[...].astype(F32)
        table_ref[MIX_ROW : MIX_ROW + 4, :] = cmix_ref[...]
        table_ref[VECTOR_ROW : VECTOR_ROW + 2, :] = vec_ref[...]
        read_ref[...] = jnp.zeros_like(read_ref)
        read_ref[0 : EXPERTS + 4, :] = router_ref[...].astype(F32)
        for place, piece in enumerate(split3(cmix_ref[...])):
            read_ref[16 + 8 * place : 20 + 8 * place, :] = piece.astype(F32)
        for place, piece in enumerate(split3(vec_ref[...])):
            read_ref[READ_VECTOR + 2 * place : READ_VECTOR + 2 * place + 2, :] = piece.astype(F32)
        square_ref[...] = jnp.zeros_like(square_ref)
        square_ref[0 : EXPERTS + 4, 0 : EXPERTS + 4] = resid_ref[...]
        mix_ref[...] = square_ref[...].T[0:16]

    def stages(at):
        x = x_ref[at].astype(F32)
        scale = lax.rsqrt(jnp.mean(x * x, axis=-1, keepdims=True) + EPSILON)
        normed = (x * scale * gain_ref[0:1, :]).astype(BF)
        normed_ref[at] = normed
        yield
        inner = mm(normed, acat_ref[...]).astype(BF)
        inner_ref[at] = inner
        yield
        for index, out_ref in enumerate((q_ref, k_ref, v_ref)):
            value = mm(normed, w_ref[index]) + mm(inner, bcat_ref[index])
            yield
            rows = pl.ds(pl.multiple_of(pl.program_id(0) * STEP + at.start, TILE), TILE)
            if index == 2:
                for pair in range(PAIRS):
                    span = slice(pair * LANES, pair * LANES + LANES)
                    out_ref[pair, rows] = value[:, span].astype(BF)
                continue
            cosine, sine = turn_rows(coarse_ref, fine_ref, pl.program_id(0) * STEP + at.start, TILE)
            for pair in range(PAIRS):
                span = slice(pair * LANES, pair * LANES + LANES)
                turned = rope(value[:, span], cosine, sine).astype(BF)
                if index == 0:
                    turned = (turned.astype(F32) * HD**-0.5).astype(BF)
                out_ref[pair, rows] = turned
            yield

    side_by_side(stages)


def attend_body(len_ref, q_ref, k_ref, v_ref, mixed_ref, q2_ref):
    tok_count = q_ref.shape[0]
    lane = iota((tok_count, LANES), 1)
    hidden_key = iota((tok_count, LANES), 0) >= len_ref[0]
    row = iota((LANES, tok_count), 0)
    row_tile = row[:, :TILE]
    causal = iota((TILE, TILE), 0) <= iota((TILE, TILE), 1)
    queries_t = q_ref[...].astype(F32).T
    values_t = v_ref[...].astype(F32).T
    keys = k_ref[...].astype(F32)
    heads = []
    for head in range(2):
        spare = HD * (1 - head)
        bias = jnp.where((lane == spare) & hidden_key, NEG, 0.0)
        one = jnp.where(row == spare, 1.0, 0.0)
        own = row // HD == head
        heads.append(
            (
                jnp.where(lane // HD == head, keys, bias).astype(BF),
                jnp.where(own, queries_t, one).astype(BF),
                jnp.where(own, values_t, one).astype(BF),
            )
        )
    units = [(start, head) for start in range(0, tok_count, TILE) for head in range(2)]

    def score(unit):
        start, head = unit
        keys, queries, _ = heads[head]
        part = queries[:, start : start + TILE]
        near = mm(keys[start : start + TILE], part)
        return near, mm(keys[:start], part) if start else None

    outs = {}
    waiting = [score(unit) for unit in units[:3]]
    for index, (start, head) in enumerate(units):
        near, far = waiting.pop(0)
        if index + 3 < len(units):
            waiting.append(score(units[index + 3]))
        spare = HD * (1 - head)
        _, queries, values = heads[head]
        near = jnp.where(causal, near, NEG)
        top = jnp.max(near, axis=0, keepdims=True)
        if start:
            top = jnp.maximum(top, jnp.max(far, axis=0, keepdims=True))
        mixed = mm(values[:, start : start + TILE], jnp.exp(near - top).astype(BF))
        if start:
            mixed = mixed + mm(values[:, :start], jnp.exp(far - top).astype(BF))
        total = mixed[spare : spare + 1]
        outs[head] = mixed * (1.0 / total)
        kept = queries[:, start : start + TILE]
        logs = jnp.zeros((LANES, TILE), F32)
        for offset, piece in enumerate(split3(top + jnp.log(total))):
            logs = jnp.where(row_tile == spare + 1 + offset, piece.astype(F32), logs)
        q2_ref[head * LANES : head * LANES + LANES, start : start + TILE] = kept + logs.astype(BF)
        if head == 1:
            mixed = jnp.where(row_tile < HD, outs[0], outs[1])
            mixed_ref[start : start + TILE] = mixed.T.astype(BF)


def pre_attend_body(steps, len_ref, *refs):
    pre_ins, pre_outs = refs[:12], refs[12:19]
    key_ref, value_ref, mixed_ref, q2_ref, q_all, k_all, v_all, square_ref = refs[19:]
    step = pl.program_id(0)

    @pl.when(step < steps)
    def _():
        pre_body(*pre_ins, *pre_outs, q_all, k_all, v_all, square_ref)

    @pl.when(step >= steps)
    def _():
        pair = step - steps
        key_ref[...] = k_all[pair]
        value_ref[...] = v_all[pair]
        attend_body(len_ref, q_all.at[pair], k_all.at[pair], v_all.at[pair], mixed_ref, q2_ref)


def pre_attend_call(
    length, ids, tokens, gains, weights, down, upper, coarse, fine, router, constant_mix, vectors,
    residual_mix,
):
    tok_count, width = tokens.shape
    steps = tok_count // STEP

    def rows_of(columns):
        return pl.BlockSpec((STEP, columns), lambda i: (jnp.minimum(i, steps - 1), 0))

    column = pl.BlockSpec((tok_count, LANES), lambda i: (0, jnp.maximum(i - steps, 0)))
    return pl.pallas_call(
        functools.partial(pre_attend_body, steps),
        grid=(steps + PAIRS,),
        in_specs=[
            smem(), smem(), rows_of(width), whole(gains.shape), whole(weights.shape), whole(down.shape),
            whole(upper.shape), whole(coarse.shape), whole(fine.shape), whole(router.shape),
            whole(constant_mix.shape), whole(vectors.shape), whole(residual_mix.shape),
        ],
        out_specs=[
            rows_of(width), rows_of(LANES), whole((width, LANES)), whole(upper.shape),
            whole((LANES, width)), whole((16, LANES)), whole((READ_ROWS, width)), column, column,
            column, pl.BlockSpec((2 * LANES, tok_count), lambda i: (jnp.maximum(i - steps, 0), 0)),
        ],
        out_shape=[
            shape_of(tok_count, width), shape_of(tok_count, LANES), shape_of(width, LANES),
            shape_of(*upper.shape), shape_of(LANES, width, dtype=F32), shape_of(16, LANES, dtype=F32),
            shape_of(READ_ROWS, width, dtype=F32), shape_of(tok_count, width),
            shape_of(tok_count, width), shape_of(tok_count, width), shape_of(2 * width, tok_count),
        ],
        scratch_shapes=[pltpu.VMEM((PAIRS, tok_count, LANES), BF)] * 3
        + [pltpu.VMEM((LANES, LANES), F32)],
        compiler_params=PARAMS,
        cost_estimate=cost(25),
        name="attention_forward",
    )(
        length, ids, tokens, gains, weights, down, upper, coarse, fine, router, constant_mix, vectors,
        residual_mix,
    )


def attend_back_body(
    len_ref, q2_ref, k_ref, v_ref, mixed_ref, back_ref, coarse_ref, fine_ref,
    dq_ref, dk_ref, dv_ref, acc_ref, turn_ref,
):
    tok_count = k_ref.shape[0]

    @pl.when(pl.program_id(0) == 0)
    def _():
        turn_ref[0], turn_ref[1] = turn_rows(coarse_ref, fine_ref, 0, tok_count)

    lane = iota((tok_count, LANES), 1)
    position = iota((tok_count, LANES), 0)
    bias = jnp.where(position < len_ref[0], 0.0, NEG)
    causal = iota((TILE, TILE), 0) <= iota((TILE, TILE), 1)
    row = iota((LANES, tok_count), 0)
    back = back_ref[...].astype(F32)
    product_t = (back * mixed_ref[...].astype(F32)).T
    back_t = back.T
    keys, values = k_ref[...].astype(F32), v_ref[...].astype(F32)
    heads = []
    for head in range(2):
        own = lane // HD == head
        spare = HD * (1 - head)
        minus = jnp.where((lane > spare) & (lane < spare + 4), -1.0, 0.0)
        q2 = q2_ref[head * LANES : head * LANES + LANES, :]
        k2f = jnp.where(own, keys, jnp.where(lane == spare, bias, minus))
        k2 = k2f.astype(BF)
        k2t = k2f.T.astype(BF)
        v2 = jnp.where(own, values, minus).astype(BF)
        own_row = row // HD == head
        delta = jnp.sum(jnp.where(own_row, product_t, 0.0), axis=0, keepdims=True)
        back2 = jnp.where(own_row, back_t, 0.0)
        for offset, piece in enumerate(split3(delta)):
            back2 = jnp.where(row == spare + 1 + offset, piece.astype(F32), back2)
        back2 = back2.astype(BF)
        heads.append((k2, k2t, v2, q2, back2))
    units = [(start, head) for start in range(0, tok_count, TILE) for head in range(2)]

    def score(unit):
        start, head = unit
        k2, _, v2, q2, back2 = heads[head]
        stop = start + TILE
        return mm(k2[start:stop], q2[:, start:]), mm(v2[start:stop], back2[:, start:])

    grads = [([], []), ([], [])]
    waiting = [score(unit) for unit in units[:AHEAD]]
    for index, (start, head) in enumerate(units):
        scores, slopes = waiting.pop(0)
        if index + AHEAD < len(units):
            waiting.append(score(units[index + AHEAD]))
        _, k2t, _, q2, back2 = heads[head]
        stop = start + TILE
        diagonal = jnp.where(causal, scores[:, :TILE], NEG)
        if stop < tok_count:
            diagonal = jnp.concatenate([diagonal, scores[:, TILE:]], axis=1)
        weights = jnp.exp(diagonal)
        turned = (weights * slopes).astype(BF)
        grads[head][1].append(mm_nt(weights.astype(BF), back2[:, start:]))
        grads[head][0].append(mm_nt(turned, q2[:, start:]))
        update = mm(k2t[:, start:stop], turned)
        if start == 0:
            acc_ref[head] = update
        else:
            acc_ref[head, :, start:] += update
    grads = [
        (jnp.concatenate(keys, axis=0), jnp.concatenate(values, axis=0)) for keys, values in grads
    ]
    low_lane = lane < HD
    cosine, sine = turn_ref[0], -turn_ref[1]
    dq = jnp.where(row < HD, acc_ref[0], acc_ref[1]).T * HD**-0.5
    dq_ref[...] = rope(dq, cosine, sine).astype(BF)
    dk = jnp.where(low_lane, grads[0][0], grads[1][0])
    dk_ref[...] = rope(dk, cosine, sine).astype(BF)
    dv_ref[...] = jnp.where(low_lane, grads[0][1], grads[1][1]).astype(BF)


def pack_grads(packed, id_ref, acc_ref, grad_ref):
    count, width = acc_ref.shape[0], acc_ref.shape[1] // 2
    if not packed:
        grad_ref[...] = acc_ref[...].astype(BF)
        return
    half = width // 2
    shape = (16 * RANK, count)
    place, row = iota(shape, 0), iota(shape, 1)
    total = None
    for index in range(4):
        kind, part = index // 2, index % 2
        here = (place % 4 == row % 4) & (place // 16 == row // 4)
        here = here & (place // 8 % 2 == part) & (place // 4 % 2 == kind)
        start = kind * width + part * half
        piece = mm(hot(here), acc_ref[:, start : start + half].astype(BF))
        total = piece if total is None else total + piece
    grad_ref[:, 0:half] = total.astype(BF)
    grad_ref[:, half:] = jnp.full((16 * RANK, LANES), id_ref[0].astype(F32), F32).astype(BF)


def attend_back_all_body(packed, len_ref, id_ref, *refs):
    ins, refs = refs[:7], refs[7:]
    bcat_ref, inner_ref, inner_o_ref, din_ref, ba_ref, normed_hbm, mixed_hbm = refs[:7]
    dq_ref, dk_ref, dv_ref, back_ref, grad_ref = refs[7:12]
    scratch, (inner_all, back_all, acc_ref, normed_all, mixed_all, sems) = refs[12:14], refs[14:]
    step = pl.program_id(0)
    count = inner_all.shape[1]
    width = normed_all.shape[1]
    copies = [
        pltpu.make_async_copy(normed_hbm, normed_all, sems.at[0]),
        pltpu.make_async_copy(mixed_hbm, mixed_all, sems.at[1]),
    ]

    @pl.when(step == 0)
    def _():
        for copy in copies:
            copy.start()
        inner_all[0] = inner_ref[...].astype(F32).T[0:count].astype(BF)
        inner_all[1] = inner_o_ref[...].astype(F32).T[0:count].astype(BF)
        back_all[...] = jnp.zeros_like(back_all)

    @pl.when(step < PAIRS)
    def _():
        attend_back_body(len_ref, *ins, dq_ref, dk_ref, dv_ref, *scratch)
        number = iota((count, LANES), 0) % 4
        upper = mm(inner_all[1], ba_ref[...])
        total = back_all[...]
        for index, ref in enumerate((dq_ref, dk_ref, dv_ref)):
            value = ref[...]
            upper = jnp.where(number == index, mm(inner_all[0], value), upper)
            total = total + mm_nt(value, bcat_ref[index])
        back_all[...] = total
        at = width + step * LANES
        acc_ref[:, pl.ds(pl.multiple_of(at, LANES), LANES)] = upper

    @pl.when(step == PAIRS)
    def _():
        back = back_all[...].astype(BF)
        back_ref[...] = back
        back_t = (back.astype(F32) + din_ref[...].astype(F32)).T[0:count].astype(BF)
        for copy in copies:
            copy.wait()
        number = iota((count, width), 0) % 4
        half = back_t.shape[1] // 2

        def down(rows_ref):
            return mm(back_t[:, :half], rows_ref[:half]) + mm(back_t[:, half:], rows_ref[half:])

        acc_ref[:, 0:width] = jnp.where(number < 3, down(normed_all), down(mixed_all))
        pack_grads(packed, id_ref, acc_ref, grad_ref)


def attend_back_call(
    packed, length, ids, q2, keys, values, mixed, back, coarse, fine, bcat, inner, inner_o, din, ba,
    normed,
):
    tok_count, width = keys.shape
    column = pl.BlockSpec((tok_count, LANES), lambda i: (0, jnp.minimum(i, PAIRS - 1)))
    grad_shape = (16 * RANK, width // 2 + LANES) if packed else (4 * RANK, 2 * width)
    return pl.pallas_call(
        functools.partial(attend_back_all_body, packed),
        grid=(PAIRS + 1,),
        in_specs=[
            smem(), smem(),
            pl.BlockSpec((2 * LANES, tok_count), lambda i: (jnp.minimum(i, PAIRS - 1), 0)), column,
            column, column, column, whole(coarse.shape), whole(fine.shape),
            pl.BlockSpec((4, LANES, LANES), lambda i: (0, 0, jnp.minimum(i, PAIRS - 1))),
            whole(inner.shape), whole(inner_o.shape), whole(din.shape), column,
            pl.BlockSpec(memory_space=pl.ANY), pl.BlockSpec(memory_space=pl.ANY),
        ],
        out_specs=[column] * 3 + [whole((tok_count, LANES)), whole(grad_shape)],
        out_shape=[shape_of(tok_count, width)] * 3
        + [shape_of(tok_count, LANES), shape_of(*grad_shape)],
        scratch_shapes=[
            pltpu.VMEM((2, LANES, tok_count), F32), pltpu.VMEM((2, tok_count, LANES), F32),
            pltpu.VMEM((2, 4 * RANK, tok_count), BF), pltpu.VMEM((tok_count, LANES), F32),
            pltpu.VMEM((4 * RANK, 2 * width), F32), pltpu.VMEM((tok_count, width), BF),
            pltpu.VMEM((tok_count, width), BF), pltpu.SemaphoreType.DMA((2,)),
        ],
        compiler_params=PARAMS,
        cost_estimate=cost(12),
        name="attention_backward",
    )(
        length, ids, q2, keys, values, mixed, back, coarse, fine, bcat, inner, inner_o, din, ba,
        normed, mixed,
    )


def post_body(
    local, group, me_ref, mixed_ref, x_ref, wo_ref, acat_ref, bcat_ref, gain_ref, read_ref, mix_ref,
    prev_ref, routes_ref, slot_ref, hidden_ref, ei_ref, inner_ref, data_ref, cols_ref,
):
    reader = read_ref[0:READ_VECTOR].astype(BF)

    def stages(at):
        mixed = mixed_ref[at]
        inner = mm(mixed, acat_ref[...]).astype(BF)
        inner_ref[at] = inner
        yield
        hidden = x_ref[at].astype(F32) + (mm(mixed, wo_ref[...]) + mm(inner, bcat_ref[0]))
        hidden_ref[at] = hidden
        yield
        scale = lax.rsqrt(jnp.mean(hidden * hidden, axis=-1, keepdims=True) + EPSILON)
        ei = (hidden * scale * gain_ref[1:2, :]).astype(BF)
        ei_ref[at] = ei
        yield
        read = mm_nt(reader, ei)
        yield
        logits = read[0:16]
        for index in range(EXPERTS + 4):
            logits = logits + mix_ref[:, index : index + 1] * prev_ref[index : index + 1, at]
        first, second = routes_ref[0:1, at].astype(F32), routes_ref[1:2, at].astype(F32)
        number = iota((16, TILE), 0).astype(F32)
        one = jnp.sum(jnp.where(number == first, logits, 0.0), axis=0, keepdims=True)
        two = jnp.sum(jnp.where(number == second, logits, 0.0), axis=0, keepdims=True)
        top = jnp.maximum(one, two)
        one, two = jnp.exp(one - top), jnp.exp(two - top)
        gate_a, gate_b = one / (one + two), two / (one + two)
        mixes = read[16:20] + read[24:28] + read[32:36]
        shares = []
        for index in range(2):
            left, right = mixes[2 * index : 2 * index + 1], mixes[2 * index + 1 : 2 * index + 2]
            top = jnp.maximum(left, right)
            left, right = jnp.exp(left - top), jnp.exp(right - top)
            shares += [left / (left + right), right / (left + right)]

        def both(value):
            return jnp.where(first == value, gate_a, 0.0) + jnp.where(second == value, gate_b, 0.0)

        gates = jnp.where(number == first, gate_a, 0.0) + jnp.where(number == second, gate_b, 0.0)
        beta_a, beta_b = both(EXPERTS + 2.0), both(EXPERTS + 3.0)
        keep = both(EXPERTS + 1.0) + beta_a * shares[0] + beta_b * shares[2]
        data_ref[0:8, at] = gates[0:8]
        tail = [gate_a, gate_b] + shares + [beta_a, beta_b]
        data_ref[8:16, at] = jnp.concatenate(tail, axis=0)
        yield
        slots = slot_ref[:, at].astype(F32)
        expert = iota((EXPERTS, TILE), 0)
        partner = jnp.bitwise_xor(expert // local, me_ref[0])
        base = ((expert % local) * (group * CAP) + partner * CAP).astype(F32)
        place = jnp.where(slots >= 0, slots + base + 1.0, 0.0)
        expert = expert.astype(F32)
        target_a = jnp.sum(jnp.where(expert == first, place, 0.0), axis=0, keepdims=True) - 1.0
        target_b = jnp.sum(jnp.where(expert == second, place, 0.0), axis=0, keepdims=True) - 1.0
        stack = jnp.concatenate(
            [jnp.zeros((VECTOR_ROW, TILE), F32), beta_a * shares[1], beta_b * shares[3]]
            + [jnp.zeros((2, TILE), F32), target_a, target_b, keep]
            + [jnp.zeros((LANES - KEEP_LANE - 1, TILE), F32)],
            axis=0,
        )
        cols_ref[at] = stack.T

    side_by_side(stages)


def post_send_body(local, group, steps, me_ref, id_ref, slot_all_ref, *refs):
    post_refs, out_refs, (ei_all, data_all) = refs[:16], refs[16:-2], refs[-2:]
    step = pl.program_id(0)

    @pl.when(step < steps)
    def _():
        post_body(local, group, me_ref, *post_refs)
        span = pl.ds(pl.multiple_of(step * STEP, STEP), STEP)
        ei_all[span] = post_refs[12][...]
        data_all[:, span] = post_refs[14][...]

    @pl.when(step >= steps)
    def _():
        send_rows(local, group, step - steps, me_ref, id_ref, slot_all_ref, data_all, ei_all, out_refs)


def post_call(
    local, group, me, ids, mixed, tokens, weight, acat, bcat, gains, reader, mixer, prev, routes, slots
):
    tok_count, width = tokens.shape
    steps = tok_count // STEP
    heights = [local * PIECE] * (group // 2) + [PIECE] * ((group - group // 2) * local)

    def rows_of(columns):
        return pl.BlockSpec((STEP, columns), lambda i: (jnp.minimum(i, steps - 1), 0))

    def lanes_of(height):
        return pl.BlockSpec((height, STEP), lambda i: (0, jnp.minimum(i, steps - 1)))

    return pl.pallas_call(
        functools.partial(post_send_body, local, group, steps),
        grid=(steps + group,),
        in_specs=[
            smem(), smem(), whole(slots.shape), rows_of(width), rows_of(width), whole(weight.shape),
            whole(acat.shape), pl.BlockSpec((1, LANES, width), lambda i: (3, 0, 0)), whole(gains.shape),
            whole(reader.shape), whole(mixer.shape), lanes_of(EXPERTS + 4), lanes_of(2),
            lanes_of(EXPERTS),
        ],
        out_specs=[
            rows_of(width), rows_of(width), rows_of(LANES), lanes_of(16), rows_of(LANES)
        ] + [whole((height, width)) for height in heights],
        out_shape=[
            shape_of(tok_count, width, dtype=F32), shape_of(tok_count, width),
            shape_of(tok_count, LANES), shape_of(16, tok_count, dtype=F32),
            shape_of(tok_count, LANES, dtype=F32),
        ] + [shape_of(height, width) for height in heights],
        scratch_shapes=[pltpu.VMEM((tok_count, width), BF), pltpu.VMEM((16, tok_count), F32)],
        compiler_params=PARAMS,
        cost_estimate=cost(14),
        name="after_attention",
    )(
        me, ids, slots, mixed, tokens, weight, acat, bcat, gains, reader, mixer, prev, routes, slots
    )


def expert_body(
    local_index, pair, per_owner, group, steps, has_grad, kept, *refs
):
    count = len(pair)
    piece_refs, refs = refs[:count], refs[count:]
    cot_refs, refs = refs[:count], refs[count:]
    dn_ref, ou_ref, wg_hbm, wu_hbm, wd_hbm, up_hbm, od_hbm = refs[:7]
    refs = refs[7:]
    if has_grad:
        before_hbm, refs = refs[0], refs[1:]
    refs = refs[kept:]
    back_refs, refs = refs[:count], refs[count:]
    out_refs, refs = refs[:count], refs[count:]
    (
        grad_ref, x_ref, g_ref, gate_ref, pick_ref, dr_ref, zg_ref, zu_ref, dzd_ref, zgt_ref, zut_ref,
        dzdt_ref, racc_ref, xacc_ref, zd_acc, dzg_acc, dzu_acc, h_ref, dg_ref, du_ref, wg_all, wu_all,
        wd_all, up_all, od_all, sems, *rest
    ) = refs
    rows, width = x_ref.shape
    compact = group * RANK
    tile = h_ref.shape[1]

    def copies(step):
        span = pl.ds(pl.multiple_of(step * tile, tile), tile)
        pairs = (
            (wg_hbm.at[local_index, :, span], wg_all),
            (wu_hbm.at[local_index, :, span], wu_all),
            (wd_hbm.at[local_index, span, :], wd_all),
            (up_hbm.at[local_index, :, :, span], up_all),
            (od_hbm.at[local_index, span, :], od_all),
        )
        return [
            pltpu.make_async_copy(source, target.at[step], sems.at[step, place])
            for place, (source, target) in enumerate(pairs)
        ]

    def begin(step):
        for copy in copies(step):
            copy.start()

    begin(0)

    def fold(value):
        place = iota((compact, LANES), 0)
        block = per_owner * group
        inner = place // block * per_owner + place % per_owner
        folded = mm_nt(hot(iota((compact, LANES), 1) % RANK == inner), value)
        place = iota((compact, rows), 0)
        owner = place % block // per_owner
        mine = iota((compact, rows), 1) // CAP + pair[0]
        return jnp.where(mine == owner, folded, 0.0).astype(BF)

    def put(start, value):
        grad_ref[:, pl.ds(start, value.shape[1])] = value.astype(BF)

    for index in range(count):
        span = slice(index * CAP, index * CAP + CAP)
        x_ref[span] = piece_refs[index][0:CAP]
        g_ref[span] = cot_refs[index][...]
        meta = piece_refs[index][CAP:PIECE].astype(F32)
        gate = (meta[0:1] + meta[1:2] + meta[2:3])[:, 0 : 2 * LANES]
        gate_ref[span] = jnp.broadcast_to(gate, (LANES, 2 * LANES)).T[0:CAP]
        lane = (iota((CAP, LANES), 1) // RANK).astype(F32)
        pick_ref[span] = jnp.where(lane == meta[3:4, 0:LANES], 1.0, 0.0)
    chosen = pick_ref[...] > 0.0
    dr = (gate_ref[:, 0:1] * g_ref[...].astype(F32)).astype(BF)
    dr_ref[...] = dr
    zg = jnp.where(chosen, mm(x_ref[...], dn_ref[0]), 0.0).astype(BF)
    zu = jnp.where(chosen, mm(x_ref[...], dn_ref[1]), 0.0).astype(BF)
    dzd = jnp.where(chosen, mm_nt(dr, ou_ref[...]), 0.0).astype(BF)
    zg_ref[...] = zg
    zu_ref[...] = zu
    dzd_ref[...] = dzd
    zgt_ref[...] = fold(zg)
    zut_ref[...] = fold(zu)
    dzdt_ref[...] = fold(dzd)
    for ref in (racc_ref, xacc_ref, zd_acc, dzg_acc, dzu_acc):
        ref[...] = jnp.zeros_like(ref)

    total = steps * tile
    begin(1)
    if has_grad:
        before = pltpu.make_async_copy(before_hbm, rest[0], rest[1])
        before.start()

    def run(step, carry):
        for copy in copies(step):
            copy.wait()

        @pl.when(step + 2 < steps)
        def _():
            begin(step + 2)

        wg_ref, wu_ref, wd_ref = wg_all.at[step], wu_all.at[step], wd_all.at[step]
        up_ref, od_ref = up_all.at[step], od_all.at[step]
        gate = mm(x_ref[...], wg_ref[...]) + mm(zg_ref[...], up_ref[0])
        upper = mm(x_ref[...], wu_ref[...]) + mm(zu_ref[...], up_ref[1])
        share = 0.5 * jnp.tanh(0.5 * gate) + 0.5
        silu = gate * share
        active = (silu * upper).astype(BF)
        h_ref[...] = active
        back = mm_nt(dr_ref[...], wd_ref[...]) + mm_nt(dzd_ref[...], od_ref[...])
        du = (back * silu).astype(BF)
        dg = (back * upper * (share + silu * (1.0 - share))).astype(BF)
        du_ref[...] = du
        dg_ref[...] = dg
        racc_ref[...] += mm(active, wd_ref[...])
        zd_acc[...] += mm(active, od_ref[...])
        xacc_ref[...] += mm_nt(dg, wg_ref[...]) + mm_nt(du, wu_ref[...])
        dzg_acc[...] += mm_nt(dg, up_ref[0])
        dzu_acc[...] += mm_nt(du, up_ref[1])
        at = pl.multiple_of(step * tile, tile)
        put(at, mm(zgt_ref[...], dg_ref[...]))
        put(total + at, mm(zut_ref[...], du_ref[...]))
        put(2 * total + at, mm(dzdt_ref[...], h_ref[...]))
        return carry

    lax.fori_loop(0, steps, run, 0)
    chosen = pick_ref[...] > 0.0
    zd = jnp.where(chosen, zd_acc[...], 0.0).astype(BF)
    dzg = jnp.where(chosen, dzg_acc[...], 0.0).astype(BF)
    dzu = jnp.where(chosen, dzu_acc[...], 0.0).astype(BF)
    result = racc_ref[...] + mm(zd, ou_ref[...])
    gated = (gate_ref[:, 0:1] * result).astype(BF)
    product = g_ref[...].astype(F32) * result.astype(BF).astype(F32)
    dots = jnp.broadcast_to(jnp.sum(product, axis=-1, keepdims=True), (rows, LANES))
    back_rows = (xacc_ref[...] + mm_nt(dzg, dn_ref[0]) + mm_nt(dzu, dn_ref[1])).astype(BF)
    for index in range(count):
        span = slice(index * CAP, index * CAP + CAP)
        out_refs[index][...] = gated[span]
        back_refs[index][0:CAP, :] = back_rows[span]
        column = jnp.concatenate(
            [dots[span], jnp.zeros((2 * LANES - CAP, LANES), F32)], axis=0
        ).T[0:1]
        meta = jnp.concatenate(
            [piece.astype(F32) for piece in split3(column)]
            + [jnp.zeros((META - 3, 2 * LANES), F32)],
            axis=0,
        )
        meta = jnp.concatenate([meta, jnp.zeros((META, width - 2 * LANES), F32)], axis=1)
        back_refs[index][CAP:PIECE, :] = meta.astype(BF)
    base = 3 * total
    place = iota((compact, LANES), 0)
    owner = place % (per_owner * group) // per_owner
    ids = jnp.zeros((compact, LANES), F32)
    for index in range(count):
        meta = piece_refs[index][CAP:PIECE, 0:LANES].astype(F32)
        ids = jnp.where(owner == pair[index], meta[3:4], ids)
    put(base + 3 * width, ids)
    put(base, mm(fold(zd), dr_ref[...]))
    put(base + width, mm(fold(dzg), x_ref[...]))
    put(base + 2 * width, mm(fold(dzu), x_ref[...]))
    if has_grad:
        before.wait()
        grad_ref[...] = grad_ref[...] + rest[0][...]


def expert_call(index, pair, group, per_owner, pieces, cots, before, results, weights):
    gate_w, up_w, down_w, in_down, in_up, out_down, out_up = weights
    width, hidden = gate_w.shape[1:]
    rows = len(pair) * CAP
    steps = hidden // FTILE
    columns = 3 * hidden + 3 * width + LANES
    compact = group * RANK
    has_grad = before is not None
    return pl.pallas_call(
        functools.partial(
            expert_body, index, pair, per_owner, group, steps, has_grad, len(results)
        ),
        grid=(1,),
        in_specs=[
            pl.BlockSpec((PIECE, width), lambda f, row=piece.shape[0] // PIECE > 1: (index * row, 0))
            for piece in pieces
        ]
        + [pl.BlockSpec((CAP, width), lambda f: (index, 0))] * len(pair)
        + [
            pl.BlockSpec((None, 2, width, LANES), lambda f: (index, 0, 0, 0)),
            pl.BlockSpec((None, LANES, width), lambda f: (index, 0, 0)),
        ]
        + [pl.BlockSpec(memory_space=pl.ANY)] * 5
        + [pl.BlockSpec(memory_space=pl.ANY)] * (has_grad + len(results)),
        out_specs=[whole((PIECE, width))] * len(pair)
        + [pl.BlockSpec((CAP, width), lambda f: (index, 0))] * len(pair)
        + [whole((compact, columns))],
        out_shape=[shape_of(PIECE, width)] * len(pair)
        + [shape_of(gate_w.shape[0] * CAP, width)] * len(pair)
        + [shape_of(compact, columns)],
        input_output_aliases={
            2 * len(pair) + 7 + has_grad + place: len(pair) + place for place in range(len(results))
        },
        scratch_shapes=[pltpu.VMEM((rows, width), BF)] * 2
        + [pltpu.VMEM((rows, LANES), F32)] * 2
        + [pltpu.VMEM((rows, width), BF)]
        + [pltpu.VMEM((rows, LANES), BF)] * 3
        + [pltpu.VMEM((compact, rows), BF)] * 3
        + [pltpu.VMEM((rows, width), F32)] * 2
        + [pltpu.VMEM((rows, LANES), F32)] * 3
        + [pltpu.VMEM((rows, FTILE), BF)] * 3
        + [pltpu.VMEM((steps, width, FTILE), BF)] * 2
        + [
            pltpu.VMEM((steps, FTILE, width), BF), pltpu.VMEM((steps, 2, LANES, FTILE), BF),
            pltpu.VMEM((steps, FTILE, LANES), BF), pltpu.SemaphoreType.DMA((steps, 5)),
        ]
        + [pltpu.VMEM((compact, columns), BF), pltpu.SemaphoreType.DMA] * has_grad,
        compiler_params=PARAMS,
        cost_estimate=cost(rows / 21),
        name="expert_layer",
    )(
        *pieces, *cots, in_down, out_up, gate_w, up_w, down_w, in_up, out_down,
        *([before] if has_grad else []), *results,
    )


def spread(cols, index, count):
    return iota((TILE, count), 1).astype(F32) == cols[:, index : index + 1]


def combine_body(
    pieces, len_ref, *refs
):
    back_refs = refs[:pieces]
    (
        routes_ref, data_ref, cols_ref, cot_ref, ei_ref, hidden_ref, gain_ref, wo_ref, acat_ref, bcat_ref,
        table_ref, read_ref, bh_ref, ba_ref, din_ref, bm_ref, back_all, dots_ref,
    ) = refs[pieces:]
    count = pieces * CAP

    @pl.when(pl.program_id(0) == 0)
    def _():
        for index, back_ref in enumerate(back_refs):
            back_all[index * CAP : index * CAP + CAP, :] = back_ref[0:CAP, :]
        dots = [back_ref[CAP:PIECE, 0:CAP].astype(F32) for back_ref in back_refs]
        dots = jnp.concatenate(dots, axis=1)
        dots_ref[...] = jnp.concatenate([dots, jnp.zeros_like(dots)], axis=0).astype(BF)

    table_high, table_low = split2(table_ref[...])
    stack = dots_ref[...]
    vectors = read_ref[READ_VECTOR:READ_ROWS].astype(BF)

    def stages(at):
        start = pl.program_id(0) * STEP + at.start
        cols = cols_ref[at]
        chosen_a = hot(spread(cols, TARGET_LANE, count))
        chosen_b = hot(spread(cols, TARGET_LANE + 1, count))
        yield
        routed_a = jnp.sum(mm_nt(stack, chosen_a)[0:8], axis=0, keepdims=True)
        routed_b = jnp.sum(mm_nt(stack, chosen_b)[0:8], axis=0, keepdims=True)
        cot = cot_ref[at]
        cot_f = cot.astype(F32)
        yield
        along_x = jnp.sum(cot_f * ei_ref[at].astype(F32), axis=-1, keepdims=True)
        along_x = jnp.broadcast_to(along_x, (TILE, LANES)).T[0:1]
        yield
        along_c = mm_nt(vectors, cot)
        along_a = along_c[0:1] + along_c[2:3] + along_c[4:5]
        along_b = along_c[1:2] + along_c[3:4] + along_c[5:6]
        yield
        both = chosen_a + chosen_b
        half = count // 2
        back = mm(both[:, :half], back_all[:half]) + mm(both[:, half:], back_all[half:])
        yield
        first, second = routes_ref[0:1, at].astype(F32), routes_ref[1:2, at].astype(F32)
        token = iota((1, TILE), 1) + start
        valid = jnp.where(token < len_ref[0], 1.0, 0.0)
        gate_a, gate_b = data_ref[8:9, at], data_ref[9:10, at]
        share = [data_ref[index : index + 1, at] for index in range(10, 14)]
        beta_a, beta_b = data_ref[14:15, at], data_ref[15:16, at]
        const_a = share[0] * along_x + share[1] * along_a
        const_b = share[2] * along_x + share[3] * along_b

        def here(route):
            return (
                jnp.where(route == EXPERTS + 1.0, along_x, 0.0)
                + jnp.where(route == EXPERTS + 2.0, const_a, 0.0)
                + jnp.where(route == EXPERTS + 3.0, const_b, 0.0)
            )

        dot_a, dot_b = routed_a + here(first), routed_b + here(second)
        mean = gate_a * dot_a + gate_b * dot_b
        chosen_grad_a = valid * gate_a * (dot_a - mean)
        chosen_grad_b = valid * gate_b * (dot_b - mean)
        number = iota((16, TILE), 0).astype(F32)
        logit_grads = jnp.where(number == first, chosen_grad_a, 0.0) + jnp.where(
            number == second, chosen_grad_b, 0.0
        )
        mixes = []
        for index, (beta, along) in enumerate(((beta_a, along_a), (beta_b, along_b))):
            left, right = share[2 * index], share[2 * index + 1]
            weighted = left * along_x + right * along
            mixes += [
                valid * beta * left * (along_x - weighted),
                valid * beta * right * (along - weighted),
            ]
        small = jnp.concatenate(
            [logit_grads] + mixes + [jnp.zeros((LANES - 20, TILE), F32)], axis=0
        ).T
        high, low = split2(small)
        yield
        inside = iota((TILE, 1), 0) + start < len_ref[0]
        grad = jnp.where(inside, cot_f, 0.0)
        back = back + mm(high, table_high) + mm(low, table_high) + mm(high, table_low)
        back = back + cols[:, KEEP_LANE : KEEP_LANE + 1] * grad
        yield
        hidden = hidden_ref[at]
        scale = lax.rsqrt(jnp.mean(hidden * hidden, axis=-1, keepdims=True) + EPSILON)
        normed = hidden * scale
        back = back * gain_ref[1:2, :]
        back = grad + scale * (back - normed * jnp.mean(back * normed, axis=-1, keepdims=True))
        bh_ref[at] = back
        rounded = back.astype(BF)
        ba_ref[at] = rounded
        yield
        inner = mm_nt(rounded, bcat_ref[0]).astype(BF)
        din_ref[at] = inner
        yield
        bm_ref[at] = (mm_nt(rounded, wo_ref[...]) + mm_nt(inner, acat_ref[...])).astype(BF)

    side_by_side(stages)


def combine_call(
    length, backs, routes, data, cols, cotangent, ei, hidden, gains, weight, acat, bcat, table,
    reader,
):
    tok_count, width = cotangent.shape
    pieces = len(backs)
    return pl.pallas_call(
        functools.partial(combine_body, pieces),
        grid=(tok_count // STEP,),
        in_specs=[smem()] + [whole(back.shape) for back in backs] + [
            wide(2), wide(16), tall(LANES), tall(width), tall(width), tall(width),
            whole(gains.shape), whole(weight.shape), whole(acat.shape),
            pl.BlockSpec((1, LANES, width), lambda i: (3, 0, 0)), whole(table.shape),
            whole(reader.shape),
        ],
        out_specs=[tall(width), tall(width), tall(LANES), tall(width)],
        out_shape=[
            shape_of(tok_count, width, dtype=F32), shape_of(tok_count, width),
            shape_of(tok_count, LANES), shape_of(tok_count, width),
        ],
        scratch_shapes=[
            pltpu.VMEM((pieces * CAP, width), BF), pltpu.VMEM((2 * META, pieces * CAP), BF)
        ],
        compiler_params=PARAMS,
        cost_estimate=cost(17),
        name="combine_backward",
    )(
        length, *backs, routes, data, cols, cotangent, ei, hidden, gains, weight, acat, bcat, table,
        reader,
    )


def result_body(pieces, len_ref, *refs):
    result_refs = refs[:pieces]
    cols_ref, ei_ref, hidden_ref, table_ref, out_ref, result_all = refs[pieces:]
    count = result_all.shape[0]

    @pl.when(pl.program_id(0) == 0)
    def _():
        for index in range(count // CAP):
            start = index // pieces * CAP
            result_all[index * CAP : index * CAP + CAP] = result_refs[index % pieces][start : start + CAP]

    table_high, table_low = split2(table_ref[...])

    def stages(at):
        cols = cols_ref[at]
        both = hot(spread(cols, TARGET_LANE, count) | spread(cols, TARGET_LANE + 1, count))
        yield
        half = count // 2
        mixture = mm(both[:, :half], result_all[:half]) + mm(both[:, half:], result_all[half:])
        yield
        high, low = split2(cols)
        mixture = mixture + mm(high, table_high) + mm(low, table_high) + mm(high, table_low)
        mixture = mixture + cols[:, KEEP_LANE : KEEP_LANE + 1] * ei_ref[at].astype(F32)
        yield
        inside = iota((TILE, 1), 0) + pl.program_id(0) * STEP + at.start < len_ref[0]
        out_ref[at] = (hidden_ref[at] + jnp.where(inside, mixture, 0.0)).astype(BF)

    side_by_side(stages)


def result_call(length, results, cols, ei, hidden, table):
    tok_count, width = ei.shape
    pieces = len(results)
    return pl.pallas_call(
        functools.partial(result_body, pieces),
        grid=(tok_count // STEP,),
        in_specs=[smem()] + [whole(result.shape) for result in results] + [
            tall(LANES), tall(width), tall(width), whole(table.shape),
        ],
        out_specs=tall(width),
        out_shape=shape_of(tok_count, width),
        scratch_shapes=[pltpu.VMEM((pieces * results[0].shape[0], width), BF)],
        compiler_params=PARAMS,
        cost_estimate=cost(8),
        name="layer_output",
    )(length, *results, cols, ei, hidden, table)


def last_body(
    dq_ref, dk_ref, dv_ref, w_ref, acat_ref, back_ref, x_ref, bh_ref, gain_ref, out_ref
):
    def stages(at):
        parts = [mm_nt(back_ref[at], acat_ref[...])]
        for index, ref in enumerate((dq_ref, dk_ref, dv_ref)):
            parts.append(mm_nt(ref[at], w_ref[index]))
            yield
        total = parts[0] + parts[1] + parts[2] + parts[3]
        x = x_ref[at].astype(F32)
        scale = lax.rsqrt(jnp.mean(x * x, axis=-1, keepdims=True) + EPSILON)
        normed = x * scale
        back = total * gain_ref[0:1, :]
        back = scale * (back - normed * jnp.mean(back * normed, axis=-1, keepdims=True))
        out_ref[at] = (bh_ref[at] + back).astype(BF)

    side_by_side(stages)


def last_call(dq, dk, dv, weights, acat, back, tokens, bh, gains):
    tok_count, width = tokens.shape
    return pl.pallas_call(
        last_body,
        grid=(tok_count // STEP,),
        in_specs=[
            tall(width), tall(width), tall(width), whole(weights.shape), whole(acat.shape),
            tall(LANES), tall(width), tall(width), whole(gains.shape),
        ],
        out_specs=tall(width),
        out_shape=shape_of(tok_count, width),
        compiler_params=PARAMS,
        cost_estimate=cost(9),
        name="after_attention_backward",
    )(dq, dk, dv, weights, acat, back, tokens, bh, gains)


def exchange(value, axes):
    return lax.all_to_all(value, axes, split_axis=0, concat_axis=0, tiled=True)


def gather_all(value, axes, count):
    return exchange(jnp.broadcast_to(value[None], (count,) + value.shape), axes)


def swap(value, partner, group):
    if partner == 0:
        return value
    return lax.ppermute(value, "expert", [(index, index ^ partner) for index in range(group)])


def find_adapters(id_rows):
    count = id_rows.shape[0]
    padded = id_rows.astype(F32)
    if count % LANES:
        padded = jnp.concatenate([padded, jnp.zeros((-count % LANES, LANES), F32)], axis=0)
    return padded.T[0:1, 0:count].astype(jnp.int32)


def sum_expert_body(each, adapters, in_ref, out_ref):
    count, columns = in_ref.shape[0], out_ref.shape[1]
    found = find_adapters(in_ref[:, columns:])
    place = iota((adapters * each, count), 0)
    column = iota((adapters * each, count), 1)
    pick = hot((place // each == found) & (place % each == column % each))
    out_ref[...] = mm(pick, in_ref[:, 0:columns]).astype(BF)


def exchange_expert_grads(grads, group, owners):
    split = min(RANK, owners)
    each, parts = RANK // split, owners // split
    columns = (grads.shape[1] - LANES) // parts
    pieces = grads.reshape(split, each * group, grads.shape[1])
    if parts > 1:
        ids = jnp.broadcast_to(pieces[:, None, :, parts * columns :], (split, parts, each * group, LANES))
        pieces = pieces[:, :, : parts * columns].reshape(split, each * group, parts, columns)
        pieces = jnp.concatenate([pieces.transpose(0, 2, 1, 3), ids], axis=-1)
        pieces = pieces.reshape(owners, each * group, columns + LANES)
    return exchange(pieces, "dp").reshape(owners * group * each, columns + LANES)


def sum_expert_grads(got, adapters, owners):
    columns = got.shape[1] - LANES
    each = RANK // min(RANK, owners)
    return pl.pallas_call(
        functools.partial(sum_expert_body, each, adapters),
        out_shape=shape_of(adapters * each, columns),
        compiler_params=PARAMS,
        cost_estimate=cost(2.2),
        name="expert_gradient_part",
    )(got)


def finish_expert_body(split, adapters, hidden, in_ref, *refs):
    down_ref, up_ref, out_down_ref, out_up_ref = refs[-4:]
    each = RANK // split
    rows = adapters * each
    count = split * rows
    width = out_up_ref.shape[1]

    def place(value):
        return value // each % adapters * RANK + value // (adapters * each) * each + value % each

    move = hot(iota((count, count), 0) == place(iota((count, count), 1)))
    back = hot(iota((count, count), 1) == place(iota((count, count), 0)))

    def part(start, size):
        span = slice(start, start + size)
        rows_of = [in_ref[owner, :, span] for owner in range(split)]
        return jnp.concatenate(rows_of, axis=0)

    for index in range(2):
        up_ref[index] = mm(move, part(index * hidden, hidden))
    out_down_ref[...] = mm_tn(part(2 * hidden, hidden), back)
    base = 3 * hidden
    out_up_ref[...] = mm(move, part(base, width))
    for index in range(2):
        base += width
        down_ref[index] = mm_tn(part(base, width), back)


def finish_expert_call(index, local, everything, outs, adapters, width, hidden):
    owners, rows, columns = everything.shape
    total = adapters * RANK
    shapes = [(local, 2, width, total), (local, 2, total, hidden), (local, hidden, total),
              (local, total, width)]
    specs = [
        pl.BlockSpec((None,) + shape[1:], lambda *_, rank=len(shape): (index,) + (0,) * (rank - 1))
        for shape in shapes
    ]
    return pl.pallas_call(
        functools.partial(finish_expert_body, owners, adapters, hidden),
        grid=(1,),
        in_specs=[whole(everything.shape)] + [pl.BlockSpec(memory_space=pl.ANY)] * len(outs),
        out_specs=specs,
        out_shape=[shape_of(*shape, dtype=F32) for shape in shapes],
        input_output_aliases={1 + place: place for place in range(len(outs))},
        compiler_params=PARAMS,
        cost_estimate=cost(4),
        name="expert_gradient_sums",
    )(everything, *outs)


def spread_expert_grads(own, adapters, owners):
    split = min(RANK, owners)
    each, parts = RANK // split, owners // split
    everything = gather_all(own, "dp", owners)
    everything = everything.reshape(split, parts, adapters, each, own.shape[1])
    everything = everything.transpose(2, 0, 3, 1, 4)
    return everything.reshape(adapters * RANK, parts * own.shape[1]).astype(F32)


def expert_sums(owned, adapters, owners, width, hidden):
    sums = [spread_expert_grads(value, adapters, owners) for value in owned]
    base = 3 * hidden
    up = [[value[:, 0:hidden], value[:, hidden : 2 * hidden]] for value in sums]
    down = [
        [value[:, base + width * part : base + width * (part + 1)].T for part in (1, 2)]
        for value in sums
    ]
    return (
        jnp.stack([jnp.stack(value) for value in down]),
        jnp.stack([jnp.stack(value) for value in up]),
        jnp.stack([value[:, 2 * hidden : base].T for value in sums]),
        jnp.stack([value[:, base : base + width] for value in sums]),
    )


def finish_adapter_body(adapters, me_ref, *refs):
    piece_refs, (down_ref, up_ref, in_ref) = refs[:-3], refs[-3:]
    half = in_ref.shape[3]
    owners, group = piece_refs[0].shape[0], len(piece_refs)
    for other in range(group):
        place = jnp.bitwise_xor(me_ref[0], other)
        for owner in range(owners):
            in_ref[owner * (group // 2) + place // 2, place % 2] = piece_refs[other][owner]
    count = RANK * adapters

    def place(value):
        return value % adapters * RANK + value // adapters

    move = hot(iota((count, count), 0) == place(iota((count, count), 1)))
    back = hot(iota((count, count), 1) == place(iota((count, count), 0)))
    for part in range(2):
        span = slice(part * half, part * half + half)
        for kind in range(2):
            for index in range(4):
                first = (kind * 4 + index) * adapters
                rows = in_ref[:, part, first : first + adapters, :].astype(F32)
                rows = rows.reshape(count, half).astype(BF)
                if kind == 0:
                    down_ref[index, span, :] = mm_tn(rows, back)
                else:
                    up_ref[index, :, span] = mm(move, rows)


def sum_adapter_body(kinds, adapters, in_ref, out_ref):
    count, columns = in_ref.shape[0], out_ref.shape[-1]
    found = find_adapters(in_ref[:, columns:])
    place = iota((adapters * kinds, count), 0)
    column = iota((adapters * kinds, count), 1)
    pick = hot((place % adapters == found) & (place // adapters == column % kinds))
    own = mm(pick, in_ref[:, 0:columns]).astype(BF)
    for index in range(out_ref.shape[0]):
        out_ref[index] = own


def adapter_sums(grads, meanwhile, later, finish, parts, ids, adapters, owners, group, width):
    axes, everyone = ("dp", "expert"), owners * group
    if everyone == 2 * RANK and group == 4:
        kinds = 8
        got = exchange(grads.reshape(everyone, kinds, grads.shape[1]), axes)
        got, meanwhile = lax.optimization_barrier((got, meanwhile))
        own = pl.pallas_call(
            functools.partial(sum_adapter_body, kinds, adapters),
            out_shape=shape_of(owners, kinds * adapters, width // 2),
            compiler_params=PARAMS,
            cost_estimate=cost(2.0),
            name="adapter_gradient_part",
        )(got.reshape(everyone * kinds, grads.shape[1]))
        mine = exchange(own, "dp")
        mine, later = lax.optimization_barrier((mine, later))
        across = swap(mine, 2, group)
        full = [mine, swap(mine, 1, group), across, swap(across, 1, group)]
        total = adapters * RANK
        down, upper = pl.pallas_call(
            functools.partial(finish_adapter_body, adapters),
            in_specs=[smem()] + [pl.BlockSpec(memory_space=pltpu.VMEM)] * group,
            out_shape=[shape_of(4, width, total, dtype=F32), shape_of(4, total, width, dtype=F32)],
            scratch_shapes=[pltpu.VMEM((RANK, 2, kinds * adapters, width // 2), BF)],
            compiler_params=PARAMS,
            cost_estimate=cost(3.6),
            name="adapter_gradient_sums",
        )(lax.axis_index("expert").reshape(1).astype(jnp.int32), *full)
        (down, upper), later, parts = lax.optimization_barrier(((down, upper), later, parts))
        return down, upper, meanwhile, finish(later, parts)
    later = finish(later, parts)
    all_ids = exchange(jnp.broadcast_to(ids, (everyone,)), axes)
    pieces = grads.reshape(everyone, RANK * 4 * 2 * width // everyone)
    got = exchange(pieces, axes)
    pick = (jnp.arange(adapters, dtype=jnp.int32)[:, None] == all_ids[None, :]).astype(BF)
    own = jnp.dot(pick, got, preferred_element_type=F32).astype(BF)
    full = gather_all(own, axes, everyone)
    full = full.reshape(RANK, everyone // RANK, adapters, -1).transpose(2, 0, 1, 3)
    full = full.reshape(adapters * RANK, 4, 2, width).astype(F32)
    return full[:, :, 0].transpose(1, 2, 0), full[:, :, 1].transpose(1, 0, 2), meanwhile, later


def body(
    tokens,
    cotangent,
    lengths,
    adapter_ids,
    routes,
    prev_logits,
    norm_gains,
    input_weights,
    output_weight,
    adapter_down,
    adapter_up,
    router,
    residual_mix,
    constant_mix,
    constant_vectors,
    expert_gate,
    expert_up,
    expert_down,
    expert_adapter_down,
    expert_adapter_up,
    output_adapter_down,
    output_adapter_up,
):
    tok_count, width = tokens.shape
    hidden_width = expert_gate.shape[2]
    group, owners = lax.axis_size("expert"), lax.axis_size("dp")
    local = expert_gate.shape[0]
    adapters = adapter_down.shape[-1] // RANK
    angles = [jnp.asarray(table) for table in turn_tables(tok_count)]
    weights = (
        expert_gate, expert_up, expert_down, expert_adapter_down, expert_adapter_up,
        output_adapter_down, output_adapter_up,
    )
    per_owner = RANK // min(RANK, owners)
    everyone = owners * group
    me = lax.axis_index("expert")

    me = me.reshape(1).astype(jnp.int32)

    routes, prev_logits = routes.T, prev_logits.T
    slots, *grad_sends = route_call(local, group, lengths, me, routes, cotangent)
    cots = [swap(value, partner, group) for partner, value in enumerate(grad_sends)]
    normed, inner, acat, bcat, table, mixer, reader, keys, values, mixed, q2 = pre_attend_call(
        lengths, adapter_ids, tokens, norm_gains, input_weights, adapter_down, adapter_up, *angles,
        router.T, constant_mix.T, constant_vectors, residual_mix,
    )
    hidden, ei, inner_o, data, cols, *sends = post_call(
        local, group, me, adapter_ids, mixed, tokens, output_weight, acat, bcat, norm_gains, reader, mixer, prev_logits,
        routes, slots,
    )
    sends, cots = lax.optimization_barrier((sends, cots))
    near, far = tuple(range(group // 2)), tuple(range(group // 2, group))
    sent_near = [swap(sends[partner], partner, group) for partner in near]
    sent_far = []
    for index in range(local):
        pieces = [sends[group // 2 + place * local + index] for place in range(len(far))]
        if index > 0:
            pieces, sent_near = lax.optimization_barrier((pieces, sent_near))
        sent_far.append([swap(piece, partner, group) for piece, partner in zip(pieces, far)])
    backs = [[None] * group for _ in range(local)]
    results = [None] * group
    calls = []
    for index in range(local - 1):
        calls += [(index, near), (index, far)]
    calls += [(local - 1, near[1:] + far), (local - 1, near[:1])]
    grads, owned, parts = [None] * local, [], []
    sums = functools.partial(sum_expert_grads, adapters=adapters, owners=owners)
    last = None
    for index, some in calls:
        pieces = [
            sent_near[partner] if partner in near else sent_far[index][partner - len(near)]
            for partner in some
        ]
        if last is not None:
            pieces, last = lax.optimization_barrier((pieces, last))
        if (index, some) == calls[-1]:
            parts, last = lax.optimization_barrier((parts, last))
            owned = [sums(part) for part in parts]
            pieces, backs[:index], owned = lax.optimization_barrier((pieces, backs[:index], owned))
        outs = expert_call(
            index, some, group, per_owner, pieces, [cots[partner] for partner in some], grads[index],
            [results[partner] for partner in some] if index else [], weights,
        )
        grads[index] = last = outs[-1]
        for place, partner in enumerate(some):
            backs[index][partner] = swap(outs[place], partner, group)
            results[partner] = outs[len(some) + place]
        if index < local - 1 and some == far:
            parts.append(exchange_expert_grads(last, group, owners))
    backs = [value for some in backs for value in some]
    parts.append(exchange_expert_grads(last, group, owners))
    gather = functools.partial(lax.all_gather, axis_name="dp", axis=0, tiled=False)
    if owners <= RANK:
        owned = [gather(own) for own in owned]
    back_hidden, back_attention, back_inner_o, back_mixed = combine_call(
        lengths, backs, routes, data, cols, cotangent, ei, hidden, norm_gains, output_weight, acat, bcat,
        table, reader,
    )
    flat, back_mixed = lax.optimization_barrier((results, back_mixed))
    flat = [swap(value, partner, group) for partner, value in enumerate(flat)]

    packed = everyone == 2 * RANK and group == 4
    dq, dk, dv, back_inner, adapter_grads = attend_back_call(
        packed, lengths, adapter_ids, q2, keys, values, mixed, back_mixed, *angles, bcat, inner, inner_o,
        back_inner_o, back_attention, normed,
    )
    parts[-1], adapter_grads, flat, owned = lax.optimization_barrier(
        (parts[-1], adapter_grads, flat, owned)
    )
    own = sums(parts[-1])
    adapter_grads, own, flat = lax.optimization_barrier((adapter_grads, own, flat))
    owned.append(gather(own) if owners <= RANK else own)
    layer_out = result_call(lengths, flat, cols, ei, hidden, table)
    input_back = last_call(
        dq, dk, dv, input_weights, acat, back_inner, tokens, back_hidden, norm_gains
    )
    outs = []
    if owners <= RANK:
        for index, own in enumerate(owned[:-1]):
            outs = finish_expert_call(index, local, own, outs, adapters, width, hidden_width)
    def finish(later, part):
        input_back, outs = later
        if owners <= RANK:
            return input_back, finish_expert_call(
                local - 1, local, part, outs, adapters, width, hidden_width
            )
        return input_back, expert_sums(owned, adapters, owners, width, hidden_width)

    down_sum, upper_sum, layer_out, (input_back, outs) = adapter_sums(
        adapter_grads, layer_out, (input_back, outs), finish, owned[-1], adapter_ids, adapters, owners, group, width
    )
    in_down_sum, in_up_sum, out_down_sum, out_up_sum = outs
    return (
        layer_out,
        input_back,
        down_sum,
        upper_sum,
        in_down_sum,
        in_up_sum,
        out_down_sum,
        out_up_sum,
    )


def solution(mesh):
    tokens_spec, copied = P(("dp", "expert"), None), P()
    owned = P("expert")
    placed = (
        (tokens_spec, tokens_spec, P(("dp", "expert")), P(("dp", "expert")), tokens_spec, tokens_spec)
        + (copied,) * 9
        + (owned,) * 7
    )
    return jax.shard_map(
        body,
        mesh=mesh,
        in_specs=placed,
        out_specs=(tokens_spec, tokens_spec, copied, copied) + (owned,) * 4,
        check_vma=False,
    )
```

```python
import functools
import math

import jax
import jax.numpy as jnp
import numpy as np
from jax import lax
from jax.experimental import pallas as pl
from jax.experimental.pallas import tpu as pltpu
from jax.sharding import PartitionSpec as P

HEADS = 12
HD = 64
EXPERTS = 8
RANK = 16
CAP = 192
EPSILON = 1e-06
F32 = jnp.float32
BF = jnp.bfloat16
NEG = -1e30
LANES = 128
TILE = 256
STEP = 512
WIDE_STEP = 1024
FTILE = 512
PAIRS = HEADS // 2
AHEAD = 1
PARAMS = pltpu.CompilerParams(vmem_limit_bytes=67043328)
META = 8
MIX_ROW = 16
VECTOR_ROW = 20
TARGET_LANE = 24
KEEP_LANE = 26
READ_VECTOR = 48
READ_ROWS = 64
PIECE = CAP + META


def mm(left, right):
    return jnp.dot(left, right, preferred_element_type=F32)


def mm_nt(left, right):
    return lax.dot_general(left, right, (((1,), (1,)), ((), ())), preferred_element_type=F32)


def mm_tn(left, right):
    return lax.dot_general(left, right, (((0,), (0,)), ((), ())), preferred_element_type=F32)


def iota(shape, axis):
    return lax.broadcasted_iota(jnp.int32, shape, axis)


def hot(condition):
    return jnp.where(condition, 1.0, 0.0).astype(BF)


def split2(value):
    high = value.astype(BF)
    return high, (value - high.astype(F32)).astype(BF)


def split3(value):
    high = value.astype(BF)
    rest = value - high.astype(F32)
    middle = rest.astype(BF)
    return high, middle, (rest - middle.astype(F32)).astype(BF)


def whole(shape):
    zeros = (0,) * len(shape)
    return pl.BlockSpec(shape, lambda *_: zeros)


def smem():
    return pl.BlockSpec(memory_space=pltpu.SMEM)


def tall(width, step=STEP):
    return pl.BlockSpec((step, width), lambda i: (i, 0))


def wide(height, step=STEP):
    return pl.BlockSpec((height, step), lambda i: (0, i))


def tile(width):
    return pl.BlockSpec((TILE, width), lambda i: (i, 0))


def side_by_side(stages, step=STEP):
    running = [stages(slice(start, start + TILE)) for start in range(0, step, TILE)]
    while running:
        running = [stage for stage in running if next(stage, True) is None]


def shape_of(*shape, dtype=BF):
    return jax.ShapeDtypeStruct(shape, dtype)


def cost(microseconds):
    return pl.CostEstimate(flops=int(microseconds * 1e+09), bytes_accessed=0, transcendentals=0)


@functools.lru_cache(maxsize=None)
def turn_tables(length_in):
    half = HD // 2
    inverse = np.exp(np.arange(half, dtype=np.float64) * (-2.0 * math.log(10000.0) / HD))

    def table(positions):
        angles = np.tile(positions[:, None] * inverse[None, :], (1, 4))
        return np.stack([np.cos(angles), np.sin(angles)]).astype(np.float32)

    return table(np.arange(0.0, length_in, 32)), table(np.arange(0.0, 32))


def turn_rows(coarse_ref, fine_ref, first, count):
    fine_cos, fine_sin = fine_ref[0], fine_ref[1]
    sign = jnp.where(iota((32, LANES), 1) % HD < HD // 2, -1.0, 1.0)
    signed_cos, signed_sin = fine_cos * sign, fine_sin * sign
    cosines, sines = [], []
    for index in range(count // 32):
        row = first // 32 + index
        coarse_cos, coarse_sin = coarse_ref[0, pl.ds(row, 1), :], coarse_ref[1, pl.ds(row, 1), :]
        cosines.append(coarse_cos * fine_cos - coarse_sin * fine_sin)
        sines.append(coarse_sin * signed_cos + coarse_cos * signed_sin)
    return jnp.concatenate(cosines, axis=0), jnp.concatenate(sines, axis=0)


def rope(value, cosine, sine):
    first = iota(value.shape, 1) % HD < HD // 2
    turned = jnp.where(first, pltpu.roll(value, LANES - HD // 2, 1), pltpu.roll(value, HD // 2, 1))
    return value * cosine + turned * sine


def find_slots(length, routes_ref, slot_ref):
    tok_count = slot_ref.shape[1]
    before = hot(iota((TILE, TILE), 0) < iota((TILE, TILE), 1))
    carry = jnp.zeros((2 * EXPERTS, 1), F32)
    for start in range(0, tok_count, TILE):
        span = slice(start, start + TILE)
        expert = iota((2 * EXPERTS, TILE), 0)
        token = iota((2 * EXPERTS, TILE), 1) + start
        named = (routes_ref[0:1, span] == expert) | (routes_ref[1:2, span] == expert)
        hit = named & (token < length) & (expert < EXPERTS)
        hits = jnp.where(hit, 1.0, 0.0)
        slots = mm(hits.astype(BF), before) + carry
        carry = carry + jnp.sum(hits, axis=1, keepdims=True)
        slot_ref[:, span] = jnp.where(hit, slots, -1.0)[:EXPERTS].astype(jnp.int32)


def pick_rows(slot_ref, step, me, local):
    first = jnp.bitwise_xor(step, me) * local
    place = iota((CAP, slot_ref.shape[1]), 0)
    return first, [hot(place == slot_ref[pl.ds(first + index, 1), :]) for index in range(local)]


def pick_source(chosen, source_ref):
    half = source_ref.shape[0] // 2
    return mm(chosen[:, :half], source_ref[:half]) + mm(chosen[:, half:], source_ref[half:])


def store_piece(out_refs, step, other, index, value, start):
    @pl.when(step == other)
    def _():
        out_refs[index][start : start + value.shape[0], :] = value


def route_body(local, group, len_ref, me_ref, routes_ref, source_ref, slot_ref, *out_refs):
    step = pl.program_id(0)

    @pl.when(step == 0)
    def _():
        find_slots(len_ref[0], routes_ref, slot_ref)

    _, chosen = pick_rows(slot_ref, step, me_ref[0], local)
    rows = pick_source(jnp.concatenate(chosen, axis=0), source_ref).astype(BF)
    for other in range(group):
        store_piece(out_refs, step, other, other, rows, 0)


def route_call(local, group, length, me, routes, source):
    tok_count, width = source.shape
    return pl.pallas_call(
        functools.partial(route_body, local, group),
        grid=(group,),
        in_specs=[smem(), smem(), whole(routes.shape), whole(source.shape)],
        out_specs=[whole((EXPERTS, tok_count))] + [whole((local * CAP, width))] * group,
        out_shape=[shape_of(EXPERTS, tok_count, dtype=jnp.int32)]
        + [shape_of(local * CAP, width)] * group,
        compiler_params=PARAMS,
        cost_estimate=cost(6.5),
        name="route_rows",
    )(length, me, routes, source)


def send_rows(local, group, partner, me_ref, id_ref, slot_ref, data_ref, source_ref, out_refs):
    width = source_ref.shape[1]
    first, chosen = pick_rows(slot_ref, partner, me_ref[0], local)
    rows = pick_source(jnp.concatenate(chosen, axis=0), source_ref).astype(BF)
    for index in range(local):
        pieces = split3(data_ref[pl.ds(first + index, 1), :])
        stack = jnp.concatenate(
            [piece.astype(F32) for piece in pieces]
            + [jnp.zeros((13, chosen[index].shape[1]), F32)],
            axis=0,
        ).astype(BF)
        gates = mm_nt(stack, chosen[index])[0:META]
        gates = jnp.where(iota(gates.shape, 0) == 3, id_ref[0].astype(F32), gates)
        meta = jnp.concatenate([gates, jnp.zeros((META, width - CAP), F32)], axis=1)
        kept = rows[index * CAP : index * CAP + CAP]
        for other in range(group):
            far = other >= group // 2
            place = group // 2 + (other - group // 2) * local + index if far else other
            start = 0 if far else index * PIECE
            store_piece(out_refs, partner, other, place, kept, start)
            store_piece(out_refs, partner, other, place, meta.astype(BF), start + CAP)


def pre_body(
    id_ref, x_ref, gain_ref, w_ref, ad_ref, au_ref, coarse_ref, fine_ref, router_ref, cmix_ref, vec_ref,
    resid_ref, normed_ref, inner_ref, acat_ref, bcat_ref, table_ref, mix_ref, read_ref, q_ref, k_ref,
    v_ref, square_ref,
):
    @pl.when(pl.program_id(0) == 0)
    def _():
        first = RANK * id_ref[0]
        total = None
        for index in range(4):
            row, column = iota((LANES, LANES), 0), iota((LANES, LANES), 1)
            place = hot((row >= first) & (row < first + RANK) & (column == (row - first) * 4 + index))
            part = mm(ad_ref[index], place)
            total = part if total is None else total + part
            place = hot(
                (column >= first) & (column < first + RANK) & (row == (column - first) * 4 + index)
            )
            bcat_ref[index] = mm(place, au_ref[index]).astype(BF)
        acat_ref[...] = total.astype(BF)
        table_ref[...] = jnp.zeros_like(table_ref)
        table_ref[0 : EXPERTS + 4, :] = router_ref[...].astype(F32)
        table_ref[MIX_ROW : MIX_ROW + 4, :] = cmix_ref[...]
        table_ref[VECTOR_ROW : VECTOR_ROW + 2, :] = vec_ref[...]
        read_ref[...] = jnp.zeros_like(read_ref)
        read_ref[0 : EXPERTS + 4, :] = router_ref[...].astype(F32)
        for place, piece in enumerate(split3(cmix_ref[...])):
            read_ref[16 + 8 * place : 20 + 8 * place, :] = piece.astype(F32)
        for place, piece in enumerate(split3(vec_ref[...])):
            read_ref[READ_VECTOR + 2 * place : READ_VECTOR + 2 * place + 2, :] = piece.astype(F32)
        square_ref[...] = jnp.zeros_like(square_ref)
        square_ref[0 : EXPERTS + 4, 0 : EXPERTS + 4] = resid_ref[...]
        mix_ref[...] = square_ref[...].T[0:16]

    def stages(at):
        x = x_ref[at].astype(F32)
        scale = lax.rsqrt(jnp.mean(x * x, axis=-1, keepdims=True) + EPSILON)
        normed = (x * scale * gain_ref[0:1, :]).astype(BF)
        normed_ref[at] = normed
        yield
        inner = mm(normed, acat_ref[...]).astype(BF)
        inner_ref[at] = inner
        yield
        for index, out_ref in enumerate((q_ref, k_ref, v_ref)):
            value = mm(normed, w_ref[index]) + mm(inner, bcat_ref[index])
            yield
            rows = pl.ds(pl.multiple_of(pl.program_id(0) * STEP + at.start, TILE), TILE)
            if index == 2:
                for pair in range(PAIRS):
                    span = slice(pair * LANES, pair * LANES + LANES)
                    out_ref[pair, rows] = value[:, span].astype(BF)
                continue
            cosine, sine = turn_rows(coarse_ref, fine_ref, pl.program_id(0) * STEP + at.start, TILE)
            for pair in range(PAIRS):
                span = slice(pair * LANES, pair * LANES + LANES)
                turned = rope(value[:, span], cosine, sine).astype(BF)
                if index == 0:
                    turned = (turned.astype(F32) * HD**-0.5).astype(BF)
                out_ref[pair, rows] = turned
            yield

    side_by_side(stages)


def attend_body(len_ref, q_ref, k_ref, v_ref, mixed_ref, q2_ref):
    tok_count = q_ref.shape[0]
    lane = iota((tok_count, LANES), 1)
    hidden_key = iota((tok_count, LANES), 0) >= len_ref[0]
    row = iota((LANES, tok_count), 0)
    row_tile = row[:, :TILE]
    causal = iota((TILE, TILE), 0) <= iota((TILE, TILE), 1)
    queries_t = q_ref[...].astype(F32).T
    values_t = v_ref[...].astype(F32).T
    keys = k_ref[...].astype(F32)
    heads = []
    for head in range(2):
        spare = HD * (1 - head)
        bias = jnp.where((lane == spare) & hidden_key, NEG, 0.0)
        one = jnp.where(row == spare, 1.0, 0.0)
        own = row // HD == head
        heads.append(
            (
                jnp.where(lane // HD == head, keys, bias).astype(BF),
                jnp.where(own, queries_t, one).astype(BF),
                jnp.where(own, values_t, one).astype(BF),
            )
        )
    units = [(start, head) for start in range(0, tok_count, TILE) for head in range(2)]

    def score(unit):
        start, head = unit
        keys, queries, _ = heads[head]
        part = queries[:, start : start + TILE]
        near = mm(keys[start : start + TILE], part)
        return near, mm(keys[:start], part) if start else None

    outs = {}
    waiting = [score(unit) for unit in units[:3]]
    for index, (start, head) in enumerate(units):
        near, far = waiting.pop(0)
        if index + 3 < len(units):
            waiting.append(score(units[index + 3]))
        spare = HD * (1 - head)
        _, queries, values = heads[head]
        near = jnp.where(causal, near, NEG)
        top = jnp.max(near, axis=0, keepdims=True)
        if start:
            top = jnp.maximum(top, jnp.max(far, axis=0, keepdims=True))
        mixed = mm(values[:, start : start + TILE], jnp.exp(near - top).astype(BF))
        if start:
            mixed = mixed + mm(values[:, :start], jnp.exp(far - top).astype(BF))
        total = mixed[spare : spare + 1]
        outs[head] = mixed * (1.0 / total)
        kept = queries[:, start : start + TILE]
        logs = jnp.zeros((LANES, TILE), F32)
        for offset, piece in enumerate(split3(top + jnp.log(total))):
            logs = jnp.where(row_tile == spare + 1 + offset, piece.astype(F32), logs)
        q2_ref[head * LANES : head * LANES + LANES, start : start + TILE] = kept + logs.astype(BF)
        if head == 1:
            mixed = jnp.where(row_tile < HD, outs[0], outs[1])
            mixed_ref[start : start + TILE] = mixed.T.astype(BF)


def pre_attend_body(steps, len_ref, *refs):
    pre_ins, pre_outs = refs[:12], refs[12:19]
    key_ref, value_ref, mixed_ref, q2_ref, q_all, k_all, v_all, square_ref = refs[19:]
    step = pl.program_id(0)

    @pl.when(step < steps)
    def _():
        pre_body(*pre_ins, *pre_outs, q_all, k_all, v_all, square_ref)

    @pl.when(step >= steps)
    def _():
        pair = step - steps
        key_ref[...] = k_all[pair]
        value_ref[...] = v_all[pair]
        attend_body(len_ref, q_all.at[pair], k_all.at[pair], v_all.at[pair], mixed_ref, q2_ref)


def pre_attend_call(
    length, ids, tokens, gains, weights, down, upper, coarse, fine, router, constant_mix, vectors,
    residual_mix,
):
    tok_count, width = tokens.shape
    steps = tok_count // STEP

    def rows_of(columns):
        return pl.BlockSpec((STEP, columns), lambda i: (jnp.minimum(i, steps - 1), 0))

    column = pl.BlockSpec((tok_count, LANES), lambda i: (0, jnp.maximum(i - steps, 0)))
    return pl.pallas_call(
        functools.partial(pre_attend_body, steps),
        grid=(steps + PAIRS,),
        in_specs=[
            smem(), smem(), rows_of(width), whole(gains.shape), whole(weights.shape), whole(down.shape),
            whole(upper.shape), whole(coarse.shape), whole(fine.shape), whole(router.shape),
            whole(constant_mix.shape), whole(vectors.shape), whole(residual_mix.shape),
        ],
        out_specs=[
            rows_of(width), rows_of(LANES), whole((width, LANES)), whole(upper.shape),
            whole((LANES, width)), whole((16, LANES)), whole((READ_ROWS, width)), column, column,
            column, pl.BlockSpec((2 * LANES, tok_count), lambda i: (jnp.maximum(i - steps, 0), 0)),
        ],
        out_shape=[
            shape_of(tok_count, width), shape_of(tok_count, LANES), shape_of(width, LANES),
            shape_of(*upper.shape), shape_of(LANES, width, dtype=F32), shape_of(16, LANES, dtype=F32),
            shape_of(READ_ROWS, width, dtype=F32), shape_of(tok_count, width),
            shape_of(tok_count, width), shape_of(tok_count, width), shape_of(2 * width, tok_count),
        ],
        scratch_shapes=[pltpu.VMEM((PAIRS, tok_count, LANES), BF)] * 3
        + [pltpu.VMEM((LANES, LANES), F32)],
        compiler_params=PARAMS,
        cost_estimate=cost(25),
        name="attention_forward",
    )(
        length, ids, tokens, gains, weights, down, upper, coarse, fine, router, constant_mix, vectors,
        residual_mix,
    )


def attend_back_body(
    len_ref, q2_ref, k_ref, v_ref, mixed_ref, back_ref, coarse_ref, fine_ref,
    dq_ref, dk_ref, dv_ref, acc_ref, turn_ref,
):
    tok_count = k_ref.shape[0]

    @pl.when(pl.program_id(0) == 0)
    def _():
        turn_ref[0], turn_ref[1] = turn_rows(coarse_ref, fine_ref, 0, tok_count)

    lane = iota((tok_count, LANES), 1)
    position = iota((tok_count, LANES), 0)
    bias = jnp.where(position < len_ref[0], 0.0, NEG)
    causal = iota((TILE, TILE), 0) <= iota((TILE, TILE), 1)
    row = iota((LANES, tok_count), 0)
    back = back_ref[...].astype(F32)
    product_t = (back * mixed_ref[...].astype(F32)).T
    back_t = back.T
    keys, values = k_ref[...].astype(F32), v_ref[...].astype(F32)
    heads = []
    for head in range(2):
        own = lane // HD == head
        spare = HD * (1 - head)
        minus = jnp.where((lane > spare) & (lane < spare + 4), -1.0, 0.0)
        q2 = q2_ref[head * LANES : head * LANES + LANES, :]
        k2f = jnp.where(own, keys, jnp.where(lane == spare, bias, minus))
        k2 = k2f.astype(BF)
        k2t = k2f.T.astype(BF)
        v2 = jnp.where(own, values, minus).astype(BF)
        own_row = row // HD == head
        delta = jnp.sum(jnp.where(own_row, product_t, 0.0), axis=0, keepdims=True)
        back2 = jnp.where(own_row, back_t, 0.0)
        for offset, piece in enumerate(split3(delta)):
            back2 = jnp.where(row == spare + 1 + offset, piece.astype(F32), back2)
        back2 = back2.astype(BF)
        heads.append((k2, k2t, v2, q2, back2))
    units = [(start, head) for start in range(0, tok_count, TILE) for head in range(2)]

    def score(unit):
        start, head = unit
        k2, _, v2, q2, back2 = heads[head]
        stop = start + TILE
        return mm(k2[start:stop], q2[:, start:]), mm(v2[start:stop], back2[:, start:])

    grads = [([], []), ([], [])]
    waiting = [score(unit) for unit in units[:AHEAD]]
    for index, (start, head) in enumerate(units):
        scores, slopes = waiting.pop(0)
        if index + AHEAD < len(units):
            waiting.append(score(units[index + AHEAD]))
        _, k2t, _, q2, back2 = heads[head]
        stop = start + TILE
        diagonal = jnp.where(causal, scores[:, :TILE], NEG)
        if stop < tok_count:
            diagonal = jnp.concatenate([diagonal, scores[:, TILE:]], axis=1)
        weights = jnp.exp(diagonal)
        turned = (weights * slopes).astype(BF)
        grads[head][1].append(mm_nt(weights.astype(BF), back2[:, start:]))
        grads[head][0].append(mm_nt(turned, q2[:, start:]))
        update = mm(k2t[:, start:stop], turned)
        if start == 0:
            acc_ref[head] = update
        else:
            acc_ref[head, :, start:] += update
    grads = [
        (jnp.concatenate(keys, axis=0), jnp.concatenate(values, axis=0)) for keys, values in grads
    ]
    low_lane = lane < HD
    cosine, sine = turn_ref[0], -turn_ref[1]
    dq = jnp.where(row < HD, acc_ref[0], acc_ref[1]).T * HD**-0.5
    dq_ref[...] = rope(dq, cosine, sine).astype(BF)
    dk = jnp.where(low_lane, grads[0][0], grads[1][0])
    dk_ref[...] = rope(dk, cosine, sine).astype(BF)
    dv_ref[...] = jnp.where(low_lane, grads[0][1], grads[1][1]).astype(BF)


def pack_grads(packed, id_ref, acc_ref, grad_ref):
    count, width = acc_ref.shape[0], acc_ref.shape[1] // 2
    if not packed:
        grad_ref[...] = acc_ref[...].astype(BF)
        return
    half = width // 2
    shape = (16 * RANK, count)
    place, row = iota(shape, 0), iota(shape, 1)
    total = None
    for index in range(4):
        kind, part = index // 2, index % 2
        here = (place % 4 == row % 4) & (place // 16 == row // 4)
        here = here & (place // 8 % 2 == part) & (place // 4 % 2 == kind)
        start = kind * width + part * half
        piece = mm(hot(here), acc_ref[:, start : start + half].astype(BF))
        total = piece if total is None else total + piece
    grad_ref[:, 0:half] = total.astype(BF)
    grad_ref[:, half:] = jnp.full((16 * RANK, LANES), id_ref[0].astype(F32), F32).astype(BF)


def attend_back_all_body(packed, len_ref, id_ref, *refs):
    ins, refs = refs[:7], refs[7:]
    bcat_ref, inner_ref, inner_o_ref, din_ref, ba_ref, normed_hbm, mixed_hbm = refs[:7]
    dq_ref, dk_ref, dv_ref, back_ref, grad_ref = refs[7:12]
    scratch, (inner_all, back_all, acc_ref, normed_all, mixed_all, sems) = refs[12:14], refs[14:]
    step = pl.program_id(0)
    count = inner_all.shape[1]
    width = normed_all.shape[1]
    copies = [
        pltpu.make_async_copy(normed_hbm, normed_all, sems.at[0]),
        pltpu.make_async_copy(mixed_hbm, mixed_all, sems.at[1]),
    ]

    @pl.when(step == 0)
    def _():
        for copy in copies:
            copy.start()
        inner_all[0] = inner_ref[...].astype(F32).T[0:count].astype(BF)
        inner_all[1] = inner_o_ref[...].astype(F32).T[0:count].astype(BF)
        back_all[...] = jnp.zeros_like(back_all)

    @pl.when(step < PAIRS)
    def _():
        attend_back_body(len_ref, *ins, dq_ref, dk_ref, dv_ref, *scratch)
        number = iota((count, LANES), 0) % 4
        upper = mm(inner_all[1], ba_ref[...])
        total = back_all[...]
        for index, ref in enumerate((dq_ref, dk_ref, dv_ref)):
            value = ref[...]
            upper = jnp.where(number == index, mm(inner_all[0], value), upper)
            total = total + mm_nt(value, bcat_ref[index])
        back_all[...] = total
        at = width + step * LANES
        acc_ref[:, pl.ds(pl.multiple_of(at, LANES), LANES)] = upper

    @pl.when(step == PAIRS)
    def _():
        back = back_all[...].astype(BF)
        back_ref[...] = back
        back_t = (back.astype(F32) + din_ref[...].astype(F32)).T[0:count].astype(BF)
        for copy in copies:
            copy.wait()
        number = iota((count, width), 0) % 4
        half = back_t.shape[1] // 2

        def down(rows_ref):
            return mm(back_t[:, :half], rows_ref[:half]) + mm(back_t[:, half:], rows_ref[half:])

        acc_ref[:, 0:width] = jnp.where(number < 3, down(normed_all), down(mixed_all))
        pack_grads(packed, id_ref, acc_ref, grad_ref)


def attend_back_call(
    packed, length, ids, q2, keys, values, mixed, back, coarse, fine, bcat, inner, inner_o, din, ba,
    normed,
):
    tok_count, width = keys.shape
    column = pl.BlockSpec((tok_count, LANES), lambda i: (0, jnp.minimum(i, PAIRS - 1)))
    grad_shape = (16 * RANK, width // 2 + LANES) if packed else (4 * RANK, 2 * width)
    return pl.pallas_call(
        functools.partial(attend_back_all_body, packed),
        grid=(PAIRS + 1,),
        in_specs=[
            smem(), smem(),
            pl.BlockSpec((2 * LANES, tok_count), lambda i: (jnp.minimum(i, PAIRS - 1), 0)), column,
            column, column, column, whole(coarse.shape), whole(fine.shape),
            pl.BlockSpec((4, LANES, LANES), lambda i: (0, 0, jnp.minimum(i, PAIRS - 1))),
            whole(inner.shape), whole(inner_o.shape), whole(din.shape), column,
            pl.BlockSpec(memory_space=pl.ANY), pl.BlockSpec(memory_space=pl.ANY),
        ],
        out_specs=[column] * 3 + [whole((tok_count, LANES)), whole(grad_shape)],
        out_shape=[shape_of(tok_count, width)] * 3
        + [shape_of(tok_count, LANES), shape_of(*grad_shape)],
        scratch_shapes=[
            pltpu.VMEM((2, LANES, tok_count), F32), pltpu.VMEM((2, tok_count, LANES), F32),
            pltpu.VMEM((2, 4 * RANK, tok_count), BF), pltpu.VMEM((tok_count, LANES), F32),
            pltpu.VMEM((4 * RANK, 2 * width), F32), pltpu.VMEM((tok_count, width), BF),
            pltpu.VMEM((tok_count, width), BF), pltpu.SemaphoreType.DMA((2,)),
        ],
        compiler_params=PARAMS,
        cost_estimate=cost(12),
        name="attention_backward",
    )(
        length, ids, q2, keys, values, mixed, back, coarse, fine, bcat, inner, inner_o, din, ba,
        normed, mixed,
    )


def post_body(
    local, group, me_ref, mixed_ref, x_ref, wo_ref, acat_ref, bcat_ref, gain_ref, read_ref, mix_ref,
    prev_ref, routes_ref, slot_ref, hidden_ref, ei_ref, inner_ref, data_ref, cols_ref,
):
    reader = read_ref[0:READ_VECTOR].astype(BF)

    def stages(at):
        mixed = mixed_ref[at]
        inner = mm(mixed, acat_ref[...]).astype(BF)
        inner_ref[at] = inner
        yield
        hidden = x_ref[at].astype(F32) + (mm(mixed, wo_ref[...]) + mm(inner, bcat_ref[0]))
        hidden_ref[at] = hidden
        yield
        scale = lax.rsqrt(jnp.mean(hidden * hidden, axis=-1, keepdims=True) + EPSILON)
        ei = (hidden * scale * gain_ref[1:2, :]).astype(BF)
        ei_ref[at] = ei
        yield
        read = mm_nt(reader, ei)
        yield
        logits = read[0:16]
        for index in range(EXPERTS + 4):
            logits = logits + mix_ref[:, index : index + 1] * prev_ref[index : index + 1, at]
        first, second = routes_ref[0:1, at].astype(F32), routes_ref[1:2, at].astype(F32)
        number = iota((16, TILE), 0).astype(F32)
        one = jnp.sum(jnp.where(number == first, logits, 0.0), axis=0, keepdims=True)
        two = jnp.sum(jnp.where(number == second, logits, 0.0), axis=0, keepdims=True)
        top = jnp.maximum(one, two)
        one, two = jnp.exp(one - top), jnp.exp(two - top)
        gate_a, gate_b = one / (one + two), two / (one + two)
        mixes = read[16:20] + read[24:28] + read[32:36]
        shares = []
        for index in range(2):
            left, right = mixes[2 * index : 2 * index + 1], mixes[2 * index + 1 : 2 * index + 2]
            top = jnp.maximum(left, right)
            left, right = jnp.exp(left - top), jnp.exp(right - top)
            shares += [left / (left + right), right / (left + right)]

        def both(value):
            return jnp.where(first == value, gate_a, 0.0) + jnp.where(second == value, gate_b, 0.0)

        gates = jnp.where(number == first, gate_a, 0.0) + jnp.where(number == second, gate_b, 0.0)
        beta_a, beta_b = both(EXPERTS + 2.0), both(EXPERTS + 3.0)
        keep = both(EXPERTS + 1.0) + beta_a * shares[0] + beta_b * shares[2]
        data_ref[0:8, at] = gates[0:8]
        tail = [gate_a, gate_b] + shares + [beta_a, beta_b]
        data_ref[8:16, at] = jnp.concatenate(tail, axis=0)
        yield
        slots = slot_ref[:, at].astype(F32)
        expert = iota((EXPERTS, TILE), 0)
        partner = jnp.bitwise_xor(expert // local, me_ref[0])
        base = ((expert % local) * (group * CAP) + partner * CAP).astype(F32)
        place = jnp.where(slots >= 0, slots + base + 1.0, 0.0)
        expert = expert.astype(F32)
        target_a = jnp.sum(jnp.where(expert == first, place, 0.0), axis=0, keepdims=True) - 1.0
        target_b = jnp.sum(jnp.where(expert == second, place, 0.0), axis=0, keepdims=True) - 1.0
        stack = jnp.concatenate(
            [jnp.zeros((VECTOR_ROW, TILE), F32), beta_a * shares[1], beta_b * shares[3]]
            + [jnp.zeros((2, TILE), F32), target_a, target_b, keep]
            + [jnp.zeros((LANES - KEEP_LANE - 1, TILE), F32)],
            axis=0,
        )
        cols_ref[at] = stack.T

    side_by_side(stages)


def post_send_body(local, group, steps, me_ref, id_ref, slot_all_ref, *refs):
    post_refs, out_refs, (ei_all, data_all) = refs[:16], refs[16:-2], refs[-2:]
    step = pl.program_id(0)

    @pl.when(step < steps)
    def _():
        post_body(local, group, me_ref, *post_refs)
        span = pl.ds(pl.multiple_of(step * STEP, STEP), STEP)
        ei_all[span] = post_refs[12][...]
        data_all[:, span] = post_refs[14][...]

    @pl.when(step >= steps)
    def _():
        send_rows(local, group, step - steps, me_ref, id_ref, slot_all_ref, data_all, ei_all, out_refs)


def post_call(
    local, group, me, ids, mixed, tokens, weight, acat, bcat, gains, reader, mixer, prev, routes, slots
):
    tok_count, width = tokens.shape
    steps = tok_count // STEP
    heights = [local * PIECE] * (group // 2) + [PIECE] * ((group - group // 2) * local)

    def rows_of(columns):
        return pl.BlockSpec((STEP, columns), lambda i: (jnp.minimum(i, steps - 1), 0))

    def lanes_of(height):
        return pl.BlockSpec((height, STEP), lambda i: (0, jnp.minimum(i, steps - 1)))

    return pl.pallas_call(
        functools.partial(post_send_body, local, group, steps),
        grid=(steps + group,),
        in_specs=[
            smem(), smem(), whole(slots.shape), rows_of(width), rows_of(width), whole(weight.shape),
            whole(acat.shape), pl.BlockSpec((1, LANES, width), lambda i: (3, 0, 0)), whole(gains.shape),
            whole(reader.shape), whole(mixer.shape), lanes_of(EXPERTS + 4), lanes_of(2),
            lanes_of(EXPERTS),
        ],
        out_specs=[
            rows_of(width), rows_of(width), rows_of(LANES), lanes_of(16), rows_of(LANES)
        ] + [whole((height, width)) for height in heights],
        out_shape=[
            shape_of(tok_count, width, dtype=F32), shape_of(tok_count, width),
            shape_of(tok_count, LANES), shape_of(16, tok_count, dtype=F32),
            shape_of(tok_count, LANES, dtype=F32),
        ] + [shape_of(height, width) for height in heights],
        scratch_shapes=[pltpu.VMEM((tok_count, width), BF), pltpu.VMEM((16, tok_count), F32)],
        compiler_params=PARAMS,
        cost_estimate=cost(14),
        name="after_attention",
    )(
        me, ids, slots, mixed, tokens, weight, acat, bcat, gains, reader, mixer, prev, routes, slots
    )


def expert_body(
    local_index, pair, per_owner, group, steps, has_grad, kept, *refs
):
    count = len(pair)
    piece_refs, refs = refs[:count], refs[count:]
    cot_refs, refs = refs[:count], refs[count:]
    dn_ref, ou_ref, wg_hbm, wu_hbm, wd_hbm, up_hbm, od_hbm = refs[:7]
    refs = refs[7:]
    if has_grad:
        before_hbm, refs = refs[0], refs[1:]
    refs = refs[kept:]
    back_refs, refs = refs[:count], refs[count:]
    out_refs, refs = refs[:count], refs[count:]
    (
        grad_ref, x_ref, g_ref, gate_ref, pick_ref, dr_ref, zg_ref, zu_ref, dzd_ref, zgt_ref, zut_ref,
        dzdt_ref, racc_ref, xacc_ref, zd_acc, dzg_acc, dzu_acc, h_ref, dg_ref, du_ref, wg_all, wu_all,
        wd_all, up_all, od_all, sems, *rest
    ) = refs
    rows, width = x_ref.shape
    compact = group * RANK
    tile = h_ref.shape[1]

    def copies(step):
        span = pl.ds(pl.multiple_of(step * tile, tile), tile)
        pairs = (
            (wg_hbm.at[local_index, :, span], wg_all),
            (wu_hbm.at[local_index, :, span], wu_all),
            (wd_hbm.at[local_index, span, :], wd_all),
            (up_hbm.at[local_index, :, :, span], up_all),
            (od_hbm.at[local_index, span, :], od_all),
        )
        return [
            pltpu.make_async_copy(source, target.at[step], sems.at[step, place])
            for place, (source, target) in enumerate(pairs)
        ]

    def begin(step):
        for copy in copies(step):
            copy.start()

    begin(0)

    def fold(value):
        place = iota((compact, LANES), 0)
        block = per_owner * group
        inner = place // block * per_owner + place % per_owner
        folded = mm_nt(hot(iota((compact, LANES), 1) % RANK == inner), value)
        place = iota((compact, rows), 0)
        owner = place % block // per_owner
        mine = iota((compact, rows), 1) // CAP + pair[0]
        return jnp.where(mine == owner, folded, 0.0).astype(BF)

    def put(start, value):
        grad_ref[:, pl.ds(start, value.shape[1])] = value.astype(BF)

    for index in range(count):
        span = slice(index * CAP, index * CAP + CAP)
        x_ref[span] = piece_refs[index][0:CAP]
        g_ref[span] = cot_refs[index][...]
        meta = piece_refs[index][CAP:PIECE].astype(F32)
        gate = (meta[0:1] + meta[1:2] + meta[2:3])[:, 0 : 2 * LANES]
        gate_ref[span] = jnp.broadcast_to(gate, (LANES, 2 * LANES)).T[0:CAP]
        lane = (iota((CAP, LANES), 1) // RANK).astype(F32)
        pick_ref[span] = jnp.where(lane == meta[3:4, 0:LANES], 1.0, 0.0)
    chosen = pick_ref[...] > 0.0
    dr = (gate_ref[:, 0:1] * g_ref[...].astype(F32)).astype(BF)
    dr_ref[...] = dr
    zg = jnp.where(chosen, mm(x_ref[...], dn_ref[0]), 0.0).astype(BF)
    zu = jnp.where(chosen, mm(x_ref[...], dn_ref[1]), 0.0).astype(BF)
    dzd = jnp.where(chosen, mm_nt(dr, ou_ref[...]), 0.0).astype(BF)
    zg_ref[...] = zg
    zu_ref[...] = zu
    dzd_ref[...] = dzd
    zgt_ref[...] = fold(zg)
    zut_ref[...] = fold(zu)
    dzdt_ref[...] = fold(dzd)
    for ref in (racc_ref, xacc_ref, zd_acc, dzg_acc, dzu_acc):
        ref[...] = jnp.zeros_like(ref)

    total = steps * tile
    begin(1)
    if has_grad:
        before = pltpu.make_async_copy(before_hbm, rest[0], rest[1])
        before.start()

    def run(step, carry):
        for copy in copies(step):
            copy.wait()

        @pl.when(step + 2 < steps)
        def _():
            begin(step + 2)

        wg_ref, wu_ref, wd_ref = wg_all.at[step], wu_all.at[step], wd_all.at[step]
        up_ref, od_ref = up_all.at[step], od_all.at[step]
        gate = mm(x_ref[...], wg_ref[...]) + mm(zg_ref[...], up_ref[0])
        upper = mm(x_ref[...], wu_ref[...]) + mm(zu_ref[...], up_ref[1])
        share = 0.5 * jnp.tanh(0.5 * gate) + 0.5
        silu = gate * share
        active = (silu * upper).astype(BF)
        h_ref[...] = active
        back = mm_nt(dr_ref[...], wd_ref[...]) + mm_nt(dzd_ref[...], od_ref[...])
        du = (back * silu).astype(BF)
        dg = (back * upper * (share + silu * (1.0 - share))).astype(BF)
        du_ref[...] = du
        dg_ref[...] = dg
        racc_ref[...] += mm(active, wd_ref[...])
        zd_acc[...] += mm(active, od_ref[...])
        xacc_ref[...] += mm_nt(dg, wg_ref[...]) + mm_nt(du, wu_ref[...])
        dzg_acc[...] += mm_nt(dg, up_ref[0])
        dzu_acc[...] += mm_nt(du, up_ref[1])
        at = pl.multiple_of(step * tile, tile)
        put(at, mm(zgt_ref[...], dg_ref[...]))
        put(total + at, mm(zut_ref[...], du_ref[...]))
        put(2 * total + at, mm(dzdt_ref[...], h_ref[...]))
        return carry

    lax.fori_loop(0, steps, run, 0)
    chosen = pick_ref[...] > 0.0
    zd = jnp.where(chosen, zd_acc[...], 0.0).astype(BF)
    dzg = jnp.where(chosen, dzg_acc[...], 0.0).astype(BF)
    dzu = jnp.where(chosen, dzu_acc[...], 0.0).astype(BF)
    result = racc_ref[...] + mm(zd, ou_ref[...])
    gated = (gate_ref[:, 0:1] * result).astype(BF)
    product = g_ref[...].astype(F32) * result.astype(BF).astype(F32)
    dots = jnp.broadcast_to(jnp.sum(product, axis=-1, keepdims=True), (rows, LANES))
    back_rows = (xacc_ref[...] + mm_nt(dzg, dn_ref[0]) + mm_nt(dzu, dn_ref[1])).astype(BF)
    for index in range(count):
        span = slice(index * CAP, index * CAP + CAP)
        out_refs[index][...] = gated[span]
        back_refs[index][0:CAP, :] = back_rows[span]
        column = jnp.concatenate(
            [dots[span], jnp.zeros((2 * LANES - CAP, LANES), F32)], axis=0
        ).T[0:1]
        meta = jnp.concatenate(
            [piece.astype(F32) for piece in split3(column)]
            + [jnp.zeros((META - 3, 2 * LANES), F32)],
            axis=0,
        )
        meta = jnp.concatenate([meta, jnp.zeros((META, width - 2 * LANES), F32)], axis=1)
        back_refs[index][CAP:PIECE, :] = meta.astype(BF)
    base = 3 * total
    place = iota((compact, LANES), 0)
    owner = place % (per_owner * group) // per_owner
    ids = jnp.zeros((compact, LANES), F32)
    for index in range(count):
        meta = piece_refs[index][CAP:PIECE, 0:LANES].astype(F32)
        ids = jnp.where(owner == pair[index], meta[3:4], ids)
    put(base + 3 * width, ids)
    put(base, mm(fold(zd), dr_ref[...]))
    put(base + width, mm(fold(dzg), x_ref[...]))
    put(base + 2 * width, mm(fold(dzu), x_ref[...]))
    if has_grad:
        before.wait()
        grad_ref[...] = grad_ref[...] + rest[0][...]


def expert_call(index, pair, group, per_owner, pieces, cots, before, results, weights):
    gate_w, up_w, down_w, in_down, in_up, out_down, out_up = weights
    width, hidden = gate_w.shape[1:]
    rows = len(pair) * CAP
    steps = hidden // FTILE
    columns = 3 * hidden + 3 * width + LANES
    compact = group * RANK
    has_grad = before is not None
    return pl.pallas_call(
        functools.partial(
            expert_body, index, pair, per_owner, group, steps, has_grad, len(results)
        ),
        grid=(1,),
        in_specs=[
            pl.BlockSpec((PIECE, width), lambda f, row=piece.shape[0] // PIECE > 1: (index * row, 0))
            for piece in pieces
        ]
        + [pl.BlockSpec((CAP, width), lambda f: (index, 0))] * len(pair)
        + [
            pl.BlockSpec((None, 2, width, LANES), lambda f: (index, 0, 0, 0)),
            pl.BlockSpec((None, LANES, width), lambda f: (index, 0, 0)),
        ]
        + [pl.BlockSpec(memory_space=pl.ANY)] * 5
        + [pl.BlockSpec(memory_space=pl.ANY)] * (has_grad + len(results)),
        out_specs=[whole((PIECE, width))] * len(pair)
        + [pl.BlockSpec((CAP, width), lambda f: (index, 0))] * len(pair)
        + [whole((compact, columns))],
        out_shape=[shape_of(PIECE, width)] * len(pair)
        + [shape_of(gate_w.shape[0] * CAP, width)] * len(pair)
        + [shape_of(compact, columns)],
        input_output_aliases={
            2 * len(pair) + 7 + has_grad + place: len(pair) + place for place in range(len(results))
        },
        scratch_shapes=[pltpu.VMEM((rows, width), BF)] * 2
        + [pltpu.VMEM((rows, LANES), F32)] * 2
        + [pltpu.VMEM((rows, width), BF)]
        + [pltpu.VMEM((rows, LANES), BF)] * 3
        + [pltpu.VMEM((compact, rows), BF)] * 3
        + [pltpu.VMEM((rows, width), F32)] * 2
        + [pltpu.VMEM((rows, LANES), F32)] * 3
        + [pltpu.VMEM((rows, FTILE), BF)] * 3
        + [pltpu.VMEM((steps, width, FTILE), BF)] * 2
        + [
            pltpu.VMEM((steps, FTILE, width), BF), pltpu.VMEM((steps, 2, LANES, FTILE), BF),
            pltpu.VMEM((steps, FTILE, LANES), BF), pltpu.SemaphoreType.DMA((steps, 5)),
        ]
        + [pltpu.VMEM((compact, columns), BF), pltpu.SemaphoreType.DMA] * has_grad,
        compiler_params=PARAMS,
        cost_estimate=cost(rows / 21),
        name="expert_layer",
    )(
        *pieces, *cots, in_down, out_up, gate_w, up_w, down_w, in_up, out_down,
        *([before] if has_grad else []), *results,
    )


def spread(cols, index, count):
    return iota((TILE, count), 1).astype(F32) == cols[:, index : index + 1]


def combine_body(
    pieces, len_ref, *refs
):
    back_refs = refs[:pieces]
    (
        routes_ref, data_ref, cols_ref, cot_ref, ei_ref, hidden_ref, gain_ref, wo_ref, acat_ref, bcat_ref,
        table_ref, read_ref, bh_ref, ba_ref, din_ref, bm_ref, back_all, dots_ref,
    ) = refs[pieces:]
    count = pieces * CAP

    @pl.when(pl.program_id(0) == 0)
    def _():
        for index, back_ref in enumerate(back_refs):
            back_all[index * CAP : index * CAP + CAP, :] = back_ref[0:CAP, :]
        dots = [back_ref[CAP:PIECE, 0:CAP].astype(F32) for back_ref in back_refs]
        dots = jnp.concatenate(dots, axis=1)
        dots_ref[...] = jnp.concatenate([dots, jnp.zeros_like(dots)], axis=0).astype(BF)

    table_high, table_low = split2(table_ref[...])
    stack = dots_ref[...]
    vectors = read_ref[READ_VECTOR:READ_ROWS].astype(BF)

    def stages(at):
        start = pl.program_id(0) * WIDE_STEP + at.start
        cols = cols_ref[at]
        chosen_a = hot(spread(cols, TARGET_LANE, count))
        chosen_b = hot(spread(cols, TARGET_LANE + 1, count))
        yield
        routed_a = jnp.sum(mm_nt(stack, chosen_a)[0:8], axis=0, keepdims=True)
        routed_b = jnp.sum(mm_nt(stack, chosen_b)[0:8], axis=0, keepdims=True)
        cot = cot_ref[at]
        cot_f = cot.astype(F32)
        yield
        along_x = jnp.sum(cot_f * ei_ref[at].astype(F32), axis=-1, keepdims=True)
        along_x = jnp.broadcast_to(along_x, (TILE, LANES)).T[0:1]
        yield
        along_c = mm_nt(vectors, cot)
        along_a = along_c[0:1] + along_c[2:3] + along_c[4:5]
        along_b = along_c[1:2] + along_c[3:4] + along_c[5:6]
        yield
        both = chosen_a + chosen_b
        half = count // 2
        back = mm(both[:, :half], back_all[:half]) + mm(both[:, half:], back_all[half:])
        yield
        first, second = routes_ref[0:1, at].astype(F32), routes_ref[1:2, at].astype(F32)
        token = iota((1, TILE), 1) + start
        valid = jnp.where(token < len_ref[0], 1.0, 0.0)
        gate_a, gate_b = data_ref[8:9, at], data_ref[9:10, at]
        share = [data_ref[index : index + 1, at] for index in range(10, 14)]
        beta_a, beta_b = data_ref[14:15, at], data_ref[15:16, at]
        const_a = share[0] * along_x + share[1] * along_a
        const_b = share[2] * along_x + share[3] * along_b

        def here(route):
            return (
                jnp.where(route == EXPERTS + 1.0, along_x, 0.0)
                + jnp.where(route == EXPERTS + 2.0, const_a, 0.0)
                + jnp.where(route == EXPERTS + 3.0, const_b, 0.0)
            )

        dot_a, dot_b = routed_a + here(first), routed_b + here(second)
        mean = gate_a * dot_a + gate_b * dot_b
        chosen_grad_a = valid * gate_a * (dot_a - mean)
        chosen_grad_b = valid * gate_b * (dot_b - mean)
        number = iota((16, TILE), 0).astype(F32)
        logit_grads = jnp.where(number == first, chosen_grad_a, 0.0) + jnp.where(
            number == second, chosen_grad_b, 0.0
        )
        mixes = []
        for index, (beta, along) in enumerate(((beta_a, along_a), (beta_b, along_b))):
            left, right = share[2 * index], share[2 * index + 1]
            weighted = left * along_x + right * along
            mixes += [
                valid * beta * left * (along_x - weighted),
                valid * beta * right * (along - weighted),
            ]
        small = jnp.concatenate(
            [logit_grads] + mixes + [jnp.zeros((LANES - 20, TILE), F32)], axis=0
        ).T
        high, low = split2(small)
        yield
        inside = iota((TILE, 1), 0) + start < len_ref[0]
        grad = jnp.where(inside, cot_f, 0.0)
        back = back + mm(high, table_high) + mm(low, table_high) + mm(high, table_low)
        back = back + cols[:, KEEP_LANE : KEEP_LANE + 1] * grad
        yield
        hidden = hidden_ref[at]
        scale = lax.rsqrt(jnp.mean(hidden * hidden, axis=-1, keepdims=True) + EPSILON)
        normed = hidden * scale
        back = back * gain_ref[1:2, :]
        back = grad + scale * (back - normed * jnp.mean(back * normed, axis=-1, keepdims=True))
        bh_ref[at] = back
        rounded = back.astype(BF)
        ba_ref[at] = rounded
        yield
        inner = mm_nt(rounded, bcat_ref[0]).astype(BF)
        din_ref[at] = inner
        yield
        bm_ref[at] = (mm_nt(rounded, wo_ref[...]) + mm_nt(inner, acat_ref[...])).astype(BF)

    side_by_side(stages, WIDE_STEP)


def combine_call(
    length, backs, routes, data, cols, cotangent, ei, hidden, gains, weight, acat, bcat, table,
    reader,
):
    tok_count, width = cotangent.shape
    pieces = len(backs)
    return pl.pallas_call(
        functools.partial(combine_body, pieces),
        grid=(tok_count // WIDE_STEP,),
        in_specs=[smem()] + [whole(back.shape) for back in backs] + [
            wide(2, WIDE_STEP), wide(16, WIDE_STEP), tall(LANES, WIDE_STEP), tall(width, WIDE_STEP), tall(width, WIDE_STEP), tall(width, WIDE_STEP),
            whole(gains.shape), whole(weight.shape), whole(acat.shape),
            pl.BlockSpec((1, LANES, width), lambda i: (3, 0, 0)), whole(table.shape),
            whole(reader.shape),
        ],
        out_specs=[tall(width, WIDE_STEP), tall(width, WIDE_STEP), tall(LANES, WIDE_STEP), tall(width, WIDE_STEP)],
        out_shape=[
            shape_of(tok_count, width, dtype=F32), shape_of(tok_count, width),
            shape_of(tok_count, LANES), shape_of(tok_count, width),
        ],
        scratch_shapes=[
            pltpu.VMEM((pieces * CAP, width), BF), pltpu.VMEM((2 * META, pieces * CAP), BF)
        ],
        compiler_params=PARAMS,
        cost_estimate=cost(17),
        name="combine_backward",
    )(
        length, *backs, routes, data, cols, cotangent, ei, hidden, gains, weight, acat, bcat, table,
        reader,
    )


def result_body(pieces, len_ref, *refs):
    result_refs = refs[:pieces]
    cols_ref, ei_ref, hidden_ref, table_ref, out_ref, result_all = refs[pieces:]
    count = result_all.shape[0]

    @pl.when(pl.program_id(0) == 0)
    def _():
        for index in range(count // CAP):
            start = index // pieces * CAP
            result_all[index * CAP : index * CAP + CAP] = result_refs[index % pieces][start : start + CAP]

    table_high, table_low = split2(table_ref[...])

    def stages(at):
        cols = cols_ref[at]
        both = hot(spread(cols, TARGET_LANE, count) | spread(cols, TARGET_LANE + 1, count))
        yield
        half = count // 2
        mixture = mm(both[:, :half], result_all[:half]) + mm(both[:, half:], result_all[half:])
        yield
        high, low = split2(cols)
        mixture = mixture + mm(high, table_high) + mm(low, table_high) + mm(high, table_low)
        mixture = mixture + cols[:, KEEP_LANE : KEEP_LANE + 1] * ei_ref[at].astype(F32)
        yield
        inside = iota((TILE, 1), 0) + pl.program_id(0) * STEP + at.start < len_ref[0]
        out_ref[at] = (hidden_ref[at] + jnp.where(inside, mixture, 0.0)).astype(BF)

    side_by_side(stages)


def result_call(length, results, cols, ei, hidden, table):
    tok_count, width = ei.shape
    pieces = len(results)
    return pl.pallas_call(
        functools.partial(result_body, pieces),
        grid=(tok_count // STEP,),
        in_specs=[smem()] + [whole(result.shape) for result in results] + [
            tall(LANES), tall(width), tall(width), whole(table.shape),
        ],
        out_specs=tall(width),
        out_shape=shape_of(tok_count, width),
        scratch_shapes=[pltpu.VMEM((pieces * results[0].shape[0], width), BF)],
        compiler_params=PARAMS,
        cost_estimate=cost(8),
        name="layer_output",
    )(length, *results, cols, ei, hidden, table)


def last_body(
    dq_ref, dk_ref, dv_ref, w_ref, acat_ref, back_ref, x_ref, bh_ref, gain_ref, out_ref
):
    def stages(at):
        parts = [mm_nt(back_ref[at], acat_ref[...])]
        for index, ref in enumerate((dq_ref, dk_ref, dv_ref)):
            parts.append(mm_nt(ref[at], w_ref[index]))
            yield
        total = parts[0] + parts[1] + parts[2] + parts[3]
        x = x_ref[at].astype(F32)
        scale = lax.rsqrt(jnp.mean(x * x, axis=-1, keepdims=True) + EPSILON)
        normed = x * scale
        back = total * gain_ref[0:1, :]
        back = scale * (back - normed * jnp.mean(back * normed, axis=-1, keepdims=True))
        out_ref[at] = (bh_ref[at] + back).astype(BF)

    side_by_side(stages)


def last_call(dq, dk, dv, weights, acat, back, tokens, bh, gains):
    tok_count, width = tokens.shape
    return pl.pallas_call(
        last_body,
        grid=(tok_count // STEP,),
        in_specs=[
            tall(width), tall(width), tall(width), whole(weights.shape), whole(acat.shape),
            tall(LANES), tall(width), tall(width), whole(gains.shape),
        ],
        out_specs=tall(width),
        out_shape=shape_of(tok_count, width),
        compiler_params=PARAMS,
        cost_estimate=cost(9),
        name="after_attention_backward",
    )(dq, dk, dv, weights, acat, back, tokens, bh, gains)


def exchange(value, axes):
    return lax.all_to_all(value, axes, split_axis=0, concat_axis=0, tiled=True)


def gather_all(value, axes, count):
    return exchange(jnp.broadcast_to(value[None], (count,) + value.shape), axes)


def swap(value, partner, group):
    if partner == 0:
        return value
    return lax.ppermute(value, "expert", [(index, index ^ partner) for index in range(group)])


def find_adapters(id_rows):
    count = id_rows.shape[0]
    padded = id_rows.astype(F32)
    if count % LANES:
        padded = jnp.concatenate([padded, jnp.zeros((-count % LANES, LANES), F32)], axis=0)
    return padded.T[0:1, 0:count].astype(jnp.int32)


def sum_expert_body(each, adapters, in_ref, out_ref):
    count, columns = in_ref.shape[0], out_ref.shape[1]
    found = find_adapters(in_ref[:, columns:])
    place = iota((adapters * each, count), 0)
    column = iota((adapters * each, count), 1)
    pick = hot((place // each == found) & (place % each == column % each))
    out_ref[...] = mm(pick, in_ref[:, 0:columns]).astype(BF)


def exchange_expert_grads(grads, group, owners):
    split = min(RANK, owners)
    each, parts = RANK // split, owners // split
    columns = (grads.shape[1] - LANES) // parts
    pieces = grads.reshape(split, each * group, grads.shape[1])
    if parts > 1:
        ids = jnp.broadcast_to(pieces[:, None, :, parts * columns :], (split, parts, each * group, LANES))
        pieces = pieces[:, :, : parts * columns].reshape(split, each * group, parts, columns)
        pieces = jnp.concatenate([pieces.transpose(0, 2, 1, 3), ids], axis=-1)
        pieces = pieces.reshape(owners, each * group, columns + LANES)
    return exchange(pieces, "dp").reshape(owners * group * each, columns + LANES)


def sum_expert_grads(got, adapters, owners):
    columns = got.shape[1] - LANES
    each = RANK // min(RANK, owners)
    return pl.pallas_call(
        functools.partial(sum_expert_body, each, adapters),
        out_shape=shape_of(adapters * each, columns),
        compiler_params=PARAMS,
        cost_estimate=cost(2.2),
        name="expert_gradient_part",
    )(got)


def finish_expert_body(split, adapters, hidden, in_ref, *refs):
    down_ref, up_ref, out_down_ref, out_up_ref = refs[-4:]
    each = RANK // split
    rows = adapters * each
    count = split * rows
    width = down_ref.shape[0]

    def place(value):
        return value // each % adapters * RANK + value // (adapters * each) * each + value % each

    move = hot(iota((count, count), 0) == place(iota((count, count), 1)))
    back = hot(iota((count, count), 1) == place(iota((count, count), 0)))

    def part(start, size):
        span = pl.ds(pl.multiple_of(start, LANES), size)
        rows_of = [in_ref[owner, :, span] for owner in range(split)]
        return jnp.concatenate(rows_of, axis=0)

    step = pl.program_id(0)
    half, base = hidden // 2, 3 * hidden
    up_ref[...] = mm(move, part(step * hidden, hidden))
    out_down_ref[...] = mm_tn(part(2 * hidden + step * half, half), back)
    out_up_ref[...] = mm(move, part(base + step * (width // 2), width // 2))
    down_ref[...] = mm_tn(part(base + (1 + step) * width, width), back)


def finish_expert_call(index, local, everything, outs, adapters, width, hidden):
    owners, rows, columns = everything.shape
    total = adapters * RANK
    shapes = [(local, 2, width, total), (local, 2, total, hidden), (local, hidden, total),
              (local, total, width)]
    specs = [
        pl.BlockSpec((None, None, width, total), lambda i: (index, i, 0, 0)),
        pl.BlockSpec((None, None, total, hidden), lambda i: (index, i, 0, 0)),
        pl.BlockSpec((None, hidden // 2, total), lambda i: (index, i, 0)),
        pl.BlockSpec((None, total, width // 2), lambda i: (index, 0, i)),
    ]
    return pl.pallas_call(
        functools.partial(finish_expert_body, owners, adapters, hidden),
        grid=(2,),
        in_specs=[whole(everything.shape)] + [pl.BlockSpec(memory_space=pl.ANY)] * len(outs),
        out_specs=specs,
        out_shape=[shape_of(*shape, dtype=F32) for shape in shapes],
        input_output_aliases={1 + place: place for place in range(len(outs))},
        compiler_params=PARAMS,
        cost_estimate=cost(4),
        name="expert_gradient_sums",
    )(everything, *outs)


def spread_expert_grads(own, adapters, owners):
    split = min(RANK, owners)
    each, parts = RANK // split, owners // split
    everything = gather_all(own, "dp", owners)
    everything = everything.reshape(split, parts, adapters, each, own.shape[1])
    everything = everything.transpose(2, 0, 3, 1, 4)
    return everything.reshape(adapters * RANK, parts * own.shape[1]).astype(F32)


def expert_sums(owned, adapters, owners, width, hidden):
    sums = [spread_expert_grads(value, adapters, owners) for value in owned]
    base = 3 * hidden
    up = [[value[:, 0:hidden], value[:, hidden : 2 * hidden]] for value in sums]
    down = [
        [value[:, base + width * part : base + width * (part + 1)].T for part in (1, 2)]
        for value in sums
    ]
    return (
        jnp.stack([jnp.stack(value) for value in down]),
        jnp.stack([jnp.stack(value) for value in up]),
        jnp.stack([value[:, 2 * hidden : base].T for value in sums]),
        jnp.stack([value[:, base : base + width] for value in sums]),
    )


def finish_adapter_body(adapters, me_ref, *refs):
    piece_refs, (down_ref, up_ref, in_ref) = refs[:-3], refs[-3:]
    half = in_ref.shape[3]
    owners, group = piece_refs[0].shape[0], len(piece_refs)
    for other in range(group):
        place = jnp.bitwise_xor(me_ref[0], other)
        for owner in range(owners):
            in_ref[owner * (group // 2) + place // 2, place % 2] = piece_refs[other][owner]
    count = RANK * adapters

    def place(value):
        return value % adapters * RANK + value // adapters

    move = hot(iota((count, count), 0) == place(iota((count, count), 1)))
    back = hot(iota((count, count), 1) == place(iota((count, count), 0)))
    for part in range(2):
        span = slice(part * half, part * half + half)
        for kind in range(2):
            for index in range(4):
                first = (kind * 4 + index) * adapters
                rows = in_ref[:, part, first : first + adapters, :].astype(F32)
                rows = rows.reshape(count, half).astype(BF)
                if kind == 0:
                    down_ref[index, span, :] = mm_tn(rows, back)
                else:
                    up_ref[index, :, span] = mm(move, rows)


def sum_adapter_body(kinds, adapters, in_ref, out_ref):
    count, columns = in_ref.shape[0], out_ref.shape[-1]
    found = find_adapters(in_ref[:, columns:])
    place = iota((adapters * kinds, count), 0)
    column = iota((adapters * kinds, count), 1)
    pick = hot((place % adapters == found) & (place // adapters == column % kinds))
    own = mm(pick, in_ref[:, 0:columns]).astype(BF)
    for index in range(out_ref.shape[0]):
        out_ref[index] = own


def adapter_sums(grads, meanwhile, later, finish, parts, ids, adapters, owners, group, width):
    axes, everyone = ("dp", "expert"), owners * group
    if everyone == 2 * RANK and group == 4:
        kinds = 8
        got = exchange(grads.reshape(everyone, kinds, grads.shape[1]), axes)
        got, meanwhile = lax.optimization_barrier((got, meanwhile))
        own = pl.pallas_call(
            functools.partial(sum_adapter_body, kinds, adapters),
            out_shape=shape_of(owners, kinds * adapters, width // 2),
            compiler_params=PARAMS,
            cost_estimate=cost(2.0),
            name="adapter_gradient_part",
        )(got.reshape(everyone * kinds, grads.shape[1]))
        mine = exchange(own, "dp")
        mine, later = lax.optimization_barrier((mine, later))
        across = swap(mine, 2, group)
        full = [mine, swap(mine, 1, group), across, swap(across, 1, group)]
        total = adapters * RANK
        down, upper = pl.pallas_call(
            functools.partial(finish_adapter_body, adapters),
            in_specs=[smem()] + [pl.BlockSpec(memory_space=pltpu.VMEM)] * group,
            out_shape=[shape_of(4, width, total, dtype=F32), shape_of(4, total, width, dtype=F32)],
            scratch_shapes=[pltpu.VMEM((RANK, 2, kinds * adapters, width // 2), BF)],
            compiler_params=PARAMS,
            cost_estimate=cost(3.6),
            name="adapter_gradient_sums",
        )(lax.axis_index("expert").reshape(1).astype(jnp.int32), *full)
        (down, upper), later, parts = lax.optimization_barrier(((down, upper), later, parts))
        return down, upper, meanwhile, finish(later, parts)
    later = finish(later, parts)
    all_ids = exchange(jnp.broadcast_to(ids, (everyone,)), axes)
    pieces = grads.reshape(everyone, RANK * 4 * 2 * width // everyone)
    got = exchange(pieces, axes)
    pick = (jnp.arange(adapters, dtype=jnp.int32)[:, None] == all_ids[None, :]).astype(BF)
    own = jnp.dot(pick, got, preferred_element_type=F32).astype(BF)
    full = gather_all(own, axes, everyone)
    full = full.reshape(RANK, everyone // RANK, adapters, -1).transpose(2, 0, 1, 3)
    full = full.reshape(adapters * RANK, 4, 2, width).astype(F32)
    return full[:, :, 0].transpose(1, 2, 0), full[:, :, 1].transpose(1, 0, 2), meanwhile, later


def body(
    tokens,
    cotangent,
    lengths,
    adapter_ids,
    routes,
    prev_logits,
    norm_gains,
    input_weights,
    output_weight,
    adapter_down,
    adapter_up,
    router,
    residual_mix,
    constant_mix,
    constant_vectors,
    expert_gate,
    expert_up,
    expert_down,
    expert_adapter_down,
    expert_adapter_up,
    output_adapter_down,
    output_adapter_up,
):
    tok_count, width = tokens.shape
    hidden_width = expert_gate.shape[2]
    group, owners = lax.axis_size("expert"), lax.axis_size("dp")
    local = expert_gate.shape[0]
    adapters = adapter_down.shape[-1] // RANK
    angles = [jnp.asarray(table) for table in turn_tables(tok_count)]
    weights = (
        expert_gate, expert_up, expert_down, expert_adapter_down, expert_adapter_up,
        output_adapter_down, output_adapter_up,
    )
    per_owner = RANK // min(RANK, owners)
    everyone = owners * group
    me = lax.axis_index("expert")

    me = me.reshape(1).astype(jnp.int32)

    routes, prev_logits = routes.T, prev_logits.T
    slots, *grad_sends = route_call(local, group, lengths, me, routes, cotangent)
    cots = [swap(value, partner, group) for partner, value in enumerate(grad_sends)]
    normed, inner, acat, bcat, table, mixer, reader, keys, values, mixed, q2 = pre_attend_call(
        lengths, adapter_ids, tokens, norm_gains, input_weights, adapter_down, adapter_up, *angles,
        router.T, constant_mix.T, constant_vectors, residual_mix,
    )
    hidden, ei, inner_o, data, cols, *sends = post_call(
        local, group, me, adapter_ids, mixed, tokens, output_weight, acat, bcat, norm_gains, reader, mixer, prev_logits,
        routes, slots,
    )
    sends, cots = lax.optimization_barrier((sends, cots))
    near, far = tuple(range(group // 2)), tuple(range(group // 2, group))
    sent_near = [swap(sends[partner], partner, group) for partner in near]
    sent_far = []
    for index in range(local):
        pieces = [sends[group // 2 + place * local + index] for place in range(len(far))]
        if index > 0:
            pieces, sent_near = lax.optimization_barrier((pieces, sent_near))
        sent_far.append([swap(piece, partner, group) for piece, partner in zip(pieces, far)])
    backs = [[None] * group for _ in range(local)]
    results = [None] * group
    calls = []
    for index in range(local - 1):
        calls += [(index, near), (index, far)]
    calls += [(local - 1, near[1:] + far), (local - 1, near[:1])]
    grads, owned, parts = [None] * local, [], []
    sums = functools.partial(sum_expert_grads, adapters=adapters, owners=owners)
    last = None
    for index, some in calls:
        pieces = [
            sent_near[partner] if partner in near else sent_far[index][partner - len(near)]
            for partner in some
        ]
        if last is not None:
            pieces, last = lax.optimization_barrier((pieces, last))
        if (index, some) == calls[-1]:
            parts, last = lax.optimization_barrier((parts, last))
            owned = [sums(part) for part in parts]
            pieces, backs[:index], owned = lax.optimization_barrier((pieces, backs[:index], owned))
        outs = expert_call(
            index, some, group, per_owner, pieces, [cots[partner] for partner in some], grads[index],
            [results[partner] for partner in some] if index else [], weights,
        )
        grads[index] = last = outs[-1]
        for place, partner in enumerate(some):
            backs[index][partner] = swap(outs[place], partner, group)
            results[partner] = outs[len(some) + place]
        if index < local - 1 and some == far:
            parts.append(exchange_expert_grads(last, group, owners))
    backs = [value for some in backs for value in some]
    parts.append(exchange_expert_grads(last, group, owners))
    gather = functools.partial(lax.all_gather, axis_name="dp", axis=0, tiled=False)
    if owners <= RANK:
        owned = [gather(own) for own in owned]
    back_hidden, back_attention, back_inner_o, back_mixed = combine_call(
        lengths, backs, routes, data, cols, cotangent, ei, hidden, norm_gains, output_weight, acat, bcat,
        table, reader,
    )
    flat, back_mixed = lax.optimization_barrier((results, back_mixed))
    flat = [swap(value, partner, group) for partner, value in enumerate(flat)]

    packed = everyone == 2 * RANK and group == 4
    dq, dk, dv, back_inner, adapter_grads = attend_back_call(
        packed, lengths, adapter_ids, q2, keys, values, mixed, back_mixed, *angles, bcat, inner, inner_o,
        back_inner_o, back_attention, normed,
    )
    parts[-1], adapter_grads, flat, owned = lax.optimization_barrier(
        (parts[-1], adapter_grads, flat, owned)
    )
    own = sums(parts[-1])
    adapter_grads, own, flat = lax.optimization_barrier((adapter_grads, own, flat))
    owned.append(gather(own) if owners <= RANK else own)
    layer_out = result_call(lengths, flat, cols, ei, hidden, table)
    input_back = last_call(
        dq, dk, dv, input_weights, acat, back_inner, tokens, back_hidden, norm_gains
    )
    outs = []
    if owners <= RANK:
        for index, own in enumerate(owned[:-1]):
            outs = finish_expert_call(index, local, own, outs, adapters, width, hidden_width)
    def finish(later, part):
        input_back, outs = later
        if owners <= RANK:
            return input_back, finish_expert_call(
                local - 1, local, part, outs, adapters, width, hidden_width
            )
        return input_back, expert_sums(owned, adapters, owners, width, hidden_width)

    down_sum, upper_sum, layer_out, (input_back, outs) = adapter_sums(
        adapter_grads, layer_out, (input_back, outs), finish, owned[-1], adapter_ids, adapters, owners, group, width
    )
    in_down_sum, in_up_sum, out_down_sum, out_up_sum = outs
    return (
        layer_out,
        input_back,
        down_sum,
        upper_sum,
        in_down_sum,
        in_up_sum,
        out_down_sum,
        out_up_sum,
    )


def solution(mesh):
    tokens_spec, copied = P(("dp", "expert"), None), P()
    owned = P("expert")
    placed = (
        (tokens_spec, tokens_spec, P(("dp", "expert")), P(("dp", "expert")), tokens_spec, tokens_spec)
        + (copied,) * 9
        + (owned,) * 7
    )
    return jax.shard_map(
        body,
        mesh=mesh,
        in_specs=placed,
        out_specs=(tokens_spec, tokens_spec, copied, copied) + (owned,) * 4,
        check_vma=False,
    )
```

```python
import functools
import math

import jax
import jax.numpy as jnp
import numpy as np
from jax import lax
from jax.experimental import pallas as pl
from jax.experimental.pallas import tpu as pltpu
from jax.sharding import PartitionSpec as P

HEADS = 12
HD = 64
EXPERTS = 8
RANK = 16
CAP = 192
EPSILON = 1e-06
F32 = jnp.float32
BF = jnp.bfloat16
NEG = -1e30
LANES = 128
TILE = 256
STEP = 512
WIDE_STEP = 1024
FTILE = 512
PAIRS = HEADS // 2
AHEAD = 1
PARAMS = pltpu.CompilerParams(vmem_limit_bytes=67043328)
META = 8
MIX_ROW = 16
VECTOR_ROW = 20
TARGET_LANE = 24
KEEP_LANE = 26
READ_VECTOR = 48
READ_ROWS = 64
PIECE = CAP + META


def mm(left, right):
    return jnp.dot(left, right, preferred_element_type=F32)


def mm_nt(left, right):
    return lax.dot_general(left, right, (((1,), (1,)), ((), ())), preferred_element_type=F32)


def mm_tn(left, right):
    return lax.dot_general(left, right, (((0,), (0,)), ((), ())), preferred_element_type=F32)


def iota(shape, axis):
    return lax.broadcasted_iota(jnp.int32, shape, axis)


def hot(condition):
    return jnp.where(condition, 1.0, 0.0).astype(BF)


def split2(value):
    high = value.astype(BF)
    return high, (value - high.astype(F32)).astype(BF)


def split3(value):
    high = value.astype(BF)
    rest = value - high.astype(F32)
    middle = rest.astype(BF)
    return high, middle, (rest - middle.astype(F32)).astype(BF)


def whole(shape):
    zeros = (0,) * len(shape)
    return pl.BlockSpec(shape, lambda *_: zeros)


def smem():
    return pl.BlockSpec(memory_space=pltpu.SMEM)


def tall(width, step=STEP):
    return pl.BlockSpec((step, width), lambda i: (i, 0))


def wide(height, step=STEP):
    return pl.BlockSpec((height, step), lambda i: (0, i))


def tile(width):
    return pl.BlockSpec((TILE, width), lambda i: (i, 0))


def side_by_side(stages, step=STEP):
    running = [stages(slice(start, start + TILE)) for start in range(0, step, TILE)]
    while running:
        running = [stage for stage in running if next(stage, True) is None]


def shape_of(*shape, dtype=BF):
    return jax.ShapeDtypeStruct(shape, dtype)


def cost(microseconds):
    return pl.CostEstimate(flops=int(microseconds * 1e+09), bytes_accessed=0, transcendentals=0)


@functools.lru_cache(maxsize=None)
def turn_tables(length_in):
    half = HD // 2
    inverse = np.exp(np.arange(half, dtype=np.float64) * (-2.0 * math.log(10000.0) / HD))

    def table(positions):
        angles = np.tile(positions[:, None] * inverse[None, :], (1, 4))
        return np.stack([np.cos(angles), np.sin(angles)]).astype(np.float32)

    return table(np.arange(0.0, length_in, 32)), table(np.arange(0.0, 32))


def turn_rows(coarse_ref, fine_ref, first, count):
    fine_cos, fine_sin = fine_ref[0], fine_ref[1]
    sign = jnp.where(iota((32, LANES), 1) % HD < HD // 2, -1.0, 1.0)
    signed_cos, signed_sin = fine_cos * sign, fine_sin * sign
    cosines, sines = [], []
    for index in range(count // 32):
        row = first // 32 + index
        coarse_cos, coarse_sin = coarse_ref[0, pl.ds(row, 1), :], coarse_ref[1, pl.ds(row, 1), :]
        cosines.append(coarse_cos * fine_cos - coarse_sin * fine_sin)
        sines.append(coarse_sin * signed_cos + coarse_cos * signed_sin)
    return jnp.concatenate(cosines, axis=0), jnp.concatenate(sines, axis=0)


def rope(value, cosine, sine):
    first = iota(value.shape, 1) % HD < HD // 2
    turned = jnp.where(first, pltpu.roll(value, LANES - HD // 2, 1), pltpu.roll(value, HD // 2, 1))
    return value * cosine + turned * sine


def find_slots(length, routes_ref, slot_ref):
    tok_count = slot_ref.shape[1]
    before = hot(iota((TILE, TILE), 0) < iota((TILE, TILE), 1))
    carry = jnp.zeros((2 * EXPERTS, 1), F32)
    for start in range(0, tok_count, TILE):
        span = slice(start, start + TILE)
        expert = iota((2 * EXPERTS, TILE), 0)
        token = iota((2 * EXPERTS, TILE), 1) + start
        named = (routes_ref[0:1, span] == expert) | (routes_ref[1:2, span] == expert)
        hit = named & (token < length) & (expert < EXPERTS)
        hits = jnp.where(hit, 1.0, 0.0)
        slots = mm(hits.astype(BF), before) + carry
        carry = carry + jnp.sum(hits, axis=1, keepdims=True)
        slot_ref[:, span] = jnp.where(hit, slots, -1.0)[:EXPERTS].astype(jnp.int32)


def pick_rows(slot_ref, step, me, local):
    first = jnp.bitwise_xor(step, me) * local
    place = iota((CAP, slot_ref.shape[1]), 0)
    return first, [hot(place == slot_ref[pl.ds(first + index, 1), :]) for index in range(local)]


def pick_source(chosen, source_ref):
    half = source_ref.shape[0] // 2
    return mm(chosen[:, :half], source_ref[:half]) + mm(chosen[:, half:], source_ref[half:])


def store_piece(out_refs, step, other, index, value, start):
    @pl.when(step == other)
    def _():
        out_refs[index][start : start + value.shape[0], :] = value


def route_body(local, group, len_ref, me_ref, routes_ref, source_ref, slot_ref, *out_refs):
    step = pl.program_id(0)

    @pl.when(step == 0)
    def _():
        find_slots(len_ref[0], routes_ref, slot_ref)

    _, chosen = pick_rows(slot_ref, step, me_ref[0], local)
    rows = pick_source(jnp.concatenate(chosen, axis=0), source_ref).astype(BF)
    for other in range(group):
        store_piece(out_refs, step, other, other, rows, 0)


def route_call(local, group, length, me, routes, source):
    tok_count, width = source.shape
    return pl.pallas_call(
        functools.partial(route_body, local, group),
        grid=(group,),
        in_specs=[smem(), smem(), whole(routes.shape), whole(source.shape)],
        out_specs=[whole((EXPERTS, tok_count))] + [whole((local * CAP, width))] * group,
        out_shape=[shape_of(EXPERTS, tok_count, dtype=jnp.int32)]
        + [shape_of(local * CAP, width)] * group,
        compiler_params=PARAMS,
        cost_estimate=cost(6.5),
        name="route_rows",
    )(length, me, routes, source)


def send_rows(local, group, partner, me_ref, id_ref, slot_ref, data_ref, source_ref, out_refs):
    width = source_ref.shape[1]
    first, chosen = pick_rows(slot_ref, partner, me_ref[0], local)
    rows = pick_source(jnp.concatenate(chosen, axis=0), source_ref).astype(BF)
    for index in range(local):
        pieces = split3(data_ref[pl.ds(first + index, 1), :])
        stack = jnp.concatenate(
            [piece.astype(F32) for piece in pieces]
            + [jnp.zeros((13, chosen[index].shape[1]), F32)],
            axis=0,
        ).astype(BF)
        gates = mm_nt(stack, chosen[index])[0:META]
        gates = jnp.where(iota(gates.shape, 0) == 3, id_ref[0].astype(F32), gates)
        meta = jnp.concatenate([gates, jnp.zeros((META, width - CAP), F32)], axis=1)
        kept = rows[index * CAP : index * CAP + CAP]
        for other in range(group):
            far = other >= group // 2
            place = group // 2 + (other - group // 2) * local + index if far else other
            start = 0 if far else index * PIECE
            store_piece(out_refs, partner, other, place, kept, start)
            store_piece(out_refs, partner, other, place, meta.astype(BF), start + CAP)


def pre_body(
    id_ref, x_ref, gain_ref, w_ref, ad_ref, au_ref, coarse_ref, fine_ref, router_ref, cmix_ref, vec_ref,
    resid_ref, normed_ref, inner_ref, acat_ref, bcat_ref, table_ref, mix_ref, read_ref, q_ref, k_ref,
    v_ref, square_ref,
):
    @pl.when(pl.program_id(0) == 0)
    def _():
        first = RANK * id_ref[0]
        total = None
        for index in range(4):
            row, column = iota((LANES, LANES), 0), iota((LANES, LANES), 1)
            place = hot((row >= first) & (row < first + RANK) & (column == (row - first) * 4 + index))
            part = mm(ad_ref[index], place)
            total = part if total is None else total + part
            place = hot(
                (column >= first) & (column < first + RANK) & (row == (column - first) * 4 + index)
            )
            bcat_ref[index] = mm(place, au_ref[index]).astype(BF)
        acat_ref[...] = total.astype(BF)
        table_ref[...] = jnp.zeros_like(table_ref)
        table_ref[0 : EXPERTS + 4, :] = router_ref[...].astype(F32)
        table_ref[MIX_ROW : MIX_ROW + 4, :] = cmix_ref[...]
        table_ref[VECTOR_ROW : VECTOR_ROW + 2, :] = vec_ref[...]
        read_ref[...] = jnp.zeros_like(read_ref)
        read_ref[0 : EXPERTS + 4, :] = router_ref[...].astype(F32)
        for place, piece in enumerate(split3(cmix_ref[...])):
            read_ref[16 + 8 * place : 20 + 8 * place, :] = piece.astype(F32)
        for place, piece in enumerate(split3(vec_ref[...])):
            read_ref[READ_VECTOR + 2 * place : READ_VECTOR + 2 * place + 2, :] = piece.astype(F32)
        square_ref[...] = jnp.zeros_like(square_ref)
        square_ref[0 : EXPERTS + 4, 0 : EXPERTS + 4] = resid_ref[...]
        mix_ref[...] = square_ref[...].T[0:16]

    def stages(at):
        x = x_ref[at].astype(F32)
        scale = lax.rsqrt(jnp.mean(x * x, axis=-1, keepdims=True) + EPSILON)
        normed = (x * scale * gain_ref[0:1, :]).astype(BF)
        normed_ref[at] = normed
        yield
        inner = mm(normed, acat_ref[...]).astype(BF)
        inner_ref[at] = inner
        yield
        for index, out_ref in enumerate((q_ref, k_ref, v_ref)):
            value = mm(normed, w_ref[index]) + mm(inner, bcat_ref[index])
            yield
            rows = pl.ds(pl.multiple_of(pl.program_id(0) * STEP + at.start, TILE), TILE)
            if index == 2:
                for pair in range(PAIRS):
                    span = slice(pair * LANES, pair * LANES + LANES)
                    out_ref[pair, rows] = value[:, span].astype(BF)
                continue
            cosine, sine = turn_rows(coarse_ref, fine_ref, pl.program_id(0) * STEP + at.start, TILE)
            for pair in range(PAIRS):
                span = slice(pair * LANES, pair * LANES + LANES)
                turned = rope(value[:, span], cosine, sine).astype(BF)
                if index == 0:
                    turned = (turned.astype(F32) * HD**-0.5).astype(BF)
                out_ref[pair, rows] = turned
            yield

    side_by_side(stages)


def attend_body(len_ref, q_ref, k_ref, v_ref, mixed_ref, q2_ref):
    tok_count = q_ref.shape[0]
    lane = iota((tok_count, LANES), 1)
    hidden_key = iota((tok_count, LANES), 0) >= len_ref[0]
    row = iota((LANES, tok_count), 0)
    row_tile = row[:, :TILE]
    causal = iota((TILE, TILE), 0) <= iota((TILE, TILE), 1)
    queries_t = q_ref[...].astype(F32).T
    values_t = v_ref[...].astype(F32).T
    keys = k_ref[...].astype(F32)
    heads = []
    for head in range(2):
        spare = HD * (1 - head)
        bias = jnp.where((lane == spare) & hidden_key, NEG, 0.0)
        one = jnp.where(row == spare, 1.0, 0.0)
        own = row // HD == head
        heads.append(
            (
                jnp.where(lane // HD == head, keys, bias).astype(BF),
                jnp.where(own, queries_t, one).astype(BF),
                jnp.where(own, values_t, one).astype(BF),
            )
        )
    units = [(start, head) for start in range(0, tok_count, TILE) for head in range(2)]

    def score(unit):
        start, head = unit
        keys, queries, _ = heads[head]
        part = queries[:, start : start + TILE]
        near = mm(keys[start : start + TILE], part)
        return near, mm(keys[:start], part) if start else None

    outs = {}
    waiting = [score(unit) for unit in units[:3]]
    for index, (start, head) in enumerate(units):
        near, far = waiting.pop(0)
        if index + 3 < len(units):
            waiting.append(score(units[index + 3]))
        spare = HD * (1 - head)
        _, queries, values = heads[head]
        near = jnp.where(causal, near, NEG)
        top = jnp.max(near, axis=0, keepdims=True)
        if start:
            top = jnp.maximum(top, jnp.max(far, axis=0, keepdims=True))
        mixed = mm(values[:, start : start + TILE], jnp.exp(near - top).astype(BF))
        if start:
            mixed = mixed + mm(values[:, :start], jnp.exp(far - top).astype(BF))
        total = mixed[spare : spare + 1]
        outs[head] = mixed * (1.0 / total)
        kept = queries[:, start : start + TILE]
        logs = jnp.zeros((LANES, TILE), F32)
        for offset, piece in enumerate(split3(top + jnp.log(total))):
            logs = jnp.where(row_tile == spare + 1 + offset, piece.astype(F32), logs)
        q2_ref[head * LANES : head * LANES + LANES, start : start + TILE] = kept + logs.astype(BF)
        if head == 1:
            mixed = jnp.where(row_tile < HD, outs[0], outs[1])
            mixed_ref[start : start + TILE] = mixed.T.astype(BF)


def pre_attend_body(steps, len_ref, *refs):
    pre_ins, pre_outs = refs[:12], refs[12:19]
    key_ref, value_ref, mixed_ref, q2_ref, q_all, k_all, v_all, square_ref = refs[19:]
    step = pl.program_id(0)

    @pl.when(step < steps)
    def _():
        pre_body(*pre_ins, *pre_outs, q_all, k_all, v_all, square_ref)

    @pl.when(step >= steps)
    def _():
        pair = step - steps
        key_ref[...] = k_all[pair]
        value_ref[...] = v_all[pair]
        attend_body(len_ref, q_all.at[pair], k_all.at[pair], v_all.at[pair], mixed_ref, q2_ref)


def pre_attend_call(
    length, ids, tokens, gains, weights, down, upper, coarse, fine, router, constant_mix, vectors,
    residual_mix,
):
    tok_count, width = tokens.shape
    steps = tok_count // STEP

    def rows_of(columns):
        return pl.BlockSpec((STEP, columns), lambda i: (jnp.minimum(i, steps - 1), 0))

    column = pl.BlockSpec((tok_count, LANES), lambda i: (0, jnp.maximum(i - steps, 0)))
    return pl.pallas_call(
        functools.partial(pre_attend_body, steps),
        grid=(steps + PAIRS,),
        in_specs=[
            smem(), smem(), rows_of(width), whole(gains.shape), whole(weights.shape), whole(down.shape),
            whole(upper.shape), whole(coarse.shape), whole(fine.shape), whole(router.shape),
            whole(constant_mix.shape), whole(vectors.shape), whole(residual_mix.shape),
        ],
        out_specs=[
            rows_of(width), rows_of(LANES), whole((width, LANES)), whole(upper.shape),
            whole((LANES, width)), whole((16, LANES)), whole((READ_ROWS, width)), column, column,
            column, pl.BlockSpec((2 * LANES, tok_count), lambda i: (jnp.maximum(i - steps, 0), 0)),
        ],
        out_shape=[
            shape_of(tok_count, width), shape_of(tok_count, LANES), shape_of(width, LANES),
            shape_of(*upper.shape), shape_of(LANES, width, dtype=F32), shape_of(16, LANES, dtype=F32),
            shape_of(READ_ROWS, width, dtype=F32), shape_of(tok_count, width),
            shape_of(tok_count, width), shape_of(tok_count, width), shape_of(2 * width, tok_count),
        ],
        scratch_shapes=[pltpu.VMEM((PAIRS, tok_count, LANES), BF)] * 3
        + [pltpu.VMEM((LANES, LANES), F32)],
        compiler_params=PARAMS,
        cost_estimate=cost(25),
        name="attention_forward",
    )(
        length, ids, tokens, gains, weights, down, upper, coarse, fine, router, constant_mix, vectors,
        residual_mix,
    )


def attend_back_body(
    len_ref, q2_ref, k_ref, v_ref, mixed_ref, back_ref, coarse_ref, fine_ref,
    dq_ref, dk_ref, dv_ref, acc_ref, turn_ref,
):
    tok_count = k_ref.shape[0]

    @pl.when(pl.program_id(0) == 0)
    def _():
        turn_ref[0], turn_ref[1] = turn_rows(coarse_ref, fine_ref, 0, tok_count)

    lane = iota((tok_count, LANES), 1)
    position = iota((tok_count, LANES), 0)
    bias = jnp.where(position < len_ref[0], 0.0, NEG)
    causal = iota((TILE, TILE), 0) <= iota((TILE, TILE), 1)
    row = iota((LANES, tok_count), 0)
    back = back_ref[...].astype(F32)
    product_t = (back * mixed_ref[...].astype(F32)).T
    back_t = back.T
    keys, values = k_ref[...].astype(F32), v_ref[...].astype(F32)
    heads = []
    for head in range(2):
        own = lane // HD == head
        spare = HD * (1 - head)
        minus = jnp.where((lane > spare) & (lane < spare + 4), -1.0, 0.0)
        q2 = q2_ref[head * LANES : head * LANES + LANES, :]
        k2f = jnp.where(own, keys, jnp.where(lane == spare, bias, minus))
        k2 = k2f.astype(BF)
        k2t = k2f.T.astype(BF)
        v2 = jnp.where(own, values, minus).astype(BF)
        own_row = row // HD == head
        delta = jnp.sum(jnp.where(own_row, product_t, 0.0), axis=0, keepdims=True)
        back2 = jnp.where(own_row, back_t, 0.0)
        for offset, piece in enumerate(split3(delta)):
            back2 = jnp.where(row == spare + 1 + offset, piece.astype(F32), back2)
        back2 = back2.astype(BF)
        heads.append((k2, k2t, v2, q2, back2))
    units = [(start, head) for start in range(0, tok_count, TILE) for head in range(2)]

    def score(unit):
        start, head = unit
        k2, _, v2, q2, back2 = heads[head]
        stop = start + TILE
        return mm(k2[start:stop], q2[:, start:]), mm(v2[start:stop], back2[:, start:])

    grads = [([], []), ([], [])]
    waiting = [score(unit) for unit in units[:AHEAD]]
    for index, (start, head) in enumerate(units):
        scores, slopes = waiting.pop(0)
        if index + AHEAD < len(units):
            waiting.append(score(units[index + AHEAD]))
        _, k2t, _, q2, back2 = heads[head]
        stop = start + TILE
        diagonal = jnp.where(causal, scores[:, :TILE], NEG)
        if stop < tok_count:
            diagonal = jnp.concatenate([diagonal, scores[:, TILE:]], axis=1)
        weights = jnp.exp(diagonal)
        turned = (weights * slopes).astype(BF)
        grads[head][1].append(mm_nt(weights.astype(BF), back2[:, start:]))
        grads[head][0].append(mm_nt(turned, q2[:, start:]))
        update = mm(k2t[:, start:stop], turned)
        if start == 0:
            acc_ref[head] = update
        else:
            acc_ref[head, :, start:] += update
    grads = [
        (jnp.concatenate(keys, axis=0), jnp.concatenate(values, axis=0)) for keys, values in grads
    ]
    low_lane = lane < HD
    cosine, sine = turn_ref[0], -turn_ref[1]
    dq = jnp.where(row < HD, acc_ref[0], acc_ref[1]).T * HD**-0.5
    dq_ref[...] = rope(dq, cosine, sine).astype(BF)
    dk = jnp.where(low_lane, grads[0][0], grads[1][0])
    dk_ref[...] = rope(dk, cosine, sine).astype(BF)
    dv_ref[...] = jnp.where(low_lane, grads[0][1], grads[1][1]).astype(BF)


def pack_grads(packed, id_ref, acc_ref, grad_ref):
    count, width = acc_ref.shape[0], acc_ref.shape[1] // 2
    if not packed:
        grad_ref[...] = acc_ref[...].astype(BF)
        return
    half = width // 2
    shape = (16 * RANK, count)
    place, row = iota(shape, 0), iota(shape, 1)
    total = None
    for index in range(4):
        kind, part = index // 2, index % 2
        here = (place % 4 == row % 4) & (place // 16 == row // 4)
        here = here & (place // 8 % 2 == part) & (place // 4 % 2 == kind)
        start = kind * width + part * half
        piece = mm(hot(here), acc_ref[:, start : start + half].astype(BF))
        total = piece if total is None else total + piece
    grad_ref[:, 0:half] = total.astype(BF)
    grad_ref[:, half:] = jnp.full((16 * RANK, LANES), id_ref[0].astype(F32), F32).astype(BF)


def attend_back_all_body(packed, len_ref, id_ref, *refs):
    ins, refs = refs[:7], refs[7:]
    bcat_ref, inner_ref, inner_o_ref, din_ref, ba_ref, normed_hbm, mixed_hbm = refs[:7]
    dq_ref, dk_ref, dv_ref, back_ref, grad_ref = refs[7:12]
    scratch, (inner_all, back_all, acc_ref, normed_all, mixed_all, sems) = refs[12:14], refs[14:]
    step = pl.program_id(0)
    count = inner_all.shape[1]
    width = normed_all.shape[1]
    copies = [
        pltpu.make_async_copy(normed_hbm, normed_all, sems.at[0]),
        pltpu.make_async_copy(mixed_hbm, mixed_all, sems.at[1]),
    ]

    @pl.when(step == 0)
    def _():
        for copy in copies:
            copy.start()
        inner_all[0] = inner_ref[...].astype(F32).T[0:count].astype(BF)
        inner_all[1] = inner_o_ref[...].astype(F32).T[0:count].astype(BF)
        back_all[...] = jnp.zeros_like(back_all)

    @pl.when(step < PAIRS)
    def _():
        attend_back_body(len_ref, *ins, dq_ref, dk_ref, dv_ref, *scratch)
        number = iota((count, LANES), 0) % 4
        upper = mm(inner_all[1], ba_ref[...])
        total = back_all[...]
        for index, ref in enumerate((dq_ref, dk_ref, dv_ref)):
            value = ref[...]
            upper = jnp.where(number == index, mm(inner_all[0], value), upper)
            total = total + mm_nt(value, bcat_ref[index])
        back_all[...] = total
        at = width + step * LANES
        acc_ref[:, pl.ds(pl.multiple_of(at, LANES), LANES)] = upper

    @pl.when(step == PAIRS)
    def _():
        back = back_all[...].astype(BF)
        back_ref[...] = back
        back_t = (back.astype(F32) + din_ref[...].astype(F32)).T[0:count].astype(BF)
        for copy in copies:
            copy.wait()
        number = iota((count, width), 0) % 4
        half = back_t.shape[1] // 2

        def down(rows_ref):
            return mm(back_t[:, :half], rows_ref[:half]) + mm(back_t[:, half:], rows_ref[half:])

        acc_ref[:, 0:width] = jnp.where(number < 3, down(normed_all), down(mixed_all))
        pack_grads(packed, id_ref, acc_ref, grad_ref)


def attend_back_call(
    packed, length, ids, q2, keys, values, mixed, back, coarse, fine, bcat, inner, inner_o, din, ba,
    normed,
):
    tok_count, width = keys.shape
    column = pl.BlockSpec((tok_count, LANES), lambda i: (0, jnp.minimum(i, PAIRS - 1)))
    grad_shape = (16 * RANK, width // 2 + LANES) if packed else (4 * RANK, 2 * width)
    return pl.pallas_call(
        functools.partial(attend_back_all_body, packed),
        grid=(PAIRS + 1,),
        in_specs=[
            smem(), smem(),
            pl.BlockSpec((2 * LANES, tok_count), lambda i: (jnp.minimum(i, PAIRS - 1), 0)), column,
            column, column, column, whole(coarse.shape), whole(fine.shape),
            pl.BlockSpec((4, LANES, LANES), lambda i: (0, 0, jnp.minimum(i, PAIRS - 1))),
            whole(inner.shape), whole(inner_o.shape), whole(din.shape), column,
            pl.BlockSpec(memory_space=pl.ANY), pl.BlockSpec(memory_space=pl.ANY),
        ],
        out_specs=[column] * 3 + [whole((tok_count, LANES)), whole(grad_shape)],
        out_shape=[shape_of(tok_count, width)] * 3
        + [shape_of(tok_count, LANES), shape_of(*grad_shape)],
        scratch_shapes=[
            pltpu.VMEM((2, LANES, tok_count), F32), pltpu.VMEM((2, tok_count, LANES), F32),
            pltpu.VMEM((2, 4 * RANK, tok_count), BF), pltpu.VMEM((tok_count, LANES), F32),
            pltpu.VMEM((4 * RANK, 2 * width), F32), pltpu.VMEM((tok_count, width), BF),
            pltpu.VMEM((tok_count, width), BF), pltpu.SemaphoreType.DMA((2,)),
        ],
        compiler_params=PARAMS,
        cost_estimate=cost(12),
        name="attention_backward",
    )(
        length, ids, q2, keys, values, mixed, back, coarse, fine, bcat, inner, inner_o, din, ba,
        normed, mixed,
    )


def post_body(
    local, group, me_ref, mixed_ref, x_ref, wo_ref, acat_ref, bcat_ref, gain_ref, read_ref, mix_ref,
    prev_ref, routes_ref, slot_ref, hidden_ref, ei_ref, inner_ref, data_ref, cols_ref,
):
    reader = read_ref[0:READ_VECTOR].astype(BF)

    def stages(at):
        mixed = mixed_ref[at]
        inner = mm(mixed, acat_ref[...]).astype(BF)
        inner_ref[at] = inner
        yield
        hidden = x_ref[at].astype(F32) + (mm(mixed, wo_ref[...]) + mm(inner, bcat_ref[0]))
        hidden_ref[at] = hidden
        yield
        scale = lax.rsqrt(jnp.mean(hidden * hidden, axis=-1, keepdims=True) + EPSILON)
        ei = (hidden * scale * gain_ref[1:2, :]).astype(BF)
        ei_ref[at] = ei
        yield
        read = mm_nt(reader, ei)
        yield
        logits = read[0:16]
        for index in range(EXPERTS + 4):
            logits = logits + mix_ref[:, index : index + 1] * prev_ref[index : index + 1, at]
        first, second = routes_ref[0:1, at].astype(F32), routes_ref[1:2, at].astype(F32)
        number = iota((16, TILE), 0).astype(F32)
        one = jnp.sum(jnp.where(number == first, logits, 0.0), axis=0, keepdims=True)
        two = jnp.sum(jnp.where(number == second, logits, 0.0), axis=0, keepdims=True)
        top = jnp.maximum(one, two)
        one, two = jnp.exp(one - top), jnp.exp(two - top)
        gate_a, gate_b = one / (one + two), two / (one + two)
        mixes = read[16:20] + read[24:28] + read[32:36]
        shares = []
        for index in range(2):
            left, right = mixes[2 * index : 2 * index + 1], mixes[2 * index + 1 : 2 * index + 2]
            top = jnp.maximum(left, right)
            left, right = jnp.exp(left - top), jnp.exp(right - top)
            shares += [left / (left + right), right / (left + right)]

        def both(value):
            return jnp.where(first == value, gate_a, 0.0) + jnp.where(second == value, gate_b, 0.0)

        gates = jnp.where(number == first, gate_a, 0.0) + jnp.where(number == second, gate_b, 0.0)
        beta_a, beta_b = both(EXPERTS + 2.0), both(EXPERTS + 3.0)
        keep = both(EXPERTS + 1.0) + beta_a * shares[0] + beta_b * shares[2]
        data_ref[0:8, at] = gates[0:8]
        tail = [gate_a, gate_b] + shares + [beta_a, beta_b]
        data_ref[8:16, at] = jnp.concatenate(tail, axis=0)
        yield
        slots = slot_ref[:, at].astype(F32)
        expert = iota((EXPERTS, TILE), 0)
        partner = jnp.bitwise_xor(expert // local, me_ref[0])
        base = ((expert % local) * (group * CAP) + partner * CAP).astype(F32)
        place = jnp.where(slots >= 0, slots + base + 1.0, 0.0)
        expert = expert.astype(F32)
        target_a = jnp.sum(jnp.where(expert == first, place, 0.0), axis=0, keepdims=True) - 1.0
        target_b = jnp.sum(jnp.where(expert == second, place, 0.0), axis=0, keepdims=True) - 1.0
        stack = jnp.concatenate(
            [jnp.zeros((VECTOR_ROW, TILE), F32), beta_a * shares[1], beta_b * shares[3]]
            + [jnp.zeros((2, TILE), F32), target_a, target_b, keep]
            + [jnp.zeros((LANES - KEEP_LANE - 1, TILE), F32)],
            axis=0,
        )
        cols_ref[at] = stack.T

    side_by_side(stages)


def post_send_body(local, group, steps, me_ref, id_ref, slot_all_ref, *refs):
    post_refs, out_refs, (ei_all, data_all) = refs[:16], refs[16:-2], refs[-2:]
    step = pl.program_id(0)

    @pl.when(step < steps)
    def _():
        post_body(local, group, me_ref, *post_refs)
        span = pl.ds(pl.multiple_of(step * STEP, STEP), STEP)
        ei_all[span] = post_refs[12][...]
        data_all[:, span] = post_refs[14][...]

    @pl.when(step >= steps)
    def _():
        send_rows(local, group, step - steps, me_ref, id_ref, slot_all_ref, data_all, ei_all, out_refs)


def post_call(
    local, group, me, ids, mixed, tokens, weight, acat, bcat, gains, reader, mixer, prev, routes, slots
):
    tok_count, width = tokens.shape
    steps = tok_count // STEP
    heights = [local * PIECE] * (group // 2) + [PIECE] * ((group - group // 2) * local)

    def rows_of(columns):
        return pl.BlockSpec((STEP, columns), lambda i: (jnp.minimum(i, steps - 1), 0))

    def lanes_of(height):
        return pl.BlockSpec((height, STEP), lambda i: (0, jnp.minimum(i, steps - 1)))

    return pl.pallas_call(
        functools.partial(post_send_body, local, group, steps),
        grid=(steps + group,),
        in_specs=[
            smem(), smem(), whole(slots.shape), rows_of(width), rows_of(width), whole(weight.shape),
            whole(acat.shape), pl.BlockSpec((1, LANES, width), lambda i: (3, 0, 0)), whole(gains.shape),
            whole(reader.shape), whole(mixer.shape), lanes_of(EXPERTS + 4), lanes_of(2),
            lanes_of(EXPERTS),
        ],
        out_specs=[
            rows_of(width), rows_of(width), rows_of(LANES), lanes_of(16), rows_of(LANES)
        ] + [whole((height, width)) for height in heights],
        out_shape=[
            shape_of(tok_count, width, dtype=F32), shape_of(tok_count, width),
            shape_of(tok_count, LANES), shape_of(16, tok_count, dtype=F32),
            shape_of(tok_count, LANES, dtype=F32),
        ] + [shape_of(height, width) for height in heights],
        scratch_shapes=[pltpu.VMEM((tok_count, width), BF), pltpu.VMEM((16, tok_count), F32)],
        compiler_params=PARAMS,
        cost_estimate=cost(14),
        name="after_attention",
    )(
        me, ids, slots, mixed, tokens, weight, acat, bcat, gains, reader, mixer, prev, routes, slots
    )


def expert_body(
    local_index, pair, per_owner, group, steps, has_grad, kept, *refs
):
    count = len(pair)
    piece_refs, refs = refs[:count], refs[count:]
    cot_refs, refs = refs[:count], refs[count:]
    dn_ref, ou_ref, wg_hbm, wu_hbm, wd_hbm, up_hbm, od_hbm = refs[:7]
    refs = refs[7:]
    if has_grad:
        before_hbm, refs = refs[0], refs[1:]
    refs = refs[kept:]
    back_refs, refs = refs[:count], refs[count:]
    out_refs, refs = refs[:count], refs[count:]
    (
        grad_ref, x_ref, g_ref, gate_ref, pick_ref, dr_ref, zg_ref, zu_ref, dzd_ref, zgt_ref, zut_ref,
        dzdt_ref, racc_ref, xacc_ref, zd_acc, dzg_acc, dzu_acc, h_ref, dg_ref, du_ref, wg_all, wu_all,
        wd_all, up_all, od_all, sems, *rest
    ) = refs
    rows, width = x_ref.shape
    compact = group * RANK
    tile = h_ref.shape[1]

    def copies(step):
        span = pl.ds(pl.multiple_of(step * tile, tile), tile)
        pairs = (
            (wg_hbm.at[local_index, :, span], wg_all),
            (wu_hbm.at[local_index, :, span], wu_all),
            (wd_hbm.at[local_index, span, :], wd_all),
            (up_hbm.at[local_index, :, :, span], up_all),
            (od_hbm.at[local_index, span, :], od_all),
        )
        return [
            pltpu.make_async_copy(source, target.at[step], sems.at[step, place])
            for place, (source, target) in enumerate(pairs)
        ]

    def begin(step):
        for copy in copies(step):
            copy.start()

    begin(0)

    def fold(value):
        place = iota((compact, LANES), 0)
        block = per_owner * group
        inner = place // block * per_owner + place % per_owner
        folded = mm_nt(hot(iota((compact, LANES), 1) % RANK == inner), value)
        place = iota((compact, rows), 0)
        owner = place % block // per_owner
        mine = iota((compact, rows), 1) // CAP + pair[0]
        return jnp.where(mine == owner, folded, 0.0).astype(BF)

    def put(start, value):
        grad_ref[:, pl.ds(start, value.shape[1])] = value.astype(BF)

    for index in range(count):
        span = slice(index * CAP, index * CAP + CAP)
        x_ref[span] = piece_refs[index][0:CAP]
        g_ref[span] = cot_refs[index][...]
        meta = piece_refs[index][CAP:PIECE].astype(F32)
        gate = (meta[0:1] + meta[1:2] + meta[2:3])[:, 0 : 2 * LANES]
        gate_ref[span] = jnp.broadcast_to(gate, (LANES, 2 * LANES)).T[0:CAP]
        lane = (iota((CAP, LANES), 1) // RANK).astype(F32)
        pick_ref[span] = jnp.where(lane == meta[3:4, 0:LANES], 1.0, 0.0)
    chosen = pick_ref[...] > 0.0
    dr = (gate_ref[:, 0:1] * g_ref[...].astype(F32)).astype(BF)
    dr_ref[...] = dr
    zg = jnp.where(chosen, mm(x_ref[...], dn_ref[0]), 0.0).astype(BF)
    zu = jnp.where(chosen, mm(x_ref[...], dn_ref[1]), 0.0).astype(BF)
    dzd = jnp.where(chosen, mm_nt(dr, ou_ref[...]), 0.0).astype(BF)
    zg_ref[...] = zg
    zu_ref[...] = zu
    dzd_ref[...] = dzd
    zgt_ref[...] = fold(zg)
    zut_ref[...] = fold(zu)
    dzdt_ref[...] = fold(dzd)
    for ref in (racc_ref, xacc_ref, zd_acc, dzg_acc, dzu_acc):
        ref[...] = jnp.zeros_like(ref)

    total = steps * tile
    begin(1)
    if has_grad:
        before = pltpu.make_async_copy(before_hbm, rest[0], rest[1])
        before.start()

    def run(step, carry):
        for copy in copies(step):
            copy.wait()

        @pl.when(step + 2 < steps)
        def _():
            begin(step + 2)

        wg_ref, wu_ref, wd_ref = wg_all.at[step], wu_all.at[step], wd_all.at[step]
        up_ref, od_ref = up_all.at[step], od_all.at[step]
        gate = mm(x_ref[...], wg_ref[...]) + mm(zg_ref[...], up_ref[0])
        upper = mm(x_ref[...], wu_ref[...]) + mm(zu_ref[...], up_ref[1])
        share = 0.5 * jnp.tanh(0.5 * gate) + 0.5
        silu = gate * share
        active = (silu * upper).astype(BF)
        h_ref[...] = active
        back = mm_nt(dr_ref[...], wd_ref[...]) + mm_nt(dzd_ref[...], od_ref[...])
        du = (back * silu).astype(BF)
        dg = (back * upper * (share + silu * (1.0 - share))).astype(BF)
        du_ref[...] = du
        dg_ref[...] = dg
        racc_ref[...] += mm(active, wd_ref[...])
        zd_acc[...] += mm(active, od_ref[...])
        xacc_ref[...] += mm_nt(dg, wg_ref[...]) + mm_nt(du, wu_ref[...])
        dzg_acc[...] += mm_nt(dg, up_ref[0])
        dzu_acc[...] += mm_nt(du, up_ref[1])
        at = pl.multiple_of(step * tile, tile)
        put(at, mm(zgt_ref[...], dg_ref[...]))
        put(total + at, mm(zut_ref[...], du_ref[...]))
        put(2 * total + at, mm(dzdt_ref[...], h_ref[...]))
        return carry

    lax.fori_loop(0, steps, run, 0)
    chosen = pick_ref[...] > 0.0
    zd = jnp.where(chosen, zd_acc[...], 0.0).astype(BF)
    dzg = jnp.where(chosen, dzg_acc[...], 0.0).astype(BF)
    dzu = jnp.where(chosen, dzu_acc[...], 0.0).astype(BF)
    result = racc_ref[...] + mm(zd, ou_ref[...])
    gated = (gate_ref[:, 0:1] * result).astype(BF)
    product = g_ref[...].astype(F32) * result.astype(BF).astype(F32)
    dots = jnp.broadcast_to(jnp.sum(product, axis=-1, keepdims=True), (rows, LANES))
    back_rows = (xacc_ref[...] + mm_nt(dzg, dn_ref[0]) + mm_nt(dzu, dn_ref[1])).astype(BF)
    for index in range(count):
        span = slice(index * CAP, index * CAP + CAP)
        out_refs[index][...] = gated[span]
        back_refs[index][0:CAP, :] = back_rows[span]
        column = jnp.concatenate(
            [dots[span], jnp.zeros((2 * LANES - CAP, LANES), F32)], axis=0
        ).T[0:1]
        meta = jnp.concatenate(
            [piece.astype(F32) for piece in split3(column)]
            + [jnp.zeros((META - 3, 2 * LANES), F32)],
            axis=0,
        )
        meta = jnp.concatenate([meta, jnp.zeros((META, width - 2 * LANES), F32)], axis=1)
        back_refs[index][CAP:PIECE, :] = meta.astype(BF)
    base = 3 * total
    place = iota((compact, LANES), 0)
    owner = place % (per_owner * group) // per_owner
    ids = jnp.zeros((compact, LANES), F32)
    for index in range(count):
        meta = piece_refs[index][CAP:PIECE, 0:LANES].astype(F32)
        ids = jnp.where(owner == pair[index], meta[3:4], ids)
    put(base + 3 * width, ids)
    put(base, mm(fold(zd), dr_ref[...]))
    put(base + width, mm(fold(dzg), x_ref[...]))
    put(base + 2 * width, mm(fold(dzu), x_ref[...]))
    if has_grad:
        before.wait()
        grad_ref[...] = grad_ref[...] + rest[0][...]


def expert_call(index, pair, group, per_owner, pieces, cots, before, results, weights):
    gate_w, up_w, down_w, in_down, in_up, out_down, out_up = weights
    width, hidden = gate_w.shape[1:]
    rows = len(pair) * CAP
    steps = hidden // FTILE
    columns = 3 * hidden + 3 * width + LANES
    compact = group * RANK
    has_grad = before is not None
    return pl.pallas_call(
        functools.partial(
            expert_body, index, pair, per_owner, group, steps, has_grad, len(results)
        ),
        grid=(1,),
        in_specs=[
            pl.BlockSpec((PIECE, width), lambda f, row=piece.shape[0] // PIECE > 1: (index * row, 0))
            for piece in pieces
        ]
        + [pl.BlockSpec((CAP, width), lambda f: (index, 0))] * len(pair)
        + [
            pl.BlockSpec((None, 2, width, LANES), lambda f: (index, 0, 0, 0)),
            pl.BlockSpec((None, LANES, width), lambda f: (index, 0, 0)),
        ]
        + [pl.BlockSpec(memory_space=pl.ANY)] * 5
        + [pl.BlockSpec(memory_space=pl.ANY)] * (has_grad + len(results)),
        out_specs=[whole((PIECE, width))] * len(pair)
        + [pl.BlockSpec((CAP, width), lambda f: (index, 0))] * len(pair)
        + [whole((compact, columns))],
        out_shape=[shape_of(PIECE, width)] * len(pair)
        + [shape_of(gate_w.shape[0] * CAP, width)] * len(pair)
        + [shape_of(compact, columns)],
        input_output_aliases={
            2 * len(pair) + 7 + has_grad + place: len(pair) + place for place in range(len(results))
        },
        scratch_shapes=[pltpu.VMEM((rows, width), BF)] * 2
        + [pltpu.VMEM((rows, LANES), F32)] * 2
        + [pltpu.VMEM((rows, width), BF)]
        + [pltpu.VMEM((rows, LANES), BF)] * 3
        + [pltpu.VMEM((compact, rows), BF)] * 3
        + [pltpu.VMEM((rows, width), F32)] * 2
        + [pltpu.VMEM((rows, LANES), F32)] * 3
        + [pltpu.VMEM((rows, FTILE), BF)] * 3
        + [pltpu.VMEM((steps, width, FTILE), BF)] * 2
        + [
            pltpu.VMEM((steps, FTILE, width), BF), pltpu.VMEM((steps, 2, LANES, FTILE), BF),
            pltpu.VMEM((steps, FTILE, LANES), BF), pltpu.SemaphoreType.DMA((steps, 5)),
        ]
        + [pltpu.VMEM((compact, columns), BF), pltpu.SemaphoreType.DMA] * has_grad,
        compiler_params=PARAMS,
        cost_estimate=cost(rows / 21),
        name="expert_layer",
    )(
        *pieces, *cots, in_down, out_up, gate_w, up_w, down_w, in_up, out_down,
        *([before] if has_grad else []), *results,
    )


def spread(cols, index, count):
    return iota((TILE, count), 1).astype(F32) == cols[:, index : index + 1]


def combine_body(
    pieces, len_ref, *refs
):
    back_refs = refs[:pieces]
    (
        routes_ref, data_ref, cols_ref, cot_ref, ei_ref, hidden_ref, gain_ref, wo_ref, acat_ref, bcat_ref,
        table_ref, read_ref, bh_ref, ba_ref, din_ref, bm_ref, back_all, dots_ref,
    ) = refs[pieces:]
    count = pieces * CAP

    @pl.when(pl.program_id(0) == 0)
    def _():
        for index, back_ref in enumerate(back_refs):
            back_all[index * CAP : index * CAP + CAP, :] = back_ref[0:CAP, :]
        dots = [back_ref[CAP:PIECE, 0:CAP].astype(F32) for back_ref in back_refs]
        dots = jnp.concatenate(dots, axis=1)
        dots_ref[...] = jnp.concatenate([dots, jnp.zeros_like(dots)], axis=0).astype(BF)

    table_high, table_low = split2(table_ref[...])
    stack = dots_ref[...]
    vectors = read_ref[READ_VECTOR:READ_ROWS].astype(BF)

    def stages(at):
        start = pl.program_id(0) * WIDE_STEP + at.start
        cols = cols_ref[at]
        chosen_a = hot(spread(cols, TARGET_LANE, count))
        chosen_b = hot(spread(cols, TARGET_LANE + 1, count))
        yield
        routed_a = jnp.sum(mm_nt(stack, chosen_a)[0:8], axis=0, keepdims=True)
        routed_b = jnp.sum(mm_nt(stack, chosen_b)[0:8], axis=0, keepdims=True)
        cot = cot_ref[at]
        cot_f = cot.astype(F32)
        yield
        along_x = jnp.sum(cot_f * ei_ref[at].astype(F32), axis=-1, keepdims=True)
        along_x = jnp.broadcast_to(along_x, (TILE, LANES)).T[0:1]
        yield
        along_c = mm_nt(vectors, cot)
        along_a = along_c[0:1] + along_c[2:3] + along_c[4:5]
        along_b = along_c[1:2] + along_c[3:4] + along_c[5:6]
        yield
        both = chosen_a + chosen_b
        half = count // 2
        back = mm(both[:, :half], back_all[:half]) + mm(both[:, half:], back_all[half:])
        yield
        first, second = routes_ref[0:1, at].astype(F32), routes_ref[1:2, at].astype(F32)
        token = iota((1, TILE), 1) + start
        valid = jnp.where(token < len_ref[0], 1.0, 0.0)
        gate_a, gate_b = data_ref[8:9, at], data_ref[9:10, at]
        share = [data_ref[index : index + 1, at] for index in range(10, 14)]
        beta_a, beta_b = data_ref[14:15, at], data_ref[15:16, at]
        const_a = share[0] * along_x + share[1] * along_a
        const_b = share[2] * along_x + share[3] * along_b

        def here(route):
            return (
                jnp.where(route == EXPERTS + 1.0, along_x, 0.0)
                + jnp.where(route == EXPERTS + 2.0, const_a, 0.0)
                + jnp.where(route == EXPERTS + 3.0, const_b, 0.0)
            )

        dot_a, dot_b = routed_a + here(first), routed_b + here(second)
        mean = gate_a * dot_a + gate_b * dot_b
        chosen_grad_a = valid * gate_a * (dot_a - mean)
        chosen_grad_b = valid * gate_b * (dot_b - mean)
        number = iota((16, TILE), 0).astype(F32)
        logit_grads = jnp.where(number == first, chosen_grad_a, 0.0) + jnp.where(
            number == second, chosen_grad_b, 0.0
        )
        mixes = []
        for index, (beta, along) in enumerate(((beta_a, along_a), (beta_b, along_b))):
            left, right = share[2 * index], share[2 * index + 1]
            weighted = left * along_x + right * along
            mixes += [
                valid * beta * left * (along_x - weighted),
                valid * beta * right * (along - weighted),
            ]
        small = jnp.concatenate(
            [logit_grads] + mixes + [jnp.zeros((LANES - 20, TILE), F32)], axis=0
        ).T
        high, low = split2(small)
        yield
        inside = iota((TILE, 1), 0) + start < len_ref[0]
        grad = jnp.where(inside, cot_f, 0.0)
        back = back + mm(high, table_high) + mm(low, table_high) + mm(high, table_low)
        back = back + cols[:, KEEP_LANE : KEEP_LANE + 1] * grad
        yield
        hidden = hidden_ref[at]
        scale = lax.rsqrt(jnp.mean(hidden * hidden, axis=-1, keepdims=True) + EPSILON)
        normed = hidden * scale
        back = back * gain_ref[1:2, :]
        back = grad + scale * (back - normed * jnp.mean(back * normed, axis=-1, keepdims=True))
        bh_ref[at] = back
        rounded = back.astype(BF)
        ba_ref[at] = rounded
        yield
        inner = mm_nt(rounded, bcat_ref[0]).astype(BF)
        din_ref[at] = inner
        yield
        bm_ref[at] = (mm_nt(rounded, wo_ref[...]) + mm_nt(inner, acat_ref[...])).astype(BF)

    side_by_side(stages, WIDE_STEP)


def combine_call(
    length, backs, routes, data, cols, cotangent, ei, hidden, gains, weight, acat, bcat, table,
    reader,
):
    tok_count, width = cotangent.shape
    pieces = len(backs)
    return pl.pallas_call(
        functools.partial(combine_body, pieces),
        grid=(tok_count // WIDE_STEP,),
        in_specs=[smem()] + [whole(back.shape) for back in backs] + [
            wide(2, WIDE_STEP), wide(16, WIDE_STEP), tall(LANES, WIDE_STEP), tall(width, WIDE_STEP), tall(width, WIDE_STEP), tall(width, WIDE_STEP),
            whole(gains.shape), whole(weight.shape), whole(acat.shape),
            pl.BlockSpec((1, LANES, width), lambda i: (3, 0, 0)), whole(table.shape),
            whole(reader.shape),
        ],
        out_specs=[tall(width, WIDE_STEP), tall(width, WIDE_STEP), tall(LANES, WIDE_STEP), tall(width, WIDE_STEP)],
        out_shape=[
            shape_of(tok_count, width, dtype=F32), shape_of(tok_count, width),
            shape_of(tok_count, LANES), shape_of(tok_count, width),
        ],
        scratch_shapes=[
            pltpu.VMEM((pieces * CAP, width), BF), pltpu.VMEM((2 * META, pieces * CAP), BF)
        ],
        compiler_params=PARAMS,
        cost_estimate=cost(17),
        name="combine_backward",
    )(
        length, *backs, routes, data, cols, cotangent, ei, hidden, gains, weight, acat, bcat, table,
        reader,
    )


def result_body(pieces, len_ref, *refs):
    result_refs = refs[:pieces]
    cols_ref, ei_ref, hidden_ref, table_ref, out_ref, result_all = refs[pieces:]
    count = result_all.shape[0]

    @pl.when(pl.program_id(0) == 0)
    def _():
        for index in range(count // CAP):
            start = index // pieces * CAP
            result_all[index * CAP : index * CAP + CAP] = result_refs[index % pieces][start : start + CAP]

    table_high, table_low = split2(table_ref[...])

    def stages(at):
        cols = cols_ref[at]
        both = hot(spread(cols, TARGET_LANE, count) | spread(cols, TARGET_LANE + 1, count))
        yield
        half = count // 2
        mixture = mm(both[:, :half], result_all[:half]) + mm(both[:, half:], result_all[half:])
        yield
        high, low = split2(cols)
        mixture = mixture + mm(high, table_high) + mm(low, table_high) + mm(high, table_low)
        mixture = mixture + cols[:, KEEP_LANE : KEEP_LANE + 1] * ei_ref[at].astype(F32)
        yield
        inside = iota((TILE, 1), 0) + pl.program_id(0) * STEP + at.start < len_ref[0]
        out_ref[at] = (hidden_ref[at] + jnp.where(inside, mixture, 0.0)).astype(BF)

    side_by_side(stages)


def result_call(length, results, cols, ei, hidden, table):
    tok_count, width = ei.shape
    pieces = len(results)
    return pl.pallas_call(
        functools.partial(result_body, pieces),
        grid=(tok_count // STEP,),
        in_specs=[smem()] + [whole(result.shape) for result in results] + [
            tall(LANES), tall(width), tall(width), whole(table.shape),
        ],
        out_specs=tall(width),
        out_shape=shape_of(tok_count, width),
        scratch_shapes=[pltpu.VMEM((pieces * results[0].shape[0], width), BF)],
        compiler_params=PARAMS,
        cost_estimate=cost(8),
        name="layer_output",
    )(length, *results, cols, ei, hidden, table)


def last_body(
    dq_ref, dk_ref, dv_ref, w_ref, acat_ref, back_ref, x_ref, bh_ref, gain_ref, out_ref
):
    def stages(at):
        parts = [mm_nt(back_ref[at], acat_ref[...])]
        for index, ref in enumerate((dq_ref, dk_ref, dv_ref)):
            parts.append(mm_nt(ref[at], w_ref[index]))
            yield
        total = parts[0] + parts[1] + parts[2] + parts[3]
        x = x_ref[at].astype(F32)
        scale = lax.rsqrt(jnp.mean(x * x, axis=-1, keepdims=True) + EPSILON)
        normed = x * scale
        back = total * gain_ref[0:1, :]
        back = scale * (back - normed * jnp.mean(back * normed, axis=-1, keepdims=True))
        out_ref[at] = (bh_ref[at] + back).astype(BF)

    side_by_side(stages)


def last_call(dq, dk, dv, weights, acat, back, tokens, bh, gains):
    tok_count, width = tokens.shape
    return pl.pallas_call(
        last_body,
        grid=(tok_count // STEP,),
        in_specs=[
            tall(width), tall(width), tall(width), whole(weights.shape), whole(acat.shape),
            tall(LANES), tall(width), tall(width), whole(gains.shape),
        ],
        out_specs=tall(width),
        out_shape=shape_of(tok_count, width),
        compiler_params=PARAMS,
        cost_estimate=cost(9),
        name="after_attention_backward",
    )(dq, dk, dv, weights, acat, back, tokens, bh, gains)


def exchange(value, axes):
    return lax.all_to_all(value, axes, split_axis=0, concat_axis=0, tiled=True)


def gather_all(value, axes, count):
    return exchange(jnp.broadcast_to(value[None], (count,) + value.shape), axes)


def swap(value, partner, group):
    if partner == 0:
        return value
    return lax.ppermute(value, "expert", [(index, index ^ partner) for index in range(group)])


def find_adapters(id_rows):
    count = id_rows.shape[0]
    padded = id_rows.astype(F32)
    if count % LANES:
        padded = jnp.concatenate([padded, jnp.zeros((-count % LANES, LANES), F32)], axis=0)
    return padded.T[0:1, 0:count].astype(jnp.int32)


def sum_expert_body(each, adapters, in_ref, out_ref):
    count, columns = in_ref.shape[0], out_ref.shape[1]
    found = find_adapters(in_ref[:, columns:])
    place = iota((adapters * each, count), 0)
    column = iota((adapters * each, count), 1)
    pick = hot((place // each == found) & (place % each == column % each))
    out_ref[...] = mm(pick, in_ref[:, 0:columns]).astype(BF)


def exchange_expert_grads(grads, group, owners):
    split = min(RANK, owners)
    each, parts = RANK // split, owners // split
    columns = (grads.shape[1] - LANES) // parts
    pieces = grads.reshape(split, each * group, grads.shape[1])
    if parts > 1:
        ids = jnp.broadcast_to(pieces[:, None, :, parts * columns :], (split, parts, each * group, LANES))
        pieces = pieces[:, :, : parts * columns].reshape(split, each * group, parts, columns)
        pieces = jnp.concatenate([pieces.transpose(0, 2, 1, 3), ids], axis=-1)
        pieces = pieces.reshape(owners, each * group, columns + LANES)
    return exchange(pieces, "dp").reshape(owners * group * each, columns + LANES)


def sum_expert_grads(got, adapters, owners):
    columns = got.shape[1] - LANES
    each = RANK // min(RANK, owners)
    return pl.pallas_call(
        functools.partial(sum_expert_body, each, adapters),
        out_shape=shape_of(adapters * each, columns),
        compiler_params=PARAMS,
        cost_estimate=cost(2.2),
        name="expert_gradient_part",
    )(got)


def finish_expert_body(split, adapters, hidden, in_ref, *refs):
    down_ref, up_ref, out_down_ref, out_up_ref = refs[-4:]
    each = RANK // split
    rows = adapters * each
    count = split * rows
    width = down_ref.shape[0]

    def place(value):
        return value // each % adapters * RANK + value // (adapters * each) * each + value % each

    move = hot(iota((count, count), 0) == place(iota((count, count), 1)))
    back = hot(iota((count, count), 1) == place(iota((count, count), 0)))

    def part(start, size):
        span = pl.ds(pl.multiple_of(start, LANES), size)
        rows_of = [in_ref[owner, :, span] for owner in range(split)]
        return jnp.concatenate(rows_of, axis=0)

    step = pl.program_id(0)
    half, base = hidden // 2, 3 * hidden
    up_ref[...] = mm(move, part(step * hidden, hidden))
    out_down_ref[...] = mm_tn(part(2 * hidden + step * half, half), back)
    out_up_ref[...] = mm(move, part(base + step * (width // 2), width // 2))
    down_ref[...] = mm_tn(part(base + (1 + step) * width, width), back)


def finish_expert_call(index, local, everything, outs, adapters, width, hidden):
    owners, rows, columns = everything.shape
    total = adapters * RANK
    shapes = [(local, 2, width, total), (local, 2, total, hidden), (local, hidden, total),
              (local, total, width)]
    specs = [
        pl.BlockSpec((None, None, width, total), lambda i: (index, i, 0, 0)),
        pl.BlockSpec((None, None, total, hidden), lambda i: (index, i, 0, 0)),
        pl.BlockSpec((None, hidden // 2, total), lambda i: (index, i, 0)),
        pl.BlockSpec((None, total, width // 2), lambda i: (index, 0, i)),
    ]
    return pl.pallas_call(
        functools.partial(finish_expert_body, owners, adapters, hidden),
        grid=(2,),
        in_specs=[whole(everything.shape)] + [pl.BlockSpec(memory_space=pl.ANY)] * len(outs),
        out_specs=specs,
        out_shape=[shape_of(*shape, dtype=F32) for shape in shapes],
        input_output_aliases={1 + place: place for place in range(len(outs))},
        compiler_params=PARAMS,
        cost_estimate=cost(4),
        name="expert_gradient_sums",
    )(everything, *outs)


def spread_expert_grads(own, adapters, owners):
    split = min(RANK, owners)
    each, parts = RANK // split, owners // split
    everything = gather_all(own, "dp", owners)
    everything = everything.reshape(split, parts, adapters, each, own.shape[1])
    everything = everything.transpose(2, 0, 3, 1, 4)
    return everything.reshape(adapters * RANK, parts * own.shape[1]).astype(F32)


def expert_sums(owned, adapters, owners, width, hidden):
    sums = [spread_expert_grads(value, adapters, owners) for value in owned]
    base = 3 * hidden
    up = [[value[:, 0:hidden], value[:, hidden : 2 * hidden]] for value in sums]
    down = [
        [value[:, base + width * part : base + width * (part + 1)].T for part in (1, 2)]
        for value in sums
    ]
    return (
        jnp.stack([jnp.stack(value) for value in down]),
        jnp.stack([jnp.stack(value) for value in up]),
        jnp.stack([value[:, 2 * hidden : base].T for value in sums]),
        jnp.stack([value[:, base : base + width] for value in sums]),
    )


def finish_adapter_body(adapters, me_ref, *refs):
    piece_refs, (down_ref, up_ref, in_ref) = refs[:-3], refs[-3:]
    half = in_ref.shape[3]
    owners, group = piece_refs[0].shape[0], len(piece_refs)
    step = pl.program_id(0)

    @pl.when(step == 0)
    def _():
        for other in range(group):
            place = jnp.bitwise_xor(me_ref[0], other)
            for owner in range(owners):
                in_ref[owner * (group // 2) + place // 2, place % 2] = piece_refs[other][owner]

    count = RANK * adapters

    def place(value):
        return value % adapters * RANK + value // adapters

    move = hot(iota((count, count), 0) == place(iota((count, count), 1)))
    back = hot(iota((count, count), 1) == place(iota((count, count), 0)))
    for part in range(2):
        span = slice(part * half, part * half + half)
        for kind in range(2):
            first = pl.multiple_of((kind * 4 + step * 2) * adapters, 2 * adapters)
            both = in_ref[:, part, pl.ds(first, 2 * adapters), :].astype(F32)
            for index in range(2):
                rows = both[:, index * adapters : (index + 1) * adapters]
                rows = rows.reshape(count, half).astype(BF)
                if kind == 0:
                    down_ref[index, span, :] = mm_tn(rows, back)
                else:
                    up_ref[index, :, span] = mm(move, rows)


def sum_adapter_body(kinds, adapters, in_ref, out_ref):
    count, columns = in_ref.shape[0], out_ref.shape[-1]
    found = find_adapters(in_ref[:, columns:])
    place = iota((adapters * kinds, count), 0)
    column = iota((adapters * kinds, count), 1)
    pick = hot((place % adapters == found) & (place // adapters == column % kinds))
    own = mm(pick, in_ref[:, 0:columns]).astype(BF)
    for index in range(out_ref.shape[0]):
        out_ref[index] = own


def adapter_sums(grads, meanwhile, later, finish, parts, ids, adapters, owners, group, width):
    axes, everyone = ("dp", "expert"), owners * group
    if everyone == 2 * RANK and group == 4:
        kinds = 8
        got = exchange(grads.reshape(everyone, kinds, grads.shape[1]), axes)
        got, meanwhile = lax.optimization_barrier((got, meanwhile))
        own = pl.pallas_call(
            functools.partial(sum_adapter_body, kinds, adapters),
            out_shape=shape_of(owners, kinds * adapters, width // 2),
            compiler_params=PARAMS,
            cost_estimate=cost(2.0),
            name="adapter_gradient_part",
        )(got.reshape(everyone * kinds, grads.shape[1]))
        mine = exchange(own, "dp")
        mine, later = lax.optimization_barrier((mine, later))
        across = swap(mine, 2, group)
        full = [mine, swap(mine, 1, group), across, swap(across, 1, group)]
        total = adapters * RANK
        down, upper = pl.pallas_call(
            functools.partial(finish_adapter_body, adapters),
            grid=(2,),
            in_specs=[smem()] + [whole(piece.shape) for piece in full],
            out_specs=[
                pl.BlockSpec((2, width, total), lambda i: (i, 0, 0)),
                pl.BlockSpec((2, total, width), lambda i: (i, 0, 0)),
            ],
            out_shape=[shape_of(4, width, total, dtype=F32), shape_of(4, total, width, dtype=F32)],
            scratch_shapes=[pltpu.VMEM((RANK, 2, kinds * adapters, width // 2), BF)],
            compiler_params=PARAMS,
            cost_estimate=cost(3.6),
            name="adapter_gradient_sums",
        )(lax.axis_index("expert").reshape(1).astype(jnp.int32), *full)
        (down, upper), later, parts = lax.optimization_barrier(((down, upper), later, parts))
        return down, upper, meanwhile, finish(later, parts)
    later = finish(later, parts)
    all_ids = exchange(jnp.broadcast_to(ids, (everyone,)), axes)
    pieces = grads.reshape(everyone, RANK * 4 * 2 * width // everyone)
    got = exchange(pieces, axes)
    pick = (jnp.arange(adapters, dtype=jnp.int32)[:, None] == all_ids[None, :]).astype(BF)
    own = jnp.dot(pick, got, preferred_element_type=F32).astype(BF)
    full = gather_all(own, axes, everyone)
    full = full.reshape(RANK, everyone // RANK, adapters, -1).transpose(2, 0, 1, 3)
    full = full.reshape(adapters * RANK, 4, 2, width).astype(F32)
    return full[:, :, 0].transpose(1, 2, 0), full[:, :, 1].transpose(1, 0, 2), meanwhile, later


def body(
    tokens,
    cotangent,
    lengths,
    adapter_ids,
    routes,
    prev_logits,
    norm_gains,
    input_weights,
    output_weight,
    adapter_down,
    adapter_up,
    router,
    residual_mix,
    constant_mix,
    constant_vectors,
    expert_gate,
    expert_up,
    expert_down,
    expert_adapter_down,
    expert_adapter_up,
    output_adapter_down,
    output_adapter_up,
):
    tok_count, width = tokens.shape
    hidden_width = expert_gate.shape[2]
    group, owners = lax.axis_size("expert"), lax.axis_size("dp")
    local = expert_gate.shape[0]
    adapters = adapter_down.shape[-1] // RANK
    angles = [jnp.asarray(table) for table in turn_tables(tok_count)]
    weights = (
        expert_gate, expert_up, expert_down, expert_adapter_down, expert_adapter_up,
        output_adapter_down, output_adapter_up,
    )
    per_owner = RANK // min(RANK, owners)
    everyone = owners * group
    me = lax.axis_index("expert")

    me = me.reshape(1).astype(jnp.int32)

    routes, prev_logits = routes.T, prev_logits.T
    slots, *grad_sends = route_call(local, group, lengths, me, routes, cotangent)
    cots = [swap(value, partner, group) for partner, value in enumerate(grad_sends)]
    normed, inner, acat, bcat, table, mixer, reader, keys, values, mixed, q2 = pre_attend_call(
        lengths, adapter_ids, tokens, norm_gains, input_weights, adapter_down, adapter_up, *angles,
        router.T, constant_mix.T, constant_vectors, residual_mix,
    )
    hidden, ei, inner_o, data, cols, *sends = post_call(
        local, group, me, adapter_ids, mixed, tokens, output_weight, acat, bcat, norm_gains, reader, mixer, prev_logits,
        routes, slots,
    )
    sends, cots = lax.optimization_barrier((sends, cots))
    near, far = tuple(range(group // 2)), tuple(range(group // 2, group))
    sent_near = [swap(sends[partner], partner, group) for partner in near]
    sent_far = []
    for index in range(local):
        pieces = [sends[group // 2 + place * local + index] for place in range(len(far))]
        if index > 0:
            pieces, sent_near = lax.optimization_barrier((pieces, sent_near))
        sent_far.append([swap(piece, partner, group) for piece, partner in zip(pieces, far)])
    backs = [[None] * group for _ in range(local)]
    results = [None] * group
    calls = []
    for index in range(local - 1):
        calls += [(index, near), (index, far)]
    calls += [(local - 1, near[1:] + far), (local - 1, near[:1])]
    grads, owned, parts = [None] * local, [], []
    sums = functools.partial(sum_expert_grads, adapters=adapters, owners=owners)
    last = None
    for index, some in calls:
        pieces = [
            sent_near[partner] if partner in near else sent_far[index][partner - len(near)]
            for partner in some
        ]
        if last is not None:
            pieces, last = lax.optimization_barrier((pieces, last))
        if (index, some) == calls[-1]:
            parts, last = lax.optimization_barrier((parts, last))
            owned = [sums(part) for part in parts]
            pieces, backs[:index], owned = lax.optimization_barrier((pieces, backs[:index], owned))
        outs = expert_call(
            index, some, group, per_owner, pieces, [cots[partner] for partner in some], grads[index],
            [results[partner] for partner in some] if index else [], weights,
        )
        grads[index] = last = outs[-1]
        for place, partner in enumerate(some):
            backs[index][partner] = swap(outs[place], partner, group)
            results[partner] = outs[len(some) + place]
        if index < local - 1 and some == far:
            parts.append(exchange_expert_grads(last, group, owners))
    backs = [value for some in backs for value in some]
    parts.append(exchange_expert_grads(last, group, owners))
    gather = functools.partial(lax.all_gather, axis_name="dp", axis=0, tiled=False)
    if owners <= RANK:
        owned = [gather(own) for own in owned]
    back_hidden, back_attention, back_inner_o, back_mixed = combine_call(
        lengths, backs, routes, data, cols, cotangent, ei, hidden, norm_gains, output_weight, acat, bcat,
        table, reader,
    )
    flat, back_mixed = lax.optimization_barrier((results, back_mixed))
    flat = [swap(value, partner, group) for partner, value in enumerate(flat)]

    packed = everyone == 2 * RANK and group == 4
    dq, dk, dv, back_inner, adapter_grads = attend_back_call(
        packed, lengths, adapter_ids, q2, keys, values, mixed, back_mixed, *angles, bcat, inner, inner_o,
        back_inner_o, back_attention, normed,
    )
    parts[-1], adapter_grads, flat, owned = lax.optimization_barrier(
        (parts[-1], adapter_grads, flat, owned)
    )
    own = sums(parts[-1])
    adapter_grads, own, flat = lax.optimization_barrier((adapter_grads, own, flat))
    owned.append(gather(own) if owners <= RANK else own)
    layer_out = result_call(lengths, flat, cols, ei, hidden, table)
    input_back = last_call(
        dq, dk, dv, input_weights, acat, back_inner, tokens, back_hidden, norm_gains
    )
    outs = []
    if owners <= RANK:
        for index, own in enumerate(owned[:-1]):
            outs = finish_expert_call(index, local, own, outs, adapters, width, hidden_width)
    def finish(later, part):
        input_back, outs = later
        if owners <= RANK:
            return input_back, finish_expert_call(
                local - 1, local, part, outs, adapters, width, hidden_width
            )
        return input_back, expert_sums(owned, adapters, owners, width, hidden_width)

    down_sum, upper_sum, layer_out, (input_back, outs) = adapter_sums(
        adapter_grads, layer_out, (input_back, outs), finish, owned[-1], adapter_ids, adapters, owners, group, width
    )
    in_down_sum, in_up_sum, out_down_sum, out_up_sum = outs
    return (
        layer_out,
        input_back,
        down_sum,
        upper_sum,
        in_down_sum,
        in_up_sum,
        out_down_sum,
        out_up_sum,
    )


def solution(mesh):
    tokens_spec, copied = P(("dp", "expert"), None), P()
    owned = P("expert")
    placed = (
        (tokens_spec, tokens_spec, P(("dp", "expert")), P(("dp", "expert")), tokens_spec, tokens_spec)
        + (copied,) * 9
        + (owned,) * 7
    )
    return jax.shard_map(
        body,
        mesh=mesh,
        in_specs=placed,
        out_specs=(tokens_spec, tokens_spec, copied, copied) + (owned,) * 4,
        check_vma=False,
    )
```
